32 devices in a mesh: dp: 8 (over z, y), tensor: 4 (over x, core).
Axes of the slice: x: 2, y: 2, z: 4, core: 2. Of those that a mesh axis runs over, the one named last changes fastest.
Arguments:
- tokens: bfloat16 [16384, 768], P(('dp', 'tensor')), may hold values from -6 to 6
- bank: bfloat16 [16, 4096, 768], P('dp', 'tensor'), may hold values from -6 to 6
- prefix: int32 [16], P('dp'), may hold values from 102 to 512
- blocks: int32 [16, 16], P('dp'), may hold values from 0 to 63, all different within a row
- out_grad: bfloat16 [16384, 768], P(('dp', 'tensor')), may hold values from -6 to 6
- selfq_weight: float32 [768, 768], P('dp', 'tensor'), may hold values from -0.21875 to 0.21875
- selfq_bias: float32 [768], P('tensor'), may hold values from -3 to 3
- selfk_weight: float32 [768, 768], P('dp', 'tensor'), may hold values from -0.21875 to 0.21875
- selfv_weight: float32 [768, 768], P('dp', 'tensor'), may hold values from -0.21875 to 0.21875
- selfv_bias: float32 [768], P('tensor'), may hold values from -3 to 3
- selfo_weight: float32 [768, 768], P('tensor', 'dp'), may hold values from -2.5 to 2.5
- selfo_bias: float32 [768], replicated, may hold values from -3 to 3
- first_gain: float32 [768], replicated, may hold values from 0.5 to 1.5
- first_shift: float32 [768], replicated, may hold values from -2 to 2
- crossq_weight: float32 [768, 768], P('dp', 'tensor'), may hold values from -0.21875 to 0.21875
- crossq_bias: float32 [768], P('tensor'), may hold values from -3 to 3
- crossk_weight: float32 [768, 768], P('dp', 'tensor'), may hold values from -0.21875 to 0.21875
- crossv_weight: float32 [768, 768], P('dp', 'tensor'), may hold values from -0.21875 to 0.21875
- crossv_bias: float32 [768], P('tensor'), may hold values from -3 to 3
- crosso_weight: float32 [768, 768], P('tensor', 'dp'), may hold values from -2.5 to 2.5
- crosso_bias: float32 [768], replicated, may hold values from -3 to 3
- second_gain: float32 [768], replicated, may hold values from 0.5 to 1.5
- second_shift: float32 [768], replicated, may hold values from -2 to 2
- expand_weight: float32 [768, 3072], P('dp', 'tensor'), may hold values from -0.21875 to 0.21875
- expand_bias: float32 [3072], P('tensor'), may hold values from -3 to 3
- shrink_weight: float32 [3072, 768], P('tensor', 'dp'), may hold values from -0.15625 to 0.15625
- shrink_bias: float32 [768], replicated, may hold values from -3 to 3
- third_gain: float32 [768], replicated, may hold values from 0.5 to 1.5
- third_shift: float32 [768], replicated, may hold values from -2 to 2
Outputs:
- out_act: bfloat16 [16384, 768], P(('dp', 'tensor'))
- in_grad: bfloat16 [16384, 768], P(('dp', 'tensor'))
- bank_grad: float32 [16, 4096, 768], P('dp', 'tensor')
- selfq_wgrad: float32 [768, 768], P('dp', 'tensor')
- selfq_bgrad: float32 [768], P('tensor')
- selfk_wgrad: float32 [768, 768], P('dp', 'tensor')
- selfv_wgrad: float32 [768, 768], P('dp', 'tensor')
- selfv_bgrad: float32 [768], P('tensor')
- selfo_wgrad: float32 [768, 768], P('tensor', 'dp')
- selfo_bgrad: float32 [768], replicated
- first_ggrad: float32 [768], replicated
- first_sgrad: float32 [768], replicated
- crossq_wgrad: float32 [768, 768], P('dp', 'tensor')
- crossq_bgrad: float32 [768], P('tensor')
- crossk_wgrad: float32 [768, 768], P('dp', 'tensor')
- crossv_wgrad: float32 [768, 768], P('dp', 'tensor')
- crossv_bgrad: float32 [768], P('tensor')
- crosso_wgrad: float32 [768, 768], P('tensor', 'dp')
- crosso_bgrad: float32 [768], replicated
- second_ggrad: float32 [768], replicated
- second_sgrad: float32 [768], replicated
- expand_wgrad: float32 [768, 3072], P('dp', 'tensor')
- expand_bgrad: float32 [3072], P('tensor')
- shrink_wgrad: float32 [3072, 768], P('tensor', 'dp')
- shrink_bgrad: float32 [768], replicated
- third_ggrad: float32 [768], replicated
- third_sgrad: float32 [768], replicated
The draws below stay inside these ranges and needn't reach their ends.
Inputs may be any that keep to these rules, and one draw needn't show every extreme that they name: The 16 blocks of one sequence are distinct.
All inputs are finite; a program needn't handle non-finite values.
Results may differ from the reference program's by a relative error of at most 0.025.
Values may be sent and summed in bfloat16 or wider, within the bound.
No kernel may reach another device: no remote copies, remote signals or barrier semaphores. Data moves between devices by JAX's collectives and lax.ppermute only.
A program may use at most 192 MiB of HBM per device.

```python
import math
import jax
import jax.numpy as jnp
from jax import lax

D = 768
H = 12
HD = 64
FF = 3072
L = 1024
BLK = 64
NBLK = 16
NB = 64
R = 1024
BANK = 4096
SEQS = 16
TOKENS = 16384


def with_ends(values, rng, least, top_value):
    shape = values.shape
    place = [jax.random.randint(jax.random.fold_in(rng, axis), (), 0, shape[axis]) for axis in range(len(shape))]
    values = values.at[tuple(place)].set(least)
    longest = shape.index(max(shape))
    place[longest] = (place[longest] + 1) % shape[longest]
    return values.at[tuple(place)].set(top_value)


def shard_levels(key, extent, cuts, low, largest):
    loudness, own = 1.0, jax.random.fold_in(key, 6)
    for dim, parts in cuts:
        heights = jnp.exp(jax.random.uniform(jax.random.fold_in(own, dim), (parts,), jnp.float32, low / len(cuts), largest / len(cuts)))
        loudness = loudness * jnp.repeat(heights, extent[dim] // parts).reshape([-1 if axis == dim else 1 for axis in range(len(extent))])
    return loudness


def distinct(own_key, rows, count, top, lift):
    order = jax.random.permutation(jax.random.fold_in(own_key, 1), count)
    pull = order
    for power in range(3):
        pull = pull * pull // count
    pull = pull * lift // count
    lots = jax.random.randint(jax.random.fold_in(own_key, 2), (rows, count), 0, 4096) + pull
    holders = jax.random.permutation(jax.random.fold_in(own_key, 3), rows)[jnp.arange(count) % rows]
    lots = jnp.where(jnp.arange(rows)[:, None] == holders[None, :], 1 << 14, lots)
    score = lots * count + jnp.arange(count)
    return lax.top_k(score.astype(jnp.int32), top)[1].astype(jnp.int32)


def normal_values(own_key, shape, deviation, bound, split=(), held_as=jnp.bfloat16):
    loudness = shard_levels(own_key, shape, split, -0.22, 0.18) if split else 1.0
    drawn = jax.random.normal(own_key, shape, jnp.float32) * deviation * loudness
    return jnp.minimum(jnp.maximum(drawn, -bound), bound).astype(held_as)


def setup_inputs(seed: int = 0) -> dict:
    keys = jax.random.split(jax.random.key(seed), 30)
    return {
        "tokens": normal_values(keys[0], (TOKENS, D), 1.0, 6.0, ((0, 32),)),
        "bank": normal_values(keys[1], (SEQS, BANK, D), 1.0, 6.0, ((0, 8), (1, 4))),
        "prefix": with_ends(jax.random.randint(keys[2], (SEQS,), L // 10, L // 2 + 1), jax.random.fold_in(keys[2], 1), L // 10, (L // 2 + 1) - 1).astype(jnp.int32),
        "blocks": distinct(keys[3], SEQS, NB, NBLK, 0),
        "out_grad": normal_values(keys[4], (TOKENS, D), 1.0, 6.0, ((0, 32),)),
        "selfq_weight": normal_values(keys[5], (D, D), D ** -0.5, 0.21875, ((0, 8), (1, 4)), jnp.float32),
        "selfq_bias": normal_values(keys[6], (D,), 0.5, 3.0, ((0, 4),), jnp.float32),
        "selfk_weight": normal_values(keys[7], (D, D), D ** -0.5, 0.21875, ((0, 8), (1, 4)), jnp.float32),
        "selfv_weight": normal_values(keys[8], (D, D), D ** -0.5, 0.21875, ((0, 8), (1, 4)), jnp.float32),
        "selfv_bias": normal_values(keys[9], (D,), 0.5, 3.0, ((0, 4),), jnp.float32),
        "selfo_weight": normal_values(keys[10], (D, D), (max(D // 128, 4)) ** -0.5, 2.5, ((0, 4), (1, 8)), jnp.float32),
        "selfo_bias": normal_values(keys[11], (D,), 0.5, 3.0, (), jnp.float32),
        "first_gain": jnp.clip(1.0 + 0.1 * jax.random.normal(keys[12], (D,), jnp.float32), 0.5, 1.5),
        "first_shift": normal_values(keys[13], (D,), 0.3, 2.0, (), jnp.float32),
        "crossq_weight": normal_values(keys[14], (D, D), D ** -0.5, 0.21875, ((0, 8), (1, 4)), jnp.float32),
        "crossq_bias": normal_values(keys[15], (D,), 0.5, 3.0, ((0, 4),), jnp.float32),
        "crossk_weight": normal_values(keys[16], (D, D), D ** -0.5, 0.21875, ((0, 8), (1, 4)), jnp.float32),
        "crossv_weight": normal_values(keys[17], (D, D), D ** -0.5, 0.21875, ((0, 8), (1, 4)), jnp.float32),
        "crossv_bias": normal_values(keys[18], (D,), 0.5, 3.0, ((0, 4),), jnp.float32),
        "crosso_weight": normal_values(keys[19], (D, D), (max(D // 128, 4)) ** -0.5, 2.5, ((0, 4), (1, 8)), jnp.float32),
        "crosso_bias": normal_values(keys[20], (D,), 0.5, 3.0, (), jnp.float32),
        "second_gain": jnp.clip(1.0 + 0.1 * jax.random.normal(keys[21], (D,), jnp.float32), 0.5, 1.5),
        "second_shift": normal_values(keys[22], (D,), 0.3, 2.0, (), jnp.float32),
        "expand_weight": normal_values(keys[23], (D, FF), D ** -0.5, 0.21875, ((0, 8), (1, 4)), jnp.float32),
        "expand_bias": normal_values(keys[24], (FF,), 0.5, 3.0, ((0, 4),), jnp.float32),
        "shrink_weight": normal_values(keys[25], (FF, D), (FF // 2) ** -0.5, 0.15625, ((0, 4), (1, 8)), jnp.float32),
        "shrink_bias": normal_values(keys[26], (D,), 0.5, 3.0, (), jnp.float32),
        "third_gain": jnp.clip(1.0 + 0.1 * jax.random.normal(keys[27], (D,), jnp.float32), 0.5, 1.5),
        "third_shift": normal_values(keys[28], (D,), 0.3, 2.0, (), jnp.float32),
    }


@jax.custom_vjp
def low(v):
    return lax.optimization_barrier(v.astype(jnp.bfloat16)).astype(jnp.float32)

@jax.custom_vjp
def low_back(v):
    return v

def low_keep(v):
    return (low(v), None)

def low_pass(kept, grad):
    return (grad,)

def back_keep(v):
    return (v, None)

def back_low(kept, grad):
    return (low(grad),)
low.defvjp(low_keep, low_pass)
low_back.defvjp(back_keep, back_low)
EPS = 1e-05
NEGATIVE = -1e+30

def matmul(left_mat, right_mat):
    return jnp.dot(left_mat, right_mat, precision=lax.Precision.HIGHEST, preferred_element_type=jnp.float32)

def layer_norm(resid_sum, norm_gain, norm_shift):
    center = resid_sum - lax.optimization_barrier(jnp.mean(resid_sum, axis=-1, keepdims=True))
    spread = lax.optimization_barrier(jnp.mean(center * center, axis=-1, keepdims=True))
    return center * lax.rsqrt(spread + EPS) * norm_gain + norm_shift

def attention(source, memory, query_mat, query_bias, key_mat, value_mat, value_bias, out_mat, out_bias, prefix_len):
    query_scale = 1.0 / math.sqrt(HD)
    queries = low(low_back((matmul(source, query_mat) + query_bias) * query_scale)).reshape(-1, H, HD)
    key_heads = low(low_back(matmul(memory, key_mat))).reshape(-1, H, HD)
    value_heads = low(low_back(matmul(memory, value_mat) + value_bias)).reshape(-1, H, HD)
    query_rows = queries.shape[0]
    memory_rows = key_heads.shape[0]
    rows_block = min(512, query_rows)
    block_count = query_rows // rows_block
    query_blocks = queries.reshape(block_count, rows_block, H, HD)
    starts = jnp.arange(block_count, dtype=jnp.int32) * rows_block

    def one_block(item):
        query_block, start = item
        scores = low_back(jnp.einsum('qhd,khd->hqk', query_block, key_heads, precision=lax.Precision.HIGHEST))
        if prefix_len is not None:
            query_pos = start + jnp.arange(rows_block, dtype=jnp.int32)
            key_pos = jnp.arange(memory_rows, dtype=jnp.int32)
            visible = (key_pos[None, :] <= query_pos[:, None]) | (key_pos[None, :] < prefix_len)
            scores = jnp.where(visible[None], scores, NEGATIVE)
        soft_probs = low(jax.nn.softmax(scores, axis=-1))
        return jnp.einsum('hqk,khd->qhd', soft_probs, value_heads, precision=lax.Precision.HIGHEST)
    mixed_heads = lax.map(jax.checkpoint(one_block), (query_blocks, starts))
    mixed_heads = low_back(low(mixed_heads.reshape(query_rows, H * HD)))
    return low_back(matmul(mixed_heads, out_mat) + out_bias)

def layer(params, seq_rows, bank_rows, prefix_len, block_ids):
    selfq_weight, selfq_bias, selfk_weight, selfv_weight, selfv_bias, selfo_weight, selfo_bias, first_gain, first_shift, crossq_weight, crossq_bias, crossk_weight, crossv_weight, crossv_bias, crosso_weight, crosso_bias, second_gain, second_shift, expand_weight, expand_bias, shrink_weight, shrink_bias, third_gain, third_shift = params
    source = low(seq_rows)
    self_branch = attention(source, source, low(selfq_weight), selfq_bias, low(selfk_weight), low(selfv_weight), selfv_bias, low(selfo_weight), selfo_bias, prefix_len)
    first_out = layer_norm(seq_rows + self_branch, first_gain, first_shift)
    select = (block_ids[:, None] == jnp.arange(NB, dtype=jnp.int32)[None, :]).astype(jnp.float32)
    fetched = jnp.einsum('sb,bre->sre', select, bank_rows.reshape(NB, BLK, D), precision=lax.Precision.HIGHEST).reshape(R, D)
    cross_branch = attention(low(first_out), fetched, low(crossq_weight), crossq_bias, low(crossk_weight), low(crossv_weight), crossv_bias, low(crosso_weight), crosso_bias, None)
    second_out = layer_norm(first_out + cross_branch, second_gain, second_shift)
    inner_sum = low_back(matmul(low(second_out), low(expand_weight)) + expand_bias)
    hidden = low(jax.nn.gelu(inner_sum, approximate=False))
    feed_branch = low_back(matmul(hidden, low(shrink_weight)) + shrink_bias)
    return layer_norm(second_out + feed_branch, third_gain, third_shift)

def add_up(former, latter):
    return former + latter

def reference(tokens, bank, prefix, blocks, out_grad, selfq_weight, selfq_bias, selfk_weight, selfv_weight, selfv_bias, selfo_weight, selfo_bias, first_gain, first_shift, crossq_weight, crossq_bias, crossk_weight, crossv_weight, crossv_bias, crosso_weight, crosso_bias, second_gain, second_shift, expand_weight, expand_bias, shrink_weight, shrink_bias, third_gain, third_shift):
    params = (selfq_weight, selfq_bias, selfk_weight, selfv_weight, selfv_bias, selfo_weight, selfo_bias, first_gain, first_shift, crossq_weight, crossq_bias, crossk_weight, crossv_weight, crossv_bias, crosso_weight, crosso_bias, second_gain, second_shift, expand_weight, expand_bias, shrink_weight, shrink_bias, third_gain, third_shift)
    rows_all = tokens.astype(jnp.float32).reshape(SEQS, L, D)
    cot_all = out_grad.astype(jnp.float32).reshape(SEQS, L, D)
    bank_all = bank.astype(jnp.float32)

    def advance(totals, batch_item):
        seq_rows, bank_rows, prefix_len, block_ids, cotangent = batch_item

        def forward(weights, rows_in, bank_in):
            return layer(weights, rows_in, bank_in, prefix_len, block_ids)
        result, pullback = jax.vjp(forward, params, seq_rows, bank_rows)
        weight_grads, rows_grad, bank_part = pullback(cotangent)
        totals = jax.tree.map(add_up, totals, weight_grads)
        return (totals, (result, rows_grad, bank_part))
    zero_sums = jax.tree.map(jnp.zeros_like, params)
    totals, (results, rows_grads, bank_grads) = lax.scan(advance, zero_sums, (rows_all, bank_all, prefix, blocks, cot_all))
    return (results.reshape(TOKENS, D).astype(jnp.bfloat16), rows_grads.reshape(TOKENS, D).astype(jnp.bfloat16), bank_grads, totals[0], totals[1], totals[2], totals[3], totals[4], totals[5], totals[6], totals[7], totals[8], totals[9], totals[10], totals[11], totals[12], totals[13], totals[14], totals[15], totals[16], totals[17], totals[18], totals[19], totals[20], totals[21], totals[22], totals[23])
```

```python
import functools
import math

import jax
import jax.numpy as jnp
from jax import lax
from jax.experimental import pallas as pl
from jax.experimental.pallas import tpu as pltpu
from jax.sharding import PartitionSpec as P

HD = 64
BLK = 64
NBLK = 16
EPS = 1e-05
NEGATIVE = -1e30
BF = jnp.bfloat16
F32 = jnp.float32

NT = (((1,), (1,)), ((), ()))
NN = (((1,), (0,)), ((), ()))
TN = (((0,), (0,)), ((), ()))

CORE_SWAP = ((0, 1), (1, 0), (2, 3), (3, 2))
X_SWAP = ((0, 2), (2, 0), (1, 3), (3, 1))
VMEM_LIMIT = 48 << 20


def mm(left, right, dims=NN):
    return lax.dot_general(left, right, dims, preferred_element_type=F32)


def swap_core(value):
    return lax.ppermute(value, "tensor", CORE_SWAP)


def swap_x(value):
    return lax.ppermute(value, "tensor", X_SWAP)


def swap_dp(value, bit):
    count = lax.axis_size("dp")
    return lax.ppermute(value, "dp", tuple((i, i ^ bit) for i in range(count)))


def dp_bits():
    count = lax.axis_size("dp")
    bits = []
    bit = count // 2
    while bit >= 1:
        bits.append(bit)
        bit //= 2
    return bits


def self_fwd_kernel(info, q_ref, k_ref, v_ref, o_ref, lse_ref):
    half = q_ref.shape[1]
    first = info[0]
    second = 1 - first
    prefix = info[1]
    key_pos = lax.broadcasted_iota(jnp.int32, (half, half), 0)
    query_pos = lax.broadcasted_iota(jnp.int32, (half, half), 1)
    causal = key_pos <= query_pos
    seen = causal | (key_pos < prefix)
    for h in range(2):
        cols = slice(HD * h, HD * h + HD)
        k0 = k_ref[first, :, cols]
        v0 = v_ref[first, :, cols]
        score = mm(k0, q_ref[first, :, cols], NT)
        score = jnp.where(seen, score, NEGATIVE)
        top = jnp.max(score, 0, keepdims=True)
        expo = jnp.exp(score - top)
        total = jnp.sum(expo, 0, keepdims=True)
        mixed = mm(v0, expo.astype(BF), TN) / total
        o_ref[first, :, cols] = mixed.T.astype(BF)
        lse_ref[0, h, pl.ds(first, 1), :] = top + jnp.log(total)

        k1 = k_ref[second, :, cols]
        v1 = v_ref[second, :, cols]
        q1 = q_ref[second, :, cols]
        score_a = mm(k0, q1, NT)
        score_b = jnp.where(causal, mm(k1, q1, NT), NEGATIVE)
        top = jnp.maximum(
            jnp.max(score_a, 0, keepdims=True), jnp.max(score_b, 0, keepdims=True)
        )
        expo_a = jnp.exp(score_a - top)
        expo_b = jnp.exp(score_b - top)
        total = jnp.sum(expo_a, 0, keepdims=True) + jnp.sum(expo_b, 0, keepdims=True)
        mixed = (mm(v0, expo_a.astype(BF), TN) + mm(v1, expo_b.astype(BF), TN)) / total
        o_ref[second, :, cols] = mixed.T.astype(BF)
        lse_ref[0, h, pl.ds(second, 1), :] = top + jnp.log(total)


def self_forward(info, qkv):
    half, width = qkv.shape[1], qkv.shape[2] // 3
    pairs = width // 128

    def spec(which):
        return pl.BlockSpec((2, half, 128), lambda i, info: (0, 0, which * pairs + i))

    cells = 3 * half * half * pairs * 2
    return pl.pallas_call(
        self_fwd_kernel,
        grid_spec=pltpu.PrefetchScalarGridSpec(
            num_scalar_prefetch=1,
            grid=(pairs,),
            in_specs=[spec(0), spec(1), spec(2)],
            out_specs=[
                pl.BlockSpec((2, half, 128), lambda i, info: (0, 0, i)),
                pl.BlockSpec((1, 2, 2, half), lambda i, info: (i, 0, 0, 0)),
            ],
        ),
        out_shape=[
            jax.ShapeDtypeStruct((2, half, width), BF),
            jax.ShapeDtypeStruct((pairs, 2, 2, half), F32),
        ],
        compiler_params=pltpu.CompilerParams(vmem_limit_bytes=VMEM_LIMIT),
        cost_estimate=pl.CostEstimate(
            flops=cells * HD * 4 * 4, transcendentals=cells, bytes_accessed=qkv.size * 3
        ),
        name="self_fwd",
    )(info, qkv, qkv, qkv)


def pair_backward(q, k, v, grad, lse, delta, mask):
    score = mm(k, q, NT)
    prob = jnp.exp(score - lse)
    if mask is not None:
        prob = jnp.where(mask, prob, 0.0)
    slope = prob * (mm(v, grad, NT) - delta)
    prob = prob.astype(BF)
    slope = slope.astype(BF)
    return mm(slope, k, TN), mm(slope, q, NN), mm(prob, grad, NN)


def delta_row(grad, mixed):
    return jnp.sum((grad.astype(F32) * mixed.astype(F32)).T, 0, keepdims=True)


def self_bwd_kernel(info, q_ref, k_ref, v_ref, o_ref, lse_ref, g_ref, dq_ref, dk_ref, dv_ref):
    half = q_ref.shape[1]
    first = info[0]
    second = 1 - first
    prefix = info[1]
    key_pos = lax.broadcasted_iota(jnp.int32, (half, half), 0)
    query_pos = lax.broadcasted_iota(jnp.int32, (half, half), 1)
    causal = key_pos <= query_pos
    seen = causal | (key_pos < prefix)
    scale = 1.0 / math.sqrt(HD)
    for h in range(2):
        cols = slice(HD * h, HD * h + HD)

        def rows(ref, at):
            return ref[at, :, cols]

        def one(q_at, k_at, mask):
            grad = rows(g_ref, q_at)
            delta = delta_row(grad, rows(o_ref, q_at))
            lse = lse_ref[0, h, pl.ds(q_at, 1), :]
            return pair_backward(
                rows(q_ref, q_at), rows(k_ref, k_at), rows(v_ref, k_at), grad, lse, delta, mask
            )

        dq, dk_a, dv_a = one(first, first, seen)
        dq_ref[first, :, cols] = (dq.astype(BF) * scale).astype(BF)
        dq_b, dk_b, dv_b = one(second, first, None)
        dk_ref[first, :, cols] = (dk_a + dk_b).astype(BF)
        dv_ref[first, :, cols] = (dv_a + dv_b).astype(BF)
        dq_c, dk_c, dv_c = one(second, second, causal)
        dq_ref[second, :, cols] = ((dq_b + dq_c).astype(BF) * scale).astype(BF)
        dk_ref[second, :, cols] = dk_c.astype(BF)
        dv_ref[second, :, cols] = dv_c.astype(BF)


def self_backward(info, qkv, mixed, lse, grad):
    half, width = qkv.shape[1], qkv.shape[2] // 3
    pairs = width // 128

    def spec(which):
        return pl.BlockSpec((2, half, 128), lambda i, info: (0, 0, which * pairs + i))

    cells = 3 * half * half * pairs * 2
    out = jax.ShapeDtypeStruct((2, half, width), BF)
    return pl.pallas_call(
        self_bwd_kernel,
        grid_spec=pltpu.PrefetchScalarGridSpec(
            num_scalar_prefetch=1,
            grid=(pairs,),
            in_specs=[
                spec(0),
                spec(1),
                spec(2),
                spec(0),
                pl.BlockSpec((1, 2, 2, half), lambda i, info: (i, 0, 0, 0)),
                spec(0),
            ],
            out_specs=[spec(0), spec(0), spec(0)],
        ),
        out_shape=[out, out, out],
        compiler_params=pltpu.CompilerParams(vmem_limit_bytes=VMEM_LIMIT),
        cost_estimate=pl.CostEstimate(
            flops=cells * HD * 10 * 4, transcendentals=cells, bytes_accessed=qkv.size * 6
        ),
        name="self_bwd",
    )(info, qkv, qkv, qkv, mixed, lse, grad)


def cross_fwd_kernel(q_ref, ka_ref, kb_ref, va_ref, vb_ref, o_ref, lse_ref):
    for h in range(2):
        cols = slice(HD * h, HD * h + HD)
        q = q_ref[:, cols]
        score_a = mm(ka_ref[:, cols], q, NT)
        score_b = mm(kb_ref[:, cols], q, NT)
        top = jnp.maximum(
            jnp.max(score_a, 0, keepdims=True), jnp.max(score_b, 0, keepdims=True)
        )
        expo_a = jnp.exp(score_a - top)
        expo_b = jnp.exp(score_b - top)
        total = jnp.sum(expo_a, 0, keepdims=True) + jnp.sum(expo_b, 0, keepdims=True)
        mixed = (
            mm(va_ref[:, cols], expo_a.astype(BF), TN) + mm(vb_ref[:, cols], expo_b.astype(BF), TN)
        ) / total
        o_ref[:, cols] = mixed.T.astype(BF)
        lse_ref[0, h : h + 1, :] = top + jnp.log(total)


def cross_specs(rows, pairs):
    whole = pl.BlockSpec((rows, 128), lambda i: (0, i))
    turned = pl.BlockSpec((rows, 128), lambda i: (0, (i + pairs // 2) % pairs))
    value = pl.BlockSpec((rows, 128), lambda i: (0, pairs + i))
    value_turned = pl.BlockSpec((rows, 128), lambda i: (0, pairs + (i + pairs // 2) % pairs))
    return whole, turned, value, value_turned


def cross_forward(queries, kv_own, kv_oth):
    rows, width = queries.shape
    pairs = width // 128
    whole, turned, value, value_turned = cross_specs(rows, pairs)
    cells = 2 * rows * rows * pairs * 2
    return pl.pallas_call(
        cross_fwd_kernel,
        grid=(pairs,),
        in_specs=[whole, whole, turned, value, value_turned],
        out_specs=[whole, pl.BlockSpec((1, 2, rows), lambda i: (i, 0, 0))],
        out_shape=[
            jax.ShapeDtypeStruct((rows, width), BF),
            jax.ShapeDtypeStruct((pairs, 2, rows), F32),
        ],
        compiler_params=pltpu.CompilerParams(vmem_limit_bytes=VMEM_LIMIT),
        cost_estimate=pl.CostEstimate(
            flops=cells * HD * 4 * 4, transcendentals=cells, bytes_accessed=queries.size * 12
        ),
        name="cross_fwd",
    )(queries, kv_own, kv_oth, kv_own, kv_oth)


def cross_bwd_kernel(
    q_ref, ka_ref, kb_ref, va_ref, vb_ref, o_ref, lse_ref, g_ref,
    dq_ref, dka_ref, dva_ref, dkb_ref, dvb_ref,
):
    scale = 1.0 / math.sqrt(HD)
    for h in range(2):
        cols = slice(HD * h, HD * h + HD)
        grad = g_ref[:, cols]
        delta = delta_row(grad, o_ref[:, cols])
        lse = lse_ref[0, h : h + 1, :]
        q = q_ref[:, cols]
        dq_a, dk, dv = pair_backward(q, ka_ref[:, cols], va_ref[:, cols], grad, lse, delta, None)
        dka_ref[:, cols] = dk.astype(BF)
        dva_ref[:, cols] = dv.astype(BF)
        dq_b, dk, dv = pair_backward(q, kb_ref[:, cols], vb_ref[:, cols], grad, lse, delta, None)
        dkb_ref[:, cols] = dk.astype(BF)
        dvb_ref[:, cols] = dv.astype(BF)
        dq_ref[:, cols] = ((dq_a + dq_b).astype(BF) * scale).astype(BF)


def cross_backward(queries, kv_own, kv_oth, mixed, lse, grad):
    rows, width = queries.shape
    pairs = width // 128
    whole, turned, value, value_turned = cross_specs(rows, pairs)
    cells = 2 * rows * rows * pairs * 2
    out = jax.ShapeDtypeStruct((rows, width), BF)
    return pl.pallas_call(
        cross_bwd_kernel,
        grid=(pairs,),
        in_specs=[
            whole, whole, turned, value, value_turned, whole,
            pl.BlockSpec((1, 2, rows), lambda i: (i, 0, 0)), whole,
        ],
        out_specs=[whole, whole, whole, turned, turned],
        out_shape=[out, out, out, out, out],
        compiler_params=pltpu.CompilerParams(vmem_limit_bytes=VMEM_LIMIT),
        cost_estimate=pl.CostEstimate(
            flops=cells * HD * 10 * 4, transcendentals=cells, bytes_accessed=queries.size * 24
        ),
        name="cross_bwd",
    )(queries, kv_own, kv_oth, kv_own, kv_oth, mixed, lse, grad)


def norm_parts(resid):
    center = resid - jnp.mean(resid, axis=-1, keepdims=True)
    rstd = lax.rsqrt(jnp.mean(center * center, axis=-1, keepdims=True) + EPS)
    return center * rstd, rstd


def norm_back(normed, rstd, grad, gain):
    scaled = grad * gain
    return rstd * (
        scaled
        - jnp.mean(scaled, axis=-1, keepdims=True)
        - normed * jnp.mean(scaled * normed, axis=-1, keepdims=True)
    )


def gather_bit(value, bit, axis):
    other = swap_dp(value, bit)
    upper = (lax.axis_index("dp") & bit) != 0
    return jnp.stack(
        [jnp.where(upper, other, value), jnp.where(upper, value, other)], axis=axis
    )


def gather_x_last(shard):
    depth, cols = shard.shape
    value = shard
    for axis, bit in enumerate(dp_bits()):
        value = gather_bit(value, bit, axis)
    own = value.reshape(-1, cols)
    return own, swap_x(own)


def gather_x_inside(shards):
    depth = shards[0].shape[0]
    value = jnp.concatenate(shards, axis=1)
    bits = dp_bits()
    for axis, bit in enumerate(bits[:-1]):
        value = gather_bit(value, bit, axis)
    other = swap_x(value)
    pieces = []
    at = 0
    for shard in shards:
        cols = shard.shape[1]
        pieces += [value[..., at : at + cols], other[..., at : at + cols]]
        at += cols
    value = jnp.concatenate(pieces, axis=-1)
    value = gather_bit(value, bits[-1], len(bits) - 1)
    return value.reshape(-1, value.shape[-1])


def reduce_bit(value, bit, axis, last):
    upper = ((lax.axis_index("dp") & bit) != 0).astype(jnp.int32)
    keep = lax.dynamic_index_in_dim(value, upper, axis, keepdims=False)
    send = lax.dynamic_index_in_dim(value, 1 - upper, axis, keepdims=False)
    total = keep.astype(F32) + swap_dp(send, bit).astype(F32)
    return total if last else total.astype(BF)


def reduce_x(value):
    cols = value.shape[-1] // 2
    got = swap_x(value[..., cols:])
    return (value[..., :cols].astype(F32) + got.astype(F32)).astype(BF)


def reduce_core(value):
    cols = value.shape[-1] // 2
    got = swap_core(value[:, cols:])
    return (value[:, :cols].astype(F32) + got.astype(F32)).astype(BF)


def reduce_pack(value, x_first):
    bits = dp_bits()
    cols = value.shape[1]
    value = value.reshape((2,) * len(bits) + (-1, cols))
    if x_first:
        value = reduce_x(value)
        value = reduce_bit(value, bits[-1], len(bits) - 1, len(bits) == 1)
    else:
        value = reduce_bit(value, bits[-1], len(bits) - 1, False)
        value = reduce_x(value)
    rest = bits[:-1]
    for at, bit in enumerate(rest):
        value = reduce_bit(value, bit, 0, at == len(rest) - 1)
    return value


def total_dp(value):
    for bit in dp_bits():
        value = value + swap_dp(value, bit)
    return value


def local(
    tokens,
    bank,
    prefix,
    blocks,
    out_grad,
    selfq_weight,
    selfq_bias,
    selfk_weight,
    selfv_weight,
    selfv_bias,
    selfo_weight,
    selfo_bias,
    first_gain,
    first_shift,
    crossq_weight,
    crossq_bias,
    crossk_weight,
    crossv_weight,
    crossv_bias,
    crosso_weight,
    crosso_bias,
    second_gain,
    second_shift,
    expand_weight,
    expand_bias,
    shrink_weight,
    shrink_bias,
    third_gain,
    third_shift,
):
    rank = lax.axis_index("tensor")
    core = rank % 2
    chip = rank // 2
    half, width = tokens.shape
    seq_count = prefix.shape[0]
    local_blocks = bank.shape[1] // BLK
    head_cols = selfq_bias.shape[0]
    hidden_cols = expand_bias.shape[0]
    scale = 1.0 / math.sqrt(HD)
    slots = NBLK // 2

    tokens_oth = swap_core(tokens)
    self_in = gather_x_inside(
        [selfq_weight.astype(BF), selfk_weight.astype(BF), selfv_weight.astype(BF)]
    )
    bias_own = jnp.concatenate(
        [selfq_bias, selfv_bias, crossq_bias, crossv_bias, expand_bias]
    ).reshape(1, -1)
    bias_two = jnp.concatenate([bias_own, swap_x(bias_own)], axis=0)
    bias_four = jnp.concatenate([bias_two, swap_core(bias_two)], axis=0)
    sq_bias = bias_two[:, :head_cols].reshape(-1)
    sv_bias = bias_two[:, head_cols : 2 * head_cols].reshape(-1)
    cq_bias = bias_four[:, 2 * head_cols : 3 * head_cols].reshape(-1)
    cv_bias = bias_four[:, 3 * head_cols : 4 * head_cols].reshape(-1)
    ex_bias = bias_four[:, 4 * head_cols :].reshape(-1)

    block_ids = rank * local_blocks + jnp.arange(local_blocks)
    select = (blocks[:, :, None] == block_ids[None, None, :]).astype(BF)
    part = jnp.einsum(
        "snb,sbre->snre",
        select,
        bank.reshape(seq_count, local_blocks, BLK, width),
        preferred_element_type=F32,
    ).astype(BF)
    part_mine = lax.dynamic_slice_in_dim(part, core * slots, slots, 1)
    part_send = lax.dynamic_slice_in_dim(part, (1 - core) * slots, slots, 1)
    part_chip = part_mine + swap_core(part_send)
    part_keep = lax.dynamic_index_in_dim(part_chip, chip, 0, keepdims=False)
    part_away = lax.dynamic_index_in_dim(part_chip, 1 - chip, 0, keepdims=False)
    fetched = (part_keep + swap_x(part_away)).reshape(slots * BLK, width)

    attn_in = gather_x_inside(
        [w.astype(BF) for w in (crossk_weight, crossv_weight, crossq_weight)]
        + [selfo_weight.astype(BF).T, crosso_weight.astype(BF).T]
    )
    attn_oth = swap_core(attn_in)
    two = 2 * head_cols

    def whole(which):
        at = which * two
        return jnp.concatenate([attn_in[:, at : at + two], attn_oth[:, at : at + two]], axis=1)

    cross_kv = jnp.concatenate([whole(0), whole(1)], axis=1)
    cross_q = whole(2)
    self_o = whole(3)
    cross_o = whole(4)

    expand_own, expand_x = gather_x_last(expand_weight.astype(BF))
    expand_mat = jnp.concatenate(
        [expand_own, expand_x, swap_core(expand_own), swap_core(expand_x)], axis=1
    )
    shrink_own, shrink_x = gather_x_last(shrink_weight.astype(BF).T)
    shrink_mat = jnp.concatenate(
        [shrink_own, shrink_x, swap_core(shrink_own), swap_core(shrink_x)], axis=1
    )

    source = jnp.concatenate([tokens, tokens_oth], axis=0)
    sums = mm(source, self_in)
    qkv = jnp.concatenate(
        [
            (sums[:, :two] + sq_bias) * scale,
            sums[:, two : 2 * two],
            sums[:, 2 * two :] + sv_bias,
        ],
        axis=1,
    ).astype(BF)
    qkv = qkv.reshape(2, half, 3 * two)
    my_prefix = lax.dynamic_index_in_dim(prefix, chip, 0, keepdims=False)
    info = jnp.stack([core, my_prefix]).astype(jnp.int32)
    self_mixed, self_lse = self_forward(info, qkv)
    mixed_one = jnp.concatenate([self_mixed[0], swap_core(self_mixed[1])], axis=1)

    resid_in = tokens.astype(F32)
    first_sum = resid_in + mm(mixed_one, self_o, NT) + selfo_bias
    first_normed, first_rstd = norm_parts(first_sum)
    first_out = first_normed * first_gain + first_shift
    first_low = first_out.astype(BF)

    kv_bias = jnp.concatenate([jnp.zeros_like(cv_bias), cv_bias])
    kv_own = (mm(fetched, cross_kv) + kv_bias).astype(BF)
    kv_oth = swap_core(kv_own)
    queries = ((mm(first_low, cross_q) + cq_bias) * scale).astype(BF)
    mixed_two, cross_lse = cross_forward(queries, kv_own, kv_oth)
    second_sum = first_out + mm(mixed_two, cross_o, NT) + crosso_bias
    second_normed, second_rstd = norm_parts(second_sum)
    second_out = second_normed * second_gain + second_shift
    second_low = second_out.astype(BF)

    inner = mm(second_low, expand_mat) + ex_bias
    phi = 0.5 * (1.0 + lax.erf(inner * (1.0 / math.sqrt(2.0))))
    hidden = (inner * phi).astype(BF)
    slope = (phi + inner * jnp.exp(-0.5 * inner * inner) * (1.0 / math.sqrt(2.0 * math.pi))).astype(BF)
    third_sum = second_out + mm(hidden, shrink_mat, NT) + shrink_bias
    third_normed, third_rstd = norm_parts(third_sum)
    out_act = (third_normed * third_gain + third_shift).astype(BF)

    cot = out_grad.astype(F32)
    third_in = norm_back(third_normed, third_rstd, cot, third_gain)
    feed_low = third_in.astype(BF)
    inner_low = (mm(feed_low, shrink_mat) * slope.astype(F32)).astype(BF)
    second_grad = third_in + mm(inner_low, expand_mat, NT)
    shrink_full = mm(feed_low, hidden, TN).astype(BF)
    expand_full = mm(second_low, inner_low, TN).astype(BF)
    second_in = norm_back(second_normed, second_rstd, second_grad, second_gain)
    cross_low = second_in.astype(BF)
    crosso_full = mm(cross_low, mixed_two, TN).astype(BF)
    shrink_wgrad = reduce_pack(reduce_core(shrink_full), False)
    expand_wgrad = reduce_pack(reduce_core(expand_full), True)

    cross_grad = mm(cross_low, cross_o).astype(BF)
    dq, dk_own, dv_own, dk_oth, dv_oth = cross_backward(
        queries, kv_own, kv_oth, mixed_two, cross_lse, cross_grad
    )
    dkv_got = swap_core(jnp.concatenate([dk_oth, dv_oth], axis=1))
    dkv = (jnp.concatenate([dk_own, dv_own], axis=1).astype(F32) + dkv_got.astype(F32)).astype(BF)
    first_grad = second_in + mm(dq, cross_q, NT)
    first_in = norm_back(first_normed, first_rstd, first_grad, first_gain)
    self_low = first_in.astype(BF)
    self_grad = mm(self_low, self_o).astype(BF)
    self_got = swap_core(self_grad[:, two:])
    mixed_grad = jnp.stack([self_grad[:, :two], self_got])

    fetched_grad = mm(dkv, cross_kv, NT).astype(BF)
    crosskv_full = mm(fetched, dkv, TN).astype(BF)
    crossq_full = mm(first_low, dq, TN).astype(BF)
    selfo_full = mm(self_low, mixed_one, TN).astype(BF)

    def halves(which):
        at = 2 * two * which
        return crosskv_full[:, at : at + two], crosskv_full[:, at + two : at + 2 * two]

    def quarters(full):
        return [full[:, i * head_cols : (i + 1) * head_cols] for i in range(4)]

    parts = [
        quarters(crosskv_full[:, : 2 * two]),
        quarters(crosskv_full[:, 2 * two :]),
        quarters(crossq_full),
        quarters(selfo_full),
        quarters(crosso_full),
    ]
    attn_full = jnp.concatenate([p[j] for j in range(4) for p in parts], axis=1)
    attn_wgrad = reduce_pack(reduce_core(attn_full), False)

    fetched_away = swap_x(fetched_grad)
    away = (chip == 1)
    fetched_both = jnp.stack(
        [jnp.where(away, fetched_away, fetched_grad), jnp.where(away, fetched_grad, fetched_away)]
    )
    both_oth = swap_core(fetched_both)
    late = (core == 1)
    slot_grads = jnp.concatenate(
        [jnp.where(late, both_oth, fetched_both), jnp.where(late, fetched_both, both_oth)], axis=1
    ).reshape(seq_count, NBLK, BLK, width)
    bank_grad = jnp.einsum(
        "snb,snre->sbre", select, slot_grads, preferred_element_type=F32
    ).reshape(bank.shape)

    dsq, dsk, dsv = self_backward(info, qkv, self_mixed, self_lse, mixed_grad)
    dqkv = jnp.concatenate([dsq, dsk, dsv], axis=2).reshape(2 * half, 3 * two)
    self_full = mm(source, dqkv, TN).astype(BF)
    self_parts = [
        self_full[:, i * head_cols : (i + 1) * head_cols] for i in (0, 2, 4, 1, 3, 5)
    ]
    self_wgrad = reduce_pack(jnp.concatenate(self_parts, axis=1), False)
    back = mm(dqkv, self_in, NT)
    back_got = swap_core(back[half:].astype(BF))
    in_grad = (first_in + back[:half] + back_got.astype(F32)).astype(BF)

    def rowsum(values):
        return jnp.sum(values.astype(F32), axis=0)

    order = jnp.arange(4) ^ rank
    order = 2 * (order % 2) + order // 2

    def straight(vec):
        return vec.reshape(4, -1)[order].reshape(-1)

    late_vec = jnp.concatenate(
        [
            rowsum(cot),
            rowsum(cot * third_normed),
            rowsum(feed_low),
            rowsum(second_grad),
            rowsum(second_grad * second_normed),
            rowsum(cross_low),
            straight(rowsum(inner_low)),
        ]
    )
    early_vec = jnp.concatenate(
        [
            rowsum(first_grad),
            rowsum(first_grad * first_normed),
            rowsum(self_low),
            straight(rowsum(dq)),
            straight(rowsum(dkv[:, 2 * two :])),
        ]
    )
    late_vec = late_vec + swap_core(late_vec)
    late_vec = late_vec + swap_x(late_vec)
    late_vec = total_dp(late_vec)
    early_vec = early_vec + swap_core(early_vec)
    early_vec = early_vec + swap_x(early_vec)
    early_vec = total_dp(early_vec)
    sq_rows = rowsum(dqkv[:, :two])
    sv_rows = rowsum(dqkv[:, 2 * two :])
    keep = jnp.concatenate([sq_rows[:head_cols], sv_rows[:head_cols]])
    send = jnp.concatenate([sq_rows[head_cols:], sv_rows[head_cols:]])
    self_vec = total_dp(keep + swap_x(send))

    def own_part(vec, start, part_len):
        return lax.dynamic_slice_in_dim(vec, start + rank * part_len, part_len, 0)

    def vec(source_vec, which):
        return source_vec[which * width : (which + 1) * width]

    def attn_cols(which):
        return attn_wgrad[:, which * head_cols : (which + 1) * head_cols]

    def self_cols(which):
        return self_wgrad[:, which * head_cols : (which + 1) * head_cols]

    return (
        out_act,
        in_grad,
        bank_grad,
        self_cols(0),
        self_vec[:head_cols],
        self_cols(1),
        self_cols(2),
        self_vec[head_cols:],
        attn_cols(3).T,
        vec(early_vec, 2),
        vec(early_vec, 1),
        vec(early_vec, 0),
        attn_cols(2),
        own_part(early_vec, 3 * width, head_cols),
        attn_cols(0),
        attn_cols(1),
        own_part(early_vec, 4 * width, head_cols),
        attn_cols(4).T,
        vec(late_vec, 5),
        vec(late_vec, 4),
        vec(late_vec, 3),
        expand_wgrad,
        own_part(late_vec, 6 * width, hidden_cols),
        shrink_wgrad.T,
        vec(late_vec, 2),
        vec(late_vec, 1),
        vec(late_vec, 0),
    )


def solution(mesh):
    rows = P(("dp", "tensor"), None)
    wide = P("dp", "tensor")
    tall = P("tensor", "dp")
    part = P("tensor")
    full = P()
    return jax.shard_map(
        local,
        mesh=mesh,
        in_specs=(
            rows, P("dp", "tensor", None), P("dp"), P("dp", None), rows,
            wide, part, wide, wide, part, tall, full, full, full,
            wide, part, wide, wide, part, tall, full, full, full,
            wide, part, tall, full, full, full,
        ),
        out_specs=(
            rows, rows, P("dp", "tensor", None),
            wide, part, wide, wide, part, tall, full, full, full,
            wide, part, wide, wide, part, tall, full, full, full,
            wide, part, tall, full, full, full,
        ),
        check_vma=False,
    )
```

```python
import functools
import math

import jax
import jax.numpy as jnp
from jax import lax
from jax.experimental import pallas as pl
from jax.experimental.pallas import tpu as pltpu
from jax.sharding import PartitionSpec as P

HD = 64
BLK = 64
NBLK = 16
EPS = 1e-05
NEGATIVE = -1e30
BF = jnp.bfloat16
F32 = jnp.float32

NT = (((1,), (1,)), ((), ()))
NN = (((1,), (0,)), ((), ()))
TN = (((0,), (0,)), ((), ()))

CORE_SWAP = ((0, 1), (1, 0), (2, 3), (3, 2))
X_SWAP = ((0, 2), (2, 0), (1, 3), (3, 1))
VMEM_LIMIT = 48 << 20


def mm(left, right, dims=NN):
    return lax.dot_general(left, right, dims, preferred_element_type=F32)


def swap_core(value):
    return lax.ppermute(value, "tensor", CORE_SWAP)


def swap_x(value):
    return lax.ppermute(value, "tensor", X_SWAP)


def swap_dp(value, bit):
    count = lax.axis_size("dp")
    return lax.ppermute(value, "dp", tuple((i, i ^ bit) for i in range(count)))


def dp_bits():
    count = lax.axis_size("dp")
    bits = []
    bit = count // 2
    while bit >= 1:
        bits.append(bit)
        bit //= 2
    return bits


def pair_backward(q, k, v, grad, lse, delta, mask):
    score = mm(k, q, NT)
    prob = jnp.exp(score - lse)
    if mask is not None:
        prob = jnp.where(mask, prob, 0.0)
    slope = prob * (mm(v, grad, NT) - delta)
    prob = prob.astype(BF)
    slope = slope.astype(BF)
    return mm(slope, k, TN), mm(slope, q, NN), mm(prob, grad, NN)


def delta_row(grad, mixed):
    return jnp.sum((grad.astype(F32) * mixed.astype(F32)).T, 0, keepdims=True)


def self_bwd_kernel(info, q_ref, k_ref, v_ref, oa_ref, ob_ref, lse_ref, ga_ref, gb_ref, *rest):
    out_ref, sums_ref, o_ref, g_ref = rest[-4:]
    dq_ref, dk_ref, dv_ref = out_ref.at[0], out_ref.at[1], out_ref.at[2]
    o_ref[0], o_ref[1] = oa_ref[...], ob_ref[...]
    g_ref[0], g_ref[1] = ga_ref[...], gb_ref[...]
    half = q_ref.shape[1]
    first = info[0]
    second = 1 - first
    prefix = info[1]
    key_pos = lax.broadcasted_iota(jnp.int32, (half, half), 0)
    query_pos = lax.broadcasted_iota(jnp.int32, (half, half), 1)
    causal = key_pos <= query_pos
    seen = causal | (key_pos < prefix)
    scale = 1.0 / math.sqrt(HD)
    for h in range(2):
        cols = slice(HD * h, HD * h + HD)

        def rows(ref, at):
            return ref[at, :, cols]

        def one(q_at, k_at, mask):
            grad = rows(g_ref, q_at)
            delta = delta_row(grad, rows(o_ref, q_at))
            lse = lse_ref[0, h, pl.ds(q_at, 1), :]
            return pair_backward(
                rows(q_ref, q_at), rows(k_ref, k_at), rows(v_ref, k_at), grad, lse, delta, mask
            )

        dq, dk_a, dv_a = one(first, first, seen)
        dq_ref[first, :, cols] = (dq.astype(BF) * scale).astype(BF)
        dq_b, dk_b, dv_b = one(second, first, None)
        dk_ref[first, :, cols] = (dk_a + dk_b).astype(BF)
        dv_ref[first, :, cols] = (dv_a + dv_b).astype(BF)
        dq_c, dk_c, dv_c = one(second, second, causal)
        dq_ref[second, :, cols] = ((dq_b + dq_c).astype(BF) * scale).astype(BF)
        dk_ref[second, :, cols] = dk_c.astype(BF)
        dv_ref[second, :, cols] = dv_c.astype(BF)
    for i in range(3):
        both = out_ref[i, 0].astype(F32) + out_ref[i, 1].astype(F32)
        sums_ref[0, i : i + 1, :] = jnp.sum(both, 0, keepdims=True)


def self_backward(info, qkv, mixed_own, mixed_oth, lse, grad_own, grad_oth, start, count, former=()):
    half, width = qkv.shape[1], qkv.shape[2] // 3
    pairs = width // 128

    def spec(which):
        return pl.BlockSpec((2, half, 128), lambda i, info: (0, 0, which * pairs + start + i))

    flat = pl.BlockSpec((half, 128), lambda i, info: (0, start + i))
    cells = 3 * half * half * count * 2
    return pl.pallas_call(
        self_bwd_kernel,
        grid_spec=pltpu.PrefetchScalarGridSpec(
            num_scalar_prefetch=1,
            grid=(count,),
            in_specs=[
                spec(0),
                spec(1),
                spec(2),
                flat,
                flat,
                pl.BlockSpec((1, 2, 2, half), lambda i, info: (start + i, 0, 0, 0)),
                flat,
                flat,
            ]
            + [pl.BlockSpec(memory_space=pl.ANY)] * len(former),
            out_specs=[
                pl.BlockSpec((3, 2, half, 128), lambda i, info: (0, 0, 0, start + i)),
                pl.BlockSpec((1, 8, 128), lambda i, info: (start + i, 0, 0)),
            ],
            scratch_shapes=[pltpu.VMEM((2, half, 128), BF)] * 2,
        ),
        out_shape=[
            jax.ShapeDtypeStruct((3, 2, half, width), BF),
            jax.ShapeDtypeStruct((pairs, 8, 128), F32),
        ],
        input_output_aliases={9 + i: i for i in range(len(former))},
        compiler_params=pltpu.CompilerParams(vmem_limit_bytes=VMEM_LIMIT),
        cost_estimate=pl.CostEstimate(
            flops=cells * HD * 10 * 4, transcendentals=cells, bytes_accessed=qkv.size * 2 * count
        ),
        name="self_bwd",
    )(info, qkv, qkv, qkv, mixed_own, mixed_oth, lse, grad_own, grad_oth, *former)


def cross_fwd_kernel(q_ref, ka_ref, kb_ref, va_ref, vb_ref, o_ref, lse_ref):
    for h in range(2):
        cols = slice(HD * h, HD * h + HD)
        q = q_ref[:, cols]
        score_a = mm(ka_ref[:, cols], q, NT)
        score_b = mm(kb_ref[:, cols], q, NT)
        top = jnp.maximum(
            jnp.max(score_a, 0, keepdims=True), jnp.max(score_b, 0, keepdims=True)
        )
        expo_a = jnp.exp(score_a - top)
        expo_b = jnp.exp(score_b - top)
        total = jnp.sum(expo_a, 0, keepdims=True) + jnp.sum(expo_b, 0, keepdims=True)
        mixed = (
            mm(va_ref[:, cols], expo_a.astype(BF), TN) + mm(vb_ref[:, cols], expo_b.astype(BF), TN)
        ) / total
        o_ref[:, cols] = mixed.T.astype(BF)
        lse_ref[0, h : h + 1, :] = top + jnp.log(total)


def cross_specs(rows, pairs):
    whole = pl.BlockSpec((rows, 128), lambda i: (0, i))
    turned = pl.BlockSpec((rows, 128), lambda i: (0, (i + pairs // 2) % pairs))
    value = pl.BlockSpec((rows, 128), lambda i: (0, pairs + i))
    value_turned = pl.BlockSpec((rows, 128), lambda i: (0, pairs + (i + pairs // 2) % pairs))
    return whole, turned, value, value_turned


def cross_forward(queries, kv_own, kv_oth):
    rows, width = queries.shape
    pairs = width // 128
    whole, turned, value, value_turned = cross_specs(rows, pairs)
    cells = 2 * rows * rows * pairs * 2
    return pl.pallas_call(
        cross_fwd_kernel,
        grid=(pairs,),
        in_specs=[whole, whole, turned, value, value_turned],
        out_specs=[whole, pl.BlockSpec((1, 2, rows), lambda i: (i, 0, 0))],
        out_shape=[
            jax.ShapeDtypeStruct((rows, width), BF),
            jax.ShapeDtypeStruct((pairs, 2, rows), F32),
        ],
        compiler_params=pltpu.CompilerParams(vmem_limit_bytes=VMEM_LIMIT),
        cost_estimate=pl.CostEstimate(
            flops=cells * HD * 4 * 4, transcendentals=cells, bytes_accessed=queries.size * 12
        ),
        name="cross_fwd",
    )(queries, kv_own, kv_oth, kv_own, kv_oth)


def cross_bwd_kernel(
    q_ref, ka_ref, kb_ref, va_ref, vb_ref, o_ref, lse_ref, g_ref,
    *rest,
):
    dq_ref, da_ref, db_ref = rest[-3:]
    scale = 1.0 / math.sqrt(HD)
    for h in range(2):
        cols = slice(HD * h, HD * h + HD)
        grad = g_ref[:, cols]
        delta = delta_row(grad, o_ref[:, cols])
        lse = lse_ref[0, h : h + 1, :]
        q = q_ref[:, cols]
        dq_a, dk, dv = pair_backward(q, ka_ref[:, cols], va_ref[:, cols], grad, lse, delta, None)
        da_ref[0, :, cols] = dk.astype(BF)
        da_ref[1, :, cols] = dv.astype(BF)
        dq_b, dk, dv = pair_backward(q, kb_ref[:, cols], vb_ref[:, cols], grad, lse, delta, None)
        db_ref[0, :, cols] = dk.astype(BF)
        db_ref[1, :, cols] = dv.astype(BF)
        dq_ref[:, cols] = ((dq_a + dq_b).astype(BF) * scale).astype(BF)


def cross_backward(queries, kv_own, kv_oth, mixed, lse, grad, start, count, former=()):
    rows, width = queries.shape
    pairs = width // 128

    def turn(i):
        return (start + i + pairs // 2) % pairs

    whole = pl.BlockSpec((rows, 128), lambda i: (0, start + i))
    turned = pl.BlockSpec((rows, 128), lambda i: (0, turn(i)))
    value = pl.BlockSpec((rows, 128), lambda i: (0, pairs + start + i))
    value_turned = pl.BlockSpec((rows, 128), lambda i: (0, pairs + turn(i)))
    cells = 2 * rows * rows * count * 2
    both = jax.ShapeDtypeStruct((2, rows, width), BF)
    return pl.pallas_call(
        cross_bwd_kernel,
        grid=(count,),
        in_specs=[
            whole, whole, turned, value, value_turned, whole,
            pl.BlockSpec((1, 2, rows), lambda i: (start + i, 0, 0)), whole,
        ]
        + [pl.BlockSpec(memory_space=pl.ANY)] * len(former),
        out_specs=[
            whole,
            pl.BlockSpec((2, rows, 128), lambda i: (0, 0, start + i)),
            pl.BlockSpec((2, rows, 128), lambda i: (0, 0, turn(i))),
        ],
        out_shape=[jax.ShapeDtypeStruct((rows, width), BF), both, both],
        input_output_aliases={8 + i: i for i in range(len(former))},
        compiler_params=pltpu.CompilerParams(vmem_limit_bytes=VMEM_LIMIT),
        cost_estimate=pl.CostEstimate(
            flops=cells * HD * 10 * 4, transcendentals=cells, bytes_accessed=rows * 128 * 24 * count
        ),
        name="cross_bwd",
    )(queries, kv_own, kv_oth, kv_own, kv_oth, mixed, lse, grad, *former)


def norm_parts(resid):
    center = resid - jnp.mean(resid, axis=-1, keepdims=True)
    rstd = lax.rsqrt(jnp.mean(center * center, axis=-1, keepdims=True) + EPS)
    return center * rstd, rstd


def norm_back(normed, rstd, grad, gain):
    scaled = grad * gain
    return rstd * (
        scaled
        - jnp.mean(scaled, axis=-1, keepdims=True)
        - normed * jnp.mean(scaled * normed, axis=-1, keepdims=True)
    )


def cross_first_kernel(
    q_ref, ka_ref, kb_ref, va_ref, vb_ref, o_ref, lse_ref, g_ref,
    q_mat, second_ref, resid_ref, vec_ref, o_mat, dq_in, former_a, former_b,
    dq_ref, da_ref, db_ref, first_ref, low_ref, keep_ref, send_ref, sums_ref, dq_part,
    *, start, count,
):
    step = pl.program_id(0)

    @pl.when(step == 0)
    def _():
        dq_ref[...] = dq_in[...]

    cross_bwd_kernel(
        q_ref, ka_ref, kb_ref, va_ref, vb_ref, o_ref, lse_ref, g_ref, dq_part, da_ref, db_ref
    )
    at = pl.multiple_of((start + step) * 128, 128)
    dq_ref[:, pl.ds(at, 128)] = dq_part[...]

    @pl.when(step == count - 1)
    def _():
        grad = second_ref[...] + mm(dq_ref[...], q_mat[...], NT)
        normed, rstd = norm_parts(resid_ref[...])
        sums_ref[0:1, :] = jnp.sum(grad, 0, keepdims=True)
        sums_ref[1:2, :] = jnp.sum(grad * normed, 0, keepdims=True)
        first_in = norm_back(normed, rstd, grad, vec_ref[0:1, :])
        first_ref[...] = first_in
        low = first_in.astype(BF)
        low_ref[...] = low
        sums_ref[2:3, :] = jnp.sum(low.astype(F32), 0, keepdims=True)
        sums_ref[3:4, :] = jnp.sum(dq_ref[...].astype(F32), 0, keepdims=True)
        sums_ref[4:8, :] = jnp.zeros((4, sums_ref.shape[1]), F32)
        mixed_grad = mm(low, o_mat[...]).astype(BF)
        cols = keep_ref.shape[1]
        keep_ref[...] = mixed_grad[:, :cols]
        send_ref[...] = mixed_grad[:, cols:]


def cross_first_backward(
    queries, kv_own, kv_oth, mixed, lse, grad, start, former, q_mat, second_in, resid, vec, o_mat
):
    rows, width = queries.shape
    pairs = width // 128
    count = pairs - start

    def turn(i):
        return (start + i + pairs // 2) % pairs

    whole = pl.BlockSpec((rows, 128), lambda i: (0, start + i))
    turned = pl.BlockSpec((rows, 128), lambda i: (0, turn(i)))
    value = pl.BlockSpec((rows, 128), lambda i: (0, pairs + start + i))
    value_turned = pl.BlockSpec((rows, 128), lambda i: (0, pairs + turn(i)))

    def fixed(shape):
        return pl.BlockSpec(shape, lambda i: (0, 0))

    both = jax.ShapeDtypeStruct((2, rows, width), BF)
    return pl.pallas_call(
        functools.partial(cross_first_kernel, start=start, count=count),
        grid=(count,),
        in_specs=[
            whole, whole, turned, value, value_turned, whole,
            pl.BlockSpec((1, 2, rows), lambda i: (start + i, 0, 0)), whole,
            fixed((width, width)), fixed((rows, width)), fixed((rows, width)),
            fixed((1, width)), fixed((width, width)), fixed((rows, width)),
            pl.BlockSpec(memory_space=pl.ANY), pl.BlockSpec(memory_space=pl.ANY),
        ],
        out_specs=[
            fixed((rows, width)),
            pl.BlockSpec((2, rows, 128), lambda i: (0, 0, start + i)),
            pl.BlockSpec((2, rows, 128), lambda i: (0, 0, turn(i))),
            fixed((rows, width)),
            fixed((rows, width)),
            fixed((rows, width // 2)),
            fixed((rows, width // 2)),
            fixed((8, width)),
        ],
        out_shape=[
            jax.ShapeDtypeStruct((rows, width), BF),
            both,
            both,
            jax.ShapeDtypeStruct((rows, width), F32),
            jax.ShapeDtypeStruct((rows, width), BF),
            jax.ShapeDtypeStruct((rows, width // 2), BF),
            jax.ShapeDtypeStruct((rows, width // 2), BF),
            jax.ShapeDtypeStruct((8, width), F32),
        ],
        scratch_shapes=[pltpu.VMEM((rows, 128), BF)],
        input_output_aliases={14: 1, 15: 2},
        compiler_params=pltpu.CompilerParams(vmem_limit_bytes=VMEM_LIMIT),
        cost_estimate=pl.CostEstimate(
            flops=2 * rows * rows * count * 2 * HD * 40, transcendentals=0,
            bytes_accessed=rows * 128 * 24 * count,
        ),
        name="cross_first",
    )(
        queries, kv_own, kv_oth, kv_own, kv_oth, mixed, lse, grad,
        q_mat, second_in, resid, vec, o_mat, *former,
    )


def gate(value, *others):
    return lax.optimization_barrier((value,) + others)[0]


def outer_count():
    return lax.axis_size("dp") // 2


def swap_both(value):
    count = lax.axis_size("dp")
    pairs = tuple(
        (d * 4 + t, (d ^ 1) * 4 + (t ^ 2)) for d in range(count) for t in range(4)
    )
    return lax.ppermute(value, ("dp", "tensor"), pairs)


def outer_exchange(value):
    groups = [[inner + 2 * o for o in range(outer_count())] for inner in range(2)]
    return lax.all_to_all(value, "dp", 0, 0, axis_index_groups=groups, tiled=True)


def plane_exchange(value):
    groups = [
        [(o * 2 + inner) * 4 + chip * 2 + core for chip in range(2) for inner in range(2)]
        for o in range(outer_count())
        for core in range(2)
    ]
    return lax.all_to_all(value, ("dp", "tensor"), 0, 0, axis_index_groups=groups, tiled=True)


def add_low(left, right):
    return (left.astype(F32) + right.astype(F32)).astype(BF)


def total_dp(value):
    for bit in dp_bits():
        value = value + swap_dp(value, bit)
    return value


ANY = pl.BlockSpec(memory_space=pl.ANY)
VM = pl.BlockSpec(memory_space=pltpu.VMEM)
SM = pl.BlockSpec(memory_space=pltpu.SMEM)


def call(kernel, out_shape, args, in_specs, out_specs, scratch=(), flops=0, moved=0, name=None):
    return pl.pallas_call(
        kernel,
        out_shape=out_shape,
        in_specs=in_specs,
        out_specs=out_specs,
        scratch_shapes=list(scratch),
        compiler_params=pltpu.CompilerParams(vmem_limit_bytes=58 << 20),
        cost_estimate=pl.CostEstimate(flops=flops, bytes_accessed=moved, transcendentals=0),
        name=name,
    )(*args)


def struct(shape, dtype):
    return jax.ShapeDtypeStruct(shape, dtype)


def pack_self_kernel(q_ref, k_ref, v_ref, out_ref):
    cols = q_ref.shape[1]
    for i, ref in enumerate((q_ref, k_ref, v_ref)):
        low = ref[...].astype(BF)
        for copy in range(out_ref.shape[0]):
            out_ref[copy, :, i * cols : (i + 1) * cols] = low


def turned(ref):
    depth = ref.shape[1]
    eye = (
        lax.broadcasted_iota(jnp.int32, (depth, depth), 0)
        == lax.broadcasted_iota(jnp.int32, (depth, depth), 1)
    )
    eye = jnp.where(eye, 1.0, 0.0).astype(BF)
    return mm(eye, ref[...].astype(BF), NT).astype(BF)


def pack_rest_kernel(ck_ref, cv_ref, cq_ref, so_ref, co_ref, ex_ref, sh_ref, attn_ref, ex_out, sh_out):
    cols = ck_ref.shape[1]
    parts = [ref[...].astype(BF) for ref in (ck_ref, cv_ref, cq_ref)]
    parts += [turned(so_ref), turned(co_ref)]
    expand = ex_ref[...].astype(BF)
    shrink = turned(sh_ref)
    for copy in range(attn_ref.shape[0]):
        for i, low in enumerate(parts):
            attn_ref[copy, :, i * cols : (i + 1) * cols] = low
        ex_out[copy] = expand
    sh_out[...] = shrink


def self_forward_kernel(
    info, own_ref, oth_ref, bias_ref, w_ref, wx_ref, wy_ref, wxy_ref,
    qkv_ref, mat_ref, oa_ref, ob_ref, lse_ref, w_own, w_x, o_ref, sems,
):
    pair = pl.program_id(0)
    width = own_ref.shape[1]
    half = own_ref.shape[0]
    wide = qkv_ref.shape[2] // 3

    @pl.when(pair == 0)
    def _():
        place = info[0]
        cols = w_own.shape[3]
        copies = [
            pltpu.make_async_copy(w_ref, w_own.at[:, place], sems.at[0]),
            pltpu.make_async_copy(wy_ref, w_own.at[:, 1 - place], sems.at[1]),
            pltpu.make_async_copy(wx_ref, w_x.at[:, place], sems.at[2]),
            pltpu.make_async_copy(wxy_ref, w_x.at[:, 1 - place], sems.at[3]),
        ]
        for copy in copies:
            copy.start()
        for copy in copies:
            copy.wait()
        piece = cols // 3
        scale = 1.0 / math.sqrt(HD)
        for x, ref in enumerate((w_own, w_x)):
            mat = ref[...].reshape(width, cols)
            for i in range(3):
                at = (2 * i + x) * piece
                mat_ref[:, at : at + piece] = mat[:, i * piece : (i + 1) * piece]
        for rel, src in enumerate((own_ref, oth_ref)):
            for i in range(3):
                at = slice(wide * i, wide * (i + 1))
                part = mm(src[...], mat_ref[:, at]) + bias_ref[i : i + 1, :]
                if i == 0:
                    part = part * scale
                qkv_ref[rel, :, at] = part.astype(BF)

    first = info[3]
    second = 1 - first
    prefix = info[4]
    key_pos = lax.broadcasted_iota(jnp.int32, (half, half), 0)
    query_pos = lax.broadcasted_iota(jnp.int32, (half, half), 1)
    causal = key_pos <= query_pos
    seen = causal | (key_pos < prefix)

    def load(which, at):
        start = pl.multiple_of(which * wide + pair * 128, 128)
        return qkv_ref[at, :, pl.ds(start, 128)]

    q_both = (load(0, first), load(0, second))
    k_both = (load(1, first), load(1, second))
    v_both = (load(2, first), load(2, second))
    for h in range(2):
        cols = slice(HD * h, HD * h + HD)
        k0, k1 = (k[:, cols] for k in k_both)
        v0, v1 = (v[:, cols] for v in v_both)
        q0, q1 = (q[:, cols] for q in q_both)
        score = jnp.where(seen, mm(k0, q0, NT), NEGATIVE)
        top = jnp.max(score, 0, keepdims=True)
        expo = jnp.exp(score - top)
        total = jnp.sum(expo, 0, keepdims=True)
        mixed = mm(v0, expo.astype(BF), TN) / total
        o_ref[first, :, cols] = mixed.T.astype(BF)
        lse_ref[0, h, pl.ds(first, 1), :] = top + jnp.log(total)

        score_a = mm(k0, q1, NT)
        score_b = jnp.where(causal, mm(k1, q1, NT), NEGATIVE)
        top = jnp.maximum(
            jnp.max(score_a, 0, keepdims=True), jnp.max(score_b, 0, keepdims=True)
        )
        expo_a = jnp.exp(score_a - top)
        expo_b = jnp.exp(score_b - top)
        total = jnp.sum(expo_a, 0, keepdims=True) + jnp.sum(expo_b, 0, keepdims=True)
        mixed = (mm(v0, expo_a.astype(BF), TN) + mm(v1, expo_b.astype(BF), TN)) / total
        o_ref[second, :, cols] = mixed.T.astype(BF)
        lse_ref[0, h, pl.ds(second, 1), :] = top + jnp.log(total)
    oa_ref[...] = o_ref[0]
    ob_ref[...] = o_ref[1]


def self_forward(info, own, oth, bias, pieces):
    half, width = own.shape
    outer, depth, cols = pieces[0].shape
    wide = 2 * cols // 3
    pairs = wide // 128
    fixed2 = pl.BlockSpec((half, width), lambda i, info: (0, 0))
    pair_cols = pl.BlockSpec((half, 128), lambda i, info: (0, i))
    return pl.pallas_call(
        self_forward_kernel,
        grid_spec=pltpu.PrefetchScalarGridSpec(
            num_scalar_prefetch=1,
            grid=(pairs,),
            in_specs=[
                fixed2,
                fixed2,
                pl.BlockSpec(bias.shape, lambda i, info: (0, 0)),
                ANY,
                ANY,
                ANY,
                ANY,
            ],
            out_specs=[
                pl.BlockSpec((2, half, 3 * wide), lambda i, info: (0, 0, 0)),
                pl.BlockSpec((width, 3 * wide), lambda i, info: (0, 0)),
                pair_cols,
                pair_cols,
                pl.BlockSpec((1, 2, 2, half), lambda i, info: (i, 0, 0, 0)),
            ],
            scratch_shapes=[
                pltpu.VMEM((outer, 2, depth, cols), BF),
                pltpu.VMEM((outer, 2, depth, cols), BF),
                pltpu.VMEM((2, half, 128), BF),
                pltpu.SemaphoreType.DMA((4,)),
            ],
        ),
        out_shape=[
            struct((2, half, 3 * wide), BF),
            struct((width, 3 * wide), BF),
            struct((half, wide), BF),
            struct((half, wide), BF),
            struct((pairs, 2, 2, half), F32),
        ],
        compiler_params=pltpu.CompilerParams(vmem_limit_bytes=VMEM_LIMIT),
        cost_estimate=pl.CostEstimate(
            flops=2 * 2 * half * width * 3 * wide, bytes_accessed=own.size * 12, transcendentals=0
        ),
        name="self_fwd",
    )(info, own, oth, bias, *pieces)


def assemble_kernel(info, *refs):
    pieces, (kv_ref, q_ref, so_ref, co_ref) = refs[:8], refs[8:]
    place = info[0]
    outer, depth, cols = pieces[0].shape
    piece = cols // 5
    for j in range(4):
        for y in range(2):
            at = place if y == 0 else 1 - place
            for o in range(outer):
                value = pieces[2 * j + y][o]
                own = slice(piece * j, piece * (j + 1))
                low = slice(4 * piece + piece * j, 4 * piece + piece * (j + 1))
                kv_ref[o, at, :, own] = value[:, :piece]
                kv_ref[o, at, :, low] = value[:, piece : 2 * piece]
                q_ref[o, at, :, own] = value[:, 2 * piece : 3 * piece]
                so_ref[o, at, :, own] = value[:, 3 * piece : 4 * piece]
                co_ref[o, at, :, own] = value[:, 4 * piece :]


def assemble(info, pieces):
    outer, depth, cols = pieces[0].shape
    wide = cols // 5 * 4
    outs = call(
        assemble_kernel,
        [struct((outer, 2, depth, 2 * wide), BF)] + [struct((outer, 2, depth, wide), BF)] * 3,
        [info] + list(pieces),
        [SM] + [VM] * 8,
        [VM] * 4,
        moved=pieces[0].size * 32,
        name="assemble",
    )
    return [out.reshape(-1, out.shape[-1]) for out in outs]


def copies_kernel(info, own_ref, x_ref, y_ref, xy_ref, out_ref):
    place = info[0]
    for copy in range(out_ref.shape[0]):
        out_ref[copy, 0, place] = own_ref[...]
        out_ref[copy, 0, 1 - place] = y_ref[...]
        out_ref[copy, 1, place] = x_ref[...]
        out_ref[copy, 1, 1 - place] = xy_ref[...]


def plane_copies(info, own, x, y, xy):
    depth, cols = own.shape
    outer = outer_count()
    return call(
        copies_kernel,
        struct((outer, 2, 2, depth, cols), BF),
        [info, own, x, y, xy],
        [SM] + [VM] * 4,
        VM,
        moved=own.size * 2 * 4 * (outer + 1),
        name="plane_copies",
    )


def first_forward_kernel(
    tok_ref, own_ref, oth_ref, o_mat, vec_ref, q_mat, qb_ref,
    resid_ref, first_ref, low_ref, q_ref, mixed_ref,
):
    cols = own_ref.shape[1]
    mixed_ref[:, :cols] = own_ref[...]
    mixed_ref[:, cols:] = oth_ref[...]
    resid = tok_ref[...].astype(F32) + mm(mixed_ref[...], o_mat[...], NT) + vec_ref[0:1, :]
    resid_ref[...] = resid
    normed, rstd = norm_parts(resid)
    first = normed * vec_ref[1:2, :] + vec_ref[2:3, :]
    first_ref[...] = first
    low_ref[...] = first.astype(BF)
    scale = 1.0 / math.sqrt(HD)
    q_ref[...] = ((mm(low_ref[...], q_mat[...]) + qb_ref[...]) * scale).astype(BF)


def first_forward(tokens, own, oth, o_mat, vecs, q_mat, q_bias):
    rows, width = tokens.shape
    return call(
        first_forward_kernel,
        [struct((rows, width), F32)] * 2 + [struct((rows, width), BF)] * 3,
        [tokens, own, oth, o_mat, vecs, q_mat, q_bias],
        [VM] * 7,
        [VM] * 5,
        flops=2 * rows * width * width * 2 * 2,
        moved=width * width * 4 + rows * width * 18,
        name="first_forward",
    )


def feed_kernel(
    info, mixed_ref, first_ref, cot_ref, vec_ref, wo_hbm,
    e0, e1, e2, e3, e4, e5, e6, e7, s0, s1,
    out_ref, second_ref, low_ref, grad_ref, sums_ref,
    keep_e, keep_s, send_e, send_s,
    wo, we, ws, hid, slo, out_a, out_b, norm2, h2low, e3low, acc, wsem, osem,
):
    first_copy = pltpu.make_async_copy(wo_hbm, wo, wsem.at[0])
    first_copy.start()
    place = info[0]
    copies = []
    for j, pair in enumerate(((e0, e1), (e2, e3), (e4, e5), (e6, e7))):
        for y, ref in enumerate(pair):
            at = place if y == 0 else 1 - place
            copies.append(pltpu.make_async_copy(ref, we.at[j, :, at], wsem.at[1 + 2 * j + y]))
    for j in range(4):
        ref = (s0, s1)[j // 2]
        copies.append(pltpu.make_async_copy(ref.at[:, j % 2], ws.at[j], wsem.at[9 + j]))
    for copy in copies:
        copy.start()

    width = first_ref.shape[1]
    hidden_cols = we.shape[-1]

    def expand_mat(j):
        return we[j].reshape(width, hidden_cols)

    def shrink_mat(j):
        return ws[j].reshape(width, hidden_cols)

    def row(i):
        return vec_ref[i : i + 1, :]

    first_copy.wait()
    resid = first_ref[...] + mm(mixed_ref[...], wo[...], NT) + row(0)
    normed, rstd2 = norm_parts(resid)
    norm2[...] = normed
    second = normed * row(1) + row(2)
    h2low[...] = second.astype(BF)
    acc[...] = second + row(7)
    for copy in copies:
        copy.wait()

    def forward(j, carry):
        inner = mm(h2low[...], expand_mat(j)) + vec_ref[pl.ds(3 + j, 1), :]
        phi = 0.5 + 0.5 * lax.erf(inner * (1.0 / math.sqrt(2.0)))
        hidden = (inner * phi).astype(BF)
        hid[j] = hidden
        bell = jnp.exp(-0.5 * inner * inner) * (1.0 / math.sqrt(2.0 * math.pi))
        slo[j] = (phi + inner * bell).astype(BF)
        acc[...] += mm(hidden, shrink_mat(j), NT)
        return carry

    lax.fori_loop(0, 4, forward, 0)
    norm3, rstd3 = norm_parts(acc[...])
    out_ref[...] = (norm3 * row(8) + row(9)).astype(BF)
    cot = cot_ref[...].astype(F32)
    sums_ref[0:1, :] = jnp.sum(cot, 0, keepdims=True)
    sums_ref[1:2, :] = jnp.sum(cot * norm3, 0, keepdims=True)
    third = norm_back(norm3, rstd3, cot, row(8))
    low = third.astype(BF)
    e3low[...] = low
    sums_ref[2:3, :] = jnp.sum(low.astype(F32), 0, keepdims=True)
    acc[...] = third

    def out_copies(to_e, to_s, at, slot):
        copies = []
        for y in range(2):
            rel = y ^ place
            copies.append(
                pltpu.make_async_copy(
                    out_a.at[slot, :, y], to_e.at[at, rel], osem.at[0, slot, y]
                )
            )
            copies.append(
                pltpu.make_async_copy(
                    out_b.at[slot, :, y], to_s.at[:, at, rel], osem.at[1, slot, y]
                )
            )
        return copies

    def backward(step, carry):
        j = (step + 2) % 4
        slot = step % 2
        slope = slo[j].astype(F32)
        inner_grad = (mm(e3low[...], shrink_mat(j)) * slope).astype(BF)
        true_block = info[1] ^ (2 * (j % 2) + j // 2)
        sums_ref[pl.ds(8 + true_block, 1), :] = jnp.sum(
            inner_grad.astype(F32), 0, keepdims=True
        )

        @pl.when(step >= 2)
        def _():
            for copy in out_copies(send_e, send_s, slot, slot):
                copy.wait()

        out_a[slot] = mm(h2low[...], inner_grad, TN).astype(BF).reshape(out_a.shape[1:])
        out_b[slot] = mm(e3low[...], hid[j], TN).astype(BF).reshape(out_b.shape[1:])

        @pl.when(step < 2)
        def _():
            for copy in out_copies(send_e, send_s, slot, slot):
                copy.start()

        @pl.when(step >= 2)
        def _():
            for copy in out_copies(keep_e, keep_s, slot, slot):
                copy.start()

        acc[...] += mm(inner_grad, expand_mat(j), NT)
        return carry

    lax.fori_loop(0, 4, backward, 0)
    grad = acc[...]
    normed = norm2[...]
    sums_ref[3:4, :] = jnp.sum(grad, 0, keepdims=True)
    sums_ref[4:5, :] = jnp.sum(grad * normed, 0, keepdims=True)
    second_in = norm_back(normed, rstd2, grad, row(1))
    second_ref[...] = second_in
    low = second_in.astype(BF)
    low_ref[...] = low
    sums_ref[5:6, :] = jnp.sum(low.astype(F32), 0, keepdims=True)
    sums_ref[6:8, :] = jnp.zeros((2, sums_ref.shape[1]), F32)
    sums_ref[12:16, :] = jnp.zeros((4, sums_ref.shape[1]), F32)
    grad_ref[...] = mm(low, wo[...]).astype(BF)
    for slot in range(2):
        for copy in out_copies(keep_e, keep_s, slot, slot):
            copy.wait()


def feed(info, mixed, first, cot, vecs, wo, expand, shrink):
    rows, width = mixed.shape
    outer, depth, hidden = expand[0].shape
    grad_e = struct((2, 2, outer, depth, hidden), BF)
    grad_s = struct((outer, 2, 2, depth, hidden), BF)
    return call(
        feed_kernel,
        [
            struct((rows, width), BF),
            struct((rows, width), F32),
            struct((rows, width), BF),
            struct((rows, width), BF),
            struct((16, width), F32),
            grad_e,
            grad_s,
            grad_e,
            grad_s,
        ],
        [info, mixed, first, cot, vecs, wo] + list(expand) + list(shrink),
        [SM, VM, VM, VM, VM] + [ANY] * 11,
        [VM] * 5 + [ANY] * 4,
        [
            pltpu.VMEM((width, width), BF),
            pltpu.VMEM((4, outer, 2, depth, hidden), BF),
            pltpu.VMEM((4, outer, 2, depth, hidden), BF),
            pltpu.VMEM((4, rows, hidden), BF),
            pltpu.VMEM((4, rows, hidden), BF),
            pltpu.VMEM((2, outer, 2, depth, hidden), BF),
            pltpu.VMEM((2, outer, 2, depth, hidden), BF),
            pltpu.VMEM((rows, width), F32),
            pltpu.VMEM((rows, width), BF),
            pltpu.VMEM((rows, width), BF),
            pltpu.VMEM((rows, width), F32),
            pltpu.SemaphoreType.DMA((13,)),
            pltpu.SemaphoreType.DMA((2, 2, 2)),
        ],
        flops=2 * rows * width * (6 * 4 * hidden + 2 * width) * 2,
        moved=width * hidden * 4 * 4 * 2,
        name="feed",
    )


def first_back_kernel(
    dq_ref, q_mat, second_ref, resid_ref, vec_ref, o_mat, first_ref, low_ref, keep_ref, send_ref, sums_ref
):
    grad = second_ref[...] + mm(dq_ref[...], q_mat[...], NT)
    normed, rstd = norm_parts(resid_ref[...])
    sums_ref[0:1, :] = jnp.sum(grad, 0, keepdims=True)
    sums_ref[1:2, :] = jnp.sum(grad * normed, 0, keepdims=True)
    first_in = norm_back(normed, rstd, grad, vec_ref[0:1, :])
    first_ref[...] = first_in
    low = first_in.astype(BF)
    low_ref[...] = low
    sums_ref[2:3, :] = jnp.sum(low.astype(F32), 0, keepdims=True)
    sums_ref[3:4, :] = jnp.sum(dq_ref[...].astype(F32), 0, keepdims=True)
    sums_ref[4:8, :] = jnp.zeros((4, sums_ref.shape[1]), F32)
    mixed_grad = mm(low, o_mat[...]).astype(BF)
    cols = keep_ref.shape[1]
    keep_ref[...] = mixed_grad[:, :cols]
    send_ref[...] = mixed_grad[:, cols:]


def first_back(dq, q_mat, second_in, resid, vec, o_mat):
    rows, width = dq.shape
    cols = width // 2
    return call(
        first_back_kernel,
        [
            struct((rows, width), F32),
            struct((rows, width), BF),
            struct((rows, cols), BF),
            struct((rows, cols), BF),
            struct((8, width), F32),
        ],
        [dq, q_mat, second_in, resid, vec, o_mat],
        [VM] * 6,
        [VM] * 5,
        flops=2 * rows * width * width * 2 * 2,
        moved=width * width * 4 + rows * width * 18,
        name="first_back",
    )


def put_rows(ref, x, full, at, place):
    outer, depth = ref.shape[2], ref.shape[3]
    for o in range(outer):
        for y in range(2):
            start = (2 * o + y) * depth
            ref[x, y ^ place, o, :, at] = full[start : start + depth]


def put_blocks(keep_ref, send_ref, full, i, place):
    piece = full.shape[1] // 4
    at = slice(i * piece, (i + 1) * piece)
    for j in range(4):
        put_rows((keep_ref, send_ref)[j // 2], j % 2, full[:, j * piece : (j + 1) * piece], at, place)


def query_grads_kernel(
    info, h1_ref, dq_ref, e1_ref, o1_ref, e2_ref, o2_ref, keep_ref, send_ref
):
    for i, (left, right) in enumerate(((h1_ref, dq_ref), (e1_ref, o1_ref), (e2_ref, o2_ref))):
        full = mm(left[...], right[...], TN).astype(BF)
        put_blocks(keep_ref, send_ref, full, i, info[0])


def key_grads_kernel(info, fet_ref, own_ref, got_ref, mat_ref, keep_ref, send_ref, grad_ref, sum_ref):
    width = fet_ref.shape[1]
    total = None
    for i in range(2):
        low = add_low(own_ref[i], got_ref[i])
        full = mm(fet_ref[...], low, TN).astype(BF)
        put_blocks(keep_ref, send_ref, full, i, info[0])
        term = mm(low, mat_ref[:, i * width : (i + 1) * width], NT)
        total = term if total is None else total + term
        if i == 1:
            sum_ref[0:1, :] = jnp.sum(low.astype(F32), 0, keepdims=True)
            sum_ref[1:8, :] = jnp.zeros((7, width), F32)
    grad_ref[...] = total.astype(BF)


def query_grads(info, args, depth):
    width = args[0].shape[1]
    out = struct((2, 2, width // depth // 2, depth, 3 * width // 4), BF)
    return call(
        query_grads_kernel,
        [out, out],
        [info] + list(args),
        [SM] + [VM] * 6,
        [VM] * 2,
        flops=2 * 512 * width * width * 3,
        moved=width * width * 10,
        name="query_grads",
    )


def key_grads(info, fetched, own, got, mat, depth):
    rows, width = fetched.shape
    out = struct((2, 2, width // depth // 2, depth, 2 * width // 4), BF)
    return call(
        key_grads_kernel,
        [out, out, struct((rows, width), BF), struct((8, width), F32)],
        [info, fetched, own, got, mat],
        [SM] + [VM] * 4,
        [VM] * 4,
        flops=2 * rows * width * width * 4,
        moved=width * width * 10,
        name="key_grads",
    )


def self_grads_kernel(info, own_ref, oth_ref, d_ref, a_ref, x_ref, y_ref, xy_ref):
    place = info[0]
    cols = d_ref.shape[3]
    piece = cols // 2
    outer, depth = a_ref.shape[0], a_ref.shape[1]
    for i in range(3):
        full = mm(own_ref[...], d_ref[i, 0], TN) + mm(oth_ref[...], d_ref[i, 1], TN)
        full = full.astype(BF)
        at = slice(i * piece, (i + 1) * piece)
        for x, (near, away) in enumerate(((a_ref, y_ref), (x_ref, xy_ref))):
            for o in range(outer):
                start = 2 * o * depth
                first = full[start : start + depth, x * piece : (x + 1) * piece]
                second = full[start + depth : start + 2 * depth, x * piece : (x + 1) * piece]
                near[o, :, at] = jnp.where(place == 0, first, second)
                away[o, :, at] = jnp.where(place == 0, second, first)


def self_grads(info, own, oth, grads, depth):
    half, width = own.shape
    cols = grads.shape[3]
    out = struct((width // depth // 2, depth, 3 * cols // 2), BF)
    return call(
        self_grads_kernel,
        [out] * 4,
        [info, own, oth, grads],
        [SM] + [VM] * 3,
        [VM] * 4,
        flops=2 * 2 * half * width * 3 * cols * 2,
        moved=half * width * 4 + half * cols * 12 + width * cols * 6,
        name="self_grads",
    )


def self_back_kernel(d_ref, mat_ref, first_ref, keep_ref, send_ref):
    cols = d_ref.shape[3]
    for rel in (1, 0):
        total = mm(d_ref[0, rel], mat_ref[:, :cols], NT)
        for i in (1, 2):
            total = total + mm(d_ref[i, rel], mat_ref[:, i * cols : (i + 1) * cols], NT)
        if rel == 1:
            send_ref[...] = total.astype(BF)
        else:
            keep_ref[...] = total + first_ref[...]


def self_back(grads, mat, first_in):
    half, width = first_in.shape
    cols = grads.shape[3]
    return call(
        self_back_kernel,
        [struct((half, width), F32), struct((half, width), BF)],
        [grads, mat, first_in],
        [VM] * 3,
        [VM] * 2,
        flops=2 * 2 * half * width * 3 * cols * 2,
        moved=half * width * 10 + half * cols * 12 + width * cols * 6,
        name="self_back",
    )


def fetch_kernel(table, bank_ref, mine_ref, send_ref, sem):
    count = table.shape[0] // 2

    def each(act):
        for group, out_ref in enumerate((mine_ref, send_ref)):

            def body(i, carry, group=group, out_ref=out_ref):
                at = table[group * count + i]
                copy = pltpu.make_async_copy(
                    bank_ref.at[jnp.maximum(at, 0)], out_ref.at[i], sem.at[group * count + i]
                )
                act(copy, at >= 0, out_ref, i)
                return carry

            lax.fori_loop(0, count, body, 0)

    def start(copy, held, out_ref, i):
        @pl.when(held)
        def _():
            copy.start()

        @pl.when(jnp.logical_not(held))
        def _():
            out_ref[i] = jnp.zeros(out_ref.shape[1:], out_ref.dtype)

    def finish(copy, held, out_ref, i):
        @pl.when(held)
        def _():
            copy.wait()

    each(start)
    each(finish)


def fetch(table, bank_blocks):
    count = table.shape[0]
    blk, width = bank_blocks.shape[1:]
    out = struct((count // 2, blk, width), BF)
    mine, send = call(
        fetch_kernel,
        [out, out],
        [table, bank_blocks],
        [SM, ANY],
        [VM, VM],
        [pltpu.SemaphoreType.DMA((count,))],
        moved=count * blk * width * 4,
        name="fetch",
    )
    return [part.reshape(2, count // 4, blk, width) for part in (mine, send)]


def scatter_kernel(table, a_ref, b_ref, c_ref, d_ref, out_ref, slots, sems):
    step = pl.program_id(0)
    per = out_ref.shape[0]

    @pl.when(step == 0)
    def _():
        copies = [
            pltpu.make_async_copy(ref, slots.at[i], sems.at[i])
            for i, ref in enumerate((a_ref, b_ref, c_ref, d_ref))
        ]
        for copy in copies:
            copy.start()
        for copy in copies:
            copy.wait()

    for i in range(per):
        at = table[step * per + i]
        group = jnp.maximum(at, 0) // slots.shape[1]
        place = jnp.maximum(at, 0) % slots.shape[1]
        value = slots[group, place].astype(F32)
        out_ref[i] = jnp.where(at >= 0, value, 0.0)


def scatter(table, parts):
    count = table.shape[0]
    slots, blk, width = parts[0].shape
    per = 4
    return pl.pallas_call(
        scatter_kernel,
        grid_spec=pltpu.PrefetchScalarGridSpec(
            num_scalar_prefetch=1,
            grid=(count // per,),
            in_specs=[ANY] * 4,
            out_specs=pl.BlockSpec((per, blk, width), lambda i, t: (i, 0, 0)),
            scratch_shapes=[
                pltpu.VMEM((4, slots, blk, width), BF),
                pltpu.SemaphoreType.DMA((4,)),
            ],
        ),
        out_shape=struct((count, blk, width), F32),
        compiler_params=pltpu.CompilerParams(vmem_limit_bytes=VMEM_LIMIT),
        cost_estimate=pl.CostEstimate(
            flops=0, bytes_accessed=count * blk * width * 6, transcendentals=0
        ),
        name="scatter",
    )(table, *parts)


def sum_all(ref):
    total = ref[0].astype(F32)
    for i in range(1, ref.shape[0]):
        total = total + ref[i].astype(F32)
    return total


def sum_query_kernel(in_ref, q_ref, so_ref, co_ref):
    total = sum_all(in_ref)
    piece = total.shape[1] // 3
    q_ref[...] = total[:, :piece]
    so_ref[...] = total[:, piece : 2 * piece].T
    co_ref[...] = total[:, 2 * piece :].T


def sum_query(value):
    count, depth, cols = value.shape
    piece = cols // 3
    return call(
        sum_query_kernel,
        [struct((depth, piece), F32)] + [struct((piece, depth), F32)] * 2,
        [value],
        [VM],
        [VM] * 3,
        moved=value.size * 2 + depth * cols * 4,
        name="sum_query",
    )


def sum_turned_kernel(in_ref, out_ref):
    out_ref[...] = sum_all(in_ref).T


def sum_turned(value):
    count, depth, cols = value.shape
    return call(
        sum_turned_kernel,
        struct((cols, depth), F32),
        [value],
        [VM],
        VM,
        moved=value.size * 2 + depth * cols * 4,
        name="sum_turned",
    )


def local(
    tokens,
    bank,
    prefix,
    blocks,
    out_grad,
    selfq_weight,
    selfq_bias,
    selfk_weight,
    selfv_weight,
    selfv_bias,
    selfo_weight,
    selfo_bias,
    first_gain,
    first_shift,
    crossq_weight,
    crossq_bias,
    crossk_weight,
    crossv_weight,
    crossv_bias,
    crosso_weight,
    crosso_bias,
    second_gain,
    second_shift,
    expand_weight,
    expand_bias,
    shrink_weight,
    shrink_bias,
    third_gain,
    third_shift,
):
    rank = lax.axis_index("tensor")
    core = rank % 2
    chip = rank // 2
    inner = lax.axis_index("dp") % 2
    outer = outer_count()
    half, width = tokens.shape
    seq_count = prefix.shape[0]
    local_blocks = bank.shape[1] // BLK
    head_cols = selfq_bias.shape[0]
    hidden_cols = expand_bias.shape[0]
    depth = selfq_weight.shape[0]
    slots = NBLK // 2
    two = 2 * head_cols
    attn_cols = 5 * head_cols
    info = jnp.stack([inner, rank, chip]).astype(jnp.int32)

    self_leaf = call(
        pack_self_kernel,
        struct((outer, depth, 3 * head_cols), BF),
        [selfq_weight, selfk_weight, selfv_weight],
        [VM] * 3,
        VM,
        name="pack_self",
    )
    self_z = outer_exchange(self_leaf)
    bias_own = jnp.concatenate(
        [selfq_bias, selfv_bias, crossq_bias, crossv_bias, expand_bias]
    ).reshape(1, -1)
    bias_two = jnp.concatenate([bias_own, swap_x(bias_own)], axis=0)
    bias_four = jnp.concatenate([bias_two, swap_core(bias_two)], axis=0)
    cq_bias = bias_four[:, two : 3 * head_cols].reshape(-1)
    cv_bias = bias_four[:, 3 * head_cols : 4 * head_cols].reshape(-1)
    ex_bias = bias_four[:, 4 * head_cols :]
    self_bias = jnp.stack(
        [
            bias_two[:, :head_cols].reshape(-1),
            jnp.zeros((two,), F32),
            bias_two[:, head_cols:two].reshape(-1),
        ]
    )
    attn_leaf, expand_leaf, shrink_leaf = call(
        pack_rest_kernel,
        [
            struct((outer, depth, attn_cols), BF),
            struct((outer, depth, hidden_cols), BF),
            struct((depth, hidden_cols), BF),
        ],
        [
            gate(crossk_weight, self_leaf), crossv_weight, crossq_weight, selfo_weight,
            crosso_weight, expand_weight, shrink_weight,
        ],
        [VM] * 7,
        [VM] * 3,
        name="pack_rest",
    )
    shrink_x, shrink_y = swap_x(shrink_leaf), swap_dp(shrink_leaf, 1)
    shrink_xy = swap_both(shrink_leaf)
    tokens_oth = swap_core(tokens)
    shrink_pack = plane_copies(info, shrink_leaf, shrink_x, shrink_y, shrink_xy)

    self_z, shrink_pack, self_bias = lax.optimization_barrier((self_z, shrink_pack, self_bias))
    self_near, self_away, self_both = swap_x(self_z), swap_dp(self_z, 1), swap_both(self_z)
    attn_z = outer_exchange(gate(attn_leaf, self_z))

    seq_order = jnp.stack([chip, 1 - chip])
    near = blocks[seq_order].reshape(2, 2, slots)
    near = jnp.stack([near[:, core], near[:, 1 - core]])
    near = near - rank * local_blocks
    held = (near >= 0) & (near < local_blocks)
    fetch_table = jnp.where(held, near + seq_order[None, :, None] * local_blocks, -1)
    fetch_table = gate(fetch_table.reshape(-1).astype(jnp.int32), self_z)
    part_mine, part_send = fetch(fetch_table, bank.reshape(seq_count * local_blocks, BLK, width))
    part_got = swap_core(part_send)
    part_keep = part_mine[0] + part_got[0]
    part_away = part_mine[1] + part_got[1]
    attn_z, tokens_in, self_near, self_away, self_both, part_away = lax.optimization_barrier(
        (attn_z, tokens, self_near, self_away, self_both, part_away)
    )
    attn_x, attn_y, attn_xy = swap_x(attn_z), swap_dp(attn_z, 1), swap_both(attn_z)
    part_back = swap_x(part_away)
    expand_z = outer_exchange(gate(expand_leaf, attn_z))

    my_prefix = lax.dynamic_index_in_dim(prefix, chip, 0, keepdims=False)
    attn_info = jnp.stack([core, my_prefix]).astype(jnp.int32)
    qkv, self_mat, self_own, self_send, self_lse = self_forward(
        jnp.concatenate([info, attn_info]),
        tokens_in,
        tokens_oth,
        self_bias,
        (self_z, self_near, self_away, self_both),
    )
    self_got = swap_core(self_send)
    part_back, attn_x, attn_y, attn_xy, expand_z = lax.optimization_barrier(
        (part_back, attn_x, attn_y, attn_xy, expand_z, self_own)
    )[:5]
    shrink_z = outer_exchange(gate(shrink_pack, expand_z))
    fetched = (part_keep + part_back).reshape(slots * BLK, width)
    expand_x, expand_y, expand_xy = swap_x(expand_z), swap_dp(expand_z, 1), swap_both(expand_z)

    attn_own = (attn_z, attn_y, attn_x, attn_xy)
    attn_oth = tuple(swap_core(piece) for piece in attn_own)
    cross_kv, cross_q, self_o, cross_o = assemble(info, attn_own + attn_oth)
    first_sum, first_out, first_low, queries, mixed_one = first_forward(
        tokens,
        self_own,
        self_got,
        self_o,
        jnp.stack([selfo_bias, first_gain, first_shift]),
        cross_q,
        cq_bias.reshape(1, -1),
    )

    kv_bias = jnp.concatenate([jnp.zeros_like(cv_bias), cv_bias])
    kv_own = (mm(fetched, cross_kv) + kv_bias).astype(BF)
    kv_oth = swap_core(kv_own)
    queries, expand_x, expand_y, expand_xy, shrink_z = lax.optimization_barrier(
        (queries, expand_x, expand_y, expand_xy, shrink_z)
    )
    mixed_two, cross_lse = cross_forward(queries, kv_own, kv_oth)

    expand_own = (expand_z, expand_y, expand_x, expand_xy)
    expand_oth = tuple(swap_core(piece) for piece in expand_own)
    vecs = jnp.concatenate(
        [
            jnp.stack([crosso_bias, second_gain, second_shift]),
            ex_bias,
            jnp.stack([shrink_bias, third_gain, third_shift]),
        ]
    )
    (
        out_act, second_in, cross_low, cross_grad, late_vec,
        expand_keep, shrink_keep, expand_send, shrink_send,
    ) = feed(
        info, mixed_two, first_out, out_grad, vecs, cross_o,
        expand_own + expand_oth, (shrink_z, swap_core(shrink_z)),
    )

    def plane_send(keep, got):
        return tuple(add_low(keep[x, y], got[x, y]) for x, y in ((1, 0), (0, 1), (1, 1)))

    def plane_swap(parts):
        return swap_x(parts[0]), swap_dp(parts[1], 1), swap_both(parts[2])

    def plane_sum(own, got):
        total = sum(part.astype(F32) for part in own)
        return total + sum(part.astype(F32) for part in got)

    def fold(value, dtype):
        return jnp.sum(value.astype(F32), axis=0).astype(dtype)

    shrink_got = swap_core(shrink_send)
    expand_got = swap_core(expand_send)
    part_one = cross_backward(queries, kv_own, kv_oth, mixed_two, cross_lse, cross_grad, 0, 2)
    shrink_places, expand_plane, part_one = lax.optimization_barrier(
        (
            add_low(gate(shrink_keep, part_one[0]), shrink_got),
            plane_send(gate(expand_keep, part_one[0]), expand_got),
            tuple(part_one),
        )
    )
    expand_parts = plane_swap(expand_plane)
    shrink_parts = outer_exchange(shrink_places)

    dq, dkv_own, dkv_send, first_in, self_low, grad_own, grad_send, early_vec = cross_first_backward(
        queries, kv_own, kv_oth, mixed_two, cross_lse, cross_grad, 2, part_one,
        cross_q, second_in, first_sum, first_gain.reshape(1, -1), self_o,
    )
    dkv_got = swap_core(dkv_send)
    grad_got = swap_core(grad_send)
    self_low, expand_parts = lax.optimization_barrier((self_low, expand_parts))
    expand_three = plane_sum((expand_keep[0, 0], expand_got[0, 0]), expand_parts).astype(BF)
    query_keep, query_send = query_grads(
        info, (first_low, dq, self_low, mixed_one, cross_low, mixed_two), depth
    )
    dkv_own, query_send = lax.optimization_barrier((dkv_own, query_send))
    query_got = swap_core(query_send)
    key_keep, key_send, fetched_grad, cv_rows = key_grads(
        info, fetched, dkv_own, dkv_got, cross_kv, depth
    )
    query_plane = plane_send(gate(query_keep, cv_rows), query_got)
    query_plane, key_send, grad_got, fetched_grad = lax.optimization_barrier(
        (query_plane, key_send, grad_got, fetched_grad)
    )
    query_parts = plane_swap(query_plane)
    key_got = swap_core(key_send)

    self_args = (attn_info, qkv, self_own, self_send, self_lse, grad_own, grad_got)
    pairs = two // 128
    half_grads = self_backward(*self_args, 0, pairs - 1)
    key_plane = plane_send(gate(key_keep, half_grads[1]), key_got)
    key_plane, half_grads, query_parts, shrink_parts, expand_three, fetched_send = (
        lax.optimization_barrier(
            (key_plane, tuple(half_grads), query_parts, shrink_parts, expand_three, fetched_grad)
        )
    )
    key_parts = plane_swap(key_plane)
    expand_last = outer_exchange(expand_three)
    shrink_three = fold(shrink_parts, BF)
    query_three = plane_sum((query_keep[0, 0], query_got[0, 0]), query_parts).astype(BF)
    grads, self_sums = self_backward(*self_args, pairs - 1, 1, half_grads)

    order = jnp.arange(4) ^ rank
    order = 2 * (order % 2) + order // 2

    def straight(vecs):
        return vecs.reshape(vecs.shape[0], 4, -1)[:, order].reshape(vecs.shape[0], -1)

    self_sums = self_sums[:, :3].transpose(1, 0, 2).reshape(3, two)
    self_sums = jnp.concatenate([self_sums, jnp.zeros_like(self_sums)], axis=1)
    turned_vecs = jnp.concatenate([early_vec[3:4], cv_rows[:1], self_sums[0:1], self_sums[2:3]])
    sums = jnp.concatenate([late_vec, early_vec[:3], straight(turned_vecs)])
    sums = sums + swap_core(sums)
    sums, grads, shrink_three = lax.optimization_barrier((sums, grads, shrink_three))
    sums_got = swap_x(sums)
    shrink_near = (
        swap_x(shrink_three[1, 0]), swap_dp(shrink_three[0, 1], 1), swap_both(shrink_three[1, 1])
    )
    self_places = self_grads(info, tokens, tokens_oth, grads, depth)
    sums, self_places, grads, key_parts = lax.optimization_barrier(
        (sums + sums_got, tuple(self_places), grads, key_parts)
    )
    bits = dp_bits()
    sums_got = swap_dp(sums, bits[-1])
    self_parts = (swap_x(self_places[1]), swap_dp(self_places[2], 1), swap_both(self_places[3]))
    key_three = plane_sum((key_keep[0, 0], key_got[0, 0]), key_parts).astype(BF)
    query_last = outer_exchange(gate(query_three, expand_last))
    back_keep, back_send = self_back(grads, self_mat, first_in)
    sums = sums + gate(sums_got, back_send)
    for bit in bits[:-1]:
        sums = sums + swap_dp(sums, bit)
    fetched_send = gate(fetched_send, back_send)
    fetched_away = swap_x(fetched_send).reshape(slots, BLK, width)
    fetched_near = fetched_send.reshape(slots, BLK, width)
    self_three = plane_sum((self_places[0],), gate(self_parts, back_send)).astype(BF)
    self_last = outer_exchange(jnp.concatenate([self_three, key_three], axis=-1))
    in_grad = (back_keep + swap_core(back_send).astype(F32)).astype(BF)
    shrink_last = jnp.stack((shrink_three[0, 0],) + shrink_near)

    cq_grad, so_grad, co_grad = sum_query(query_last)
    self_total = fold(self_last, F32)
    ck_grad = self_total[:, 3 * head_cols : 4 * head_cols]
    cv_grad = self_total[:, 4 * head_cols :]
    expand_grad = fold(expand_last, F32)
    shrink_grad = sum_turned(shrink_last)

    near_core = swap_core(fetched_near)
    away_core = swap_core(fetched_away)
    slot_ids = jnp.arange(NBLK)
    places = (
        (((slot_ids[None, :] // slots) != core) * 2 + (jnp.arange(seq_count)[:, None] != chip))
        * slots
        + slot_ids[None, :] % slots
    )
    hits = blocks[:, None, :] == (rank * local_blocks + jnp.arange(local_blocks))[None, :, None]
    scatter_table = jnp.max(jnp.where(hits, places[:, None, :], -1), axis=-1)
    bank_grad = scatter(
        scatter_table.reshape(-1).astype(jnp.int32),
        (fetched_near, fetched_away, near_core, away_core),
    ).reshape(bank.shape)

    late_vec, early_vec = sums[:16], sums[16:]

    def own_part(vec, part_len):
        return lax.dynamic_slice_in_dim(vec, rank * part_len, part_len, 0)

    def self_part(which):
        return self_total[:, which * head_cols : (which + 1) * head_cols]

    return (
        out_act,
        in_grad,
        bank_grad,
        self_part(0),
        own_part(early_vec[5], head_cols),
        self_part(1),
        self_part(2),
        own_part(early_vec[6], head_cols),
        so_grad,
        early_vec[2],
        early_vec[1],
        early_vec[0],
        cq_grad,
        own_part(early_vec[3], head_cols),
        ck_grad,
        cv_grad,
        own_part(early_vec[4], head_cols),
        co_grad,
        late_vec[5],
        late_vec[4],
        late_vec[3],
        expand_grad,
        lax.dynamic_index_in_dim(late_vec, 8 + rank, 0, keepdims=False),
        shrink_grad,
        late_vec[2],
        late_vec[1],
        late_vec[0],
    )


def solution(mesh):
    rows = P(("dp", "tensor"), None)
    wide = P("dp", "tensor")
    tall = P("tensor", "dp")
    part = P("tensor")
    full = P()
    return jax.shard_map(
        local,
        mesh=mesh,
        in_specs=(
            rows, P("dp", "tensor", None), P("dp"), P("dp", None), rows,
            wide, part, wide, wide, part, tall, full, full, full,
            wide, part, wide, wide, part, tall, full, full, full,
            wide, part, tall, full, full, full,
        ),
        out_specs=(
            rows, rows, P("dp", "tensor", None),
            wide, part, wide, wide, part, tall, full, full, full,
            wide, part, wide, wide, part, tall, full, full, full,
            wide, part, tall, full, full, full,
        ),
        check_vma=False,
    )
```

```python
import functools
import math

import jax
import jax.numpy as jnp
from jax import lax
from jax.experimental import pallas as pl
from jax.experimental.pallas import tpu as pltpu
from jax.sharding import PartitionSpec as P

HD = 64
BLK = 64
NBLK = 16
EPS = 1e-05
NEGATIVE = -1e30
BF = jnp.bfloat16
F32 = jnp.float32

NT = (((1,), (1,)), ((), ()))
NN = (((1,), (0,)), ((), ()))
TN = (((0,), (0,)), ((), ()))

CORE_SWAP = ((0, 1), (1, 0), (2, 3), (3, 2))
X_SWAP = ((0, 2), (2, 0), (1, 3), (3, 1))
VMEM_LIMIT = 48 << 20
COST = pl.CostEstimate(flops=1000, bytes_accessed=1000, transcendentals=0)


def mm(left, right, dims=NN):
    return lax.dot_general(left, right, dims, preferred_element_type=F32)


def swap_core(value):
    return lax.ppermute(value, "tensor", CORE_SWAP)


def swap_x(value):
    return lax.ppermute(value, "tensor", X_SWAP)


def swap_dp(value, bit):
    count = lax.axis_size("dp")
    return lax.ppermute(value, "dp", tuple((i, i ^ bit) for i in range(count)))


def dp_bits():
    count = lax.axis_size("dp")
    bits = []
    bit = count // 2
    while bit >= 1:
        bits.append(bit)
        bit //= 2
    return bits


def pair_backward(q, k, v, grad, lse, delta, mask):
    score = mm(k, q, NT)
    prob = jnp.exp(score - lse)
    if mask is not None:
        prob = jnp.where(mask, prob, 0.0)
    slope = prob * (mm(v, grad, NT) - delta)
    prob = prob.astype(BF)
    slope = slope.astype(BF)
    return mm(slope, k, TN), mm(slope, q, NN), mm(prob, grad, NN)


def delta_row(grad, mixed):
    return jnp.sum((grad.astype(F32) * mixed.astype(F32)).T, 0, keepdims=True)


def self_bwd_kernel(info, q_ref, k_ref, v_ref, oa_ref, ob_ref, lse_ref, ga_ref, gb_ref, *rest):
    out_ref, sums_ref, o_ref, g_ref = rest[-4:]
    dq_ref, dk_ref, dv_ref = out_ref.at[0], out_ref.at[1], out_ref.at[2]
    o_ref[0], o_ref[1] = oa_ref[...], ob_ref[...]
    g_ref[0], g_ref[1] = ga_ref[...], gb_ref[...]
    half = q_ref.shape[1]
    first = info[0]
    second = 1 - first
    prefix = info[1]
    key_pos = lax.broadcasted_iota(jnp.int32, (half, half), 0)
    query_pos = lax.broadcasted_iota(jnp.int32, (half, half), 1)
    causal = key_pos <= query_pos
    seen = causal | (key_pos < prefix)
    scale = 1.0 / math.sqrt(HD)
    for h in range(2):
        cols = slice(HD * h, HD * h + HD)

        def rows(ref, at):
            return ref[at, :, cols]

        def one(q_at, k_at, mask):
            grad = rows(g_ref, q_at)
            delta = delta_row(grad, rows(o_ref, q_at))
            lse = lse_ref[0, h, pl.ds(q_at, 1), :]
            return pair_backward(
                rows(q_ref, q_at), rows(k_ref, k_at), rows(v_ref, k_at), grad, lse, delta, mask
            )

        dq, dk_a, dv_a = one(first, first, seen)
        dq_ref[first, :, cols] = (dq.astype(BF) * scale).astype(BF)
        dq_b, dk_b, dv_b = one(second, first, None)
        dk_ref[first, :, cols] = (dk_a + dk_b).astype(BF)
        dv_ref[first, :, cols] = (dv_a + dv_b).astype(BF)
        dq_c, dk_c, dv_c = one(second, second, causal)
        dq_ref[second, :, cols] = ((dq_b + dq_c).astype(BF) * scale).astype(BF)
        dk_ref[second, :, cols] = dk_c.astype(BF)
        dv_ref[second, :, cols] = dv_c.astype(BF)
    for i in range(3):
        both = out_ref[i, 0].astype(F32) + out_ref[i, 1].astype(F32)
        sums_ref[0, i : i + 1, :] = jnp.sum(both, 0, keepdims=True)


def self_backward(info, qkv, mixed_own, mixed_oth, lse, grad_own, grad_oth, start, count, former=()):
    half, width = qkv.shape[1], qkv.shape[2] // 3
    pairs = width // 128

    def spec(which):
        return pl.BlockSpec((2, half, 128), lambda i, info: (0, 0, which * pairs + start + i))

    flat = pl.BlockSpec((half, 128), lambda i, info: (0, start + i))
    cells = 3 * half * half * count * 2
    return pl.pallas_call(
        self_bwd_kernel,
        grid_spec=pltpu.PrefetchScalarGridSpec(
            num_scalar_prefetch=1,
            grid=(count,),
            in_specs=[
                spec(0),
                spec(1),
                spec(2),
                flat,
                flat,
                pl.BlockSpec((1, 2, 2, half), lambda i, info: (start + i, 0, 0, 0)),
                flat,
                flat,
            ]
            + [pl.BlockSpec(memory_space=pl.ANY)] * len(former),
            out_specs=[
                pl.BlockSpec((3, 2, half, 128), lambda i, info: (0, 0, 0, start + i)),
                pl.BlockSpec((1, 8, 128), lambda i, info: (start + i, 0, 0)),
            ],
            scratch_shapes=[pltpu.VMEM((2, half, 128), BF)] * 2,
        ),
        out_shape=[
            jax.ShapeDtypeStruct((3, 2, half, width), BF),
            jax.ShapeDtypeStruct((pairs, 8, 128), F32),
        ],
        input_output_aliases={9 + i: i for i in range(len(former))},
        compiler_params=pltpu.CompilerParams(vmem_limit_bytes=VMEM_LIMIT),
        cost_estimate=COST,
        name="self_bwd",
    )(info, qkv, qkv, qkv, mixed_own, mixed_oth, lse, grad_own, grad_oth, *former)


def cross_fwd_kernel(q_ref, ka_ref, kb_ref, va_ref, vb_ref, o_ref, lse_ref):
    for h in range(2):
        cols = slice(HD * h, HD * h + HD)
        q = q_ref[:, cols]
        score_a = mm(ka_ref[:, cols], q, NT)
        score_b = mm(kb_ref[:, cols], q, NT)
        top = jnp.maximum(
            jnp.max(score_a, 0, keepdims=True), jnp.max(score_b, 0, keepdims=True)
        )
        expo_a = jnp.exp(score_a - top)
        expo_b = jnp.exp(score_b - top)
        total = jnp.sum(expo_a, 0, keepdims=True) + jnp.sum(expo_b, 0, keepdims=True)
        mixed = (
            mm(va_ref[:, cols], expo_a.astype(BF), TN) + mm(vb_ref[:, cols], expo_b.astype(BF), TN)
        ) / total
        o_ref[:, cols] = mixed.T.astype(BF)
        lse_ref[0, h : h + 1, :] = top + jnp.log(total)


def cross_specs(rows, pairs):
    whole = pl.BlockSpec((rows, 128), lambda i: (0, i))
    turned = pl.BlockSpec((rows, 128), lambda i: (0, (i + pairs // 2) % pairs))
    value = pl.BlockSpec((rows, 128), lambda i: (0, pairs + i))
    value_turned = pl.BlockSpec((rows, 128), lambda i: (0, pairs + (i + pairs // 2) % pairs))
    return whole, turned, value, value_turned


def cross_forward(queries, kv_own, kv_oth):
    rows, width = queries.shape
    pairs = width // 128
    whole, turned, value, value_turned = cross_specs(rows, pairs)
    cells = 2 * rows * rows * pairs * 2
    return pl.pallas_call(
        cross_fwd_kernel,
        grid=(pairs,),
        in_specs=[whole, whole, turned, value, value_turned],
        out_specs=[whole, pl.BlockSpec((1, 2, rows), lambda i: (i, 0, 0))],
        out_shape=[
            jax.ShapeDtypeStruct((rows, width), BF),
            jax.ShapeDtypeStruct((pairs, 2, rows), F32),
        ],
        compiler_params=pltpu.CompilerParams(vmem_limit_bytes=VMEM_LIMIT),
        cost_estimate=COST,
        name="cross_fwd",
    )(queries, kv_own, kv_oth, kv_own, kv_oth)


def cross_bwd_kernel(
    q_ref, ka_ref, kb_ref, va_ref, vb_ref, o_ref, lse_ref, g_ref,
    *rest,
):
    dq_ref, da_ref, db_ref = rest[-3:]
    scale = 1.0 / math.sqrt(HD)
    for h in range(2):
        cols = slice(HD * h, HD * h + HD)
        grad = g_ref[:, cols]
        delta = delta_row(grad, o_ref[:, cols])
        lse = lse_ref[0, h : h + 1, :]
        q = q_ref[:, cols]
        dq_a, dk, dv = pair_backward(q, ka_ref[:, cols], va_ref[:, cols], grad, lse, delta, None)
        da_ref[0, :, cols] = dk.astype(BF)
        da_ref[1, :, cols] = dv.astype(BF)
        dq_b, dk, dv = pair_backward(q, kb_ref[:, cols], vb_ref[:, cols], grad, lse, delta, None)
        db_ref[0, :, cols] = dk.astype(BF)
        db_ref[1, :, cols] = dv.astype(BF)
        dq_ref[:, cols] = ((dq_a + dq_b).astype(BF) * scale).astype(BF)


def cross_backward(queries, kv_own, kv_oth, mixed, lse, grad, start, count, former=()):
    rows, width = queries.shape
    pairs = width // 128

    def turn(i):
        return (start + i + pairs // 2) % pairs

    whole = pl.BlockSpec((rows, 128), lambda i: (0, start + i))
    turned = pl.BlockSpec((rows, 128), lambda i: (0, turn(i)))
    value = pl.BlockSpec((rows, 128), lambda i: (0, pairs + start + i))
    value_turned = pl.BlockSpec((rows, 128), lambda i: (0, pairs + turn(i)))
    cells = 2 * rows * rows * count * 2
    both = jax.ShapeDtypeStruct((2, rows, width), BF)
    return pl.pallas_call(
        cross_bwd_kernel,
        grid=(count,),
        in_specs=[
            whole, whole, turned, value, value_turned, whole,
            pl.BlockSpec((1, 2, rows), lambda i: (start + i, 0, 0)), whole,
        ]
        + [pl.BlockSpec(memory_space=pl.ANY)] * len(former),
        out_specs=[
            whole,
            pl.BlockSpec((2, rows, 128), lambda i: (0, 0, start + i)),
            pl.BlockSpec((2, rows, 128), lambda i: (0, 0, turn(i))),
        ],
        out_shape=[jax.ShapeDtypeStruct((rows, width), BF), both, both],
        input_output_aliases={8 + i: i for i in range(len(former))},
        compiler_params=pltpu.CompilerParams(vmem_limit_bytes=VMEM_LIMIT),
        cost_estimate=COST,
        name="cross_bwd",
    )(queries, kv_own, kv_oth, kv_own, kv_oth, mixed, lse, grad, *former)


def norm_parts(resid):
    center = resid - jnp.mean(resid, axis=-1, keepdims=True)
    rstd = lax.rsqrt(jnp.mean(center * center, axis=-1, keepdims=True) + EPS)
    return center * rstd, rstd


def norm_back(normed, rstd, grad, gain):
    scaled = grad * gain
    return rstd * (
        scaled
        - jnp.mean(scaled, axis=-1, keepdims=True)
        - normed * jnp.mean(scaled * normed, axis=-1, keepdims=True)
    )


def cross_first_kernel(
    q_ref, ka_ref, kb_ref, va_ref, vb_ref, o_ref, lse_ref, g_ref,
    q_mat, second_ref, resid_ref, vec_ref, o_mat, dq_in, former_a, former_b,
    dq_ref, da_ref, db_ref, first_ref, low_ref, keep_ref, send_ref, sums_ref, dq_part,
    *, start, count,
):
    step = pl.program_id(0)

    @pl.when(step == 0)
    def _():
        dq_ref[...] = dq_in[...]

    cross_bwd_kernel(
        q_ref, ka_ref, kb_ref, va_ref, vb_ref, o_ref, lse_ref, g_ref, dq_part, da_ref, db_ref
    )
    at = pl.multiple_of((start + step) * 128, 128)
    dq_ref[:, pl.ds(at, 128)] = dq_part[...]

    @pl.when(step == count - 1)
    def _():
        grad = second_ref[...] + mm(dq_ref[...], q_mat[...], NT)
        normed, rstd = norm_parts(resid_ref[...])
        sums_ref[0:1, :] = jnp.sum(grad, 0, keepdims=True)
        sums_ref[1:2, :] = jnp.sum(grad * normed, 0, keepdims=True)
        first_in = norm_back(normed, rstd, grad, vec_ref[0:1, :])
        first_ref[...] = first_in
        low = first_in.astype(BF)
        low_ref[...] = low
        sums_ref[2:3, :] = jnp.sum(low.astype(F32), 0, keepdims=True)
        sums_ref[3:4, :] = jnp.sum(dq_ref[...].astype(F32), 0, keepdims=True)
        sums_ref[4:8, :] = jnp.zeros((4, sums_ref.shape[1]), F32)
        mixed_grad = mm(low, o_mat[...]).astype(BF)
        cols = keep_ref.shape[1]
        keep_ref[...] = mixed_grad[:, :cols]
        send_ref[...] = mixed_grad[:, cols:]


def cross_first_backward(
    queries, kv_own, kv_oth, mixed, lse, grad, start, former, q_mat, second_in, resid, vec, o_mat
):
    rows, width = queries.shape
    pairs = width // 128
    count = pairs - start

    def turn(i):
        return (start + i + pairs // 2) % pairs

    whole = pl.BlockSpec((rows, 128), lambda i: (0, start + i))
    turned = pl.BlockSpec((rows, 128), lambda i: (0, turn(i)))
    value = pl.BlockSpec((rows, 128), lambda i: (0, pairs + start + i))
    value_turned = pl.BlockSpec((rows, 128), lambda i: (0, pairs + turn(i)))

    def fixed(shape):
        return pl.BlockSpec(shape, lambda i: (0, 0))

    both = jax.ShapeDtypeStruct((2, rows, width), BF)
    return pl.pallas_call(
        functools.partial(cross_first_kernel, start=start, count=count),
        grid=(count,),
        in_specs=[
            whole, whole, turned, value, value_turned, whole,
            pl.BlockSpec((1, 2, rows), lambda i: (start + i, 0, 0)), whole,
            fixed((width, width)), fixed((rows, width)), fixed((rows, width)),
            fixed((1, width)), fixed((width, width)), fixed((rows, width)),
            pl.BlockSpec(memory_space=pl.ANY), pl.BlockSpec(memory_space=pl.ANY),
        ],
        out_specs=[
            fixed((rows, width)),
            pl.BlockSpec((2, rows, 128), lambda i: (0, 0, start + i)),
            pl.BlockSpec((2, rows, 128), lambda i: (0, 0, turn(i))),
            fixed((rows, width)),
            fixed((rows, width)),
            fixed((rows, width // 2)),
            fixed((rows, width // 2)),
            fixed((8, width)),
        ],
        out_shape=[
            jax.ShapeDtypeStruct((rows, width), BF),
            both,
            both,
            jax.ShapeDtypeStruct((rows, width), F32),
            jax.ShapeDtypeStruct((rows, width), BF),
            jax.ShapeDtypeStruct((rows, width // 2), BF),
            jax.ShapeDtypeStruct((rows, width // 2), BF),
            jax.ShapeDtypeStruct((8, width), F32),
        ],
        scratch_shapes=[pltpu.VMEM((rows, 128), BF)],
        input_output_aliases={14: 1, 15: 2},
        compiler_params=pltpu.CompilerParams(vmem_limit_bytes=VMEM_LIMIT),
        cost_estimate=COST,
        name="cross_first",
    )(
        queries, kv_own, kv_oth, kv_own, kv_oth, mixed, lse, grad,
        q_mat, second_in, resid, vec, o_mat, *former,
    )


def gate(value, *others):
    return lax.optimization_barrier((value,) + others)[0]


def outer_count():
    return lax.axis_size("dp") // 2


def swap_both(value):
    count = lax.axis_size("dp")
    pairs = tuple(
        (d * 4 + t, (d ^ 1) * 4 + (t ^ 2)) for d in range(count) for t in range(4)
    )
    return lax.ppermute(value, ("dp", "tensor"), pairs)


def outer_exchange(value):
    groups = [[inner + 2 * o for o in range(outer_count())] for inner in range(2)]
    return lax.all_to_all(value, "dp", 0, 0, axis_index_groups=groups, tiled=True)


def plane_exchange(value):
    groups = [
        [(o * 2 + inner) * 4 + chip * 2 + core for chip in range(2) for inner in range(2)]
        for o in range(outer_count())
        for core in range(2)
    ]
    return lax.all_to_all(value, ("dp", "tensor"), 0, 0, axis_index_groups=groups, tiled=True)


def add_low(left, right):
    return (left.astype(F32) + right.astype(F32)).astype(BF)


def total_dp(value):
    for bit in dp_bits():
        value = value + swap_dp(value, bit)
    return value


ANY = pl.BlockSpec(memory_space=pl.ANY)
VM = pl.BlockSpec(memory_space=pltpu.VMEM)
SM = pl.BlockSpec(memory_space=pltpu.SMEM)


def call(kernel, out_shape, args, in_specs, out_specs, scratch=(), flops=0, moved=0, name=None):
    return pl.pallas_call(
        kernel,
        out_shape=out_shape,
        in_specs=in_specs,
        out_specs=out_specs,
        scratch_shapes=list(scratch),
        compiler_params=pltpu.CompilerParams(vmem_limit_bytes=58 << 20),
        cost_estimate=COST,
        name=name,
    )(*args)


def struct(shape, dtype):
    return jax.ShapeDtypeStruct(shape, dtype)


def tail_start(depth):
    return (depth + 15) // 16 * 16


def high_low(row):
    high = row.astype(BF).astype(F32)
    return high, row - high


def stack_rows(rows, count):
    cols = rows[0].shape[1]
    at = lax.broadcasted_iota(jnp.int32, (count, cols), 0)
    total = jnp.zeros((count, cols), F32)
    for i, row in enumerate(rows):
        total = jnp.where(at == i, row, total)
    return total.astype(BF)


def pack_self_kernel(q_ref, k_ref, v_ref, out_ref):
    cols = q_ref.shape[1]
    for i, ref in enumerate((q_ref, k_ref, v_ref)):
        low = ref[...].astype(BF)
        for copy in range(out_ref.shape[0]):
            out_ref[copy, :, i * cols : (i + 1) * cols] = low


def turned(ref):
    depth = ref.shape[1]
    eye = (
        lax.broadcasted_iota(jnp.int32, (depth, depth), 0)
        == lax.broadcasted_iota(jnp.int32, (depth, depth), 1)
    )
    eye = jnp.where(eye, 1.0, 0.0).astype(BF)
    return mm(eye, ref[...].astype(BF), NT).astype(BF)


def pack_rest_kernel(ck_ref, cv_ref, cq_ref, so_ref, co_ref, ex_ref, sh_ref, attn_ref, ex_out, sh_out):
    cols = ck_ref.shape[1]
    parts = [ref[...].astype(BF) for ref in (ck_ref, cv_ref, cq_ref)]
    parts += [turned(so_ref), turned(co_ref)]
    expand = ex_ref[...].astype(BF)
    shrink = sh_ref[...].astype(BF)
    for copy in range(attn_ref.shape[0]):
        for i, low in enumerate(parts):
            attn_ref[copy, :, i * cols : (i + 1) * cols] = low
        ex_out[copy] = expand
    sh_out[...] = shrink


def self_forward_kernel(
    info, own_ref, oth_ref, bias_ref, w_ref, wx_ref, wy_ref, wxy_ref,
    qkv_ref, mat_ref, oa_ref, ob_ref, lse_ref, w_own, w_x, o_ref, sems,
):
    pair = pl.program_id(0)
    width = own_ref.shape[1]
    half = own_ref.shape[0]
    wide = qkv_ref.shape[2] // 3

    @pl.when(pair == 0)
    def _():
        place = info[0]
        cols = w_own.shape[3]
        copies = [
            pltpu.make_async_copy(w_ref, w_own.at[:, place], sems.at[0]),
            pltpu.make_async_copy(wy_ref, w_own.at[:, 1 - place], sems.at[1]),
            pltpu.make_async_copy(wx_ref, w_x.at[:, place], sems.at[2]),
            pltpu.make_async_copy(wxy_ref, w_x.at[:, 1 - place], sems.at[3]),
        ]
        for copy in copies:
            copy.start()
        for copy in copies:
            copy.wait()
        piece = cols // 3
        scale = 1.0 / math.sqrt(HD)
        for x, ref in enumerate((w_own, w_x)):
            mat = ref[...].reshape(width, cols)
            for i in range(3):
                at = (2 * i + x) * piece
                mat_ref[:, at : at + piece] = mat[:, i * piece : (i + 1) * piece]
        for rel, src in enumerate((own_ref, oth_ref)):
            for i in range(3):
                at = slice(wide * i, wide * (i + 1))
                part = mm(src[...], mat_ref[:, at]) + bias_ref[i : i + 1, :]
                if i == 0:
                    part = part * scale
                qkv_ref[rel, :, at] = part.astype(BF)

    first = info[3]
    second = 1 - first
    prefix = info[4]
    key_pos = lax.broadcasted_iota(jnp.int32, (half, half), 0)
    query_pos = lax.broadcasted_iota(jnp.int32, (half, half), 1)
    causal = key_pos <= query_pos
    seen = causal | (key_pos < prefix)

    def load(which, at):
        start = pl.multiple_of(which * wide + pair * 128, 128)
        return qkv_ref[at, :, pl.ds(start, 128)]

    q_both = (load(0, first), load(0, second))
    k_both = (load(1, first), load(1, second))
    v_both = (load(2, first), load(2, second))
    for h in range(2):
        cols = slice(HD * h, HD * h + HD)
        k0, k1 = (k[:, cols] for k in k_both)
        v0, v1 = (v[:, cols] for v in v_both)
        q0, q1 = (q[:, cols] for q in q_both)
        score = jnp.where(seen, mm(k0, q0, NT), NEGATIVE)
        top = jnp.max(score, 0, keepdims=True)
        expo = jnp.exp(score - top)
        total = jnp.sum(expo, 0, keepdims=True)
        mixed = mm(v0, expo.astype(BF), TN) / total
        o_ref[first, :, cols] = mixed.T.astype(BF)
        lse_ref[0, h, pl.ds(first, 1), :] = top + jnp.log(total)

        score_a = mm(k0, q1, NT)
        score_b = jnp.where(causal, mm(k1, q1, NT), NEGATIVE)
        top = jnp.maximum(
            jnp.max(score_a, 0, keepdims=True), jnp.max(score_b, 0, keepdims=True)
        )
        expo_a = jnp.exp(score_a - top)
        expo_b = jnp.exp(score_b - top)
        total = jnp.sum(expo_a, 0, keepdims=True) + jnp.sum(expo_b, 0, keepdims=True)
        mixed = (mm(v0, expo_a.astype(BF), TN) + mm(v1, expo_b.astype(BF), TN)) / total
        o_ref[second, :, cols] = mixed.T.astype(BF)
        lse_ref[0, h, pl.ds(second, 1), :] = top + jnp.log(total)
    oa_ref[...] = o_ref[0]
    ob_ref[...] = o_ref[1]


def self_forward(info, own, oth, bias, pieces):
    half, width = own.shape
    outer, depth, cols = pieces[0].shape
    wide = 2 * cols // 3
    pairs = wide // 128
    fixed2 = pl.BlockSpec((half, width), lambda i, info: (0, 0))
    pair_cols = pl.BlockSpec((half, 128), lambda i, info: (0, i))
    return pl.pallas_call(
        self_forward_kernel,
        grid_spec=pltpu.PrefetchScalarGridSpec(
            num_scalar_prefetch=1,
            grid=(pairs,),
            in_specs=[
                fixed2,
                fixed2,
                pl.BlockSpec(bias.shape, lambda i, info: (0, 0)),
                ANY,
                ANY,
                ANY,
                ANY,
            ],
            out_specs=[
                pl.BlockSpec((2, half, 3 * wide), lambda i, info: (0, 0, 0)),
                pl.BlockSpec((width, 3 * wide), lambda i, info: (0, 0)),
                pair_cols,
                pair_cols,
                pl.BlockSpec((1, 2, 2, half), lambda i, info: (i, 0, 0, 0)),
            ],
            scratch_shapes=[
                pltpu.VMEM((outer, 2, depth, cols), BF),
                pltpu.VMEM((outer, 2, depth, cols), BF),
                pltpu.VMEM((2, half, 128), BF),
                pltpu.SemaphoreType.DMA((4,)),
            ],
        ),
        out_shape=[
            struct((2, half, 3 * wide), BF),
            struct((width, 3 * wide), BF),
            struct((half, wide), BF),
            struct((half, wide), BF),
            struct((pairs, 2, 2, half), F32),
        ],
        compiler_params=pltpu.CompilerParams(vmem_limit_bytes=VMEM_LIMIT),
        cost_estimate=COST,
        name="self_fwd",
    )(info, own, oth, bias, *pieces)


def assemble_kernel(info, *refs):
    pieces, (kv_ref, q_ref, so_ref, co_ref) = refs[:8], refs[8:]
    place = info[0]
    outer, depth, cols = pieces[0].shape
    piece = cols // 5
    for j in range(4):
        for y in range(2):
            at = place if y == 0 else 1 - place
            for o in range(outer):
                value = pieces[2 * j + y][o]
                own = slice(piece * j, piece * (j + 1))
                low = slice(4 * piece + piece * j, 4 * piece + piece * (j + 1))
                kv_ref[o, at, :, own] = value[:, :piece]
                kv_ref[o, at, :, low] = value[:, piece : 2 * piece]
                q_ref[o, at, :, own] = value[:, 2 * piece : 3 * piece]
                so_ref[o, at, :, own] = value[:, 3 * piece : 4 * piece]
                co_ref[o, at, :, own] = value[:, 4 * piece :]


def assemble(info, pieces):
    outer, depth, cols = pieces[0].shape
    wide = cols // 5 * 4
    outs = call(
        assemble_kernel,
        [struct((outer, 2, depth, 2 * wide), BF)] + [struct((outer, 2, depth, wide), BF)] * 3,
        [info] + list(pieces),
        [SM] + [VM] * 8,
        [VM] * 4,
        moved=pieces[0].size * 32,
        name="assemble",
    )
    return [out.reshape(-1, out.shape[-1]) for out in outs]


def copies_kernel(info, own_ref, x_ref, y_ref, xy_ref, out_ref):
    place = info[0]
    for copy in range(out_ref.shape[0]):
        out_ref[copy, 0, place] = own_ref[...]
        out_ref[copy, 0, 1 - place] = y_ref[...]
        out_ref[copy, 1, place] = x_ref[...]
        out_ref[copy, 1, 1 - place] = xy_ref[...]


def plane_copies(info, own, x, y, xy):
    depth, cols = own.shape
    outer = outer_count()
    return call(
        copies_kernel,
        struct((outer, 2, 2, depth, cols), BF),
        [info, own, x, y, xy],
        [SM] + [VM] * 4,
        VM,
        moved=own.size * 2 * 4 * (outer + 1),
        name="plane_copies",
    )


def first_forward_kernel(
    tok_ref, own_ref, oth_ref, o_mat, vec_ref, q_mat, qb_ref,
    resid_ref, first_ref, low_ref, q_ref, mixed_ref,
):
    cols = own_ref.shape[1]
    mixed_ref[:, :cols] = own_ref[...]
    mixed_ref[:, cols:] = oth_ref[...]
    resid = tok_ref[...].astype(F32) + mm(mixed_ref[...], o_mat[...], NT) + vec_ref[0:1, :]
    resid_ref[...] = resid
    normed, rstd = norm_parts(resid)
    first = normed * vec_ref[1:2, :] + vec_ref[2:3, :]
    first_ref[...] = first
    low_ref[...] = first.astype(BF)
    scale = 1.0 / math.sqrt(HD)
    q_ref[...] = ((mm(low_ref[...], q_mat[...]) + qb_ref[...]) * scale).astype(BF)


def first_forward(tokens, own, oth, o_mat, vecs, q_mat, q_bias):
    rows, width = tokens.shape
    return call(
        first_forward_kernel,
        [struct((rows, width), F32)] * 2 + [struct((rows, width), BF)] * 3,
        [tokens, own, oth, o_mat, vecs, q_mat, q_bias],
        [VM] * 7,
        [VM] * 5,
        flops=2 * rows * width * width * 2 * 2,
        moved=width * width * 4 + rows * width * 18,
        name="first_forward",
    )


def project_kv_kernel(keep_ref, got_ref, mat_ref, bias_ref, fet_ref, out_ref):
    fet_ref[...] = keep_ref[...] + got_ref[...]
    width = fet_ref.shape[1]
    out_ref[:, :width] = mm(fet_ref[...], mat_ref[:, :width]).astype(BF)
    out_ref[:, width:] = (mm(fet_ref[...], mat_ref[:, width:]) + bias_ref[...]).astype(BF)


def project_kv(keep, got, mat, bias):
    rows, width = keep.shape
    return call(
        project_kv_kernel,
        [struct((rows, width), BF), struct((rows, 2 * width), BF)],
        [keep, got, mat, bias],
        [VM] * 4,
        [VM] * 2,
        name="project_kv",
    )


def feed_kernel(
    info, mixed_ref, first_ref, cot_ref, vec_ref, wo_hbm,
    e0, e1, e2, e3, e4, e5, e6, e7, s0, s1,
    out_ref, second_ref, low_ref, grad_ref,
    keep_ref, send_ref, sums_ref, tail,
    wo, we, ws, hid, slo, out_a, out_b, norm2, h2low, e3low, acc, wsem, osem, tsem,
):
    first_copy = pltpu.make_async_copy(wo_hbm, wo, wsem.at[0])
    first_copy.start()
    place = info[0]
    copies = []
    for j, pair in enumerate(((e0, e1), (e2, e3), (e4, e5), (e6, e7))):
        for y, ref in enumerate(pair):
            at = place if y == 0 else 1 - place
            copies.append(pltpu.make_async_copy(ref, we.at[j, :, at], wsem.at[1 + 2 * j + y]))
    for j in range(4):
        ref = (s0, s1)[j // 2]
        copies.append(pltpu.make_async_copy(ref.at[:, j % 2], ws.at[j], wsem.at[9 + j]))
    for copy in copies:
        copy.start()

    width = first_ref.shape[1]
    hidden_cols = we.shape[-1]
    outer, depth = we.shape[1], we.shape[3]
    base = out_a.shape[3]

    def expand_mat(j):
        return we[j].reshape(width, hidden_cols)

    def shrink_mat(j):
        return ws[j].reshape(width, hidden_cols)

    def row(i):
        return vec_ref[i : i + 1, :]

    first_copy.wait()
    resid = first_ref[...] + mm(mixed_ref[...], wo[...], NT) + row(0)
    normed, rstd2 = norm_parts(resid)
    norm2[...] = normed
    second = normed * row(1) + row(2)
    h2low[...] = second.astype(BF)
    acc[...] = second + row(7)
    for copy in copies:
        copy.wait()

    def forward(j, carry):
        inner = mm(h2low[...], expand_mat(j)) + vec_ref[pl.ds(3 + j, 1), :]
        phi = 0.5 + 0.5 * lax.erf(inner * (1.0 / math.sqrt(2.0)))
        hidden = (inner * phi).astype(BF)
        hid[j] = hidden
        bell = jnp.exp(-0.5 * inner * inner) * (1.0 / math.sqrt(2.0 * math.pi))
        slo[j] = (phi + inner * bell).astype(BF)
        acc[...] += mm(hidden, shrink_mat(j), NT)
        return carry

    lax.fori_loop(0, 4, forward, 0)
    norm3, rstd3 = norm_parts(acc[...])
    out_ref[...] = (norm3 * row(8) + row(9)).astype(BF)
    cot = cot_ref[...].astype(F32)
    sums_ref[0:1, :] = jnp.sum(cot, 0, keepdims=True)
    sums_ref[1:2, :] = jnp.sum(cot * norm3, 0, keepdims=True)
    third = norm_back(norm3, rstd3, cot, row(8))
    low = third.astype(BF)
    e3low[...] = low
    sums_ref[2:3, :] = jnp.sum(low.astype(F32), 0, keepdims=True)
    acc[...] = third

    def out_copies(to, at, slot):
        copies = []
        for y in range(2):
            for i, part in enumerate((out_a, out_b)):
                copies.append(
                    pltpu.make_async_copy(
                        part.at[slot, :, y],
                        to.at[
                            at, y ^ place, :, :base, i * hidden_cols : (i + 1) * hidden_cols
                        ],
                        osem.at[i, slot, y],
                    )
                )
        return copies

    def backward(step, carry):
        j = (step + 2) % 4
        slot = step % 2
        slope = slo[j].astype(F32)
        inner_grad = (mm(e3low[...], shrink_mat(j)) * slope).astype(BF)
        sums_ref[pl.ds(8 + j, 1), :] = jnp.sum(
            inner_grad.astype(F32), 0, keepdims=True
        )

        @pl.when(step >= 2)
        def _():
            for copy in out_copies(send_ref, slot, slot):
                copy.wait()

        shape = (outer, 2, depth, hidden_cols)
        out_a[slot, :, :, :depth] = mm(h2low[...], inner_grad, TN).astype(BF).reshape(shape)
        out_b[slot, :, :, :depth] = mm(e3low[...], hid[j], TN).astype(BF).reshape(shape)

        @pl.when(step < 2)
        def _():
            for copy in out_copies(send_ref, slot, slot):
                copy.start()

        @pl.when(step >= 2)
        def _():
            for copy in out_copies(keep_ref, slot, slot):
                copy.start()

        acc[...] += mm(inner_grad, expand_mat(j), NT)
        return carry

    lax.fori_loop(0, 4, backward, 0)
    grad = acc[...]
    normed = norm2[...]
    sums_ref[3:4, :] = jnp.sum(grad, 0, keepdims=True)
    sums_ref[4:5, :] = jnp.sum(grad * normed, 0, keepdims=True)
    second_in = norm_back(normed, rstd2, grad, row(1))
    second_ref[...] = second_in
    low = second_in.astype(BF)
    low_ref[...] = low
    sums_ref[5:6, :] = jnp.sum(low.astype(F32), 0, keepdims=True)
    tails = []
    pairs = [high_low(sums_ref[i : i + 1, :]) for i in range(6)]
    for j in range(4):
        rows_e = list(high_low(sums_ref[8 + j : 9 + j, :])) + [r for p in pairs[:3] for r in p]
        rows_s = [r for p in pairs[3:] for r in p]
        for o in range(outer):
            tail[j, o, :, :hidden_cols] = stack_rows(rows_e, 8)
            tail[j, o, :, hidden_cols:] = stack_rows(rows_s, 8)
        for y in range(2):
            to = (keep_ref, send_ref)[j // 2]
            tails.append(
                pltpu.make_async_copy(tail.at[j], to.at[j % 2, y, :, base:, :], tsem.at[2 * j + y])
            )
    for copy in tails:
        copy.start()
    grad_ref[...] = mm(low, wo[...]).astype(BF)
    for slot in range(2):
        for copy in out_copies(keep_ref, slot, slot):
            copy.wait()
    for copy in tails:
        copy.wait()


def feed(info, mixed, first, cot, vecs, wo, expand, shrink):
    rows, width = mixed.shape
    outer, depth, hidden = expand[0].shape
    base = tail_start(depth)
    grads = struct((2, 2, outer, base + 8, 2 * hidden), BF)
    return call(
        feed_kernel,
        [
            struct((rows, width), BF),
            struct((rows, width), F32),
            struct((rows, width), BF),
            struct((rows, width), BF),
            grads,
            grads,
        ],
        [info, mixed, first, cot, vecs, wo] + list(expand) + list(shrink),
        [SM, VM, VM, VM, VM] + [ANY] * 11,
        [VM] * 4 + [ANY] * 2,
        [
            pltpu.VMEM((16, width), F32),
            pltpu.VMEM((4, outer, 8, 2 * hidden), BF),
            pltpu.VMEM((width, width), BF),
            pltpu.VMEM((4, outer, 2, depth, hidden), BF),
            pltpu.VMEM((4, outer, 2, depth, hidden), BF),
            pltpu.VMEM((4, rows, hidden), BF),
            pltpu.VMEM((4, rows, hidden), BF),
            pltpu.VMEM((2, outer, 2, base, hidden), BF),
            pltpu.VMEM((2, outer, 2, base, hidden), BF),
            pltpu.VMEM((rows, width), F32),
            pltpu.VMEM((rows, width), BF),
            pltpu.VMEM((rows, width), BF),
            pltpu.VMEM((rows, width), F32),
            pltpu.SemaphoreType.DMA((13,)),
            pltpu.SemaphoreType.DMA((2, 2, 2)),
            pltpu.SemaphoreType.DMA((8,)),
        ],
        flops=2 * rows * width * (6 * 4 * hidden + 2 * width) * 2,
        moved=width * hidden * 4 * 4 * 2,
        name="feed",
    )


def first_back_kernel(
    dq_ref, q_mat, second_ref, resid_ref, vec_ref, o_mat, first_ref, low_ref, keep_ref, send_ref, sums_ref
):
    grad = second_ref[...] + mm(dq_ref[...], q_mat[...], NT)
    normed, rstd = norm_parts(resid_ref[...])
    sums_ref[0:1, :] = jnp.sum(grad, 0, keepdims=True)
    sums_ref[1:2, :] = jnp.sum(grad * normed, 0, keepdims=True)
    first_in = norm_back(normed, rstd, grad, vec_ref[0:1, :])
    first_ref[...] = first_in
    low = first_in.astype(BF)
    low_ref[...] = low
    sums_ref[2:3, :] = jnp.sum(low.astype(F32), 0, keepdims=True)
    sums_ref[3:4, :] = jnp.sum(dq_ref[...].astype(F32), 0, keepdims=True)
    sums_ref[4:8, :] = jnp.zeros((4, sums_ref.shape[1]), F32)
    mixed_grad = mm(low, o_mat[...]).astype(BF)
    cols = keep_ref.shape[1]
    keep_ref[...] = mixed_grad[:, :cols]
    send_ref[...] = mixed_grad[:, cols:]


def first_back(dq, q_mat, second_in, resid, vec, o_mat):
    rows, width = dq.shape
    cols = width // 2
    return call(
        first_back_kernel,
        [
            struct((rows, width), F32),
            struct((rows, width), BF),
            struct((rows, cols), BF),
            struct((rows, cols), BF),
            struct((8, width), F32),
        ],
        [dq, q_mat, second_in, resid, vec, o_mat],
        [VM] * 6,
        [VM] * 5,
        flops=2 * rows * width * width * 2 * 2,
        moved=width * width * 4 + rows * width * 18,
        name="first_back",
    )


def put_rows(ref, x, full, at, place):
    outer = ref.shape[2]
    depth = full.shape[0] // outer // 2
    for o in range(outer):
        for y in range(2):
            start = (2 * o + y) * depth
            ref[x, y ^ place, o, :depth, at] = full[start : start + depth]


def put_blocks(keep_ref, send_ref, full, i, place):
    piece = full.shape[1] // 4
    at = slice(i * piece, (i + 1) * piece)
    for j in range(4):
        put_rows((keep_ref, send_ref)[j // 2], j % 2, full[:, j * piece : (j + 1) * piece], at, place)


def query_grads_kernel(
    info, h1_ref, dq_ref, e1_ref, o1_ref, e2_ref, o2_ref, sums_ref, keep_ref, send_ref
):
    width = dq_ref.shape[1]
    piece = width // 4
    outer, rows = keep_ref.shape[2], keep_ref.shape[3]
    parts = [high_low(sums_ref[i : i + 1, :]) for i in range(4)]
    for j in range(4):
        own = slice(j * piece, (j + 1) * piece)
        ref = (keep_ref, send_ref)[j // 2]
        for i in range(3):
            lines = [parts[i][0][:, p * piece : (p + 1) * piece] for p in range(4)]
            lines += [parts[i][1][:, p * piece : (p + 1) * piece] for p in range(4)]
            if i == 0:
                lines += [parts[3][0][:, own], parts[3][1][:, own]]
            block = stack_rows(lines, 16)
            for o in range(outer):
                for y in range(2):
                    ref[j % 2, y, o, rows - 16 :, i * piece : (i + 1) * piece] = block
    for i, (left, right) in enumerate(((h1_ref, dq_ref), (e1_ref, o1_ref), (e2_ref, o2_ref))):
        full = mm(left[...], right[...], TN).astype(BF)
        put_blocks(keep_ref, send_ref, full, i, info[0])


def key_grads_kernel(info, fet_ref, own_ref, got_ref, mat_ref, keep_ref, send_ref, grad_ref):
    width = fet_ref.shape[1]
    piece = width // 4
    outer, rows = keep_ref.shape[2], keep_ref.shape[3]
    total = None
    for i in range(2):
        low = add_low(own_ref[i], got_ref[i])
        full = mm(fet_ref[...], low, TN).astype(BF)
        put_blocks(keep_ref, send_ref, full, i, info[0])
        term = mm(low, mat_ref[:, i * width : (i + 1) * width], NT)
        total = term if total is None else total + term
        if i == 1:
            sums = high_low(jnp.sum(low.astype(F32), 0, keepdims=True))
            for j in range(4):
                own = slice(j * piece, (j + 1) * piece)
                block = stack_rows([sums[0][:, own], sums[1][:, own]], 8)
                ref = (keep_ref, send_ref)[j // 2]
                for o in range(outer):
                    for y in range(2):
                        ref[j % 2, y, o, rows - 8 :, piece:] = block
                        ref[j % 2, y, o, rows - 8 :, :piece] = jnp.zeros_like(block)
    grad_ref[...] = total.astype(BF)


def query_grads(info, args, depth):
    width = args[0].shape[1]
    out = struct((2, 2, width // depth // 2, tail_start(depth) + 16, 3 * width // 4), BF)
    return call(
        query_grads_kernel,
        [out, out],
        [info] + list(args),
        [SM] + [VM] * 7,
        [VM] * 2,
        flops=2 * 512 * width * width * 3,
        moved=width * width * 10,
        name="query_grads",
    )


def key_grads(info, fetched, own, got, mat, depth):
    rows, width = fetched.shape
    out = struct((2, 2, width // depth // 2, tail_start(depth) + 8, 2 * width // 4), BF)
    return call(
        key_grads_kernel,
        [out, out, struct((rows, width), BF)],
        [info, fetched, own, got, mat],
        [SM] + [VM] * 4,
        [VM] * 3,
        flops=2 * rows * width * width * 4,
        moved=width * width * 10,
        name="key_grads",
    )


def self_grads_kernel(info, own_ref, oth_ref, d_ref, a_ref, x_ref, y_ref, xy_ref):
    place = info[0]
    cols = d_ref.shape[3]
    piece = cols // 2
    outer, base = a_ref.shape[0], a_ref.shape[1] - 8
    depth = own_ref.shape[1] // outer // 2
    for i in range(3):
        full = mm(own_ref[...], d_ref[i, 0], TN) + mm(oth_ref[...], d_ref[i, 1], TN)
        full = full.astype(BF)
        at = slice(i * piece, (i + 1) * piece)
        both = d_ref[i, 0].astype(F32) + d_ref[i, 1].astype(F32)
        sums = jnp.sum(both, 0, keepdims=True)
        high = sums.astype(BF).astype(F32)
        row = lax.broadcasted_iota(jnp.int32, (8, cols), 0)
        tail = jnp.where(row == 0, high, jnp.where(row == 1, sums - high, 0.0)).astype(BF)
        for x, (near, away) in enumerate(((a_ref, y_ref), (x_ref, xy_ref))):
            part = slice(x * piece, (x + 1) * piece)
            for o in range(outer):
                start = 2 * o * depth
                first = full[start : start + depth, part]
                second = full[start + depth : start + 2 * depth, part]
                near[o, :depth, at] = jnp.where(place == 0, first, second)
                away[o, :depth, at] = jnp.where(place == 0, second, first)
                near[o, base:, at] = tail[:, part]
                away[o, base:, at] = tail[:, part]


def self_grads(info, own, oth, grads, depth):
    half, width = own.shape
    cols = grads.shape[3]
    out = struct((width // depth // 2, tail_start(depth) + 8, 3 * cols // 2), BF)
    return call(
        self_grads_kernel,
        [out] * 4,
        [info, own, oth, grads],
        [SM] + [VM] * 3,
        [VM] * 4,
        name="self_grads",
    )


def self_back_kernel(d_ref, mat_ref, first_ref, keep_ref, send_ref):
    cols = d_ref.shape[3]
    for rel in (1, 0):
        total = mm(d_ref[0, rel], mat_ref[:, :cols], NT)
        for i in (1, 2):
            total = total + mm(d_ref[i, rel], mat_ref[:, i * cols : (i + 1) * cols], NT)
        if rel == 1:
            send_ref[...] = total.astype(BF)
        else:
            keep_ref[...] = total + first_ref[...]


def self_back(grads, mat, first_in):
    half, width = first_in.shape
    cols = grads.shape[3]
    return call(
        self_back_kernel,
        [struct((half, width), F32), struct((half, width), BF)],
        [grads, mat, first_in],
        [VM] * 3,
        [VM] * 2,
        flops=2 * 2 * half * width * 3 * cols * 2,
        moved=half * width * 10 + half * cols * 12 + width * cols * 6,
        name="self_back",
    )


def fetch_kernel(table, bank_ref, mine_ref, send_ref, sem):
    count = table.shape[0] // 2

    def each(act):
        for group, out_ref in enumerate((mine_ref, send_ref)):

            def body(i, carry, group=group, out_ref=out_ref):
                at = table[group * count + i]
                copy = pltpu.make_async_copy(
                    bank_ref.at[jnp.maximum(at, 0)], out_ref.at[i], sem.at[group * count + i]
                )
                act(copy, at >= 0, out_ref, i)
                return carry

            lax.fori_loop(0, count, body, 0)

    def start(copy, held, out_ref, i):
        @pl.when(held)
        def _():
            copy.start()

        @pl.when(jnp.logical_not(held))
        def _():
            out_ref[i] = jnp.zeros(out_ref.shape[1:], out_ref.dtype)

    def finish(copy, held, out_ref, i):
        @pl.when(held)
        def _():
            copy.wait()

    each(start)
    each(finish)


def fetch(table, bank_blocks):
    count = table.shape[0]
    blk, width = bank_blocks.shape[1:]
    out = struct((count // 2, blk, width), BF)
    mine, send = call(
        fetch_kernel,
        [out, out],
        [table, bank_blocks],
        [SM, ANY],
        [VM, VM],
        [pltpu.SemaphoreType.DMA((count,))],
        moved=count * blk * width * 4,
        name="fetch",
    )
    return [part.reshape(2, count // 4, blk, width) for part in (mine, send)]


def scatter_kernel(table, a_ref, b_ref, c_ref, d_ref, out_ref, slots, sems):
    step = pl.program_id(0)
    per = out_ref.shape[0]

    @pl.when(step == 0)
    def _():
        copies = [
            pltpu.make_async_copy(ref, slots.at[i], sems.at[i])
            for i, ref in enumerate((a_ref, b_ref, c_ref, d_ref))
        ]
        for copy in copies:
            copy.start()
        for copy in copies:
            copy.wait()

    for i in range(per):
        at = table[step * per + i]
        group = jnp.maximum(at, 0) // slots.shape[1]
        place = jnp.maximum(at, 0) % slots.shape[1]
        value = slots[group, place].astype(F32)
        out_ref[i] = jnp.where(at >= 0, value, 0.0)


def scatter(table, parts):
    count = table.shape[0]
    slots, blk, width = parts[0].shape
    per = 4
    return pl.pallas_call(
        scatter_kernel,
        grid_spec=pltpu.PrefetchScalarGridSpec(
            num_scalar_prefetch=1,
            grid=(count // per,),
            in_specs=[ANY] * 4,
            out_specs=pl.BlockSpec((per, blk, width), lambda i, t: (i, 0, 0)),
            scratch_shapes=[
                pltpu.VMEM((4, slots, blk, width), BF),
                pltpu.SemaphoreType.DMA((4,)),
            ],
        ),
        out_shape=struct((count, blk, width), F32),
        compiler_params=pltpu.CompilerParams(vmem_limit_bytes=VMEM_LIMIT),
        cost_estimate=COST,
        name="scatter",
    )(table, *parts)


def sum_all(ref):
    total = ref[0].astype(F32)
    for i in range(1, ref.shape[0]):
        total = total + ref[i].astype(F32)
    return total


def sum_query_kernel(in_ref, q_ref, so_ref, co_ref, qb_ref, v0_ref, v1_ref, v2_ref):
    total = sum_all(in_ref)
    piece = total.shape[1] // 3
    depth = q_ref.shape[0]
    q_ref[...] = total[:depth, :piece]
    so_ref[...] = total[:depth, piece : 2 * piece].T
    co_ref[...] = total[:depth, 2 * piece :].T
    tail = total[total.shape[0] - 16 :]
    qb_ref[...] = (tail[8:9, :piece] + tail[9:10, :piece])[0]
    for i, ref in enumerate((v0_ref, v1_ref, v2_ref)):
        cols = slice(i * piece, (i + 1) * piece)
        parts = [tail[p : p + 1, cols] + tail[p + 4 : p + 5, cols] for p in range(4)]
        ref[...] = jnp.concatenate(parts, axis=1)[0]


def sum_query(value, depth):
    count, rows, cols = value.shape
    piece = cols // 3
    wide, tall = struct((depth, piece), F32), struct((piece, depth), F32)
    vec = struct((4 * piece,), F32)
    return call(
        sum_query_kernel,
        [wide, tall, tall, struct((piece,), F32), vec, vec, vec],
        [value],
        [VM],
        [VM] * 7,
        name="sum_query",
    )


def sum_cols_kernel(in_ref, *refs):
    count = len(refs) // 2
    total = sum_all(in_ref)
    depth, piece = refs[0].shape
    tail = total[total.shape[0] - 8 :]
    for i in range(count):
        cols = slice(i * piece, (i + 1) * piece)
        refs[i][...] = total[:depth, cols]
        refs[count + i][...] = (tail[0:1, cols] + tail[1:2, cols])[0]


def sum_cols(value, depth, count):
    piece = value.shape[2] // count
    return call(
        sum_cols_kernel,
        [struct((depth, piece), F32)] * count + [struct((piece,), F32)] * count,
        [value],
        [VM],
        [VM] * (2 * count),
        name="sum_cols",
    )


def sum_feed_kernel(in_ref, e_ref, s_ref, eb_ref, *vecs):
    total = sum_all(in_ref)
    depth, cols = e_ref.shape
    e_ref[...] = total[:depth, :cols]
    s_ref[...] = total[:depth, cols:]
    tail = total[total.shape[0] - 8 :]
    eb_ref[...] = (tail[0:1, :cols] + tail[1:2, :cols])[0]
    for i in range(3):
        at = 2 + 2 * i
        vecs[i][...] = (tail[at : at + 1, :cols] + tail[at + 1 : at + 2, :cols])[0]
        at = 2 * i
        vecs[3 + i][...] = (tail[at : at + 1, cols:] + tail[at + 1 : at + 2, cols:])[0]


def sum_feed(value, depth):
    cols = value.shape[2] // 2
    return call(
        sum_feed_kernel,
        [struct((depth, cols), F32)] * 2 + [struct((cols,), F32)] * 7,
        [value],
        [VM],
        [VM] * 9,
        name="sum_feed",
    )


def local(
    tokens,
    bank,
    prefix,
    blocks,
    out_grad,
    selfq_weight,
    selfq_bias,
    selfk_weight,
    selfv_weight,
    selfv_bias,
    selfo_weight,
    selfo_bias,
    first_gain,
    first_shift,
    crossq_weight,
    crossq_bias,
    crossk_weight,
    crossv_weight,
    crossv_bias,
    crosso_weight,
    crosso_bias,
    second_gain,
    second_shift,
    expand_weight,
    expand_bias,
    shrink_weight,
    shrink_bias,
    third_gain,
    third_shift,
):
    rank = lax.axis_index("tensor")
    core = rank % 2
    chip = rank // 2
    inner = lax.axis_index("dp") % 2
    outer = outer_count()
    half, width = tokens.shape
    seq_count = prefix.shape[0]
    local_blocks = bank.shape[1] // BLK
    head_cols = selfq_bias.shape[0]
    hidden_cols = expand_bias.shape[0]
    depth = selfq_weight.shape[0]
    slots = NBLK // 2
    two = 2 * head_cols
    attn_cols = 5 * head_cols
    info = jnp.stack([inner, rank, chip]).astype(jnp.int32)

    seq_order = jnp.stack([chip, 1 - chip])
    near = blocks[seq_order].reshape(2, 2, slots)
    near = jnp.stack([near[:, core], near[:, 1 - core]])
    near = near - rank * local_blocks
    held = (near >= 0) & (near < local_blocks)
    fetch_table = jnp.where(held, near + seq_order[None, :, None] * local_blocks, -1)
    fetch_table = fetch_table.reshape(-1).astype(jnp.int32)
    part_mine, part_send = fetch(fetch_table, bank.reshape(seq_count * local_blocks, BLK, width))

    self_leaf = call(
        pack_self_kernel,
        struct((outer, depth, 3 * head_cols), BF),
        [gate(selfq_weight, part_send), selfk_weight, selfv_weight],
        [VM] * 3,
        VM,
        name="pack_self",
    )
    bias_own = jnp.concatenate(
        [selfq_bias, selfv_bias, crossq_bias, crossv_bias, expand_bias]
    ).reshape(1, -1)
    bias_two = jnp.concatenate([bias_own, swap_x(bias_own)], axis=0)
    bias_four = jnp.concatenate([bias_two, swap_core(bias_two)], axis=0)
    cq_bias = bias_four[:, two : 3 * head_cols].reshape(-1)
    cv_bias = bias_four[:, 3 * head_cols : 4 * head_cols].reshape(-1)
    ex_bias = bias_four[:, 4 * head_cols :]
    self_bias = jnp.stack(
        [
            bias_two[:, :head_cols].reshape(-1),
            jnp.zeros((two,), F32),
            bias_two[:, head_cols:two].reshape(-1),
        ]
    )
    attn_leaf, expand_leaf, shrink_leaf = call(
        pack_rest_kernel,
        [
            struct((outer, depth, attn_cols), BF),
            struct((outer, depth, hidden_cols), BF),
            struct((depth, hidden_cols), BF),
        ],
        [
            gate(crossk_weight, self_leaf), crossv_weight, crossq_weight, selfo_weight,
            crosso_weight, expand_weight, shrink_weight.T,
        ],
        [VM] * 7,
        [VM] * 3,
        name="pack_rest",
    )
    tokens_oth = swap_core(tokens)
    vecs = jnp.concatenate(
        [
            jnp.stack([crosso_bias, second_gain, second_shift]),
            ex_bias,
            jnp.stack([shrink_bias, third_gain, third_shift]),
        ]
    )
    first_vecs = jnp.stack([selfo_bias, first_gain, first_shift])
    cq_bias, cv_bias = cq_bias.reshape(1, -1), cv_bias.reshape(1, -1)
    my_prefix = lax.dynamic_index_in_dim(prefix, chip, 0, keepdims=False)
    attn_info = jnp.stack([core, my_prefix]).astype(jnp.int32)

    part_got = swap_core(part_send)
    self_leaf, attn_leaf = lax.optimization_barrier((self_leaf, attn_leaf))
    self_z = outer_exchange(self_leaf)
    shrink_leaf = gate(shrink_leaf, bias_two)
    shrink_x, shrink_y = swap_x(shrink_leaf), swap_dp(shrink_leaf, 1)
    shrink_xy = swap_both(shrink_leaf)
    shrink_pack = plane_copies(info, shrink_leaf, shrink_x, shrink_y, shrink_xy)

    (
        self_z, self_bias, vecs, first_vecs, cq_bias, cv_bias, attn_leaf, attn_info,
        part_got, tokens_oth, shrink_pack,
    ) = lax.optimization_barrier(
        (
            self_z, self_bias, vecs, first_vecs, cq_bias, cv_bias, attn_leaf, attn_info,
            part_got, tokens_oth, shrink_pack,
        )
    )
    self_near, self_away, self_both = swap_x(self_z), swap_dp(self_z, 1), swap_both(self_z)
    attn_z = outer_exchange(attn_leaf)
    part_got, self_near = lax.optimization_barrier((part_got, self_near))
    part_back = swap_x(part_mine[1] + part_got[1])
    attn_z, tokens_in, self_near, self_away, self_both = lax.optimization_barrier(
        (attn_z, tokens, self_near, self_away, self_both)
    )
    attn_x, attn_y, attn_xy = swap_x(attn_z), swap_dp(attn_z, 1), swap_both(attn_z)
    expand_z = outer_exchange(gate(expand_leaf, attn_z))

    qkv, self_mat, self_own, self_send, self_lse = self_forward(
        jnp.concatenate([info, attn_info]),
        tokens_in,
        tokens_oth,
        self_bias,
        (self_z, self_near, self_away, self_both),
    )
    self_got = swap_core(self_send)
    attn_x, attn_y, shrink_pack = lax.optimization_barrier((attn_x, attn_y, shrink_pack, self_own))[:3]
    shrink_pack, expand_z = lax.optimization_barrier((shrink_pack, expand_z))
    shrink_z = outer_exchange(shrink_pack)
    expand_x, expand_y, expand_xy = swap_x(expand_z), swap_dp(expand_z, 1), swap_both(expand_z)

    attn_own = (attn_z, attn_y, attn_x, attn_xy)
    attn_oth = tuple(swap_core(piece) for piece in attn_own)
    cross_kv, cross_q, self_o, cross_o = assemble(info, attn_own + attn_oth)
    fetched, kv_own = project_kv(
        (part_mine[0] + part_got[0]).reshape(slots * BLK, width),
        part_back.reshape(slots * BLK, width),
        cross_kv,
        cv_bias,
    )
    self_got, kv_own = lax.optimization_barrier((self_got, kv_own))
    kv_oth = swap_core(kv_own)
    first_sum, first_out, first_low, queries, mixed_one = first_forward(
        tokens,
        self_own,
        self_got,
        self_o,
        first_vecs,
        cross_q,
        cq_bias,
    )

    queries, kv_oth = lax.optimization_barrier((queries, kv_oth))
    queries, expand_x, expand_y, shrink_z = lax.optimization_barrier(
        (queries, expand_x, expand_y, shrink_z)
    )
    mixed_two, cross_lse = cross_forward(queries, kv_own, kv_oth)

    expand_own = (expand_z, expand_y, expand_x, expand_xy)
    expand_oth = tuple(swap_core(piece) for piece in expand_own)
    (
        out_act, second_in, cross_low, cross_grad,
        feed_keep, feed_send,
    ) = feed(
        info, mixed_two, first_out, out_grad, vecs, cross_o,
        expand_own + expand_oth, (shrink_z, swap_core(shrink_z)),
    )

    def plane_send(keep, got):
        return tuple(add_low(keep[x, y], got[x, y]) for x, y in ((1, 0), (0, 1), (1, 1)))

    def plane_swap(parts):
        return swap_x(parts[0]), swap_dp(parts[1], 1), swap_both(parts[2])

    def plane_sum(own, got):
        total = sum(part.astype(F32) for part in own)
        return total + sum(part.astype(F32) for part in got)

    def fold(value, dtype):
        return jnp.sum(value.astype(F32), axis=0).astype(dtype)

    feed_got = swap_core(feed_send)
    part_one = cross_backward(queries, kv_own, kv_oth, mixed_two, cross_lse, cross_grad, 0, 2)
    feed_keep = gate(feed_keep, part_one[0])

    def feed_sum(x, y, which, *others):
        at = (x, y, Ellipsis, slice(which * hidden_cols, (which + 1) * hidden_cols))
        total = feed_keep[at].astype(F32) + feed_got[at].astype(F32)
        for other in others:
            total = total + other.astype(F32)
        return total.astype(BF)

    expand_send = feed_sum(1, slice(None), 0)
    shrink_send = feed_sum(slice(None), 1, 1)
    expand_send, shrink_send, part_one = lax.optimization_barrier(
        (expand_send, shrink_send, tuple(part_one))
    )
    expand_got = swap_x(expand_send)
    shrink_got = swap_dp(shrink_send, 1)

    dq, dkv_own, dkv_send, first_in, self_low, grad_own, grad_send, early_vec = cross_first_backward(
        queries, kv_own, kv_oth, mixed_two, cross_lse, cross_grad, 2, part_one,
        cross_q, second_in, first_sum, first_gain.reshape(1, -1), self_o,
    )
    expand_got, shrink_got, dkv_send, grad_send = lax.optimization_barrier(
        (expand_got, shrink_got, dkv_send, grad_send)
    )
    dkv_got = swap_core(dkv_send)
    grad_got = swap_core(grad_send)
    expand_send = feed_sum(0, 1, 0, expand_got[1])
    shrink_send = feed_sum(1, 0, 1, shrink_got[1])
    self_low, dkv_got, grad_got, expand_send, shrink_send = lax.optimization_barrier(
        (self_low, dkv_got, grad_got, expand_send, shrink_send)
    )
    expand_last = swap_dp(expand_send, 1)
    shrink_last = swap_x(shrink_send)
    query_keep, query_send = query_grads(
        info, (first_low, dq, self_low, mixed_one, cross_low, mixed_two, early_vec), depth
    )
    dkv_own, query_send = lax.optimization_barrier((dkv_own, query_send))
    query_got = swap_core(query_send)
    key_keep, key_send, fetched_grad = key_grads(
        info, fetched, dkv_own, dkv_got, cross_kv, depth
    )
    query_plane = plane_send(gate(query_keep, fetched_grad), query_got)
    query_plane, key_send, grad_got, fetched_grad, expand_last, shrink_last = (
        lax.optimization_barrier(
            (query_plane, key_send, grad_got, fetched_grad, expand_last, shrink_last)
        )
    )
    query_parts = plane_swap(query_plane)
    key_got = swap_core(key_send)

    self_args = (attn_info, qkv, self_own, self_send, self_lse, grad_own, grad_got)
    pairs = two // 128
    half_grads = self_backward(*self_args, 0, pairs - 1)
    key_plane = plane_send(gate(key_keep, half_grads[1]), key_got)
    feed_three = jnp.concatenate(
        [
            feed_sum(0, 0, 0, expand_got[0], gate(expand_last, half_grads[1])),
            feed_sum(0, 0, 1, shrink_got[0], gate(shrink_last, half_grads[1])),
        ],
        axis=-1,
    )
    query_three = plane_sum((query_keep[0, 0], query_got[0, 0]), query_parts).astype(BF)
    key_plane, half_grads, feed_three, query_three = lax.optimization_barrier(
        (key_plane, tuple(half_grads), feed_three, query_three)
    )
    key_parts = plane_swap(key_plane)
    feed_last = outer_exchange(feed_three)
    grads, self_rows = self_backward(*self_args, pairs - 1, 1, half_grads)
    grads, key_parts = lax.optimization_barrier((grads, key_parts))
    self_places = self_grads(info, tokens, tokens_oth, grads, depth)
    self_places, grads = lax.optimization_barrier((tuple(self_places), grads))
    self_parts = (swap_x(self_places[1]), swap_dp(self_places[2], 1), swap_both(self_places[3]))
    grads, feed_last, query_three = lax.optimization_barrier((grads, feed_last, query_three))
    query_last = outer_exchange(query_three)
    back_keep, back_send = self_back(grads, self_mat, first_in)
    back_send, query_last, key_parts, self_near, self_away = lax.optimization_barrier(
        (back_send, query_last, key_parts, self_parts[0], self_parts[1])
    )
    key_three = plane_sum((key_keep[0, 0], key_got[0, 0]), key_parts).astype(BF)
    back_got = swap_core(back_send)
    self_three = plane_sum((self_places[0],), (self_near, self_away, self_parts[2])).astype(BF)
    self_last = outer_exchange(
        gate(jnp.concatenate([self_three, key_three], axis=-1), query_last)
    )
    fetched_send = gate(fetched_grad, self_three)
    fetched_away = swap_x(fetched_send).reshape(slots, BLK, width)
    fetched_near = fetched_send.reshape(slots, BLK, width)
    in_grad = (back_keep + back_got.astype(F32)).astype(BF)

    cq_grad, so_grad, co_grad, cq_rows, first_shift_rows, first_gain_rows, so_rows = sum_query(
        query_last, depth
    )
    (
        sq_grad, sk_grad, sv_grad, ck_grad, cv_grad, sq_rows, sk_rows, sv_rows, ck_rows, cv_rows,
    ) = sum_cols(self_last, depth, 5)
    (
        expand_grad, shrink_grad, expand_rows, third_shift_rows, third_gain_rows, shrink_rows,
        second_shift_rows, second_gain_rows, co_rows,
    ) = sum_feed(feed_last, depth)
    shrink_grad = shrink_grad.T

    near_core = swap_core(fetched_near)
    away_core = swap_core(fetched_away)
    slot_ids = jnp.arange(NBLK)
    places = (
        (((slot_ids[None, :] // slots) != core) * 2 + (jnp.arange(seq_count)[:, None] != chip))
        * slots
        + slot_ids[None, :] % slots
    )
    hits = blocks[:, None, :] == (rank * local_blocks + jnp.arange(local_blocks))[None, :, None]
    scatter_table = jnp.max(jnp.where(hits, places[:, None, :], -1), axis=-1)
    bank_grad = scatter(
        scatter_table.reshape(-1).astype(jnp.int32),
        (fetched_near, fetched_away, near_core, away_core),
    ).reshape(bank.shape)

    def line(row):
        return row.reshape(-1)

    return (
        out_act,
        in_grad,
        bank_grad,
        sq_grad,
        line(sq_rows),
        sk_grad,
        sv_grad,
        line(sv_rows),
        so_grad,
        line(so_rows),
        line(first_gain_rows),
        line(first_shift_rows),
        cq_grad,
        line(cq_rows),
        ck_grad,
        cv_grad,
        line(cv_rows),
        co_grad,
        line(co_rows),
        line(second_gain_rows),
        line(second_shift_rows),
        expand_grad,
        line(expand_rows),
        shrink_grad,
        line(shrink_rows),
        line(third_gain_rows),
        line(third_shift_rows),
    )


def solution(mesh):
    rows = P(("dp", "tensor"), None)
    wide = P("dp", "tensor")
    tall = P("tensor", "dp")
    part = P("tensor")
    full = P()
    return jax.shard_map(
        local,
        mesh=mesh,
        in_specs=(
            rows, P("dp", "tensor", None), P("dp"), P("dp", None), rows,
            wide, part, wide, wide, part, tall, full, full, full,
            wide, part, wide, wide, part, tall, full, full, full,
            wide, part, tall, full, full, full,
        ),
        out_specs=(
            rows, rows, P("dp", "tensor", None),
            wide, part, wide, wide, part, tall, full, full, full,
            wide, part, wide, wide, part, tall, full, full, full,
            wide, part, tall, full, full, full,
        ),
        check_vma=False,
    )
```

```python
import functools
import math

import jax
import jax.numpy as jnp
from jax import lax
from jax.experimental import pallas as pl
from jax.experimental.pallas import tpu as pltpu
from jax.sharding import PartitionSpec as P

HD = 64
BLK = 64
NBLK = 16
EPS = 1e-05
NEGATIVE = -1e30
BF = jnp.bfloat16
F32 = jnp.float32

NT = (((1,), (1,)), ((), ()))
NN = (((1,), (0,)), ((), ()))
TN = (((0,), (0,)), ((), ()))

CORE_SWAP = ((0, 1), (1, 0), (2, 3), (3, 2))
X_SWAP = ((0, 2), (2, 0), (1, 3), (3, 1))
VMEM_LIMIT = 48 << 20
COST = pl.CostEstimate(flops=1000, bytes_accessed=1000, transcendentals=0)


def mm(left, right, dims=NN):
    return lax.dot_general(left, right, dims, preferred_element_type=F32)


def swap_core(value):
    return lax.ppermute(value, "tensor", CORE_SWAP)


def swap_x(value):
    return lax.ppermute(value, "tensor", X_SWAP)


def swap_dp(value, bit):
    count = lax.axis_size("dp")
    return lax.ppermute(value, "dp", tuple((i, i ^ bit) for i in range(count)))


def dp_bits():
    count = lax.axis_size("dp")
    bits = []
    bit = count // 2
    while bit >= 1:
        bits.append(bit)
        bit //= 2
    return bits


def pair_backward(q, k, v, grad, lse, delta, mask):
    score = mm(k, q, NT)
    prob = jnp.exp(score - lse)
    if mask is not None:
        prob = jnp.where(mask, prob, 0.0)
    slope = prob * (mm(v, grad, NT) - delta)
    prob = prob.astype(BF)
    slope = slope.astype(BF)
    return mm(slope, k, TN), mm(slope, q, NN), mm(prob, grad, NN)


def delta_row(grad, mixed):
    return jnp.sum((grad.astype(F32) * mixed.astype(F32)).T, 0, keepdims=True)


def self_bwd_kernel(info, q_ref, k_ref, v_ref, oa_ref, ob_ref, lse_ref, ga_ref, gb_ref, *rest):
    out_ref, sums_ref, o_ref, g_ref = rest[-4:]
    dq_ref, dk_ref, dv_ref = out_ref.at[0], out_ref.at[1], out_ref.at[2]
    o_ref[0], o_ref[1] = oa_ref[...], ob_ref[...]
    g_ref[0], g_ref[1] = ga_ref[...], gb_ref[...]
    half = q_ref.shape[1]
    first = info[0]
    second = 1 - first
    prefix = info[1]
    key_pos = lax.broadcasted_iota(jnp.int32, (half, half), 0)
    query_pos = lax.broadcasted_iota(jnp.int32, (half, half), 1)
    causal = key_pos <= query_pos
    seen = causal | (key_pos < prefix)
    scale = 1.0 / math.sqrt(HD)
    for h in range(2):
        cols = slice(HD * h, HD * h + HD)

        def rows(ref, at):
            return ref[at, :, cols]

        def one(q_at, k_at, mask):
            grad = rows(g_ref, q_at)
            delta = delta_row(grad, rows(o_ref, q_at))
            lse = lse_ref[0, h, pl.ds(q_at, 1), :]
            return pair_backward(
                rows(q_ref, q_at), rows(k_ref, k_at), rows(v_ref, k_at), grad, lse, delta, mask
            )

        dq, dk_a, dv_a = one(first, first, seen)
        dq_ref[first, :, cols] = (dq.astype(BF) * scale).astype(BF)
        dq_b, dk_b, dv_b = one(second, first, None)
        dk_ref[first, :, cols] = (dk_a + dk_b).astype(BF)
        dv_ref[first, :, cols] = (dv_a + dv_b).astype(BF)
        dq_c, dk_c, dv_c = one(second, second, causal)
        dq_ref[second, :, cols] = ((dq_b + dq_c).astype(BF) * scale).astype(BF)
        dk_ref[second, :, cols] = dk_c.astype(BF)
        dv_ref[second, :, cols] = dv_c.astype(BF)
    for i in range(3):
        both = out_ref[i, 0].astype(F32) + out_ref[i, 1].astype(F32)
        sums_ref[0, i : i + 1, :] = jnp.sum(both, 0, keepdims=True)


def self_backward(info, qkv, mixed_own, mixed_oth, lse, grad_own, grad_oth, start, count, former=()):
    half, width = qkv.shape[1], qkv.shape[2] // 3
    pairs = width // 128

    def spec(which):
        return pl.BlockSpec((2, half, 128), lambda i, info: (0, 0, which * pairs + start + i))

    flat = pl.BlockSpec((half, 128), lambda i, info: (0, start + i))
    cells = 3 * half * half * count * 2
    return pl.pallas_call(
        self_bwd_kernel,
        grid_spec=pltpu.PrefetchScalarGridSpec(
            num_scalar_prefetch=1,
            grid=(count,),
            in_specs=[
                spec(0),
                spec(1),
                spec(2),
                flat,
                flat,
                pl.BlockSpec((1, 2, 2, half), lambda i, info: (start + i, 0, 0, 0)),
                flat,
                flat,
            ]
            + [pl.BlockSpec(memory_space=pl.ANY)] * len(former),
            out_specs=[
                pl.BlockSpec((3, 2, half, 128), lambda i, info: (0, 0, 0, start + i)),
                pl.BlockSpec((1, 8, 128), lambda i, info: (start + i, 0, 0)),
            ],
            scratch_shapes=[pltpu.VMEM((2, half, 128), BF)] * 2,
        ),
        out_shape=[
            jax.ShapeDtypeStruct((3, 2, half, width), BF),
            jax.ShapeDtypeStruct((pairs, 8, 128), F32),
        ],
        input_output_aliases={9 + i: i for i in range(len(former))},
        compiler_params=pltpu.CompilerParams(vmem_limit_bytes=VMEM_LIMIT),
        cost_estimate=COST,
        name="self_bwd",
    )(info, qkv, qkv, qkv, mixed_own, mixed_oth, lse, grad_own, grad_oth, *former)


def cross_fwd_kernel(q_ref, ka_ref, kb_ref, va_ref, vb_ref, o_ref, lse_ref):
    for h in range(2):
        cols = slice(HD * h, HD * h + HD)
        q = q_ref[:, cols]
        score_a = mm(ka_ref[:, cols], q, NT)
        score_b = mm(kb_ref[:, cols], q, NT)
        top = jnp.maximum(
            jnp.max(score_a, 0, keepdims=True), jnp.max(score_b, 0, keepdims=True)
        )
        expo_a = jnp.exp(score_a - top)
        expo_b = jnp.exp(score_b - top)
        total = jnp.sum(expo_a, 0, keepdims=True) + jnp.sum(expo_b, 0, keepdims=True)
        mixed = (
            mm(va_ref[:, cols], expo_a.astype(BF), TN) + mm(vb_ref[:, cols], expo_b.astype(BF), TN)
        ) / total
        o_ref[:, cols] = mixed.T.astype(BF)
        lse_ref[0, h : h + 1, :] = top + jnp.log(total)


def cross_specs(rows, pairs):
    whole = pl.BlockSpec((rows, 128), lambda i: (0, i))
    turned = pl.BlockSpec((rows, 128), lambda i: (0, (i + pairs // 2) % pairs))
    value = pl.BlockSpec((rows, 128), lambda i: (0, pairs + i))
    value_turned = pl.BlockSpec((rows, 128), lambda i: (0, pairs + (i + pairs // 2) % pairs))
    return whole, turned, value, value_turned


def cross_forward(queries, kv_own, kv_oth):
    rows, width = queries.shape
    pairs = width // 128
    whole, turned, value, value_turned = cross_specs(rows, pairs)
    cells = 2 * rows * rows * pairs * 2
    return pl.pallas_call(
        cross_fwd_kernel,
        grid=(pairs,),
        in_specs=[whole, whole, turned, value, value_turned],
        out_specs=[whole, pl.BlockSpec((1, 2, rows), lambda i: (i, 0, 0))],
        out_shape=[
            jax.ShapeDtypeStruct((rows, width), BF),
            jax.ShapeDtypeStruct((pairs, 2, rows), F32),
        ],
        compiler_params=pltpu.CompilerParams(vmem_limit_bytes=VMEM_LIMIT),
        cost_estimate=COST,
        name="cross_fwd",
    )(queries, kv_own, kv_oth, kv_own, kv_oth)


def cross_bwd_kernel(
    q_ref, ka_ref, kb_ref, va_ref, vb_ref, o_ref, lse_ref, g_ref,
    *rest,
):
    dq_ref, da_ref, db_ref = rest[-3:]
    scale = 1.0 / math.sqrt(HD)
    for h in range(2):
        cols = slice(HD * h, HD * h + HD)
        grad = g_ref[:, cols]
        delta = delta_row(grad, o_ref[:, cols])
        lse = lse_ref[0, h : h + 1, :]
        q = q_ref[:, cols]
        dq_a, dk, dv = pair_backward(q, ka_ref[:, cols], va_ref[:, cols], grad, lse, delta, None)
        da_ref[0, :, cols] = dk.astype(BF)
        da_ref[1, :, cols] = dv.astype(BF)
        dq_b, dk, dv = pair_backward(q, kb_ref[:, cols], vb_ref[:, cols], grad, lse, delta, None)
        db_ref[0, :, cols] = dk.astype(BF)
        db_ref[1, :, cols] = dv.astype(BF)
        dq_ref[:, cols] = ((dq_a + dq_b).astype(BF) * scale).astype(BF)


def cross_backward(queries, kv_own, kv_oth, mixed, lse, grad, start, count, former=()):
    rows, width = queries.shape
    pairs = width // 128

    def turn(i):
        return (start + i + pairs // 2) % pairs

    whole = pl.BlockSpec((rows, 128), lambda i: (0, start + i))
    turned = pl.BlockSpec((rows, 128), lambda i: (0, turn(i)))
    value = pl.BlockSpec((rows, 128), lambda i: (0, pairs + start + i))
    value_turned = pl.BlockSpec((rows, 128), lambda i: (0, pairs + turn(i)))
    cells = 2 * rows * rows * count * 2
    both = jax.ShapeDtypeStruct((2, rows, width), BF)
    return pl.pallas_call(
        cross_bwd_kernel,
        grid=(count,),
        in_specs=[
            whole, whole, turned, value, value_turned, whole,
            pl.BlockSpec((1, 2, rows), lambda i: (start + i, 0, 0)), whole,
        ]
        + [pl.BlockSpec(memory_space=pl.ANY)] * len(former),
        out_specs=[
            whole,
            pl.BlockSpec((2, rows, 128), lambda i: (0, 0, start + i)),
            pl.BlockSpec((2, rows, 128), lambda i: (0, 0, turn(i))),
        ],
        out_shape=[jax.ShapeDtypeStruct((rows, width), BF), both, both],
        input_output_aliases={8 + i: i for i in range(len(former))},
        compiler_params=pltpu.CompilerParams(vmem_limit_bytes=VMEM_LIMIT),
        cost_estimate=COST,
        name="cross_bwd",
    )(queries, kv_own, kv_oth, kv_own, kv_oth, mixed, lse, grad, *former)


def norm_parts(resid):
    center = resid - jnp.mean(resid, axis=-1, keepdims=True)
    rstd = lax.rsqrt(jnp.mean(center * center, axis=-1, keepdims=True) + EPS)
    return center * rstd, rstd


def norm_back(normed, rstd, grad, gain):
    scaled = grad * gain
    return rstd * (
        scaled
        - jnp.mean(scaled, axis=-1, keepdims=True)
        - normed * jnp.mean(scaled * normed, axis=-1, keepdims=True)
    )


def cross_first_kernel(
    q_ref, ka_ref, kb_ref, va_ref, vb_ref, o_ref, lse_ref, g_ref,
    q_mat, second_ref, resid_ref, vec_ref, o_mat, dq_in, former_a, former_b,
    dq_ref, da_ref, db_ref, first_ref, low_ref, keep_ref, send_ref, sums_ref, dq_part,
    *, start, count,
):
    step = pl.program_id(0)

    @pl.when(step == 0)
    def _():
        dq_ref[...] = dq_in[...]

    cross_bwd_kernel(
        q_ref, ka_ref, kb_ref, va_ref, vb_ref, o_ref, lse_ref, g_ref, dq_part, da_ref, db_ref
    )
    at = pl.multiple_of((start + step) * 128, 128)
    dq_ref[:, pl.ds(at, 128)] = dq_part[...]

    @pl.when(step == count - 1)
    def _():
        grad = second_ref[...] + mm(dq_ref[...], q_mat[...], NT)
        normed, rstd = norm_parts(resid_ref[...])
        sums_ref[0:1, :] = jnp.sum(grad, 0, keepdims=True)
        sums_ref[1:2, :] = jnp.sum(grad * normed, 0, keepdims=True)
        first_in = norm_back(normed, rstd, grad, vec_ref[0:1, :])
        first_ref[...] = first_in
        low = first_in.astype(BF)
        low_ref[...] = low
        sums_ref[2:3, :] = jnp.sum(low.astype(F32), 0, keepdims=True)
        sums_ref[3:4, :] = jnp.sum(dq_ref[...].astype(F32), 0, keepdims=True)
        sums_ref[4:8, :] = jnp.zeros((4, sums_ref.shape[1]), F32)
        mixed_grad = mm(low, o_mat[...]).astype(BF)
        cols = keep_ref.shape[1]
        keep_ref[...] = mixed_grad[:, :cols]
        send_ref[...] = mixed_grad[:, cols:]


def cross_first_backward(
    queries, kv_own, kv_oth, mixed, lse, grad, start, former, q_mat, second_in, resid, vec, o_mat
):
    rows, width = queries.shape
    pairs = width // 128
    count = pairs - start

    def turn(i):
        return (start + i + pairs // 2) % pairs

    whole = pl.BlockSpec((rows, 128), lambda i: (0, start + i))
    turned = pl.BlockSpec((rows, 128), lambda i: (0, turn(i)))
    value = pl.BlockSpec((rows, 128), lambda i: (0, pairs + start + i))
    value_turned = pl.BlockSpec((rows, 128), lambda i: (0, pairs + turn(i)))

    def fixed(shape):
        return pl.BlockSpec(shape, lambda i: (0, 0))

    both = jax.ShapeDtypeStruct((2, rows, width), BF)
    return pl.pallas_call(
        functools.partial(cross_first_kernel, start=start, count=count),
        grid=(count,),
        in_specs=[
            whole, whole, turned, value, value_turned, whole,
            pl.BlockSpec((1, 2, rows), lambda i: (start + i, 0, 0)), whole,
            fixed((width, width)), fixed((rows, width)), fixed((rows, width)),
            fixed((1, width)), fixed((width, width)), fixed((rows, width)),
            pl.BlockSpec(memory_space=pl.ANY), pl.BlockSpec(memory_space=pl.ANY),
        ],
        out_specs=[
            fixed((rows, width)),
            pl.BlockSpec((2, rows, 128), lambda i: (0, 0, start + i)),
            pl.BlockSpec((2, rows, 128), lambda i: (0, 0, turn(i))),
            fixed((rows, width)),
            fixed((rows, width)),
            fixed((rows, width // 2)),
            fixed((rows, width // 2)),
            fixed((8, width)),
        ],
        out_shape=[
            jax.ShapeDtypeStruct((rows, width), BF),
            both,
            both,
            jax.ShapeDtypeStruct((rows, width), F32),
            jax.ShapeDtypeStruct((rows, width), BF),
            jax.ShapeDtypeStruct((rows, width // 2), BF),
            jax.ShapeDtypeStruct((rows, width // 2), BF),
            jax.ShapeDtypeStruct((8, width), F32),
        ],
        scratch_shapes=[pltpu.VMEM((rows, 128), BF)],
        input_output_aliases={14: 1, 15: 2},
        compiler_params=pltpu.CompilerParams(vmem_limit_bytes=VMEM_LIMIT),
        cost_estimate=COST,
        name="cross_first",
    )(
        queries, kv_own, kv_oth, kv_own, kv_oth, mixed, lse, grad,
        q_mat, second_in, resid, vec, o_mat, *former,
    )


def gate(value, *others):
    return lax.optimization_barrier((value,) + others)[0]


def outer_count():
    return lax.axis_size("dp") // 2


def swap_both(value):
    count = lax.axis_size("dp")
    pairs = tuple(
        (d * 4 + t, (d ^ 1) * 4 + (t ^ 2)) for d in range(count) for t in range(4)
    )
    return lax.ppermute(value, ("dp", "tensor"), pairs)


def outer_exchange(value):
    groups = [[inner + 2 * o for o in range(outer_count())] for inner in range(2)]
    return lax.all_to_all(value, "dp", 0, 0, axis_index_groups=groups, tiled=True)


def plane_exchange(value):
    groups = [
        [(o * 2 + inner) * 4 + chip * 2 + core for chip in range(2) for inner in range(2)]
        for o in range(outer_count())
        for core in range(2)
    ]
    return lax.all_to_all(value, ("dp", "tensor"), 0, 0, axis_index_groups=groups, tiled=True)


def add_low(left, right):
    return (left.astype(F32) + right.astype(F32)).astype(BF)


def total_dp(value):
    for bit in dp_bits():
        value = value + swap_dp(value, bit)
    return value


ANY = pl.BlockSpec(memory_space=pl.ANY)
VM = pl.BlockSpec(memory_space=pltpu.VMEM)
SM = pl.BlockSpec(memory_space=pltpu.SMEM)


def call(kernel, out_shape, args, in_specs, out_specs, scratch=(), flops=0, moved=0, name=None):
    return pl.pallas_call(
        kernel,
        out_shape=out_shape,
        in_specs=in_specs,
        out_specs=out_specs,
        scratch_shapes=list(scratch),
        compiler_params=pltpu.CompilerParams(vmem_limit_bytes=58 << 20),
        cost_estimate=COST,
        name=name,
    )(*args)


def struct(shape, dtype):
    return jax.ShapeDtypeStruct(shape, dtype)


def tail_start(depth):
    return (depth + 15) // 16 * 16


def high_low(row):
    high = row.astype(BF).astype(F32)
    return high, row - high


def stack_rows(rows, count):
    cols = rows[0].shape[1]
    at = lax.broadcasted_iota(jnp.int32, (count, cols), 0)
    total = jnp.zeros((count, cols), F32)
    for i, row in enumerate(rows):
        total = jnp.where(at == i, row, total)
    return total.astype(BF)


def pack_self_kernel(q_ref, k_ref, v_ref, out_ref):
    cols = q_ref.shape[1]
    for i, ref in enumerate((q_ref, k_ref, v_ref)):
        low = ref[...].astype(BF)
        for copy in range(out_ref.shape[0]):
            out_ref[copy, :, i * cols : (i + 1) * cols] = low


def turned(ref):
    depth = ref.shape[1]
    eye = (
        lax.broadcasted_iota(jnp.int32, (depth, depth), 0)
        == lax.broadcasted_iota(jnp.int32, (depth, depth), 1)
    )
    eye = jnp.where(eye, 1.0, 0.0).astype(BF)
    return mm(eye, ref[...].astype(BF), NT).astype(BF)


def pack_rest_kernel(ck_ref, cv_ref, cq_ref, so_ref, co_ref, ex_ref, sh_ref, next_ref, sh_out):
    cols = ck_ref.shape[1]
    wide = ex_ref.shape[1]
    parts = [ref[...].astype(BF) for ref in (ck_ref, cv_ref, cq_ref)]
    parts += [turned(so_ref), turned(co_ref)]
    expand = ex_ref[...].astype(BF)
    for copy in range(next_ref.shape[0]):
        next_ref[copy, :, :wide] = expand
        for i, low in enumerate(parts):
            next_ref[copy, :, wide + i * cols : wide + (i + 1) * cols] = low
    sh_out[...] = sh_ref[...].astype(BF)


def self_forward_kernel(
    info, own_ref, oth_ref, bias_ref, w_ref, wx_ref, wy_ref, wxy_ref,
    qkv_ref, mat_ref, oa_ref, ob_ref, lse_ref, w_own, w_x, o_ref, sems,
):
    pair = pl.program_id(0)
    width = own_ref.shape[1]
    half = own_ref.shape[0]
    wide = qkv_ref.shape[2] // 3

    @pl.when(pair == 0)
    def _():
        place = info[0]
        cols = w_own.shape[3]
        copies = [
            pltpu.make_async_copy(w_ref, w_own.at[:, place], sems.at[0]),
            pltpu.make_async_copy(wy_ref, w_own.at[:, 1 - place], sems.at[1]),
            pltpu.make_async_copy(wx_ref, w_x.at[:, place], sems.at[2]),
            pltpu.make_async_copy(wxy_ref, w_x.at[:, 1 - place], sems.at[3]),
        ]
        for copy in copies:
            copy.start()
        for copy in copies:
            copy.wait()
        piece = cols // 3
        scale = 1.0 / math.sqrt(HD)
        for x, ref in enumerate((w_own, w_x)):
            mat = ref[...].reshape(width, cols)
            for i in range(3):
                at = (2 * i + x) * piece
                mat_ref[:, at : at + piece] = mat[:, i * piece : (i + 1) * piece]
        for rel, src in enumerate((own_ref, oth_ref)):
            for i in range(3):
                at = slice(wide * i, wide * (i + 1))
                part = mm(src[...], mat_ref[:, at]) + bias_ref[i : i + 1, :]
                if i == 0:
                    part = part * scale
                qkv_ref[rel, :, at] = part.astype(BF)

    first = info[3]
    second = 1 - first
    prefix = info[4]
    key_pos = lax.broadcasted_iota(jnp.int32, (half, half), 0)
    query_pos = lax.broadcasted_iota(jnp.int32, (half, half), 1)
    causal = key_pos <= query_pos
    seen = causal | (key_pos < prefix)

    def load(which, at):
        start = pl.multiple_of(which * wide + pair * 128, 128)
        return qkv_ref[at, :, pl.ds(start, 128)]

    q_both = (load(0, first), load(0, second))
    k_both = (load(1, first), load(1, second))
    v_both = (load(2, first), load(2, second))
    for h in range(2):
        cols = slice(HD * h, HD * h + HD)
        k0, k1 = (k[:, cols] for k in k_both)
        v0, v1 = (v[:, cols] for v in v_both)
        q0, q1 = (q[:, cols] for q in q_both)
        score = jnp.where(seen, mm(k0, q0, NT), NEGATIVE)
        top = jnp.max(score, 0, keepdims=True)
        expo = jnp.exp(score - top)
        total = jnp.sum(expo, 0, keepdims=True)
        mixed = mm(v0, expo.astype(BF), TN) / total
        o_ref[first, :, cols] = mixed.T.astype(BF)
        lse_ref[0, h, pl.ds(first, 1), :] = top + jnp.log(total)

        score_a = mm(k0, q1, NT)
        score_b = jnp.where(causal, mm(k1, q1, NT), NEGATIVE)
        top = jnp.maximum(
            jnp.max(score_a, 0, keepdims=True), jnp.max(score_b, 0, keepdims=True)
        )
        expo_a = jnp.exp(score_a - top)
        expo_b = jnp.exp(score_b - top)
        total = jnp.sum(expo_a, 0, keepdims=True) + jnp.sum(expo_b, 0, keepdims=True)
        mixed = (mm(v0, expo_a.astype(BF), TN) + mm(v1, expo_b.astype(BF), TN)) / total
        o_ref[second, :, cols] = mixed.T.astype(BF)
        lse_ref[0, h, pl.ds(second, 1), :] = top + jnp.log(total)
    oa_ref[...] = o_ref[0]
    ob_ref[...] = o_ref[1]


def self_forward(info, own, oth, bias, pieces):
    half, width = own.shape
    outer, depth, cols = pieces[0].shape
    wide = 2 * cols // 3
    pairs = wide // 128
    fixed2 = pl.BlockSpec((half, width), lambda i, info: (0, 0))
    pair_cols = pl.BlockSpec((half, 128), lambda i, info: (0, i))
    return pl.pallas_call(
        self_forward_kernel,
        grid_spec=pltpu.PrefetchScalarGridSpec(
            num_scalar_prefetch=1,
            grid=(pairs,),
            in_specs=[
                fixed2,
                fixed2,
                pl.BlockSpec(bias.shape, lambda i, info: (0, 0)),
                ANY,
                ANY,
                ANY,
                ANY,
            ],
            out_specs=[
                pl.BlockSpec((2, half, 3 * wide), lambda i, info: (0, 0, 0)),
                pl.BlockSpec((width, 3 * wide), lambda i, info: (0, 0)),
                pair_cols,
                pair_cols,
                pl.BlockSpec((1, 2, 2, half), lambda i, info: (i, 0, 0, 0)),
            ],
            scratch_shapes=[
                pltpu.VMEM((outer, 2, depth, cols), BF),
                pltpu.VMEM((outer, 2, depth, cols), BF),
                pltpu.VMEM((2, half, 128), BF),
                pltpu.SemaphoreType.DMA((4,)),
            ],
        ),
        out_shape=[
            struct((2, half, 3 * wide), BF),
            struct((width, 3 * wide), BF),
            struct((half, wide), BF),
            struct((half, wide), BF),
            struct((pairs, 2, 2, half), F32),
        ],
        compiler_params=pltpu.CompilerParams(vmem_limit_bytes=VMEM_LIMIT),
        cost_estimate=COST,
        name="self_fwd",
    )(info, own, oth, bias, *pieces)


def assemble_kernel(info, *refs):
    pieces, (kv_ref, q_ref, so_ref, co_ref) = refs[:8], refs[8:]
    place = info[0]
    outer, depth, cols = pieces[0].shape
    piece = cols // 5
    for j in range(4):
        for y in range(2):
            at = place if y == 0 else 1 - place
            for o in range(outer):
                value = pieces[2 * j + y][o]
                own = slice(piece * j, piece * (j + 1))
                low = slice(4 * piece + piece * j, 4 * piece + piece * (j + 1))
                kv_ref[o, at, :, own] = value[:, :piece]
                kv_ref[o, at, :, low] = value[:, piece : 2 * piece]
                q_ref[o, at, :, own] = value[:, 2 * piece : 3 * piece]
                so_ref[o, at, :, own] = value[:, 3 * piece : 4 * piece]
                co_ref[o, at, :, own] = value[:, 4 * piece :]


def assemble(info, pieces):
    outer, depth, cols = pieces[0].shape
    wide = cols // 5 * 4
    outs = call(
        assemble_kernel,
        [struct((outer, 2, depth, 2 * wide), BF)] + [struct((outer, 2, depth, wide), BF)] * 3,
        [info] + list(pieces),
        [SM] + [VM] * 8,
        [VM] * 4,
        moved=pieces[0].size * 32,
        name="assemble",
    )
    return [out.reshape(-1, out.shape[-1]) for out in outs]


def copies_kernel(info, own_ref, x_ref, y_ref, xy_ref, out_ref):
    place = info[0]
    for copy in range(out_ref.shape[0]):
        out_ref[copy, 0, place] = own_ref[...]
        out_ref[copy, 0, 1 - place] = y_ref[...]
        out_ref[copy, 1, place] = x_ref[...]
        out_ref[copy, 1, 1 - place] = xy_ref[...]


def plane_copies(info, own, x, y, xy):
    depth, cols = own.shape
    outer = outer_count()
    return call(
        copies_kernel,
        struct((outer, 2, 2, depth, cols), BF),
        [info, own, x, y, xy],
        [SM] + [VM] * 4,
        VM,
        moved=own.size * 2 * 4 * (outer + 1),
        name="plane_copies",
    )


def first_forward_kernel(
    tok_ref, own_ref, oth_ref, o_mat, vec_ref, q_mat, qb_ref,
    resid_ref, first_ref, low_ref, q_ref, mixed_ref,
):
    cols = own_ref.shape[1]
    mixed_ref[:, :cols] = own_ref[...]
    mixed_ref[:, cols:] = oth_ref[...]
    resid = tok_ref[...].astype(F32) + mm(mixed_ref[...], o_mat[...], NT) + vec_ref[0:1, :]
    resid_ref[...] = resid
    normed, rstd = norm_parts(resid)
    first = normed * vec_ref[1:2, :] + vec_ref[2:3, :]
    first_ref[...] = first
    low_ref[...] = first.astype(BF)
    scale = 1.0 / math.sqrt(HD)
    q_ref[...] = ((mm(low_ref[...], q_mat[...]) + qb_ref[...]) * scale).astype(BF)


def first_forward(tokens, own, oth, o_mat, vecs, q_mat, q_bias):
    rows, width = tokens.shape
    return call(
        first_forward_kernel,
        [struct((rows, width), F32)] * 2 + [struct((rows, width), BF)] * 3,
        [tokens, own, oth, o_mat, vecs, q_mat, q_bias],
        [VM] * 7,
        [VM] * 5,
        flops=2 * rows * width * width * 2 * 2,
        moved=width * width * 4 + rows * width * 18,
        name="first_forward",
    )


def project_kv_kernel(keep_ref, got_ref, mat_ref, bias_ref, fet_ref, out_ref):
    fet_ref[...] = keep_ref[...] + got_ref[...]
    width = fet_ref.shape[1]
    out_ref[:, :width] = mm(fet_ref[...], mat_ref[:, :width]).astype(BF)
    out_ref[:, width:] = (mm(fet_ref[...], mat_ref[:, width:]) + bias_ref[...]).astype(BF)


def project_kv(keep, got, mat, bias):
    rows, width = keep.shape
    return call(
        project_kv_kernel,
        [struct((rows, width), BF), struct((rows, 2 * width), BF)],
        [keep, got, mat, bias],
        [VM] * 4,
        [VM] * 2,
        name="project_kv",
    )


def feed_kernel(
    info, mixed_ref, first_ref, cot_ref, vec_ref, wo_hbm,
    e0, e1, e2, e3, e4, e5, e6, e7, s0, s1,
    out_ref, second_ref, low_ref, grad_ref,
    keep_ref, send_ref, sums_ref, tail,
    wo, we, ws, hid, slo, out_a, out_b, norm2, h2low, e3low, acc, wsem, osem, tsem,
):
    first_copy = pltpu.make_async_copy(wo_hbm, wo, wsem.at[0])
    first_copy.start()
    place = info[0]
    copies = []
    for j, pair in enumerate(((e0, e1), (e2, e3), (e4, e5), (e6, e7))):
        for y, ref in enumerate(pair):
            at = place if y == 0 else 1 - place
            copies.append(pltpu.make_async_copy(ref, we.at[j, :, at], wsem.at[1 + 2 * j + y]))
    for j in range(4):
        ref = (s0, s1)[j // 2]
        copies.append(pltpu.make_async_copy(ref.at[:, j % 2], ws.at[j], wsem.at[9 + j]))
    for copy in copies:
        copy.start()

    width = first_ref.shape[1]
    hidden_cols = we.shape[-1]
    outer, depth = we.shape[1], we.shape[3]
    base = out_a.shape[3]

    def expand_mat(j):
        return we[j].reshape(width, hidden_cols)

    def shrink_mat(j):
        return ws[j].reshape(width, hidden_cols)

    def row(i):
        return vec_ref[i : i + 1, :]

    first_copy.wait()
    resid = first_ref[...] + mm(mixed_ref[...], wo[...], NT) + row(0)
    normed, rstd2 = norm_parts(resid)
    norm2[...] = normed
    second = normed * row(1) + row(2)
    h2low[...] = second.astype(BF)
    acc[...] = second + row(7)
    for copy in copies:
        copy.wait()

    def forward(j, carry):
        inner = mm(h2low[...], expand_mat(j)) + vec_ref[pl.ds(3 + j, 1), :]
        phi = 0.5 + 0.5 * lax.erf(inner * (1.0 / math.sqrt(2.0)))
        hidden = (inner * phi).astype(BF)
        hid[j] = hidden
        bell = jnp.exp(-0.5 * inner * inner) * (1.0 / math.sqrt(2.0 * math.pi))
        slo[j] = (phi + inner * bell).astype(BF)
        acc[...] += mm(hidden, shrink_mat(j), NT)
        return carry

    lax.fori_loop(0, 4, forward, 0)
    norm3, rstd3 = norm_parts(acc[...])
    out_ref[...] = (norm3 * row(8) + row(9)).astype(BF)
    cot = cot_ref[...].astype(F32)
    sums_ref[0:1, :] = jnp.sum(cot, 0, keepdims=True)
    sums_ref[1:2, :] = jnp.sum(cot * norm3, 0, keepdims=True)
    third = norm_back(norm3, rstd3, cot, row(8))
    low = third.astype(BF)
    e3low[...] = low
    sums_ref[2:3, :] = jnp.sum(low.astype(F32), 0, keepdims=True)
    acc[...] = third

    def out_copies(to, at, slot):
        copies = []
        for y in range(2):
            for i, part in enumerate((out_a, out_b)):
                copies.append(
                    pltpu.make_async_copy(
                        part.at[slot, :, y],
                        to.at[
                            at, y ^ place, :, :base, i * hidden_cols : (i + 1) * hidden_cols
                        ],
                        osem.at[i, slot, y],
                    )
                )
        return copies

    def backward(step, carry):
        j = (step + 2) % 4
        slot = step % 2
        slope = slo[j].astype(F32)
        inner_grad = (mm(e3low[...], shrink_mat(j)) * slope).astype(BF)
        sums_ref[pl.ds(8 + j, 1), :] = jnp.sum(
            inner_grad.astype(F32), 0, keepdims=True
        )

        @pl.when(step >= 2)
        def _():
            for copy in out_copies(send_ref, slot, slot):
                copy.wait()

        shape = (outer, 2, depth, hidden_cols)
        out_a[slot, :, :, :depth] = mm(h2low[...], inner_grad, TN).astype(BF).reshape(shape)
        out_b[slot, :, :, :depth] = mm(e3low[...], hid[j], TN).astype(BF).reshape(shape)

        @pl.when(step < 2)
        def _():
            for copy in out_copies(send_ref, slot, slot):
                copy.start()

        @pl.when(step >= 2)
        def _():
            for copy in out_copies(keep_ref, slot, slot):
                copy.start()

        acc[...] += mm(inner_grad, expand_mat(j), NT)
        return carry

    lax.fori_loop(0, 4, backward, 0)
    grad = acc[...]
    normed = norm2[...]
    sums_ref[3:4, :] = jnp.sum(grad, 0, keepdims=True)
    sums_ref[4:5, :] = jnp.sum(grad * normed, 0, keepdims=True)
    second_in = norm_back(normed, rstd2, grad, row(1))
    second_ref[...] = second_in
    low = second_in.astype(BF)
    low_ref[...] = low
    sums_ref[5:6, :] = jnp.sum(low.astype(F32), 0, keepdims=True)
    tails = []
    pairs = [high_low(sums_ref[i : i + 1, :]) for i in range(6)]
    for j in range(4):
        rows_e = list(high_low(sums_ref[8 + j : 9 + j, :])) + [r for p in pairs[:3] for r in p]
        rows_s = [r for p in pairs[3:] for r in p]
        for o in range(outer):
            tail[j, o, :, :hidden_cols] = stack_rows(rows_e, 8)
            tail[j, o, :, hidden_cols:] = stack_rows(rows_s, 8)
        for y in range(2):
            to = (keep_ref, send_ref)[j // 2]
            tails.append(
                pltpu.make_async_copy(tail.at[j], to.at[j % 2, y, :, base:, :], tsem.at[2 * j + y])
            )
    for copy in tails:
        copy.start()
    grad_ref[...] = mm(low, wo[...]).astype(BF)
    for slot in range(2):
        for copy in out_copies(keep_ref, slot, slot):
            copy.wait()
    for copy in tails:
        copy.wait()


def feed(info, mixed, first, cot, vecs, wo, expand, shrink):
    rows, width = mixed.shape
    outer, depth, hidden = expand[0].shape
    base = tail_start(depth)
    grads = struct((2, 2, outer, base + 8, 2 * hidden), BF)
    return call(
        feed_kernel,
        [
            struct((rows, width), BF),
            struct((rows, width), F32),
            struct((rows, width), BF),
            struct((rows, width), BF),
            grads,
            grads,
        ],
        [info, mixed, first, cot, vecs, wo] + list(expand) + list(shrink),
        [SM, VM, VM, VM, VM] + [ANY] * 11,
        [VM] * 4 + [ANY] * 2,
        [
            pltpu.VMEM((16, width), F32),
            pltpu.VMEM((4, outer, 8, 2 * hidden), BF),
            pltpu.VMEM((width, width), BF),
            pltpu.VMEM((4, outer, 2, depth, hidden), BF),
            pltpu.VMEM((4, outer, 2, depth, hidden), BF),
            pltpu.VMEM((4, rows, hidden), BF),
            pltpu.VMEM((4, rows, hidden), BF),
            pltpu.VMEM((2, outer, 2, base, hidden), BF),
            pltpu.VMEM((2, outer, 2, base, hidden), BF),
            pltpu.VMEM((rows, width), F32),
            pltpu.VMEM((rows, width), BF),
            pltpu.VMEM((rows, width), BF),
            pltpu.VMEM((rows, width), F32),
            pltpu.SemaphoreType.DMA((13,)),
            pltpu.SemaphoreType.DMA((2, 2, 2)),
            pltpu.SemaphoreType.DMA((8,)),
        ],
        flops=2 * rows * width * (6 * 4 * hidden + 2 * width) * 2,
        moved=width * hidden * 4 * 4 * 2,
        name="feed",
    )


def first_back_kernel(
    dq_ref, q_mat, second_ref, resid_ref, vec_ref, o_mat, first_ref, low_ref, keep_ref, send_ref, sums_ref
):
    grad = second_ref[...] + mm(dq_ref[...], q_mat[...], NT)
    normed, rstd = norm_parts(resid_ref[...])
    sums_ref[0:1, :] = jnp.sum(grad, 0, keepdims=True)
    sums_ref[1:2, :] = jnp.sum(grad * normed, 0, keepdims=True)
    first_in = norm_back(normed, rstd, grad, vec_ref[0:1, :])
    first_ref[...] = first_in
    low = first_in.astype(BF)
    low_ref[...] = low
    sums_ref[2:3, :] = jnp.sum(low.astype(F32), 0, keepdims=True)
    sums_ref[3:4, :] = jnp.sum(dq_ref[...].astype(F32), 0, keepdims=True)
    sums_ref[4:8, :] = jnp.zeros((4, sums_ref.shape[1]), F32)
    mixed_grad = mm(low, o_mat[...]).astype(BF)
    cols = keep_ref.shape[1]
    keep_ref[...] = mixed_grad[:, :cols]
    send_ref[...] = mixed_grad[:, cols:]


def first_back(dq, q_mat, second_in, resid, vec, o_mat):
    rows, width = dq.shape
    cols = width // 2
    return call(
        first_back_kernel,
        [
            struct((rows, width), F32),
            struct((rows, width), BF),
            struct((rows, cols), BF),
            struct((rows, cols), BF),
            struct((8, width), F32),
        ],
        [dq, q_mat, second_in, resid, vec, o_mat],
        [VM] * 6,
        [VM] * 5,
        flops=2 * rows * width * width * 2 * 2,
        moved=width * width * 4 + rows * width * 18,
        name="first_back",
    )


def put_rows(ref, x, full, at, place):
    outer = ref.shape[2]
    depth = full.shape[0] // outer // 2
    for o in range(outer):
        for y in range(2):
            start = (2 * o + y) * depth
            ref[x, y ^ place, o, :depth, at] = full[start : start + depth]


def put_blocks(keep_ref, send_ref, full, i, place):
    piece = full.shape[1] // 4
    at = slice(i * piece, (i + 1) * piece)
    for j in range(4):
        put_rows((keep_ref, send_ref)[j // 2], j % 2, full[:, j * piece : (j + 1) * piece], at, place)


def query_grads_kernel(
    info, h1_ref, dq_ref, e1_ref, o1_ref, e2_ref, o2_ref, sums_ref, keep_ref, send_ref
):
    width = dq_ref.shape[1]
    piece = width // 4
    outer, rows = keep_ref.shape[2], keep_ref.shape[3]
    parts = [high_low(sums_ref[i : i + 1, :]) for i in range(4)]
    for j in range(4):
        own = slice(j * piece, (j + 1) * piece)
        ref = (keep_ref, send_ref)[j // 2]
        for i in range(3):
            lines = [parts[i][0][:, p * piece : (p + 1) * piece] for p in range(4)]
            lines += [parts[i][1][:, p * piece : (p + 1) * piece] for p in range(4)]
            if i == 0:
                lines += [parts[3][0][:, own], parts[3][1][:, own]]
            block = stack_rows(lines, 16)
            for o in range(outer):
                for y in range(2):
                    ref[j % 2, y, o, rows - 16 :, i * piece : (i + 1) * piece] = block
    for i, (left, right) in enumerate(((h1_ref, dq_ref), (e1_ref, o1_ref), (e2_ref, o2_ref))):
        full = mm(left[...], right[...], TN).astype(BF)
        put_blocks(keep_ref, send_ref, full, i, info[0])


def key_grads_kernel(info, fet_ref, own_ref, got_ref, mat_ref, keep_ref, send_ref, grad_ref):
    width = fet_ref.shape[1]
    piece = width // 4
    outer, rows = keep_ref.shape[2], keep_ref.shape[3]
    total = None
    for i in range(2):
        low = add_low(own_ref[i], got_ref[i])
        full = mm(fet_ref[...], low, TN).astype(BF)
        put_blocks(keep_ref, send_ref, full, i, info[0])
        term = mm(low, mat_ref[:, i * width : (i + 1) * width], NT)
        total = term if total is None else total + term
        if i == 1:
            sums = high_low(jnp.sum(low.astype(F32), 0, keepdims=True))
            for j in range(4):
                own = slice(j * piece, (j + 1) * piece)
                block = stack_rows([sums[0][:, own], sums[1][:, own]], 8)
                ref = (keep_ref, send_ref)[j // 2]
                for o in range(outer):
                    for y in range(2):
                        ref[j % 2, y, o, rows - 8 :, piece:] = block
                        ref[j % 2, y, o, rows - 8 :, :piece] = jnp.zeros_like(block)
    grad_ref[...] = total.astype(BF)


def query_grads(info, args, depth):
    width = args[0].shape[1]
    out = struct((2, 2, width // depth // 2, tail_start(depth) + 16, 3 * width // 4), BF)
    return call(
        query_grads_kernel,
        [out, out],
        [info] + list(args),
        [SM] + [VM] * 7,
        [VM] * 2,
        flops=2 * 512 * width * width * 3,
        moved=width * width * 10,
        name="query_grads",
    )


def key_grads(info, fetched, own, got, mat, depth):
    rows, width = fetched.shape
    out = struct((2, 2, width // depth // 2, tail_start(depth) + 8, 2 * width // 4), BF)
    return call(
        key_grads_kernel,
        [out, out, struct((rows, width), BF)],
        [info, fetched, own, got, mat],
        [SM] + [VM] * 4,
        [VM] * 3,
        flops=2 * rows * width * width * 4,
        moved=width * width * 10,
        name="key_grads",
    )


def self_grads_kernel(info, own_ref, oth_ref, d_ref, a_ref, x_ref, y_ref, xy_ref):
    place = info[0]
    cols = d_ref.shape[3]
    piece = cols // 2
    outer, base = a_ref.shape[0], a_ref.shape[1] - 8
    depth = own_ref.shape[1] // outer // 2
    for i in range(3):
        full = mm(own_ref[...], d_ref[i, 0], TN) + mm(oth_ref[...], d_ref[i, 1], TN)
        full = full.astype(BF)
        at = slice(i * piece, (i + 1) * piece)
        both = d_ref[i, 0].astype(F32) + d_ref[i, 1].astype(F32)
        sums = jnp.sum(both, 0, keepdims=True)
        high = sums.astype(BF).astype(F32)
        row = lax.broadcasted_iota(jnp.int32, (8, cols), 0)
        tail = jnp.where(row == 0, high, jnp.where(row == 1, sums - high, 0.0)).astype(BF)
        for x, (near, away) in enumerate(((a_ref, y_ref), (x_ref, xy_ref))):
            part = slice(x * piece, (x + 1) * piece)
            for o in range(outer):
                start = 2 * o * depth
                first = full[start : start + depth, part]
                second = full[start + depth : start + 2 * depth, part]
                near[o, :depth, at] = jnp.where(place == 0, first, second)
                away[o, :depth, at] = jnp.where(place == 0, second, first)
                near[o, base:, at] = tail[:, part]
                away[o, base:, at] = tail[:, part]


def self_grads(info, own, oth, grads, depth):
    half, width = own.shape
    cols = grads.shape[3]
    out = struct((width // depth // 2, tail_start(depth) + 8, 3 * cols // 2), BF)
    return call(
        self_grads_kernel,
        [out] * 4,
        [info, own, oth, grads],
        [SM] + [VM] * 3,
        [VM] * 4,
        name="self_grads",
    )


def self_back_kernel(d_ref, mat_ref, first_ref, keep_ref, send_ref):
    cols = d_ref.shape[3]
    for rel in (1, 0):
        total = mm(d_ref[0, rel], mat_ref[:, :cols], NT)
        for i in (1, 2):
            total = total + mm(d_ref[i, rel], mat_ref[:, i * cols : (i + 1) * cols], NT)
        if rel == 1:
            send_ref[...] = total.astype(BF)
        else:
            keep_ref[...] = total + first_ref[...]


def self_back(grads, mat, first_in):
    half, width = first_in.shape
    cols = grads.shape[3]
    return call(
        self_back_kernel,
        [struct((half, width), F32), struct((half, width), BF)],
        [grads, mat, first_in],
        [VM] * 3,
        [VM] * 2,
        flops=2 * 2 * half * width * 3 * cols * 2,
        moved=half * width * 10 + half * cols * 12 + width * cols * 6,
        name="self_back",
    )


def fetch_kernel(table, bank_ref, mine_ref, send_ref, sem):
    count = table.shape[0] // 2

    def each(act):
        for group, out_ref in enumerate((mine_ref, send_ref)):

            def body(i, carry, group=group, out_ref=out_ref):
                at = table[group * count + i]
                copy = pltpu.make_async_copy(
                    bank_ref.at[jnp.maximum(at, 0)], out_ref.at[i], sem.at[group * count + i]
                )
                act(copy, at >= 0, out_ref, i)
                return carry

            lax.fori_loop(0, count, body, 0)

    def start(copy, held, out_ref, i):
        @pl.when(held)
        def _():
            copy.start()

        @pl.when(jnp.logical_not(held))
        def _():
            out_ref[i] = jnp.zeros(out_ref.shape[1:], out_ref.dtype)

    def finish(copy, held, out_ref, i):
        @pl.when(held)
        def _():
            copy.wait()

    each(start)
    each(finish)


def fetch(table, bank_blocks):
    count = table.shape[0]
    blk, width = bank_blocks.shape[1:]
    out = struct((count // 2, blk, width), BF)
    mine, send = call(
        fetch_kernel,
        [out, out],
        [table, bank_blocks],
        [SM, ANY],
        [VM, VM],
        [pltpu.SemaphoreType.DMA((count,))],
        moved=count * blk * width * 4,
        name="fetch",
    )
    return [part.reshape(2, count // 4, blk, width) for part in (mine, send)]


def scatter_kernel(table, a_ref, b_ref, c_ref, d_ref, out_ref, slots, sems):
    step = pl.program_id(0)
    per = out_ref.shape[0]

    @pl.when(step == 0)
    def _():
        copies = [
            pltpu.make_async_copy(ref, slots.at[i], sems.at[i])
            for i, ref in enumerate((a_ref, b_ref, c_ref, d_ref))
        ]
        for copy in copies:
            copy.start()
        for copy in copies:
            copy.wait()

    for i in range(per):
        at = table[step * per + i]
        group = jnp.maximum(at, 0) // slots.shape[1]
        place = jnp.maximum(at, 0) % slots.shape[1]
        value = slots[group, place].astype(F32)
        out_ref[i] = jnp.where(at >= 0, value, 0.0)


def scatter(table, parts):
    count = table.shape[0]
    slots, blk, width = parts[0].shape
    per = 4
    return pl.pallas_call(
        scatter_kernel,
        grid_spec=pltpu.PrefetchScalarGridSpec(
            num_scalar_prefetch=1,
            grid=(count // per,),
            in_specs=[ANY] * 4,
            out_specs=pl.BlockSpec((per, blk, width), lambda i, t: (i, 0, 0)),
            scratch_shapes=[
                pltpu.VMEM((4, slots, blk, width), BF),
                pltpu.SemaphoreType.DMA((4,)),
            ],
        ),
        out_shape=struct((count, blk, width), F32),
        compiler_params=pltpu.CompilerParams(vmem_limit_bytes=VMEM_LIMIT),
        cost_estimate=COST,
        name="scatter",
    )(table, *parts)


def sum_all(ref):
    total = ref[0].astype(F32)
    for i in range(1, ref.shape[0]):
        total = total + ref[i].astype(F32)
    return total


def sum_query_kernel(in_ref, q_ref, so_ref, co_ref, qb_ref, v0_ref, v1_ref, v2_ref):
    total = sum_all(in_ref)
    piece = total.shape[1] // 3
    depth = q_ref.shape[0]
    q_ref[...] = total[:depth, :piece]
    so_ref[...] = total[:depth, piece : 2 * piece].T
    co_ref[...] = total[:depth, 2 * piece :].T
    tail = total[total.shape[0] - 16 :]
    qb_ref[...] = (tail[8:9, :piece] + tail[9:10, :piece])[0]
    for i, ref in enumerate((v0_ref, v1_ref, v2_ref)):
        cols = slice(i * piece, (i + 1) * piece)
        parts = [tail[p : p + 1, cols] + tail[p + 4 : p + 5, cols] for p in range(4)]
        ref[...] = jnp.concatenate(parts, axis=1)[0]


def sum_query(value, depth):
    count, rows, cols = value.shape
    piece = cols // 3
    wide, tall = struct((depth, piece), F32), struct((piece, depth), F32)
    vec = struct((4 * piece,), F32)
    return call(
        sum_query_kernel,
        [wide, tall, tall, struct((piece,), F32), vec, vec, vec],
        [value],
        [VM],
        [VM] * 7,
        name="sum_query",
    )


def sum_cols_kernel(in_ref, *refs):
    count = len(refs) // 2
    total = sum_all(in_ref)
    depth, piece = refs[0].shape
    tail = total[total.shape[0] - 8 :]
    for i in range(count):
        cols = slice(i * piece, (i + 1) * piece)
        refs[i][...] = total[:depth, cols]
        refs[count + i][...] = (tail[0:1, cols] + tail[1:2, cols])[0]


def sum_cols(value, depth, count):
    piece = value.shape[2] // count
    return call(
        sum_cols_kernel,
        [struct((depth, piece), F32)] * count + [struct((piece,), F32)] * count,
        [value],
        [VM],
        [VM] * (2 * count),
        name="sum_cols",
    )


def sum_feed_kernel(in_ref, e_ref, s_ref, eb_ref, *vecs):
    total = sum_all(in_ref)
    depth, cols = e_ref.shape
    e_ref[...] = total[:depth, :cols]
    s_ref[...] = total[:depth, cols:]
    tail = total[total.shape[0] - 8 :]
    eb_ref[...] = (tail[0:1, :cols] + tail[1:2, :cols])[0]
    for i in range(3):
        at = 2 + 2 * i
        vecs[i][...] = (tail[at : at + 1, :cols] + tail[at + 1 : at + 2, :cols])[0]
        at = 2 * i
        vecs[3 + i][...] = (tail[at : at + 1, cols:] + tail[at + 1 : at + 2, cols:])[0]


def sum_feed(value, depth):
    cols = value.shape[2] // 2
    return call(
        sum_feed_kernel,
        [struct((depth, cols), F32)] * 2 + [struct((cols,), F32)] * 7,
        [value],
        [VM],
        [VM] * 9,
        name="sum_feed",
    )


def local(
    tokens,
    bank,
    prefix,
    blocks,
    out_grad,
    selfq_weight,
    selfq_bias,
    selfk_weight,
    selfv_weight,
    selfv_bias,
    selfo_weight,
    selfo_bias,
    first_gain,
    first_shift,
    crossq_weight,
    crossq_bias,
    crossk_weight,
    crossv_weight,
    crossv_bias,
    crosso_weight,
    crosso_bias,
    second_gain,
    second_shift,
    expand_weight,
    expand_bias,
    shrink_weight,
    shrink_bias,
    third_gain,
    third_shift,
):
    rank = lax.axis_index("tensor")
    core = rank % 2
    chip = rank // 2
    inner = lax.axis_index("dp") % 2
    outer = outer_count()
    half, width = tokens.shape
    seq_count = prefix.shape[0]
    local_blocks = bank.shape[1] // BLK
    head_cols = selfq_bias.shape[0]
    hidden_cols = expand_bias.shape[0]
    depth = selfq_weight.shape[0]
    slots = NBLK // 2
    two = 2 * head_cols
    attn_cols = 5 * head_cols
    info = jnp.stack([inner, rank, chip]).astype(jnp.int32)

    seq_order = jnp.stack([chip, 1 - chip])
    near = blocks[seq_order].reshape(2, 2, slots)
    near = jnp.stack([near[:, core], near[:, 1 - core]])
    near = near - rank * local_blocks
    held = (near >= 0) & (near < local_blocks)
    fetch_table = jnp.where(held, near + seq_order[None, :, None] * local_blocks, -1)
    fetch_table = fetch_table.reshape(-1).astype(jnp.int32)
    part_mine, part_send = fetch(fetch_table, bank.reshape(seq_count * local_blocks, BLK, width))

    part_got = swap_core(part_send)
    part_away = part_mine[1] + part_got[1]
    part_back = swap_x(part_away)

    self_leaf = call(
        pack_self_kernel,
        struct((outer, depth, 3 * head_cols), BF),
        [gate(selfq_weight, part_send), selfk_weight, selfv_weight],
        [VM] * 3,
        VM,
        name="pack_self",
    )
    bias_own = jnp.concatenate(
        [selfq_bias, selfv_bias, crossq_bias, crossv_bias, expand_bias]
    ).reshape(1, -1)
    bias_two = jnp.concatenate([bias_own, swap_x(bias_own)], axis=0)
    bias_four = jnp.concatenate([bias_two, swap_core(bias_two)], axis=0)
    cq_bias = bias_four[:, two : 3 * head_cols].reshape(-1)
    cv_bias = bias_four[:, 3 * head_cols : 4 * head_cols].reshape(-1)
    ex_bias = bias_four[:, 4 * head_cols :]
    self_bias = jnp.stack(
        [
            bias_two[:, :head_cols].reshape(-1),
            jnp.zeros((two,), F32),
            bias_two[:, head_cols:two].reshape(-1),
        ]
    )
    next_leaf, shrink_leaf = call(
        pack_rest_kernel,
        [
            struct((outer, depth, hidden_cols + attn_cols), BF),
            struct((depth, hidden_cols), BF),
        ],
        [
            gate(crossk_weight, self_leaf, part_away), crossv_weight, crossq_weight, selfo_weight,
            crosso_weight, expand_weight, shrink_weight.T,
        ],
        [VM] * 7,
        [VM] * 2,
        name="pack_rest",
    )
    tokens_oth = swap_core(tokens)
    vecs = jnp.concatenate(
        [
            jnp.stack([crosso_bias, second_gain, second_shift]),
            ex_bias,
            jnp.stack([shrink_bias, third_gain, third_shift]),
        ]
    )
    first_vecs = jnp.stack([selfo_bias, first_gain, first_shift])
    cq_bias, cv_bias = cq_bias.reshape(1, -1), cv_bias.reshape(1, -1)
    my_prefix = lax.dynamic_index_in_dim(prefix, chip, 0, keepdims=False)
    attn_info = jnp.stack([core, my_prefix]).astype(jnp.int32)

    self_z = outer_exchange(self_leaf)

    self_z, self_bias, vecs, first_vecs, cq_bias, cv_bias, next_leaf, attn_info, tokens_oth, part_back = (
        lax.optimization_barrier(
            (self_z, self_bias, vecs, first_vecs, cq_bias, cv_bias, next_leaf, attn_info, tokens_oth, part_back)
        )
    )
    self_near, self_away, self_both = swap_x(self_z), swap_dp(self_z, 1), swap_both(self_z)
    next_z = outer_exchange(next_leaf)

    shrink_leaf = gate(shrink_leaf, self_near)
    shrink_x, shrink_y = swap_x(shrink_leaf), swap_dp(shrink_leaf, 1)
    shrink_xy = swap_both(shrink_leaf)
    shrink_pack = plane_copies(info, shrink_leaf, shrink_x, shrink_y, shrink_xy)
    (
        next_z, tokens_in, self_near, self_away, self_both, shrink_pack, part_got,
    ) = lax.optimization_barrier(
        (next_z, tokens, self_near, self_away, self_both, shrink_pack, part_got)
    )
    expand_z, attn_z = next_z[..., :hidden_cols], next_z[..., hidden_cols:]
    shrink_z = outer_exchange(gate(shrink_pack, next_z))
    attn_x, attn_y, attn_xy = swap_x(attn_z), swap_dp(attn_z, 1), swap_both(attn_z)

    qkv, self_mat, self_own, self_send, self_lse = self_forward(
        jnp.concatenate([info, attn_info]),
        tokens_in,
        tokens_oth,
        self_bias,
        (self_z, self_near, self_away, self_both),
    )
    self_got = swap_core(self_send)
    attn_x, attn_y, attn_xy, self_got = lax.optimization_barrier(
        (attn_x, attn_y, attn_xy, self_got, self_own)
    )[:4]
    attn_own = (attn_z, attn_y, attn_x, attn_xy)
    attn_oth = tuple(swap_core(piece) for piece in attn_own)
    attn_oth, expand_z = lax.optimization_barrier((attn_oth, expand_z))
    expand_x, expand_y = swap_x(expand_z), swap_dp(expand_z, 1)
    cross_kv, cross_q, self_o, cross_o = assemble(info, attn_own + attn_oth)
    cross_kv, expand_x, expand_y = lax.optimization_barrier((cross_kv, expand_x, expand_y))
    expand_xy = swap_both(expand_z)
    fetched, kv_own = project_kv(
        (part_mine[0] + part_got[0]).reshape(slots * BLK, width),
        part_back.reshape(slots * BLK, width),
        cross_kv,
        cv_bias,
    )
    self_got, kv_own = lax.optimization_barrier((self_got, kv_own))
    kv_oth = swap_core(kv_own)
    first_sum, first_out, first_low, queries, mixed_one = first_forward(
        tokens,
        self_own,
        self_got,
        self_o,
        first_vecs,
        cross_q,
        cq_bias,
    )

    queries, kv_oth = lax.optimization_barrier((queries, kv_oth))
    queries, shrink_z = lax.optimization_barrier((queries, shrink_z))
    mixed_two, cross_lse = cross_forward(queries, kv_own, kv_oth)

    expand_oth = tuple(swap_core(piece) for piece in (expand_z, expand_y, expand_x))
    expand_xy, expand_oth, mixed_two = lax.optimization_barrier((expand_xy, expand_oth, mixed_two))
    expand_own = (expand_z, expand_y, expand_x, expand_xy)
    expand_oth = expand_oth + (swap_core(expand_xy),)
    (
        out_act, second_in, cross_low, cross_grad,
        feed_keep, feed_send,
    ) = feed(
        info, mixed_two, first_out, out_grad, vecs, cross_o,
        expand_own + expand_oth, (shrink_z, swap_core(shrink_z)),
    )

    def plane_send(keep, got):
        return tuple(add_low(keep[x, y], got[x, y]) for x, y in ((1, 0), (0, 1), (1, 1)))

    def plane_swap(parts):
        return swap_x(parts[0]), swap_dp(parts[1], 1), swap_both(parts[2])

    def plane_sum(own, got):
        total = sum(part.astype(F32) for part in own)
        return total + sum(part.astype(F32) for part in got)

    def fold(value, dtype):
        return jnp.sum(value.astype(F32), axis=0).astype(dtype)

    feed_got = swap_core(feed_send)
    part_one = cross_backward(queries, kv_own, kv_oth, mixed_two, cross_lse, cross_grad, 0, 2)
    feed_keep = gate(feed_keep, part_one[0])

    def feed_sum(x, y, which, *others):
        at = (x, y, Ellipsis, slice(which * hidden_cols, (which + 1) * hidden_cols))
        total = feed_keep[at].astype(F32) + feed_got[at].astype(F32)
        for other in others:
            total = total + other.astype(F32)
        return total.astype(BF)

    expand_send = feed_sum(1, slice(None), 0)
    shrink_send = feed_sum(slice(None), 1, 1)
    expand_send, shrink_send, part_one = lax.optimization_barrier(
        (expand_send, shrink_send, tuple(part_one))
    )
    expand_got = swap_x(expand_send)
    shrink_got = swap_dp(shrink_send, 1)

    dq, dkv_own, dkv_send, first_in, self_low, grad_own, grad_send, early_vec = cross_first_backward(
        queries, kv_own, kv_oth, mixed_two, cross_lse, cross_grad, 2, part_one,
        cross_q, second_in, first_sum, first_gain.reshape(1, -1), self_o,
    )
    expand_got, shrink_got, dkv_send, grad_send = lax.optimization_barrier(
        (expand_got, shrink_got, dkv_send, grad_send)
    )
    dkv_got = swap_core(dkv_send)
    grad_got = swap_core(grad_send)
    expand_send = feed_sum(0, 1, 0, expand_got[1])
    shrink_send = feed_sum(1, 0, 1, shrink_got[1])
    self_low, dkv_got, grad_got, expand_send, shrink_send = lax.optimization_barrier(
        (self_low, dkv_got, grad_got, expand_send, shrink_send)
    )
    expand_last = swap_dp(expand_send, 1)
    shrink_last = swap_x(shrink_send)
    query_keep, query_send = query_grads(
        info, (first_low, dq, self_low, mixed_one, cross_low, mixed_two, early_vec), depth
    )
    dkv_own, query_send = lax.optimization_barrier((dkv_own, query_send))
    query_got = swap_core(query_send)
    key_keep, key_send, fetched_grad = key_grads(
        info, fetched, dkv_own, dkv_got, cross_kv, depth
    )
    query_plane = plane_send(gate(query_keep, fetched_grad), query_got)
    query_plane, key_send, grad_got, fetched_grad, expand_last, shrink_last = (
        lax.optimization_barrier(
            (query_plane, key_send, grad_got, fetched_grad, expand_last, shrink_last)
        )
    )
    query_parts = plane_swap(query_plane)
    key_got = swap_core(key_send)

    self_args = (attn_info, qkv, self_own, self_send, self_lse, grad_own, grad_got)
    pairs = two // 128
    half_grads = self_backward(*self_args, 0, pairs - 1)
    key_plane = plane_send(gate(key_keep, half_grads[1]), key_got)
    feed_three = jnp.concatenate(
        [
            feed_sum(0, 0, 0, expand_got[0], gate(expand_last, half_grads[1])),
            feed_sum(0, 0, 1, shrink_got[0], gate(shrink_last, half_grads[1])),
        ],
        axis=-1,
    )
    query_three = plane_sum((query_keep[0, 0], query_got[0, 0]), query_parts).astype(BF)
    key_plane, half_grads, feed_three, query_three = lax.optimization_barrier(
        (key_plane, tuple(half_grads), feed_three, query_three)
    )
    key_parts = plane_swap(key_plane)
    feed_last = outer_exchange(feed_three)
    grads, self_rows = self_backward(*self_args, pairs - 1, 1, half_grads)
    grads, key_parts = lax.optimization_barrier((grads, key_parts))
    self_places = self_grads(info, tokens, tokens_oth, grads, depth)
    self_places, grads = lax.optimization_barrier((tuple(self_places), grads))
    self_parts = (swap_x(self_places[1]), swap_dp(self_places[2], 1), swap_both(self_places[3]))
    grads, feed_last, query_three = lax.optimization_barrier((grads, feed_last, query_three))
    query_last = outer_exchange(query_three)
    back_keep, back_send = self_back(grads, self_mat, first_in)
    back_send, query_last, key_parts, self_near, self_away = lax.optimization_barrier(
        (back_send, query_last, key_parts, self_parts[0], self_parts[1])
    )
    key_three = plane_sum((key_keep[0, 0], key_got[0, 0]), key_parts).astype(BF)
    back_got = swap_core(back_send)
    self_three = plane_sum((self_places[0],), (self_near, self_away, self_parts[2])).astype(BF)
    self_last = outer_exchange(
        gate(jnp.concatenate([self_three, key_three], axis=-1), query_last)
    )
    fetched_send = gate(fetched_grad, self_three)
    fetched_away = swap_x(fetched_send).reshape(slots, BLK, width)
    fetched_near = fetched_send.reshape(slots, BLK, width)
    in_grad = (back_keep + back_got.astype(F32)).astype(BF)

    cq_grad, so_grad, co_grad, cq_rows, first_shift_rows, first_gain_rows, so_rows = sum_query(
        query_last, depth
    )
    (
        sq_grad, sk_grad, sv_grad, ck_grad, cv_grad, sq_rows, sk_rows, sv_rows, ck_rows, cv_rows,
    ) = sum_cols(self_last, depth, 5)
    (
        expand_grad, shrink_grad, expand_rows, third_shift_rows, third_gain_rows, shrink_rows,
        second_shift_rows, second_gain_rows, co_rows,
    ) = sum_feed(feed_last, depth)
    shrink_grad = shrink_grad.T

    near_core = swap_core(fetched_near)
    away_core = swap_core(fetched_away)
    slot_ids = jnp.arange(NBLK)
    places = (
        (((slot_ids[None, :] // slots) != core) * 2 + (jnp.arange(seq_count)[:, None] != chip))
        * slots
        + slot_ids[None, :] % slots
    )
    hits = blocks[:, None, :] == (rank * local_blocks + jnp.arange(local_blocks))[None, :, None]
    scatter_table = jnp.max(jnp.where(hits, places[:, None, :], -1), axis=-1)
    bank_grad = scatter(
        scatter_table.reshape(-1).astype(jnp.int32),
        (fetched_near, fetched_away, near_core, away_core),
    ).reshape(bank.shape)

    def line(row):
        return row.reshape(-1)

    return (
        out_act,
        in_grad,
        bank_grad,
        sq_grad,
        line(sq_rows),
        sk_grad,
        sv_grad,
        line(sv_rows),
        so_grad,
        line(so_rows),
        line(first_gain_rows),
        line(first_shift_rows),
        cq_grad,
        line(cq_rows),
        ck_grad,
        cv_grad,
        line(cv_rows),
        co_grad,
        line(co_rows),
        line(second_gain_rows),
        line(second_shift_rows),
        expand_grad,
        line(expand_rows),
        shrink_grad,
        line(shrink_rows),
        line(third_gain_rows),
        line(third_shift_rows),
    )


def solution(mesh):
    rows = P(("dp", "tensor"), None)
    wide = P("dp", "tensor")
    tall = P("tensor", "dp")
    part = P("tensor")
    full = P()
    return jax.shard_map(
        local,
        mesh=mesh,
        in_specs=(
            rows, P("dp", "tensor", None), P("dp"), P("dp", None), rows,
            wide, part, wide, wide, part, tall, full, full, full,
            wide, part, wide, wide, part, tall, full, full, full,
            wide, part, tall, full, full, full,
        ),
        out_specs=(
            rows, rows, P("dp", "tensor", None),
            wide, part, wide, wide, part, tall, full, full, full,
            wide, part, wide, wide, part, tall, full, full, full,
            wide, part, tall, full, full, full,
        ),
        check_vma=False,
    )
```

```python
import functools
import math

import jax
import jax.numpy as jnp
from jax import lax
from jax.experimental import pallas as pl
from jax.experimental.pallas import tpu as pltpu
from jax.sharding import PartitionSpec as P

HD = 64
BLK = 64
NBLK = 16
EPS = 1e-05
NEGATIVE = -1e30
BF = jnp.bfloat16
F32 = jnp.float32

NT = (((1,), (1,)), ((), ()))
NN = (((1,), (0,)), ((), ()))
TN = (((0,), (0,)), ((), ()))

CORE_SWAP = ((0, 1), (1, 0), (2, 3), (3, 2))
X_SWAP = ((0, 2), (2, 0), (1, 3), (3, 1))
VMEM_LIMIT = 48 << 20
COST = pl.CostEstimate(flops=1000, bytes_accessed=1000, transcendentals=0)


def mm(left, right, dims=NN):
    return lax.dot_general(left, right, dims, preferred_element_type=F32)


def swap_core(value):
    return lax.ppermute(value, "tensor", CORE_SWAP)


def swap_x(value):
    return lax.ppermute(value, "tensor", X_SWAP)


def swap_dp(value, bit):
    count = lax.axis_size("dp")
    return lax.ppermute(value, "dp", tuple((i, i ^ bit) for i in range(count)))


def dp_bits():
    count = lax.axis_size("dp")
    bits = []
    bit = count // 2
    while bit >= 1:
        bits.append(bit)
        bit //= 2
    return bits


def pair_backward(q, k, v, grad, lse, delta, mask):
    score = mm(k, q, NT)
    prob = jnp.exp(score - lse)
    if mask is not None:
        prob = jnp.where(mask, prob, 0.0)
    slope = prob * (mm(v, grad, NT) - delta)
    prob = prob.astype(BF)
    slope = slope.astype(BF)
    return mm(k, slope, TN), mm(slope, q, NN), mm(prob, grad, NN)


def delta_row(grad, mixed):
    return jnp.sum((grad.astype(F32) * mixed.astype(F32)).T, 0, keepdims=True)


def self_bwd_kernel(info, q_ref, k_ref, v_ref, oa_ref, ob_ref, lse_ref, ga_ref, gb_ref, *rest):
    out_ref, o_ref, g_ref = rest[-3:]
    dq_ref, dk_ref, dv_ref = out_ref.at[0], out_ref.at[1], out_ref.at[2]
    o_ref[0], o_ref[1] = oa_ref[...], ob_ref[...]
    g_ref[0], g_ref[1] = ga_ref[...], gb_ref[...]
    half = q_ref.shape[1]
    first = info[0]
    second = 1 - first
    prefix = info[1]
    def positions(rows):
        shape = (rows, half)
        return lax.broadcasted_iota(jnp.int32, shape, 0), lax.broadcasted_iota(jnp.int32, shape, 1)

    key_pos, query_pos = positions(half)
    seen = (key_pos <= query_pos) | (key_pos < prefix)
    key_pos, query_pos = positions(2 * half)
    seen_late = key_pos <= query_pos + half
    scale = 1.0 / math.sqrt(HD)
    for h in range(2):
        cols = slice(HD * h, HD * h + HD)

        def rows(ref, at):
            return ref[at, :, cols]

        def both(ref):
            return jnp.concatenate([rows(ref, first), rows(ref, second)], axis=0)

        def one(at, key, value, mask):
            grad = rows(g_ref, at)
            delta = delta_row(grad, rows(o_ref, at))
            lse = lse_ref[0, h, pl.ds(at, 1), :]
            dq, dk, dv = pair_backward(rows(q_ref, at), key, value, grad, lse, delta, mask)
            dq_ref[at, :, cols] = (dq.T.astype(BF) * scale).astype(BF)
            return dk, dv

        dk_a, dv_a = one(first, rows(k_ref, first), rows(v_ref, first), seen)
        dk_b, dv_b = one(second, both(k_ref), both(v_ref), seen_late)
        dk_ref[first, :, cols] = (dk_a + dk_b[:half]).astype(BF)
        dv_ref[first, :, cols] = (dv_a + dv_b[:half]).astype(BF)
        dk_ref[second, :, cols] = dk_b[half:].astype(BF)
        dv_ref[second, :, cols] = dv_b[half:].astype(BF)


def self_backward(info, qkv, mixed_own, mixed_oth, lse, grad_own, grad_oth, start, count, former=()):
    half, width = qkv.shape[1], qkv.shape[2] // 3
    pairs = width // 128

    def spec(which):
        return pl.BlockSpec((2, half, 128), lambda i, info: (0, 0, which * pairs + start + i))

    flat = pl.BlockSpec((half, 128), lambda i, info: (0, start + i))
    cells = 3 * half * half * count * 2
    return pl.pallas_call(
        self_bwd_kernel,
        grid_spec=pltpu.PrefetchScalarGridSpec(
            num_scalar_prefetch=1,
            grid=(count,),
            in_specs=[
                spec(0),
                spec(1),
                spec(2),
                flat,
                flat,
                pl.BlockSpec((1, 2, 2, half), lambda i, info: (start + i, 0, 0, 0)),
                flat,
                flat,
            ]
            + [pl.BlockSpec(memory_space=pl.ANY)] * len(former),
            out_specs=pl.BlockSpec((3, 2, half, 128), lambda i, info: (0, 0, 0, start + i)),
            scratch_shapes=[pltpu.VMEM((2, half, 128), BF)] * 2,
        ),
        out_shape=jax.ShapeDtypeStruct((3, 2, half, width), BF),
        input_output_aliases={9 + i: i for i in range(len(former))},
        compiler_params=pltpu.CompilerParams(vmem_limit_bytes=VMEM_LIMIT),
        cost_estimate=COST,
        name="self_bwd",
    )(info, qkv, qkv, qkv, mixed_own, mixed_oth, lse, grad_own, grad_oth, *former)


def cross_fwd_kernel(q_ref, ka_ref, kb_ref, va_ref, vb_ref, o_ref, lse_ref):
    for h in range(2):
        cols = slice(HD * h, HD * h + HD)
        q = q_ref[:, cols]
        score_a = mm(ka_ref[:, cols], q, NT)
        score_b = mm(kb_ref[:, cols], q, NT)
        top = jnp.maximum(
            jnp.max(score_a, 0, keepdims=True), jnp.max(score_b, 0, keepdims=True)
        )
        expo_a = jnp.exp(score_a - top)
        expo_b = jnp.exp(score_b - top)
        total = jnp.sum(expo_a, 0, keepdims=True) + jnp.sum(expo_b, 0, keepdims=True)
        mixed = (
            mm(va_ref[:, cols], expo_a.astype(BF), TN) + mm(vb_ref[:, cols], expo_b.astype(BF), TN)
        ) / total
        o_ref[:, cols] = mixed.T.astype(BF)
        lse_ref[0, h : h + 1, :] = top + jnp.log(total)


def cross_specs(rows, pairs):
    whole = pl.BlockSpec((rows, 128), lambda i: (0, i))
    turned = pl.BlockSpec((rows, 128), lambda i: (0, (i + pairs // 2) % pairs))
    value = pl.BlockSpec((rows, 128), lambda i: (0, pairs + i))
    value_turned = pl.BlockSpec((rows, 128), lambda i: (0, pairs + (i + pairs // 2) % pairs))
    return whole, turned, value, value_turned


def cross_forward(queries, kv_own, kv_oth):
    rows, width = queries.shape
    pairs = width // 128
    whole, turned, value, value_turned = cross_specs(rows, pairs)
    cells = 2 * rows * rows * pairs * 2
    return pl.pallas_call(
        cross_fwd_kernel,
        grid=(pairs,),
        in_specs=[whole, whole, turned, value, value_turned],
        out_specs=[whole, pl.BlockSpec((1, 2, rows), lambda i: (i, 0, 0))],
        out_shape=[
            jax.ShapeDtypeStruct((rows, width), BF),
            jax.ShapeDtypeStruct((pairs, 2, rows), F32),
        ],
        compiler_params=pltpu.CompilerParams(vmem_limit_bytes=VMEM_LIMIT),
        cost_estimate=COST,
        name="cross_fwd",
    )(queries, kv_own, kv_oth, kv_own, kv_oth)


def cross_bwd_kernel(
    q_ref, ka_ref, kb_ref, va_ref, vb_ref, o_ref, lse_ref, g_ref,
    *rest,
):
    dq_ref, da_ref, db_ref = rest[-3:]
    scale = 1.0 / math.sqrt(HD)
    for h in range(2):
        cols = slice(HD * h, HD * h + HD)
        grad = g_ref[:, cols]
        delta = delta_row(grad, o_ref[:, cols])
        lse = lse_ref[0, h : h + 1, :]
        q = q_ref[:, cols]
        rows = q.shape[0]
        key = jnp.concatenate([ka_ref[:, cols], kb_ref[:, cols]], axis=0)
        value = jnp.concatenate([va_ref[:, cols], vb_ref[:, cols]], axis=0)
        dq, dk, dv = pair_backward(q, key, value, grad, lse, delta, None)
        da_ref[0, :, cols] = dk[:rows].astype(BF)
        da_ref[1, :, cols] = dv[:rows].astype(BF)
        db_ref[0, :, cols] = dk[rows:].astype(BF)
        db_ref[1, :, cols] = dv[rows:].astype(BF)
        dq_ref[:, cols] = (dq.T.astype(BF) * scale).astype(BF)


def cross_backward(queries, kv_own, kv_oth, mixed, lse, grad, start, count, former=()):
    rows, width = queries.shape
    pairs = width // 128

    def turn(i):
        return (start + i + pairs // 2) % pairs

    whole = pl.BlockSpec((rows, 128), lambda i: (0, start + i))
    turned = pl.BlockSpec((rows, 128), lambda i: (0, turn(i)))
    value = pl.BlockSpec((rows, 128), lambda i: (0, pairs + start + i))
    value_turned = pl.BlockSpec((rows, 128), lambda i: (0, pairs + turn(i)))
    cells = 2 * rows * rows * count * 2
    both = jax.ShapeDtypeStruct((2, rows, width), BF)
    return pl.pallas_call(
        cross_bwd_kernel,
        grid=(count,),
        in_specs=[
            whole, whole, turned, value, value_turned, whole,
            pl.BlockSpec((1, 2, rows), lambda i: (start + i, 0, 0)), whole,
        ]
        + [pl.BlockSpec(memory_space=pl.ANY)] * len(former),
        out_specs=[
            whole,
            pl.BlockSpec((2, rows, 128), lambda i: (0, 0, start + i)),
            pl.BlockSpec((2, rows, 128), lambda i: (0, 0, turn(i))),
        ],
        out_shape=[jax.ShapeDtypeStruct((rows, width), BF), both, both],
        input_output_aliases={8 + i: i for i in range(len(former))},
        compiler_params=pltpu.CompilerParams(vmem_limit_bytes=VMEM_LIMIT),
        cost_estimate=COST,
        name="cross_bwd",
    )(queries, kv_own, kv_oth, kv_own, kv_oth, mixed, lse, grad, *former)


def norm_parts(resid):
    center = resid - jnp.mean(resid, axis=-1, keepdims=True)
    rstd = lax.rsqrt(jnp.mean(center * center, axis=-1, keepdims=True) + EPS)
    return center * rstd, rstd


def norm_back(normed, rstd, grad, gain):
    scaled = grad * gain
    return rstd * (
        scaled
        - jnp.mean(scaled, axis=-1, keepdims=True)
        - normed * jnp.mean(scaled * normed, axis=-1, keepdims=True)
    )


def cross_first_kernel(
    q_ref, ka_ref, kb_ref, va_ref, vb_ref, o_ref, lse_ref, g_ref,
    q_mat, second_ref, resid_ref, vec_ref, o_mat, dq_in, former_a, former_b,
    dq_ref, da_ref, db_ref, first_ref, low_ref, keep_ref, send_ref, sums_ref, dq_part,
    *, start, count,
):
    step = pl.program_id(0)

    @pl.when(step == 0)
    def _():
        dq_ref[...] = dq_in[...]

    cross_bwd_kernel(
        q_ref, ka_ref, kb_ref, va_ref, vb_ref, o_ref, lse_ref, g_ref, dq_part, da_ref, db_ref
    )
    at = pl.multiple_of((start + step) * 128, 128)
    dq_ref[:, pl.ds(at, 128)] = dq_part[...]

    @pl.when(step == count - 1)
    def _():
        grad = second_ref[...] + mm(dq_ref[...], q_mat[...], NT)
        normed, rstd = norm_parts(resid_ref[...])
        sums_ref[0:1, :] = jnp.sum(grad, 0, keepdims=True)
        sums_ref[1:2, :] = jnp.sum(grad * normed, 0, keepdims=True)
        first_in = norm_back(normed, rstd, grad, vec_ref[0:1, :])
        first_ref[...] = first_in
        low = first_in.astype(BF)
        low_ref[...] = low
        sums_ref[2:3, :] = jnp.sum(low.astype(F32), 0, keepdims=True)
        sums_ref[3:4, :] = jnp.sum(dq_ref[...].astype(F32), 0, keepdims=True)
        sums_ref[4:8, :] = jnp.zeros((4, sums_ref.shape[1]), F32)
        mixed_grad = mm(low, o_mat[...]).astype(BF)
        cols = keep_ref.shape[1]
        keep_ref[...] = mixed_grad[:, :cols]
        send_ref[...] = mixed_grad[:, cols:]


def cross_first_backward(
    queries, kv_own, kv_oth, mixed, lse, grad, start, former, q_mat, second_in, resid, vec, o_mat
):
    rows, width = queries.shape
    pairs = width // 128
    count = pairs - start

    def turn(i):
        return (start + i + pairs // 2) % pairs

    whole = pl.BlockSpec((rows, 128), lambda i: (0, start + i))
    turned = pl.BlockSpec((rows, 128), lambda i: (0, turn(i)))
    value = pl.BlockSpec((rows, 128), lambda i: (0, pairs + start + i))
    value_turned = pl.BlockSpec((rows, 128), lambda i: (0, pairs + turn(i)))

    def fixed(shape):
        return pl.BlockSpec(shape, lambda i: (0, 0))

    both = jax.ShapeDtypeStruct((2, rows, width), BF)
    return pl.pallas_call(
        functools.partial(cross_first_kernel, start=start, count=count),
        grid=(count,),
        in_specs=[
            whole, whole, turned, value, value_turned, whole,
            pl.BlockSpec((1, 2, rows), lambda i: (start + i, 0, 0)), whole,
            fixed((width, width)), fixed((rows, width)), fixed((rows, width)),
            fixed((1, width)), fixed((width, width)), fixed((rows, width)),
            pl.BlockSpec(memory_space=pl.ANY), pl.BlockSpec(memory_space=pl.ANY),
        ],
        out_specs=[
            fixed((rows, width)),
            pl.BlockSpec((2, rows, 128), lambda i: (0, 0, start + i)),
            pl.BlockSpec((2, rows, 128), lambda i: (0, 0, turn(i))),
            fixed((rows, width)),
            fixed((rows, width)),
            fixed((rows, width // 2)),
            fixed((rows, width // 2)),
            fixed((8, width)),
        ],
        out_shape=[
            jax.ShapeDtypeStruct((rows, width), BF),
            both,
            both,
            jax.ShapeDtypeStruct((rows, width), F32),
            jax.ShapeDtypeStruct((rows, width), BF),
            jax.ShapeDtypeStruct((rows, width // 2), BF),
            jax.ShapeDtypeStruct((rows, width // 2), BF),
            jax.ShapeDtypeStruct((8, width), F32),
        ],
        scratch_shapes=[pltpu.VMEM((rows, 128), BF)],
        input_output_aliases={14: 1, 15: 2},
        compiler_params=pltpu.CompilerParams(vmem_limit_bytes=VMEM_LIMIT),
        cost_estimate=COST,
        name="cross_first",
    )(
        queries, kv_own, kv_oth, kv_own, kv_oth, mixed, lse, grad,
        q_mat, second_in, resid, vec, o_mat, *former,
    )


def gate(value, *others):
    return lax.optimization_barrier((value,) + others)[0]


def outer_count():
    return lax.axis_size("dp") // 2


def swap_both(value):
    count = lax.axis_size("dp")
    pairs = tuple(
        (d * 4 + t, (d ^ 1) * 4 + (t ^ 2)) for d in range(count) for t in range(4)
    )
    return lax.ppermute(value, ("dp", "tensor"), pairs)


def outer_exchange(value):
    groups = [[inner + 2 * o for o in range(outer_count())] for inner in range(2)]
    return lax.all_to_all(value, "dp", 0, 0, axis_index_groups=groups, tiled=True)


def plane_exchange(value):
    groups = [
        [(o * 2 + inner) * 4 + chip * 2 + core for chip in range(2) for inner in range(2)]
        for o in range(outer_count())
        for core in range(2)
    ]
    return lax.all_to_all(value, ("dp", "tensor"), 0, 0, axis_index_groups=groups, tiled=True)


def add_low(left, right):
    return (left.astype(F32) + right.astype(F32)).astype(BF)


def total_dp(value):
    for bit in dp_bits():
        value = value + swap_dp(value, bit)
    return value


ANY = pl.BlockSpec(memory_space=pl.ANY)
VM = pl.BlockSpec(memory_space=pltpu.VMEM)
SM = pl.BlockSpec(memory_space=pltpu.SMEM)


def call(kernel, out_shape, args, in_specs, out_specs, scratch=(), flops=0, moved=0, name=None):
    return pl.pallas_call(
        kernel,
        out_shape=out_shape,
        in_specs=in_specs,
        out_specs=out_specs,
        scratch_shapes=list(scratch),
        compiler_params=pltpu.CompilerParams(vmem_limit_bytes=58 << 20),
        cost_estimate=COST,
        name=name,
    )(*args)


def struct(shape, dtype):
    return jax.ShapeDtypeStruct(shape, dtype)


def tail_start(depth):
    return (depth + 15) // 16 * 16


def high_low(row):
    high = row.astype(BF).astype(F32)
    return high, row - high


def stack_rows(rows, count):
    cols = rows[0].shape[1]
    at = lax.broadcasted_iota(jnp.int32, (count, cols), 0)
    total = jnp.zeros((count, cols), F32)
    for i, row in enumerate(rows):
        total = jnp.where(at == i, row, total)
    return total.astype(BF)


def pack_self_kernel(q_ref, k_ref, v_ref, out_ref):
    cols = q_ref.shape[1]
    for i, ref in enumerate((q_ref, k_ref, v_ref)):
        low = ref[...].astype(BF)
        for copy in range(out_ref.shape[0]):
            out_ref[copy, :, i * cols : (i + 1) * cols] = low


def turned(ref):
    depth = ref.shape[1]
    eye = (
        lax.broadcasted_iota(jnp.int32, (depth, depth), 0)
        == lax.broadcasted_iota(jnp.int32, (depth, depth), 1)
    )
    eye = jnp.where(eye, 1.0, 0.0).astype(BF)
    return mm(eye, ref[...].astype(BF), NT).astype(BF)


def pack_rest_kernel(ck_ref, cv_ref, cq_ref, so_ref, co_ref, ex_ref, sh_ref, next_ref, sh_out):
    cols = ck_ref.shape[1]
    wide = ex_ref.shape[1]
    parts = [ref[...].astype(BF) for ref in (ck_ref, cv_ref, cq_ref)]
    parts += [turned(so_ref), turned(co_ref)]
    expand = ex_ref[...].astype(BF)
    for copy in range(next_ref.shape[0]):
        next_ref[copy, :, :wide] = expand
        for i, low in enumerate(parts):
            next_ref[copy, :, wide + i * cols : wide + (i + 1) * cols] = low
    sh_out[...] = sh_ref[...].astype(BF)


def self_forward_kernel(
    info, own_ref, oth_ref, bias_ref, w_ref, wx_ref, wy_ref, wxy_ref,
    qkv_ref, mat_ref, oa_ref, ob_ref, lse_ref, w_own, w_x, o_ref, sems,
):
    pair = pl.program_id(0)
    width = own_ref.shape[1]
    half = own_ref.shape[0]
    wide = qkv_ref.shape[2] // 3

    @pl.when(pair == 0)
    def _():
        place = info[0]
        cols = w_own.shape[3]
        copies = [
            pltpu.make_async_copy(w_ref, w_own.at[:, place], sems.at[0]),
            pltpu.make_async_copy(wy_ref, w_own.at[:, 1 - place], sems.at[1]),
            pltpu.make_async_copy(wx_ref, w_x.at[:, place], sems.at[2]),
            pltpu.make_async_copy(wxy_ref, w_x.at[:, 1 - place], sems.at[3]),
        ]
        for copy in copies:
            copy.start()
        for copy in copies:
            copy.wait()
        piece = cols // 3
        scale = 1.0 / math.sqrt(HD)
        for x, ref in enumerate((w_own, w_x)):
            mat = ref[...].reshape(width, cols)
            for i in range(3):
                at = (2 * i + x) * piece
                mat_ref[:, at : at + piece] = mat[:, i * piece : (i + 1) * piece]
        for rel, src in enumerate((own_ref, oth_ref)):
            for i in range(3):
                at = slice(wide * i, wide * (i + 1))
                part = mm(src[...], mat_ref[:, at]) + bias_ref[i : i + 1, :]
                if i == 0:
                    part = part * scale
                qkv_ref[rel, :, at] = part.astype(BF)

    first = info[3]
    second = 1 - first
    prefix = info[4]
    key_pos = lax.broadcasted_iota(jnp.int32, (half, half), 0)
    query_pos = lax.broadcasted_iota(jnp.int32, (half, half), 1)
    causal = key_pos <= query_pos
    seen = causal | (key_pos < prefix)

    def load(which, at):
        start = pl.multiple_of(which * wide + pair * 128, 128)
        return qkv_ref[at, :, pl.ds(start, 128)]

    q_both = (load(0, first), load(0, second))
    k_both = (load(1, first), load(1, second))
    v_both = (load(2, first), load(2, second))
    for h in range(2):
        cols = slice(HD * h, HD * h + HD)
        k0, k1 = (k[:, cols] for k in k_both)
        v0, v1 = (v[:, cols] for v in v_both)
        q0, q1 = (q[:, cols] for q in q_both)
        score = jnp.where(seen, mm(k0, q0, NT), NEGATIVE)
        top = jnp.max(score, 0, keepdims=True)
        expo = jnp.exp(score - top)
        total = jnp.sum(expo, 0, keepdims=True)
        mixed = mm(v0, expo.astype(BF), TN) / total
        o_ref[first, :, cols] = mixed.T.astype(BF)
        lse_ref[0, h, pl.ds(first, 1), :] = top + jnp.log(total)

        score_a = mm(k0, q1, NT)
        score_b = jnp.where(causal, mm(k1, q1, NT), NEGATIVE)
        top = jnp.maximum(
            jnp.max(score_a, 0, keepdims=True), jnp.max(score_b, 0, keepdims=True)
        )
        expo_a = jnp.exp(score_a - top)
        expo_b = jnp.exp(score_b - top)
        total = jnp.sum(expo_a, 0, keepdims=True) + jnp.sum(expo_b, 0, keepdims=True)
        mixed = (mm(v0, expo_a.astype(BF), TN) + mm(v1, expo_b.astype(BF), TN)) / total
        o_ref[second, :, cols] = mixed.T.astype(BF)
        lse_ref[0, h, pl.ds(second, 1), :] = top + jnp.log(total)
    oa_ref[...] = o_ref[0]
    ob_ref[...] = o_ref[1]


def self_forward(info, own, oth, bias, pieces):
    half, width = own.shape
    outer, depth, cols = pieces[0].shape
    wide = 2 * cols // 3
    pairs = wide // 128
    fixed2 = pl.BlockSpec((half, width), lambda i, info: (0, 0))
    pair_cols = pl.BlockSpec((half, 128), lambda i, info: (0, i))
    return pl.pallas_call(
        self_forward_kernel,
        grid_spec=pltpu.PrefetchScalarGridSpec(
            num_scalar_prefetch=1,
            grid=(pairs,),
            in_specs=[
                fixed2,
                fixed2,
                pl.BlockSpec(bias.shape, lambda i, info: (0, 0)),
                ANY,
                ANY,
                ANY,
                ANY,
            ],
            out_specs=[
                pl.BlockSpec((2, half, 3 * wide), lambda i, info: (0, 0, 0)),
                pl.BlockSpec((width, 3 * wide), lambda i, info: (0, 0)),
                pair_cols,
                pair_cols,
                pl.BlockSpec((1, 2, 2, half), lambda i, info: (i, 0, 0, 0)),
            ],
            scratch_shapes=[
                pltpu.VMEM((outer, 2, depth, cols), BF),
                pltpu.VMEM((outer, 2, depth, cols), BF),
                pltpu.VMEM((2, half, 128), BF),
                pltpu.SemaphoreType.DMA((4,)),
            ],
        ),
        out_shape=[
            struct((2, half, 3 * wide), BF),
            struct((width, 3 * wide), BF),
            struct((half, wide), BF),
            struct((half, wide), BF),
            struct((pairs, 2, 2, half), F32),
        ],
        compiler_params=pltpu.CompilerParams(vmem_limit_bytes=VMEM_LIMIT),
        cost_estimate=COST,
        name="self_fwd",
    )(info, own, oth, bias, *pieces)


def assemble_kernel(info, *refs):
    pieces, (kv_ref, q_ref, so_ref, co_ref) = refs[:8], refs[8:]
    place = info[0]
    outer, depth, cols = pieces[0].shape
    piece = cols // 5
    for j in range(4):
        for y in range(2):
            at = place if y == 0 else 1 - place
            for o in range(outer):
                value = pieces[2 * j + y][o]
                own = slice(piece * j, piece * (j + 1))
                low = slice(4 * piece + piece * j, 4 * piece + piece * (j + 1))
                kv_ref[o, at, :, own] = value[:, :piece]
                kv_ref[o, at, :, low] = value[:, piece : 2 * piece]
                q_ref[o, at, :, own] = value[:, 2 * piece : 3 * piece]
                so_ref[o, at, :, own] = value[:, 3 * piece : 4 * piece]
                co_ref[o, at, :, own] = value[:, 4 * piece :]


def assemble(info, pieces):
    outer, depth, cols = pieces[0].shape
    wide = cols // 5 * 4
    outs = call(
        assemble_kernel,
        [struct((outer, 2, depth, 2 * wide), BF)] + [struct((outer, 2, depth, wide), BF)] * 3,
        [info] + list(pieces),
        [SM] + [VM] * 8,
        [VM] * 4,
        moved=pieces[0].size * 32,
        name="assemble",
    )
    return [out.reshape(-1, out.shape[-1]) for out in outs]


def copies_kernel(info, own_ref, x_ref, y_ref, xy_ref, out_ref):
    place = info[0]
    for copy in range(out_ref.shape[0]):
        out_ref[copy, 0, place] = own_ref[...]
        out_ref[copy, 0, 1 - place] = y_ref[...]
        out_ref[copy, 1, place] = x_ref[...]
        out_ref[copy, 1, 1 - place] = xy_ref[...]


def plane_copies(info, own, x, y, xy):
    depth, cols = own.shape
    outer = outer_count()
    return call(
        copies_kernel,
        struct((outer, 2, 2, depth, cols), BF),
        [info, own, x, y, xy],
        [SM] + [VM] * 4,
        VM,
        moved=own.size * 2 * 4 * (outer + 1),
        name="plane_copies",
    )


def first_forward_kernel(
    tok_ref, own_ref, oth_ref, o_mat, vec_ref, q_mat, qb_ref,
    resid_ref, first_ref, low_ref, q_ref, mixed_ref,
):
    cols = own_ref.shape[1]
    mixed_ref[:, :cols] = own_ref[...]
    mixed_ref[:, cols:] = oth_ref[...]
    resid = tok_ref[...].astype(F32) + mm(mixed_ref[...], o_mat[...], NT) + vec_ref[0:1, :]
    resid_ref[...] = resid
    normed, rstd = norm_parts(resid)
    first = normed * vec_ref[1:2, :] + vec_ref[2:3, :]
    first_ref[...] = first
    low_ref[...] = first.astype(BF)
    scale = 1.0 / math.sqrt(HD)
    q_ref[...] = ((mm(low_ref[...], q_mat[...]) + qb_ref[...]) * scale).astype(BF)


def first_forward(tokens, own, oth, o_mat, vecs, q_mat, q_bias):
    rows, width = tokens.shape
    return call(
        first_forward_kernel,
        [struct((rows, width), F32)] * 2 + [struct((rows, width), BF)] * 3,
        [tokens, own, oth, o_mat, vecs, q_mat, q_bias],
        [VM] * 7,
        [VM] * 5,
        flops=2 * rows * width * width * 2 * 2,
        moved=width * width * 4 + rows * width * 18,
        name="first_forward",
    )


def project_kv_kernel(keep_ref, got_ref, mat_ref, bias_ref, fet_ref, out_ref):
    fet_ref[...] = keep_ref[...] + got_ref[...]
    width = fet_ref.shape[1]
    out_ref[:, :width] = mm(fet_ref[...], mat_ref[:, :width]).astype(BF)
    out_ref[:, width:] = (mm(fet_ref[...], mat_ref[:, width:]) + bias_ref[...]).astype(BF)


def project_kv(keep, got, mat, bias):
    rows, width = keep.shape
    return call(
        project_kv_kernel,
        [struct((rows, width), BF), struct((rows, 2 * width), BF)],
        [keep, got, mat, bias],
        [VM] * 4,
        [VM] * 2,
        name="project_kv",
    )


def feed_kernel(
    info, mixed_ref, first_ref, cot_ref, vec_ref, wo_hbm,
    e0, e1, e2, e3, e4, e5, e6, e7, s0, s1,
    out_ref, second_ref, low_ref, grad_ref,
    keep_ref, send_ref, sums_ref, tail,
    wo, we, ws, hid, slo, out_a, out_b, norm2, h2low, e3low, acc, wsem, osem, tsem,
):
    first_copy = pltpu.make_async_copy(wo_hbm, wo, wsem.at[0])
    first_copy.start()
    place = info[0]
    copies = []
    for j, pair in enumerate(((e0, e1), (e2, e3), (e4, e5), (e6, e7))):
        for y, ref in enumerate(pair):
            at = place if y == 0 else 1 - place
            copies.append(pltpu.make_async_copy(ref, we.at[j, :, at], wsem.at[1 + 2 * j + y]))
    for j in range(4):
        ref = (s0, s1)[j // 2]
        copies.append(pltpu.make_async_copy(ref.at[:, j % 2], ws.at[j], wsem.at[9 + j]))
    for copy in copies:
        copy.start()

    width = first_ref.shape[1]
    hidden_cols = we.shape[-1]
    outer, depth = we.shape[1], we.shape[3]
    base = out_a.shape[3]

    def expand_mat(j):
        return we[j].reshape(width, hidden_cols)

    def shrink_mat(j):
        return ws[j].reshape(width, hidden_cols)

    def row(i):
        return vec_ref[i : i + 1, :]

    first_copy.wait()
    resid = first_ref[...] + mm(mixed_ref[...], wo[...], NT) + row(0)
    normed, rstd2 = norm_parts(resid)
    norm2[...] = normed
    second = normed * row(1) + row(2)
    h2low[...] = second.astype(BF)
    acc[...] = second + row(7)
    for copy in copies:
        copy.wait()

    def forward(j, carry):
        inner = mm(h2low[...], expand_mat(j)) + vec_ref[pl.ds(3 + j, 1), :]
        phi = 0.5 + 0.5 * lax.erf(inner * (1.0 / math.sqrt(2.0)))
        hidden = (inner * phi).astype(BF)
        hid[j] = hidden
        bell = jnp.exp(-0.5 * inner * inner) * (1.0 / math.sqrt(2.0 * math.pi))
        slo[j] = (phi + inner * bell).astype(BF)
        acc[...] += mm(hidden, shrink_mat(j), NT)
        return carry

    lax.fori_loop(0, 4, forward, 0)
    norm3, rstd3 = norm_parts(acc[...])
    out_ref[...] = (norm3 * row(8) + row(9)).astype(BF)
    cot = cot_ref[...].astype(F32)
    sums_ref[0:1, :] = jnp.sum(cot, 0, keepdims=True)
    sums_ref[1:2, :] = jnp.sum(cot * norm3, 0, keepdims=True)
    third = norm_back(norm3, rstd3, cot, row(8))
    low = third.astype(BF)
    e3low[...] = low
    sums_ref[2:3, :] = jnp.sum(low.astype(F32), 0, keepdims=True)
    acc[...] = third

    def out_copies(to, at, slot):
        copies = []
        for y in range(2):
            for i, part in enumerate((out_a, out_b)):
                copies.append(
                    pltpu.make_async_copy(
                        part.at[slot, :, y],
                        to.at[
                            at, y ^ place, :, :base, i * hidden_cols : (i + 1) * hidden_cols
                        ],
                        osem.at[i, slot, y],
                    )
                )
        return copies

    def backward(step, carry):
        j = (step + 2) % 4
        slot = step % 2
        slope = slo[j].astype(F32)
        inner_grad = (mm(e3low[...], shrink_mat(j)) * slope).astype(BF)
        sums_ref[pl.ds(8 + j, 1), :] = jnp.sum(
            inner_grad.astype(F32), 0, keepdims=True
        )

        @pl.when(step >= 2)
        def _():
            for copy in out_copies(send_ref, slot, slot):
                copy.wait()

        shape = (outer, 2, depth, hidden_cols)
        out_a[slot, :, :, :depth] = mm(h2low[...], inner_grad, TN).astype(BF).reshape(shape)
        out_b[slot, :, :, :depth] = mm(e3low[...], hid[j], TN).astype(BF).reshape(shape)

        @pl.when(step < 2)
        def _():
            for copy in out_copies(send_ref, slot, slot):
                copy.start()

        @pl.when(step >= 2)
        def _():
            for copy in out_copies(keep_ref, slot, slot):
                copy.start()

        acc[...] += mm(inner_grad, expand_mat(j), NT)
        return carry

    lax.fori_loop(0, 4, backward, 0)
    grad = acc[...]
    normed = norm2[...]
    sums_ref[3:4, :] = jnp.sum(grad, 0, keepdims=True)
    sums_ref[4:5, :] = jnp.sum(grad * normed, 0, keepdims=True)
    second_in = norm_back(normed, rstd2, grad, row(1))
    second_ref[...] = second_in
    low = second_in.astype(BF)
    low_ref[...] = low
    sums_ref[5:6, :] = jnp.sum(low.astype(F32), 0, keepdims=True)
    tails = []
    pairs = [high_low(sums_ref[i : i + 1, :]) for i in range(6)]
    for j in range(4):
        rows_e = list(high_low(sums_ref[8 + j : 9 + j, :])) + [r for p in pairs[:3] for r in p]
        rows_s = [r for p in pairs[3:] for r in p]
        for o in range(outer):
            tail[j, o, :, :hidden_cols] = stack_rows(rows_e, 8)
            tail[j, o, :, hidden_cols:] = stack_rows(rows_s, 8)
        for y in range(2):
            to = (keep_ref, send_ref)[j // 2]
            tails.append(
                pltpu.make_async_copy(tail.at[j], to.at[j % 2, y, :, base:, :], tsem.at[2 * j + y])
            )
    for copy in tails:
        copy.start()
    grad_ref[...] = mm(low, wo[...]).astype(BF)
    for slot in range(2):
        for copy in out_copies(keep_ref, slot, slot):
            copy.wait()
    for copy in tails:
        copy.wait()


def feed(info, mixed, first, cot, vecs, wo, expand, shrink):
    rows, width = mixed.shape
    outer, depth, hidden = expand[0].shape
    base = tail_start(depth)
    grads = struct((2, 2, outer, base + 8, 2 * hidden), BF)
    return call(
        feed_kernel,
        [
            struct((rows, width), BF),
            struct((rows, width), F32),
            struct((rows, width), BF),
            struct((rows, width), BF),
            grads,
            grads,
        ],
        [info, mixed, first, cot, vecs, wo] + list(expand) + list(shrink),
        [SM, VM, VM, VM, VM] + [ANY] * 11,
        [VM] * 4 + [ANY] * 2,
        [
            pltpu.VMEM((16, width), F32),
            pltpu.VMEM((4, outer, 8, 2 * hidden), BF),
            pltpu.VMEM((width, width), BF),
            pltpu.VMEM((4, outer, 2, depth, hidden), BF),
            pltpu.VMEM((4, outer, 2, depth, hidden), BF),
            pltpu.VMEM((4, rows, hidden), BF),
            pltpu.VMEM((4, rows, hidden), BF),
            pltpu.VMEM((2, outer, 2, base, hidden), BF),
            pltpu.VMEM((2, outer, 2, base, hidden), BF),
            pltpu.VMEM((rows, width), F32),
            pltpu.VMEM((rows, width), BF),
            pltpu.VMEM((rows, width), BF),
            pltpu.VMEM((rows, width), F32),
            pltpu.SemaphoreType.DMA((13,)),
            pltpu.SemaphoreType.DMA((2, 2, 2)),
            pltpu.SemaphoreType.DMA((8,)),
        ],
        flops=2 * rows * width * (6 * 4 * hidden + 2 * width) * 2,
        moved=width * hidden * 4 * 4 * 2,
        name="feed",
    )


def first_back_kernel(
    dq_ref, q_mat, second_ref, resid_ref, vec_ref, o_mat, first_ref, low_ref, keep_ref, send_ref, sums_ref
):
    grad = second_ref[...] + mm(dq_ref[...], q_mat[...], NT)
    normed, rstd = norm_parts(resid_ref[...])
    sums_ref[0:1, :] = jnp.sum(grad, 0, keepdims=True)
    sums_ref[1:2, :] = jnp.sum(grad * normed, 0, keepdims=True)
    first_in = norm_back(normed, rstd, grad, vec_ref[0:1, :])
    first_ref[...] = first_in
    low = first_in.astype(BF)
    low_ref[...] = low
    sums_ref[2:3, :] = jnp.sum(low.astype(F32), 0, keepdims=True)
    sums_ref[3:4, :] = jnp.sum(dq_ref[...].astype(F32), 0, keepdims=True)
    sums_ref[4:8, :] = jnp.zeros((4, sums_ref.shape[1]), F32)
    mixed_grad = mm(low, o_mat[...]).astype(BF)
    cols = keep_ref.shape[1]
    keep_ref[...] = mixed_grad[:, :cols]
    send_ref[...] = mixed_grad[:, cols:]


def first_back(dq, q_mat, second_in, resid, vec, o_mat):
    rows, width = dq.shape
    cols = width // 2
    return call(
        first_back_kernel,
        [
            struct((rows, width), F32),
            struct((rows, width), BF),
            struct((rows, cols), BF),
            struct((rows, cols), BF),
            struct((8, width), F32),
        ],
        [dq, q_mat, second_in, resid, vec, o_mat],
        [VM] * 6,
        [VM] * 5,
        flops=2 * rows * width * width * 2 * 2,
        moved=width * width * 4 + rows * width * 18,
        name="first_back",
    )


def put_rows(ref, x, full, at, place):
    outer = ref.shape[2]
    depth = full.shape[0] // outer // 2
    for o in range(outer):
        for y in range(2):
            start = (2 * o + y) * depth
            ref[x, y ^ place, o, :depth, at] = full[start : start + depth]


def put_blocks(keep_ref, send_ref, full, i, place):
    piece = full.shape[1] // 4
    at = slice(i * piece, (i + 1) * piece)
    for j in range(4):
        put_rows((keep_ref, send_ref)[j // 2], j % 2, full[:, j * piece : (j + 1) * piece], at, place)


def attn_grads_kernel(
    info, h1_ref, dq_ref, e1_ref, o1_ref, e2_ref, o2_ref, sums_ref,
    fet_ref, own_ref, got_ref, mat_ref, keep_ref, send_ref, grad_ref,
):
    place = info[0]
    width = dq_ref.shape[1]
    piece = width // 4
    outer, rows = keep_ref.shape[2], keep_ref.shape[3]
    for i, (left, right) in enumerate(((h1_ref, dq_ref), (e1_ref, o1_ref), (e2_ref, o2_ref))):
        full = mm(left[...], right[...], TN).astype(BF)
        put_blocks(keep_ref, send_ref, full, i, place)
    total = None
    for i in range(2):
        low = add_low(own_ref[i], got_ref[i])
        full = mm(fet_ref[...], low, TN).astype(BF)
        put_blocks(keep_ref, send_ref, full, 3 + i, place)
        term = mm(low, mat_ref[:, i * width : (i + 1) * width], NT)
        total = term if total is None else total + term
    grad_ref[...] = total.astype(BF)
    parts = [high_low(sums_ref[i : i + 1, :]) for i in range(4)]
    value_sums = high_low(jnp.sum(low.astype(F32), 0, keepdims=True))
    empty = jnp.zeros((1, piece), F32)
    for j in range(4):
        own = slice(j * piece, (j + 1) * piece)
        ref = (keep_ref, send_ref)[j // 2]
        for i in range(5):
            lines = [empty] * 8
            if i < 3:
                lines = [parts[i][0][:, p * piece : (p + 1) * piece] for p in range(4)]
                lines += [parts[i][1][:, p * piece : (p + 1) * piece] for p in range(4)]
            if i == 0:
                lines += [parts[3][0][:, own], parts[3][1][:, own]]
            if i == 4:
                lines += [value_sums[0][:, own], value_sums[1][:, own]]
            block = stack_rows(lines, 16)
            for o in range(outer):
                for y in range(2):
                    ref[j % 2, y, o, rows - 16 :, i * piece : (i + 1) * piece] = block


def attn_grads(info, args, depth):
    rows, width = args[0].shape
    out = struct((2, 2, width // depth // 2, tail_start(depth) + 16, 5 * width // 4), BF)
    return call(
        attn_grads_kernel,
        [out, out, struct((rows, width), BF)],
        [info] + list(args),
        [SM] + [VM] * 11,
        [VM] * 3,
        name="attn_grads",
    )


def self_grads_kernel(info, own_ref, oth_ref, d_ref, a_ref, x_ref, y_ref, xy_ref):
    place = info[0]
    cols = d_ref.shape[3]
    piece = cols // 2
    outer, base = a_ref.shape[0], a_ref.shape[1] - 8
    depth = own_ref.shape[1] // outer // 2
    for i in range(3):
        full = mm(own_ref[...], d_ref[i, 0], TN) + mm(oth_ref[...], d_ref[i, 1], TN)
        full = full.astype(BF)
        at = slice(i * piece, (i + 1) * piece)
        both = d_ref[i, 0].astype(F32) + d_ref[i, 1].astype(F32)
        sums = jnp.sum(both, 0, keepdims=True)
        high = sums.astype(BF).astype(F32)
        row = lax.broadcasted_iota(jnp.int32, (8, cols), 0)
        tail = jnp.where(row == 0, high, jnp.where(row == 1, sums - high, 0.0)).astype(BF)
        for x, (near, away) in enumerate(((a_ref, y_ref), (x_ref, xy_ref))):
            part = slice(x * piece, (x + 1) * piece)
            for o in range(outer):
                start = 2 * o * depth
                first = full[start : start + depth, part]
                second = full[start + depth : start + 2 * depth, part]
                near[o, :depth, at] = jnp.where(place == 0, first, second)
                away[o, :depth, at] = jnp.where(place == 0, second, first)
                near[o, base:, at] = tail[:, part]
                away[o, base:, at] = tail[:, part]


def self_grads(info, own, oth, grads, depth):
    half, width = own.shape
    cols = grads.shape[3]
    out = struct((width // depth // 2, tail_start(depth) + 8, 3 * cols // 2), BF)
    return call(
        self_grads_kernel,
        [out] * 4,
        [info, own, oth, grads],
        [SM] + [VM] * 3,
        [VM] * 4,
        name="self_grads",
    )


def self_back_kernel(d_ref, mat_ref, first_ref, keep_ref, send_ref):
    cols = d_ref.shape[3]
    for rel in (1, 0):
        total = mm(d_ref[0, rel], mat_ref[:, :cols], NT)
        for i in (1, 2):
            total = total + mm(d_ref[i, rel], mat_ref[:, i * cols : (i + 1) * cols], NT)
        if rel == 1:
            send_ref[...] = total.astype(BF)
        else:
            keep_ref[...] = total + first_ref[...]


def self_back(grads, mat, first_in):
    half, width = first_in.shape
    cols = grads.shape[3]
    return call(
        self_back_kernel,
        [struct((half, width), F32), struct((half, width), BF)],
        [grads, mat, first_in],
        [VM] * 3,
        [VM] * 2,
        flops=2 * 2 * half * width * 3 * cols * 2,
        moved=half * width * 10 + half * cols * 12 + width * cols * 6,
        name="self_back",
    )


def fetch_kernel(table, bank_ref, mine_ref, send_ref, sem):
    count = table.shape[0] // 2

    def each(act):
        for group, out_ref in enumerate((mine_ref, send_ref)):

            def body(i, carry, group=group, out_ref=out_ref):
                at = table[group * count + i]
                copy = pltpu.make_async_copy(
                    bank_ref.at[jnp.maximum(at, 0)], out_ref.at[i], sem.at[group * count + i]
                )
                act(copy, at >= 0, out_ref, i)
                return carry

            lax.fori_loop(0, count, body, 0)

    def start(copy, held, out_ref, i):
        @pl.when(held)
        def _():
            copy.start()

        @pl.when(jnp.logical_not(held))
        def _():
            out_ref[i] = jnp.zeros(out_ref.shape[1:], out_ref.dtype)

    def finish(copy, held, out_ref, i):
        @pl.when(held)
        def _():
            copy.wait()

    each(start)
    each(finish)


def fetch(table, bank_blocks):
    count = table.shape[0]
    blk, width = bank_blocks.shape[1:]
    out = struct((count // 2, blk, width), BF)
    mine, send = call(
        fetch_kernel,
        [out, out],
        [table, bank_blocks],
        [SM, ANY],
        [VM, VM],
        [pltpu.SemaphoreType.DMA((count,))],
        moved=count * blk * width * 4,
        name="fetch",
    )
    return [part.reshape(2, count // 4, blk, width) for part in (mine, send)]


def scatter_kernel(table, a_ref, b_ref, c_ref, d_ref, out_ref, slots, sems):
    step = pl.program_id(0)
    per = out_ref.shape[0]

    @pl.when(step == 0)
    def _():
        copies = [
            pltpu.make_async_copy(ref, slots.at[i], sems.at[i])
            for i, ref in enumerate((a_ref, b_ref, c_ref, d_ref))
        ]
        for copy in copies:
            copy.start()
        for copy in copies:
            copy.wait()

    for i in range(per):
        at = table[step * per + i]
        group = jnp.maximum(at, 0) // slots.shape[1]
        place = jnp.maximum(at, 0) % slots.shape[1]
        value = slots[group, place].astype(F32)
        out_ref[i] = jnp.where(at >= 0, value, 0.0)


def scatter(table, parts):
    count = table.shape[0]
    slots, blk, width = parts[0].shape
    per = 4
    return pl.pallas_call(
        scatter_kernel,
        grid_spec=pltpu.PrefetchScalarGridSpec(
            num_scalar_prefetch=1,
            grid=(count // per,),
            in_specs=[ANY] * 4,
            out_specs=pl.BlockSpec((per, blk, width), lambda i, t: (i, 0, 0)),
            scratch_shapes=[
                pltpu.VMEM((4, slots, blk, width), BF),
                pltpu.SemaphoreType.DMA((4,)),
            ],
        ),
        out_shape=struct((count, blk, width), F32),
        compiler_params=pltpu.CompilerParams(vmem_limit_bytes=VMEM_LIMIT),
        cost_estimate=COST,
        name="scatter",
    )(table, *parts)


def sum_all(ref):
    total = ref[0].astype(F32)
    for i in range(1, ref.shape[0]):
        total = total + ref[i].astype(F32)
    return total


def sum_attn_kernel(
    in_ref, q_ref, so_ref, co_ref, k_ref, v_ref, qb_ref, vb_ref, v0_ref, v1_ref, v2_ref
):
    total = sum_all(in_ref)
    piece = total.shape[1] // 5
    depth = q_ref.shape[0]
    q_ref[...] = total[:depth, :piece]
    so_ref[...] = total[:depth, piece : 2 * piece].T
    co_ref[...] = total[:depth, 2 * piece : 3 * piece].T
    k_ref[...] = total[:depth, 3 * piece : 4 * piece]
    v_ref[...] = total[:depth, 4 * piece :]
    tail = total[total.shape[0] - 16 :]
    qb_ref[...] = (tail[8:9, :piece] + tail[9:10, :piece])[0]
    vb_ref[...] = (tail[8:9, 4 * piece :] + tail[9:10, 4 * piece :])[0]
    for i, ref in enumerate((v0_ref, v1_ref, v2_ref)):
        cols = slice(i * piece, (i + 1) * piece)
        parts = [tail[p : p + 1, cols] + tail[p + 4 : p + 5, cols] for p in range(4)]
        ref[...] = jnp.concatenate(parts, axis=1)[0]


def sum_attn(value, depth):
    count, rows, cols = value.shape
    piece = cols // 5
    wide, tall = struct((depth, piece), F32), struct((piece, depth), F32)
    row, vec = struct((piece,), F32), struct((4 * piece,), F32)
    return call(
        sum_attn_kernel,
        [wide, tall, tall, wide, wide, row, row, vec, vec, vec],
        [value],
        [VM],
        [VM] * 10,
        name="sum_attn",
    )


def sum_cols_kernel(in_ref, *refs):
    count = len(refs) // 2
    total = sum_all(in_ref)
    depth, piece = refs[0].shape
    tail = total[total.shape[0] - 8 :]
    for i in range(count):
        cols = slice(i * piece, (i + 1) * piece)
        refs[i][...] = total[:depth, cols]
        refs[count + i][...] = (tail[0:1, cols] + tail[1:2, cols])[0]


def sum_cols(value, depth, count):
    piece = value.shape[2] // count
    return call(
        sum_cols_kernel,
        [struct((depth, piece), F32)] * count + [struct((piece,), F32)] * count,
        [value],
        [VM],
        [VM] * (2 * count),
        name="sum_cols",
    )


def sum_feed_kernel(in_ref, e_ref, s_ref, eb_ref, *vecs):
    total = sum_all(in_ref)
    depth, cols = e_ref.shape
    e_ref[...] = total[:depth, :cols]
    s_ref[...] = total[:depth, cols:]
    tail = total[total.shape[0] - 8 :]
    eb_ref[...] = (tail[0:1, :cols] + tail[1:2, :cols])[0]
    for i in range(3):
        at = 2 + 2 * i
        vecs[i][...] = (tail[at : at + 1, :cols] + tail[at + 1 : at + 2, :cols])[0]
        at = 2 * i
        vecs[3 + i][...] = (tail[at : at + 1, cols:] + tail[at + 1 : at + 2, cols:])[0]


def sum_feed(value, depth):
    cols = value.shape[2] // 2
    return call(
        sum_feed_kernel,
        [struct((depth, cols), F32)] * 2 + [struct((cols,), F32)] * 7,
        [value],
        [VM],
        [VM] * 9,
        name="sum_feed",
    )


def local(
    tokens,
    bank,
    prefix,
    blocks,
    out_grad,
    selfq_weight,
    selfq_bias,
    selfk_weight,
    selfv_weight,
    selfv_bias,
    selfo_weight,
    selfo_bias,
    first_gain,
    first_shift,
    crossq_weight,
    crossq_bias,
    crossk_weight,
    crossv_weight,
    crossv_bias,
    crosso_weight,
    crosso_bias,
    second_gain,
    second_shift,
    expand_weight,
    expand_bias,
    shrink_weight,
    shrink_bias,
    third_gain,
    third_shift,
):
    rank = lax.axis_index("tensor")
    core = rank % 2
    chip = rank // 2
    inner = lax.axis_index("dp") % 2
    outer = outer_count()
    half, width = tokens.shape
    seq_count = prefix.shape[0]
    local_blocks = bank.shape[1] // BLK
    head_cols = selfq_bias.shape[0]
    hidden_cols = expand_bias.shape[0]
    depth = selfq_weight.shape[0]
    slots = NBLK // 2
    two = 2 * head_cols
    attn_cols = 5 * head_cols
    info = jnp.stack([inner, rank, chip]).astype(jnp.int32)

    seq_order = jnp.stack([chip, 1 - chip])
    near = blocks[seq_order].reshape(2, 2, slots)
    near = jnp.stack([near[:, core], near[:, 1 - core]])
    near = near - rank * local_blocks
    held = (near >= 0) & (near < local_blocks)
    fetch_table = jnp.where(held, near + seq_order[None, :, None] * local_blocks, -1)
    fetch_table = fetch_table.reshape(-1).astype(jnp.int32)
    part_mine, part_send = fetch(fetch_table, bank.reshape(seq_count * local_blocks, BLK, width))

    part_got = swap_core(part_send)
    part_away = part_mine[1] + part_got[1]
    part_back = swap_x(part_away)

    self_leaf = call(
        pack_self_kernel,
        struct((outer, depth, 3 * head_cols), BF),
        [gate(selfq_weight, part_send), selfk_weight, selfv_weight],
        [VM] * 3,
        VM,
        name="pack_self",
    )
    bias_own = jnp.concatenate(
        [selfq_bias, selfv_bias, crossq_bias, crossv_bias, expand_bias]
    ).reshape(1, -1)
    bias_two = jnp.concatenate([bias_own, swap_x(bias_own)], axis=0)
    bias_four = jnp.concatenate([bias_two, swap_core(bias_two)], axis=0)
    cq_bias = bias_four[:, two : 3 * head_cols].reshape(-1)
    cv_bias = bias_four[:, 3 * head_cols : 4 * head_cols].reshape(-1)
    ex_bias = bias_four[:, 4 * head_cols :]
    self_bias = jnp.stack(
        [
            bias_two[:, :head_cols].reshape(-1),
            jnp.zeros((two,), F32),
            bias_two[:, head_cols:two].reshape(-1),
        ]
    )
    next_leaf, shrink_leaf = call(
        pack_rest_kernel,
        [
            struct((outer, depth, hidden_cols + attn_cols), BF),
            struct((depth, hidden_cols), BF),
        ],
        [
            gate(crossk_weight, self_leaf, part_away), crossv_weight, crossq_weight, selfo_weight,
            crosso_weight, expand_weight, shrink_weight.T,
        ],
        [VM] * 7,
        [VM] * 2,
        name="pack_rest",
    )
    tokens_oth = swap_core(tokens)
    vecs = jnp.concatenate(
        [
            jnp.stack([crosso_bias, second_gain, second_shift]),
            ex_bias,
            jnp.stack([shrink_bias, third_gain, third_shift]),
        ]
    )
    first_vecs = jnp.stack([selfo_bias, first_gain, first_shift])
    cq_bias, cv_bias = cq_bias.reshape(1, -1), cv_bias.reshape(1, -1)
    my_prefix = lax.dynamic_index_in_dim(prefix, chip, 0, keepdims=False)
    attn_info = jnp.stack([core, my_prefix]).astype(jnp.int32)

    self_z = outer_exchange(self_leaf)

    self_z, self_bias, vecs, first_vecs, cq_bias, cv_bias, next_leaf, attn_info, tokens_oth, part_back = (
        lax.optimization_barrier(
            (self_z, self_bias, vecs, first_vecs, cq_bias, cv_bias, next_leaf, attn_info, tokens_oth, part_back)
        )
    )
    self_near, self_away, self_both = swap_x(self_z), swap_dp(self_z, 1), swap_both(self_z)
    next_z = outer_exchange(next_leaf)

    shrink_leaf = gate(shrink_leaf, self_near)
    shrink_x, shrink_y = swap_x(shrink_leaf), swap_dp(shrink_leaf, 1)
    shrink_xy = swap_both(shrink_leaf)
    shrink_pack = plane_copies(info, shrink_leaf, shrink_x, shrink_y, shrink_xy)
    (
        next_z, tokens_in, self_near, self_away, self_both, shrink_pack, part_got,
    ) = lax.optimization_barrier(
        (next_z, tokens, self_near, self_away, self_both, shrink_pack, part_got)
    )
    expand_z, attn_z = next_z[..., :hidden_cols], next_z[..., hidden_cols:]
    shrink_z = outer_exchange(gate(shrink_pack, next_z))
    attn_x, attn_y, attn_xy = swap_x(attn_z), swap_dp(attn_z, 1), swap_both(attn_z)

    qkv, self_mat, self_own, self_send, self_lse = self_forward(
        jnp.concatenate([info, attn_info]),
        tokens_in,
        tokens_oth,
        self_bias,
        (self_z, self_near, self_away, self_both),
    )
    self_got = swap_core(self_send)
    attn_x, attn_y, attn_xy, self_got = lax.optimization_barrier(
        (attn_x, attn_y, attn_xy, self_got, self_own)
    )[:4]
    attn_own = (attn_z, attn_y, attn_x, attn_xy)
    attn_oth = tuple(swap_core(piece) for piece in attn_own)
    attn_oth, expand_z = lax.optimization_barrier((attn_oth, expand_z))
    expand_x, expand_y = swap_x(expand_z), swap_dp(expand_z, 1)
    cross_kv, cross_q, self_o, cross_o = assemble(info, attn_own + attn_oth)
    cross_kv, expand_x, expand_y = lax.optimization_barrier((cross_kv, expand_x, expand_y))
    expand_xy = swap_both(expand_z)
    fetched, kv_own = project_kv(
        (part_mine[0] + part_got[0]).reshape(slots * BLK, width),
        part_back.reshape(slots * BLK, width),
        cross_kv,
        cv_bias,
    )
    self_got, kv_own = lax.optimization_barrier((self_got, kv_own))
    kv_oth = swap_core(kv_own)
    first_sum, first_out, first_low, queries, mixed_one = first_forward(
        tokens,
        self_own,
        self_got,
        self_o,
        first_vecs,
        cross_q,
        cq_bias,
    )

    queries, kv_oth = lax.optimization_barrier((queries, kv_oth))
    queries, shrink_z = lax.optimization_barrier((queries, shrink_z))
    mixed_two, cross_lse = cross_forward(queries, kv_own, kv_oth)

    expand_oth = tuple(swap_core(piece) for piece in (expand_z, expand_y, expand_x))
    expand_xy, expand_oth, mixed_two = lax.optimization_barrier((expand_xy, expand_oth, mixed_two))
    expand_own = (expand_z, expand_y, expand_x, expand_xy)
    expand_oth = expand_oth + (swap_core(expand_xy),)
    (
        out_act, second_in, cross_low, cross_grad,
        feed_keep, feed_send,
    ) = feed(
        info, mixed_two, first_out, out_grad, vecs, cross_o,
        expand_own + expand_oth, (shrink_z, swap_core(shrink_z)),
    )

    def plane_send(keep, got):
        return tuple(add_low(keep[x, y], got[x, y]) for x, y in ((1, 0), (0, 1), (1, 1)))

    def plane_swap(parts):
        return swap_x(parts[0]), swap_dp(parts[1], 1), swap_both(parts[2])

    def plane_sum(own, got):
        total = sum(part.astype(F32) for part in own)
        return total + sum(part.astype(F32) for part in got)

    def fold(value, dtype):
        return jnp.sum(value.astype(F32), axis=0).astype(dtype)

    feed_got = swap_core(feed_send)
    part_one = cross_backward(queries, kv_own, kv_oth, mixed_two, cross_lse, cross_grad, 0, 2)
    feed_keep = gate(feed_keep, part_one[0])

    def feed_sum(x, y, which, *others):
        at = (x, y, Ellipsis, slice(which * hidden_cols, (which + 1) * hidden_cols))
        total = feed_keep[at].astype(F32) + feed_got[at].astype(F32)
        for other in others:
            total = total + other.astype(F32)
        return total.astype(BF)

    expand_send = feed_sum(1, slice(None), 0)
    shrink_send = feed_sum(slice(None), 1, 1)
    expand_send, shrink_send, part_one = lax.optimization_barrier(
        (expand_send, shrink_send, tuple(part_one))
    )
    expand_got = swap_x(expand_send)
    shrink_got = swap_dp(shrink_send, 1)

    dq, dkv_own, dkv_send, first_in, self_low, grad_own, grad_send, early_vec = cross_first_backward(
        queries, kv_own, kv_oth, mixed_two, cross_lse, cross_grad, 2, part_one,
        cross_q, second_in, first_sum, first_gain.reshape(1, -1), self_o,
    )
    expand_got, shrink_got, dkv_send, grad_send = lax.optimization_barrier(
        (expand_got, shrink_got, dkv_send, grad_send)
    )
    dkv_got = swap_core(dkv_send)
    grad_got = swap_core(grad_send)
    expand_send = feed_sum(0, 1, 0, expand_got[1])
    shrink_send = feed_sum(1, 0, 1, shrink_got[1])
    self_low, dkv_got, grad_got, expand_send, shrink_send = lax.optimization_barrier(
        (self_low, dkv_got, grad_got, expand_send, shrink_send)
    )
    expand_last = swap_dp(expand_send, 1)
    shrink_last = swap_x(shrink_send)
    attn_keep, attn_send, fetched_grad = attn_grads(
        info,
        (
            first_low, dq, self_low, mixed_one, cross_low, mixed_two, early_vec,
            fetched, dkv_own, dkv_got, cross_kv,
        ),
        depth,
    )
    attn_send, grad_got, expand_last, shrink_last = lax.optimization_barrier(
        (attn_send, grad_got, expand_last, shrink_last)
    )
    attn_got = swap_core(attn_send)
    feed_three = jnp.concatenate(
        [
            feed_sum(0, 0, 0, expand_got[0], expand_last),
            feed_sum(0, 0, 1, shrink_got[0], shrink_last),
        ],
        axis=-1,
    )
    feed_three, grad_got = lax.optimization_barrier((feed_three, grad_got))
    feed_last = outer_exchange(feed_three)

    self_args = (attn_info, qkv, self_own, self_send, self_lse, grad_own, grad_got)
    pairs = two // 128
    half_grads = self_backward(*self_args, 0, pairs - 1)
    attn_plane, half_grads, fetched_away = lax.optimization_barrier(
        (plane_send(gate(attn_keep, half_grads), attn_got), half_grads, swap_x(fetched_grad))
    )
    fetched_away = fetched_away.reshape(slots, BLK, width)
    fetched_near = fetched_grad.reshape(slots, BLK, width)
    attn_parts = plane_swap(attn_plane)
    grads = self_backward(*self_args, pairs - 1, 1, (half_grads,))
    self_places = self_grads(info, tokens, tokens_oth, grads, depth)
    self_places, grads = lax.optimization_barrier((tuple(self_places), grads))
    self_parts = (swap_x(self_places[1]), swap_dp(self_places[2], 1), swap_both(self_places[3]))
    back_keep, back_send = self_back(grads, self_mat, first_in)
    back_send, feed_last, attn_parts = lax.optimization_barrier((back_send, feed_last, attn_parts))
    attn_three = plane_sum((attn_keep[0, 0], attn_got[0, 0]), attn_parts).astype(BF)
    attn_last = outer_exchange(attn_three)
    self_three = plane_sum((self_places[0],), self_parts).astype(BF)
    self_last = outer_exchange(
        gate(self_three, attn_last)
    )
    back_got = swap_core(gate(back_send, self_three))
    in_grad = (back_keep + back_got.astype(F32)).astype(BF)

    (
        cq_grad, so_grad, co_grad, ck_grad, cv_grad, cq_rows, cv_rows,
        first_shift_rows, first_gain_rows, so_rows,
    ) = sum_attn(attn_last, depth)
    sq_grad, sk_grad, sv_grad, sq_rows, sk_rows, sv_rows = sum_cols(self_last, depth, 3)
    (
        expand_grad, shrink_grad, expand_rows, third_shift_rows, third_gain_rows, shrink_rows,
        second_shift_rows, second_gain_rows, co_rows,
    ) = sum_feed(feed_last, depth)
    shrink_grad = shrink_grad.T

    near_core = swap_core(gate(fetched_near, self_three))
    away_core = swap_core(gate(fetched_away, near_core))
    slot_ids = jnp.arange(NBLK)
    places = (
        (((slot_ids[None, :] // slots) != core) * 2 + (jnp.arange(seq_count)[:, None] != chip))
        * slots
        + slot_ids[None, :] % slots
    )
    hits = blocks[:, None, :] == (rank * local_blocks + jnp.arange(local_blocks))[None, :, None]
    scatter_table = jnp.max(jnp.where(hits, places[:, None, :], -1), axis=-1)
    bank_grad = scatter(
        scatter_table.reshape(-1).astype(jnp.int32),
        (fetched_near, fetched_away, near_core, away_core),
    ).reshape(bank.shape)

    def line(row):
        return row.reshape(-1)

    return (
        out_act,
        in_grad,
        bank_grad,
        sq_grad,
        line(sq_rows),
        sk_grad,
        sv_grad,
        line(sv_rows),
        so_grad,
        line(so_rows),
        line(first_gain_rows),
        line(first_shift_rows),
        cq_grad,
        line(cq_rows),
        ck_grad,
        cv_grad,
        line(cv_rows),
        co_grad,
        line(co_rows),
        line(second_gain_rows),
        line(second_shift_rows),
        expand_grad,
        line(expand_rows),
        shrink_grad,
        line(shrink_rows),
        line(third_gain_rows),
        line(third_shift_rows),
    )


def solution(mesh):
    rows = P(("dp", "tensor"), None)
    wide = P("dp", "tensor")
    tall = P("tensor", "dp")
    part = P("tensor")
    full = P()
    return jax.shard_map(
        local,
        mesh=mesh,
        in_specs=(
            rows, P("dp", "tensor", None), P("dp"), P("dp", None), rows,
            wide, part, wide, wide, part, tall, full, full, full,
            wide, part, wide, wide, part, tall, full, full, full,
            wide, part, tall, full, full, full,
        ),
        out_specs=(
            rows, rows, P("dp", "tensor", None),
            wide, part, wide, wide, part, tall, full, full, full,
            wide, part, wide, wide, part, tall, full, full, full,
            wide, part, tall, full, full, full,
        ),
        check_vma=False,
    )
```

```python
import functools
import math

import jax
import jax.numpy as jnp
from jax import lax
from jax.experimental import pallas as pl
from jax.experimental.pallas import tpu as pltpu
from jax.sharding import PartitionSpec as P

HD = 64
BLK = 64
NBLK = 16
EPS = 1e-05
NEGATIVE = -1e30
BF = jnp.bfloat16
F32 = jnp.float32

NT = (((1,), (1,)), ((), ()))
NN = (((1,), (0,)), ((), ()))
TN = (((0,), (0,)), ((), ()))

CORE_SWAP = ((0, 1), (1, 0), (2, 3), (3, 2))
X_SWAP = ((0, 2), (2, 0), (1, 3), (3, 1))
VMEM_LIMIT = 48 << 20
COST = pl.CostEstimate(flops=1000, bytes_accessed=1000, transcendentals=0)


def mm(left, right, dims=NN):
    return lax.dot_general(left, right, dims, preferred_element_type=F32)


def swap_core(value):
    return lax.ppermute(value, "tensor", CORE_SWAP)


def swap_x(value):
    return lax.ppermute(value, "tensor", X_SWAP)


def swap_dp(value, bit):
    count = lax.axis_size("dp")
    return lax.ppermute(value, "dp", tuple((i, i ^ bit) for i in range(count)))


def dp_bits():
    count = lax.axis_size("dp")
    bits = []
    bit = count // 2
    while bit >= 1:
        bits.append(bit)
        bit //= 2
    return bits


def pair_backward(q, k, v, grad, lse, delta, mask):
    score = mm(k, q, NT)
    prob = jnp.exp(score - lse)
    if mask is not None:
        prob = jnp.where(mask, prob, 0.0)
    slope = prob * (mm(v, grad, NT) - delta)
    prob = prob.astype(BF)
    slope = slope.astype(BF)
    return mm(k, slope, TN), mm(slope, q, NN), mm(prob, grad, NN)


def delta_row(grad, mixed):
    return jnp.sum((grad.astype(F32) * mixed.astype(F32)).T, 0, keepdims=True)


def self_bwd_kernel(info, q_ref, k_ref, v_ref, oa_ref, ob_ref, lse_ref, ga_ref, gb_ref, *rest):
    out_ref, o_ref, g_ref = rest[-3:]
    dq_ref, dk_ref, dv_ref = out_ref.at[0], out_ref.at[1], out_ref.at[2]
    o_ref[0], o_ref[1] = oa_ref[...], ob_ref[...]
    g_ref[0], g_ref[1] = ga_ref[...], gb_ref[...]
    half = q_ref.shape[1]
    first = info[0]
    second = 1 - first
    prefix = info[1]
    def positions(rows):
        shape = (rows, half)
        return lax.broadcasted_iota(jnp.int32, shape, 0), lax.broadcasted_iota(jnp.int32, shape, 1)

    key_pos, query_pos = positions(half)
    seen = (key_pos <= query_pos) | (key_pos < prefix)
    key_pos, query_pos = positions(2 * half)
    seen_late = key_pos <= query_pos + half
    scale = 1.0 / math.sqrt(HD)
    for h in range(2):
        cols = slice(HD * h, HD * h + HD)

        def rows(ref, at):
            return ref[at, :, cols]

        def both(ref):
            return jnp.concatenate([rows(ref, first), rows(ref, second)], axis=0)

        def one(at, key, value, mask):
            grad = rows(g_ref, at)
            delta = delta_row(grad, rows(o_ref, at))
            lse = lse_ref[0, h, pl.ds(at, 1), :]
            dq, dk, dv = pair_backward(rows(q_ref, at), key, value, grad, lse, delta, mask)
            dq_ref[at, :, cols] = (dq.T.astype(BF) * scale).astype(BF)
            return dk, dv

        dk_a, dv_a = one(first, rows(k_ref, first), rows(v_ref, first), seen)
        dk_b, dv_b = one(second, both(k_ref), both(v_ref), seen_late)
        dk_ref[first, :, cols] = (dk_a + dk_b[:half]).astype(BF)
        dv_ref[first, :, cols] = (dv_a + dv_b[:half]).astype(BF)
        dk_ref[second, :, cols] = dk_b[half:].astype(BF)
        dv_ref[second, :, cols] = dv_b[half:].astype(BF)


def self_backward(info, qkv, mixed_own, mixed_oth, lse, grad_own, grad_oth, start, count, former=()):
    half, width = qkv.shape[1], qkv.shape[2] // 3
    pairs = width // 128

    def spec(which):
        return pl.BlockSpec((2, half, 128), lambda i, info: (0, 0, which * pairs + start + i))

    flat = pl.BlockSpec((half, 128), lambda i, info: (0, start + i))
    cells = 3 * half * half * count * 2
    return pl.pallas_call(
        self_bwd_kernel,
        grid_spec=pltpu.PrefetchScalarGridSpec(
            num_scalar_prefetch=1,
            grid=(count,),
            in_specs=[
                spec(0),
                spec(1),
                spec(2),
                flat,
                flat,
                pl.BlockSpec((1, 2, 2, half), lambda i, info: (start + i, 0, 0, 0)),
                flat,
                flat,
            ]
            + [pl.BlockSpec(memory_space=pl.ANY)] * len(former),
            out_specs=pl.BlockSpec((3, 2, half, 128), lambda i, info: (0, 0, 0, start + i)),
            scratch_shapes=[pltpu.VMEM((2, half, 128), BF)] * 2,
        ),
        out_shape=jax.ShapeDtypeStruct((3, 2, half, width), BF),
        input_output_aliases={9 + i: i for i in range(len(former))},
        compiler_params=pltpu.CompilerParams(vmem_limit_bytes=VMEM_LIMIT),
        cost_estimate=COST,
        name="self_bwd",
    )(info, qkv, qkv, qkv, mixed_own, mixed_oth, lse, grad_own, grad_oth, *former)


def cross_fwd_kernel(q_ref, ka_ref, kb_ref, va_ref, vb_ref, o_ref, lse_ref):
    for h in range(2):
        cols = slice(HD * h, HD * h + HD)
        q = q_ref[:, cols]
        score_a = mm(ka_ref[:, cols], q, NT)
        score_b = mm(kb_ref[:, cols], q, NT)
        top = jnp.maximum(
            jnp.max(score_a, 0, keepdims=True), jnp.max(score_b, 0, keepdims=True)
        )
        expo_a = jnp.exp(score_a - top)
        expo_b = jnp.exp(score_b - top)
        total = jnp.sum(expo_a, 0, keepdims=True) + jnp.sum(expo_b, 0, keepdims=True)
        mixed = (
            mm(va_ref[:, cols], expo_a.astype(BF), TN) + mm(vb_ref[:, cols], expo_b.astype(BF), TN)
        ) / total
        o_ref[:, cols] = mixed.T.astype(BF)
        lse_ref[0, h : h + 1, :] = top + jnp.log(total)


def cross_specs(rows, pairs):
    whole = pl.BlockSpec((rows, 128), lambda i: (0, i))
    turned = pl.BlockSpec((rows, 128), lambda i: (0, (i + pairs // 2) % pairs))
    value = pl.BlockSpec((rows, 128), lambda i: (0, pairs + i))
    value_turned = pl.BlockSpec((rows, 128), lambda i: (0, pairs + (i + pairs // 2) % pairs))
    return whole, turned, value, value_turned


def cross_forward(queries, kv_own, kv_oth):
    rows, width = queries.shape
    pairs = width // 128
    whole, turned, value, value_turned = cross_specs(rows, pairs)
    cells = 2 * rows * rows * pairs * 2
    return pl.pallas_call(
        cross_fwd_kernel,
        grid=(pairs,),
        in_specs=[whole, whole, turned, value, value_turned],
        out_specs=[whole, pl.BlockSpec((1, 2, rows), lambda i: (i, 0, 0))],
        out_shape=[
            jax.ShapeDtypeStruct((rows, width), BF),
            jax.ShapeDtypeStruct((pairs, 2, rows), F32),
        ],
        compiler_params=pltpu.CompilerParams(vmem_limit_bytes=VMEM_LIMIT),
        cost_estimate=COST,
        name="cross_fwd",
    )(queries, kv_own, kv_oth, kv_own, kv_oth)


def cross_bwd_kernel(
    q_ref, ka_ref, kb_ref, va_ref, vb_ref, o_ref, lse_ref, g_ref,
    *rest,
):
    dq_ref, da_ref, db_ref = rest[-3:]
    scale = 1.0 / math.sqrt(HD)
    for h in range(2):
        cols = slice(HD * h, HD * h + HD)
        grad = g_ref[:, cols]
        delta = delta_row(grad, o_ref[:, cols])
        lse = lse_ref[0, h : h + 1, :]
        q = q_ref[:, cols]
        rows = q.shape[0]
        key = jnp.concatenate([ka_ref[:, cols], kb_ref[:, cols]], axis=0)
        value = jnp.concatenate([va_ref[:, cols], vb_ref[:, cols]], axis=0)
        dq, dk, dv = pair_backward(q, key, value, grad, lse, delta, None)
        da_ref[0, :, cols] = dk[:rows].astype(BF)
        da_ref[1, :, cols] = dv[:rows].astype(BF)
        db_ref[0, :, cols] = dk[rows:].astype(BF)
        db_ref[1, :, cols] = dv[rows:].astype(BF)
        dq_ref[:, cols] = (dq.T.astype(BF) * scale).astype(BF)


def cross_backward(queries, kv_own, kv_oth, mixed, lse, grad, start, count, former=()):
    rows, width = queries.shape
    pairs = width // 128

    def turn(i):
        return (start + i + pairs // 2) % pairs

    whole = pl.BlockSpec((rows, 128), lambda i: (0, start + i))
    turned = pl.BlockSpec((rows, 128), lambda i: (0, turn(i)))
    value = pl.BlockSpec((rows, 128), lambda i: (0, pairs + start + i))
    value_turned = pl.BlockSpec((rows, 128), lambda i: (0, pairs + turn(i)))
    cells = 2 * rows * rows * count * 2
    both = jax.ShapeDtypeStruct((2, rows, width), BF)
    return pl.pallas_call(
        cross_bwd_kernel,
        grid=(count,),
        in_specs=[
            whole, whole, turned, value, value_turned, whole,
            pl.BlockSpec((1, 2, rows), lambda i: (start + i, 0, 0)), whole,
        ]
        + [pl.BlockSpec(memory_space=pl.ANY)] * len(former),
        out_specs=[
            whole,
            pl.BlockSpec((2, rows, 128), lambda i: (0, 0, start + i)),
            pl.BlockSpec((2, rows, 128), lambda i: (0, 0, turn(i))),
        ],
        out_shape=[jax.ShapeDtypeStruct((rows, width), BF), both, both],
        input_output_aliases={8 + i: i for i in range(len(former))},
        compiler_params=pltpu.CompilerParams(vmem_limit_bytes=VMEM_LIMIT),
        cost_estimate=COST,
        name="cross_bwd",
    )(queries, kv_own, kv_oth, kv_own, kv_oth, mixed, lse, grad, *former)


def norm_parts(resid):
    center = resid - jnp.mean(resid, axis=-1, keepdims=True)
    rstd = lax.rsqrt(jnp.mean(center * center, axis=-1, keepdims=True) + EPS)
    return center * rstd, rstd


def norm_back(normed, rstd, grad, gain):
    scaled = grad * gain
    return rstd * (
        scaled
        - jnp.mean(scaled, axis=-1, keepdims=True)
        - normed * jnp.mean(scaled * normed, axis=-1, keepdims=True)
    )


def cross_first_kernel(
    q_ref, ka_ref, kb_ref, va_ref, vb_ref, o_ref, lse_ref, g_ref,
    q_mat, second_ref, resid_ref, vec_ref, o_mat, dq_in, former_a, former_b,
    dq_ref, da_ref, db_ref, first_ref, low_ref, keep_ref, send_ref, sums_ref, dq_part,
    *, start, count,
):
    step = pl.program_id(0)

    @pl.when(step == 0)
    def _():
        dq_ref[...] = dq_in[...]

    cross_bwd_kernel(
        q_ref, ka_ref, kb_ref, va_ref, vb_ref, o_ref, lse_ref, g_ref, dq_part, da_ref, db_ref
    )
    at = pl.multiple_of((start + step) * 128, 128)
    dq_ref[:, pl.ds(at, 128)] = dq_part[...]

    @pl.when(step == count - 1)
    def _():
        grad = second_ref[...] + mm(dq_ref[...], q_mat[...], NT)
        normed, rstd = norm_parts(resid_ref[...])
        sums_ref[0:1, :] = jnp.sum(grad, 0, keepdims=True)
        sums_ref[1:2, :] = jnp.sum(grad * normed, 0, keepdims=True)
        first_in = norm_back(normed, rstd, grad, vec_ref[0:1, :])
        first_ref[...] = first_in
        low = first_in.astype(BF)
        low_ref[...] = low
        sums_ref[2:3, :] = jnp.sum(low.astype(F32), 0, keepdims=True)
        sums_ref[3:4, :] = jnp.sum(dq_ref[...].astype(F32), 0, keepdims=True)
        sums_ref[4:8, :] = jnp.zeros((4, sums_ref.shape[1]), F32)
        mixed_grad = mm(low, o_mat[...]).astype(BF)
        cols = keep_ref.shape[1]
        keep_ref[...] = mixed_grad[:, :cols]
        send_ref[...] = mixed_grad[:, cols:]


def cross_first_backward(
    queries, kv_own, kv_oth, mixed, lse, grad, start, former, q_mat, second_in, resid, vec, o_mat
):
    rows, width = queries.shape
    pairs = width // 128
    count = pairs - start

    def turn(i):
        return (start + i + pairs // 2) % pairs

    whole = pl.BlockSpec((rows, 128), lambda i: (0, start + i))
    turned = pl.BlockSpec((rows, 128), lambda i: (0, turn(i)))
    value = pl.BlockSpec((rows, 128), lambda i: (0, pairs + start + i))
    value_turned = pl.BlockSpec((rows, 128), lambda i: (0, pairs + turn(i)))

    def fixed(shape):
        return pl.BlockSpec(shape, lambda i: (0, 0))

    both = jax.ShapeDtypeStruct((2, rows, width), BF)
    return pl.pallas_call(
        functools.partial(cross_first_kernel, start=start, count=count),
        grid=(count,),
        in_specs=[
            whole, whole, turned, value, value_turned, whole,
            pl.BlockSpec((1, 2, rows), lambda i: (start + i, 0, 0)), whole,
            fixed((width, width)), fixed((rows, width)), fixed((rows, width)),
            fixed((1, width)), fixed((width, width)), fixed((rows, width)),
            pl.BlockSpec(memory_space=pl.ANY), pl.BlockSpec(memory_space=pl.ANY),
        ],
        out_specs=[
            fixed((rows, width)),
            pl.BlockSpec((2, rows, 128), lambda i: (0, 0, start + i)),
            pl.BlockSpec((2, rows, 128), lambda i: (0, 0, turn(i))),
            fixed((rows, width)),
            fixed((rows, width)),
            fixed((rows, width // 2)),
            fixed((rows, width // 2)),
            fixed((8, width)),
        ],
        out_shape=[
            jax.ShapeDtypeStruct((rows, width), BF),
            both,
            both,
            jax.ShapeDtypeStruct((rows, width), F32),
            jax.ShapeDtypeStruct((rows, width), BF),
            jax.ShapeDtypeStruct((rows, width // 2), BF),
            jax.ShapeDtypeStruct((rows, width // 2), BF),
            jax.ShapeDtypeStruct((8, width), F32),
        ],
        scratch_shapes=[pltpu.VMEM((rows, 128), BF)],
        input_output_aliases={14: 1, 15: 2},
        compiler_params=pltpu.CompilerParams(vmem_limit_bytes=VMEM_LIMIT),
        cost_estimate=COST,
        name="cross_first",
    )(
        queries, kv_own, kv_oth, kv_own, kv_oth, mixed, lse, grad,
        q_mat, second_in, resid, vec, o_mat, *former,
    )


def gate(value, *others):
    return lax.optimization_barrier((value,) + others)[0]


def outer_count():
    return lax.axis_size("dp") // 2


def swap_both(value):
    count = lax.axis_size("dp")
    pairs = tuple(
        (d * 4 + t, (d ^ 1) * 4 + (t ^ 2)) for d in range(count) for t in range(4)
    )
    return lax.ppermute(value, ("dp", "tensor"), pairs)


def outer_exchange(value):
    groups = [[inner + 2 * o for o in range(outer_count())] for inner in range(2)]
    return lax.all_to_all(value, "dp", 0, 0, axis_index_groups=groups, tiled=True)


def plane_exchange(value):
    groups = [
        [(o * 2 + inner) * 4 + chip * 2 + core for chip in range(2) for inner in range(2)]
        for o in range(outer_count())
        for core in range(2)
    ]
    return lax.all_to_all(value, ("dp", "tensor"), 0, 0, axis_index_groups=groups, tiled=True)


def add_low(left, right):
    return (left.astype(F32) + right.astype(F32)).astype(BF)


def total_dp(value):
    for bit in dp_bits():
        value = value + swap_dp(value, bit)
    return value


ANY = pl.BlockSpec(memory_space=pl.ANY)
VM = pl.BlockSpec(memory_space=pltpu.VMEM)
SM = pl.BlockSpec(memory_space=pltpu.SMEM)


def call(kernel, out_shape, args, in_specs, out_specs, scratch=(), flops=0, moved=0, name=None):
    return pl.pallas_call(
        kernel,
        out_shape=out_shape,
        in_specs=in_specs,
        out_specs=out_specs,
        scratch_shapes=list(scratch),
        compiler_params=pltpu.CompilerParams(vmem_limit_bytes=58 << 20),
        cost_estimate=COST,
        name=name,
    )(*args)


def struct(shape, dtype):
    return jax.ShapeDtypeStruct(shape, dtype)


def tail_start(depth):
    return (depth + 15) // 16 * 16


def high_low(row):
    high = row.astype(BF).astype(F32)
    return high, row - high


def stack_rows(rows, count):
    cols = rows[0].shape[1]
    at = lax.broadcasted_iota(jnp.int32, (count, cols), 0)
    total = jnp.zeros((count, cols), F32)
    for i, row in enumerate(rows):
        total = jnp.where(at == i, row, total)
    return total.astype(BF)


def pack_self_kernel(q_ref, k_ref, v_ref, out_ref):
    cols = q_ref.shape[1]
    for i, ref in enumerate((q_ref, k_ref, v_ref)):
        low = ref[...].astype(BF)
        for copy in range(out_ref.shape[0]):
            out_ref[copy, :, i * cols : (i + 1) * cols] = low


def turned(ref):
    depth = ref.shape[1]
    eye = (
        lax.broadcasted_iota(jnp.int32, (depth, depth), 0)
        == lax.broadcasted_iota(jnp.int32, (depth, depth), 1)
    )
    eye = jnp.where(eye, 1.0, 0.0).astype(BF)
    return mm(eye, ref[...].astype(BF), NT).astype(BF)


def pack_rest_kernel(ck_ref, cv_ref, cq_ref, so_ref, co_ref, ex_ref, sh_ref, next_ref, sh_out):
    cols = ck_ref.shape[1]
    wide = ex_ref.shape[1]
    parts = [ref[...].astype(BF) for ref in (ck_ref, cv_ref, cq_ref)]
    parts += [turned(so_ref), turned(co_ref)]
    expand = ex_ref[...].astype(BF)
    for copy in range(next_ref.shape[0]):
        next_ref[copy, :, :wide] = expand
        for i, low in enumerate(parts):
            next_ref[copy, :, wide + i * cols : wide + (i + 1) * cols] = low
    sh_out[...] = sh_ref[...].astype(BF)


def self_forward_kernel(
    info, own_ref, oth_ref, bias_ref, w_ref, wx_ref, wy_ref, wxy_ref,
    qkv_ref, mat_ref, oa_ref, ob_ref, lse_ref, w_own, w_x, o_ref, sems,
):
    pair = pl.program_id(0)
    width = own_ref.shape[1]
    half = own_ref.shape[0]
    wide = qkv_ref.shape[2] // 3

    @pl.when(pair == 0)
    def _():
        place = info[0]
        cols = w_own.shape[3]
        copies = [
            pltpu.make_async_copy(w_ref, w_own.at[:, place], sems.at[0]),
            pltpu.make_async_copy(wy_ref, w_own.at[:, 1 - place], sems.at[1]),
            pltpu.make_async_copy(wx_ref, w_x.at[:, place], sems.at[2]),
            pltpu.make_async_copy(wxy_ref, w_x.at[:, 1 - place], sems.at[3]),
        ]
        for copy in copies:
            copy.start()
        for copy in copies:
            copy.wait()
        piece = cols // 3
        scale = 1.0 / math.sqrt(HD)
        for x, ref in enumerate((w_own, w_x)):
            mat = ref[...].reshape(width, cols)
            for i in range(3):
                at = (2 * i + x) * piece
                mat_ref[:, at : at + piece] = mat[:, i * piece : (i + 1) * piece]
        for rel, src in enumerate((own_ref, oth_ref)):
            for i in range(3):
                at = slice(wide * i, wide * (i + 1))
                part = mm(src[...], mat_ref[:, at]) + bias_ref[i : i + 1, :]
                if i == 0:
                    part = part * scale
                qkv_ref[rel, :, at] = part.astype(BF)

    first = info[3]
    second = 1 - first
    prefix = info[4]
    key_pos = lax.broadcasted_iota(jnp.int32, (half, half), 0)
    query_pos = lax.broadcasted_iota(jnp.int32, (half, half), 1)
    causal = key_pos <= query_pos
    seen = causal | (key_pos < prefix)

    def load(which, at):
        start = pl.multiple_of(which * wide + pair * 128, 128)
        return qkv_ref[at, :, pl.ds(start, 128)]

    q_both = (load(0, first), load(0, second))
    k_both = (load(1, first), load(1, second))
    v_both = (load(2, first), load(2, second))
    for h in range(2):
        cols = slice(HD * h, HD * h + HD)
        k0, k1 = (k[:, cols] for k in k_both)
        v0, v1 = (v[:, cols] for v in v_both)
        q0, q1 = (q[:, cols] for q in q_both)
        score = jnp.where(seen, mm(k0, q0, NT), NEGATIVE)
        top = jnp.max(score, 0, keepdims=True)
        expo = jnp.exp(score - top)
        total = jnp.sum(expo, 0, keepdims=True)
        mixed = mm(v0, expo.astype(BF), TN) / total
        o_ref[first, :, cols] = mixed.T.astype(BF)
        lse_ref[0, h, pl.ds(first, 1), :] = top + jnp.log(total)

        score_a = mm(k0, q1, NT)
        score_b = jnp.where(causal, mm(k1, q1, NT), NEGATIVE)
        top = jnp.maximum(
            jnp.max(score_a, 0, keepdims=True), jnp.max(score_b, 0, keepdims=True)
        )
        expo_a = jnp.exp(score_a - top)
        expo_b = jnp.exp(score_b - top)
        total = jnp.sum(expo_a, 0, keepdims=True) + jnp.sum(expo_b, 0, keepdims=True)
        mixed = (mm(v0, expo_a.astype(BF), TN) + mm(v1, expo_b.astype(BF), TN)) / total
        o_ref[second, :, cols] = mixed.T.astype(BF)
        lse_ref[0, h, pl.ds(second, 1), :] = top + jnp.log(total)
    oa_ref[...] = o_ref[0]
    ob_ref[...] = o_ref[1]


def self_forward(info, own, oth, bias, pieces):
    half, width = own.shape
    outer, depth, cols = pieces[0].shape
    wide = 2 * cols // 3
    pairs = wide // 128
    fixed2 = pl.BlockSpec((half, width), lambda i, info: (0, 0))
    pair_cols = pl.BlockSpec((half, 128), lambda i, info: (0, i))
    return pl.pallas_call(
        self_forward_kernel,
        grid_spec=pltpu.PrefetchScalarGridSpec(
            num_scalar_prefetch=1,
            grid=(pairs,),
            in_specs=[
                fixed2,
                fixed2,
                pl.BlockSpec(bias.shape, lambda i, info: (0, 0)),
                ANY,
                ANY,
                ANY,
                ANY,
            ],
            out_specs=[
                pl.BlockSpec((2, half, 3 * wide), lambda i, info: (0, 0, 0)),
                pl.BlockSpec((width, 3 * wide), lambda i, info: (0, 0)),
                pair_cols,
                pair_cols,
                pl.BlockSpec((1, 2, 2, half), lambda i, info: (i, 0, 0, 0)),
            ],
            scratch_shapes=[
                pltpu.VMEM((outer, 2, depth, cols), BF),
                pltpu.VMEM((outer, 2, depth, cols), BF),
                pltpu.VMEM((2, half, 128), BF),
                pltpu.SemaphoreType.DMA((4,)),
            ],
        ),
        out_shape=[
            struct((2, half, 3 * wide), BF),
            struct((width, 3 * wide), BF),
            struct((half, wide), BF),
            struct((half, wide), BF),
            struct((pairs, 2, 2, half), F32),
        ],
        compiler_params=pltpu.CompilerParams(vmem_limit_bytes=VMEM_LIMIT),
        cost_estimate=COST,
        name="self_fwd",
    )(info, own, oth, bias, *pieces)


def assemble_kernel(info, *refs):
    pieces, (kv_ref, q_ref, so_ref, co_ref) = refs[:8], refs[8:]
    place = info[0]
    outer, depth, cols = pieces[0].shape
    piece = cols // 5
    for j in range(4):
        for y in range(2):
            at = place if y == 0 else 1 - place
            for o in range(outer):
                value = pieces[2 * j + y][o]
                own = slice(piece * j, piece * (j + 1))
                low = slice(4 * piece + piece * j, 4 * piece + piece * (j + 1))
                kv_ref[o, at, :, own] = value[:, :piece]
                kv_ref[o, at, :, low] = value[:, piece : 2 * piece]
                q_ref[o, at, :, own] = value[:, 2 * piece : 3 * piece]
                so_ref[o, at, :, own] = value[:, 3 * piece : 4 * piece]
                co_ref[o, at, :, own] = value[:, 4 * piece :]


def assemble(info, pieces):
    outer, depth, cols = pieces[0].shape
    wide = cols // 5 * 4
    outs = call(
        assemble_kernel,
        [struct((outer, 2, depth, 2 * wide), BF)] + [struct((outer, 2, depth, wide), BF)] * 3,
        [info] + list(pieces),
        [SM] + [VM] * 8,
        [VM] * 4,
        moved=pieces[0].size * 32,
        name="assemble",
    )
    return [out.reshape(-1, out.shape[-1]) for out in outs]


def copies_kernel(info, own_ref, x_ref, y_ref, xy_ref, out_ref):
    place = info[0]
    for copy in range(out_ref.shape[0]):
        out_ref[copy, 0, place] = own_ref[...]
        out_ref[copy, 0, 1 - place] = y_ref[...]
        out_ref[copy, 1, place] = x_ref[...]
        out_ref[copy, 1, 1 - place] = xy_ref[...]


def plane_copies(info, own, x, y, xy):
    depth, cols = own.shape
    outer = outer_count()
    return call(
        copies_kernel,
        struct((outer, 2, 2, depth, cols), BF),
        [info, own, x, y, xy],
        [SM] + [VM] * 4,
        VM,
        moved=own.size * 2 * 4 * (outer + 1),
        name="plane_copies",
    )


def first_forward_kernel(
    tok_ref, own_ref, oth_ref, o_mat, vec_ref, q_mat, qb_ref,
    resid_ref, first_ref, low_ref, q_ref, mixed_ref,
):
    cols = own_ref.shape[1]
    mixed_ref[:, :cols] = own_ref[...]
    mixed_ref[:, cols:] = oth_ref[...]
    resid = tok_ref[...].astype(F32) + mm(mixed_ref[...], o_mat[...], NT) + vec_ref[0:1, :]
    resid_ref[...] = resid
    normed, rstd = norm_parts(resid)
    first = normed * vec_ref[1:2, :] + vec_ref[2:3, :]
    first_ref[...] = first
    low_ref[...] = first.astype(BF)
    scale = 1.0 / math.sqrt(HD)
    q_ref[...] = ((mm(low_ref[...], q_mat[...]) + qb_ref[...]) * scale).astype(BF)


def first_forward(tokens, own, oth, o_mat, vecs, q_mat, q_bias):
    rows, width = tokens.shape
    return call(
        first_forward_kernel,
        [struct((rows, width), F32)] * 2 + [struct((rows, width), BF)] * 3,
        [tokens, own, oth, o_mat, vecs, q_mat, q_bias],
        [VM] * 7,
        [VM] * 5,
        flops=2 * rows * width * width * 2 * 2,
        moved=width * width * 4 + rows * width * 18,
        name="first_forward",
    )


def project_kv_kernel(keep_ref, got_ref, mat_ref, bias_ref, fet_ref, out_ref):
    fet_ref[...] = keep_ref[...] + got_ref[...]
    width = fet_ref.shape[1]
    out_ref[:, :width] = mm(fet_ref[...], mat_ref[:, :width]).astype(BF)
    out_ref[:, width:] = (mm(fet_ref[...], mat_ref[:, width:]) + bias_ref[...]).astype(BF)


def project_kv(keep, got, mat, bias):
    rows, width = keep.shape
    return call(
        project_kv_kernel,
        [struct((rows, width), BF), struct((rows, 2 * width), BF)],
        [keep, got, mat, bias],
        [VM] * 4,
        [VM] * 2,
        name="project_kv",
    )


def feed_kernel(
    info, mixed_ref, first_ref, cot_ref, vec_ref, wo_hbm,
    e0, e1, e2, e3, e4, e5, e6, e7, s0, s1,
    out_ref, second_ref, low_ref, grad_ref,
    keep_ref, send_ref, sums_ref, tail,
    wo, we, ws, hid, slo, out_a, out_b, norm2, h2low, e3low, acc, wsem, osem, tsem,
):
    first_copy = pltpu.make_async_copy(wo_hbm, wo, wsem.at[0])
    first_copy.start()
    place = info[0]
    copies = []
    for j, pair in enumerate(((e0, e1), (e2, e3), (e4, e5), (e6, e7))):
        for y, ref in enumerate(pair):
            at = place if y == 0 else 1 - place
            copies.append(pltpu.make_async_copy(ref, we.at[j, :, at], wsem.at[1 + 2 * j + y]))
    for j in range(4):
        ref = (s0, s1)[j // 2]
        copies.append(pltpu.make_async_copy(ref.at[:, j % 2], ws.at[j], wsem.at[9 + j]))
    for copy in copies:
        copy.start()

    width = first_ref.shape[1]
    hidden_cols = we.shape[-1]
    outer, depth = we.shape[1], we.shape[3]
    base = out_a.shape[3]

    def expand_mat(j):
        return we[j].reshape(width, hidden_cols)

    def shrink_mat(j):
        return ws[j].reshape(width, hidden_cols)

    def row(i):
        return vec_ref[i : i + 1, :]

    first_copy.wait()
    resid = first_ref[...] + mm(mixed_ref[...], wo[...], NT) + row(0)
    normed, rstd2 = norm_parts(resid)
    norm2[...] = normed
    second = normed * row(1) + row(2)
    h2low[...] = second.astype(BF)
    acc[...] = second + row(7)
    for copy in copies:
        copy.wait()

    def forward(j, carry):
        inner = mm(h2low[...], expand_mat(j)) + vec_ref[pl.ds(3 + j, 1), :]
        phi = 0.5 + 0.5 * lax.erf(inner * (1.0 / math.sqrt(2.0)))
        hidden = (inner * phi).astype(BF)
        hid[j] = hidden
        bell = jnp.exp(-0.5 * inner * inner) * (1.0 / math.sqrt(2.0 * math.pi))
        slo[j] = (phi + inner * bell).astype(BF)
        acc[...] += mm(hidden, shrink_mat(j), NT)
        return carry

    lax.fori_loop(0, 4, forward, 0)
    norm3, rstd3 = norm_parts(acc[...])
    out_ref[...] = (norm3 * row(8) + row(9)).astype(BF)
    cot = cot_ref[...].astype(F32)
    sums_ref[0:1, :] = jnp.sum(cot, 0, keepdims=True)
    sums_ref[1:2, :] = jnp.sum(cot * norm3, 0, keepdims=True)
    third = norm_back(norm3, rstd3, cot, row(8))
    low = third.astype(BF)
    e3low[...] = low
    sums_ref[2:3, :] = jnp.sum(low.astype(F32), 0, keepdims=True)
    acc[...] = third

    def out_copies(to, at, slot):
        copies = []
        for y in range(2):
            for i, part in enumerate((out_a, out_b)):
                copies.append(
                    pltpu.make_async_copy(
                        part.at[slot, :, y],
                        to.at[
                            at, y ^ place, :, :base, i * hidden_cols : (i + 1) * hidden_cols
                        ],
                        osem.at[i, slot, y],
                    )
                )
        return copies

    def backward(step, carry):
        j = (step + 2) % 4
        slot = step % 2
        slope = slo[j].astype(F32)
        inner_grad = (mm(e3low[...], shrink_mat(j)) * slope).astype(BF)
        sums_ref[pl.ds(8 + j, 1), :] = jnp.sum(
            inner_grad.astype(F32), 0, keepdims=True
        )

        @pl.when(step >= 2)
        def _():
            for copy in out_copies(send_ref, slot, slot):
                copy.wait()

        shape = (outer, 2, depth, hidden_cols)
        out_a[slot, :, :, :depth] = mm(h2low[...], inner_grad, TN).astype(BF).reshape(shape)
        out_b[slot, :, :, :depth] = mm(e3low[...], hid[j], TN).astype(BF).reshape(shape)

        @pl.when(step < 2)
        def _():
            for copy in out_copies(send_ref, slot, slot):
                copy.start()

        @pl.when(step >= 2)
        def _():
            for copy in out_copies(keep_ref, slot, slot):
                copy.start()

        acc[...] += mm(inner_grad, expand_mat(j), NT)
        return carry

    lax.fori_loop(0, 4, backward, 0)
    grad = acc[...]
    normed = norm2[...]
    sums_ref[3:4, :] = jnp.sum(grad, 0, keepdims=True)
    sums_ref[4:5, :] = jnp.sum(grad * normed, 0, keepdims=True)
    second_in = norm_back(normed, rstd2, grad, row(1))
    second_ref[...] = second_in
    low = second_in.astype(BF)
    low_ref[...] = low
    sums_ref[5:6, :] = jnp.sum(low.astype(F32), 0, keepdims=True)
    tails = []
    pairs = [high_low(sums_ref[i : i + 1, :]) for i in range(6)]
    for j in range(4):
        rows_e = list(high_low(sums_ref[8 + j : 9 + j, :])) + [r for p in pairs[:3] for r in p]
        rows_s = [r for p in pairs[3:] for r in p]
        for o in range(outer):
            tail[j, o, :, :hidden_cols] = stack_rows(rows_e, 8)
            tail[j, o, :, hidden_cols:] = stack_rows(rows_s, 8)
        for y in range(2):
            to = (keep_ref, send_ref)[j // 2]
            tails.append(
                pltpu.make_async_copy(tail.at[j], to.at[j % 2, y, :, base:, :], tsem.at[2 * j + y])
            )
    for copy in tails:
        copy.start()
    grad_ref[...] = mm(low, wo[...]).astype(BF)
    for slot in range(2):
        for copy in out_copies(keep_ref, slot, slot):
            copy.wait()
    for copy in tails:
        copy.wait()


def feed(info, mixed, first, cot, vecs, wo, expand, shrink):
    rows, width = mixed.shape
    outer, depth, hidden = expand[0].shape
    base = tail_start(depth)
    grads = struct((2, 2, outer, base + 8, 2 * hidden), BF)
    return call(
        feed_kernel,
        [
            struct((rows, width), BF),
            struct((rows, width), F32),
            struct((rows, width), BF),
            struct((rows, width), BF),
            grads,
            grads,
        ],
        [info, mixed, first, cot, vecs, wo] + list(expand) + list(shrink),
        [SM, VM, VM, VM, VM] + [ANY] * 11,
        [VM] * 4 + [ANY] * 2,
        [
            pltpu.VMEM((16, width), F32),
            pltpu.VMEM((4, outer, 8, 2 * hidden), BF),
            pltpu.VMEM((width, width), BF),
            pltpu.VMEM((4, outer, 2, depth, hidden), BF),
            pltpu.VMEM((4, outer, 2, depth, hidden), BF),
            pltpu.VMEM((4, rows, hidden), BF),
            pltpu.VMEM((4, rows, hidden), BF),
            pltpu.VMEM((2, outer, 2, base, hidden), BF),
            pltpu.VMEM((2, outer, 2, base, hidden), BF),
            pltpu.VMEM((rows, width), F32),
            pltpu.VMEM((rows, width), BF),
            pltpu.VMEM((rows, width), BF),
            pltpu.VMEM((rows, width), F32),
            pltpu.SemaphoreType.DMA((13,)),
            pltpu.SemaphoreType.DMA((2, 2, 2)),
            pltpu.SemaphoreType.DMA((8,)),
        ],
        flops=2 * rows * width * (6 * 4 * hidden + 2 * width) * 2,
        moved=width * hidden * 4 * 4 * 2,
        name="feed",
    )


def first_back_kernel(
    dq_ref, q_mat, second_ref, resid_ref, vec_ref, o_mat, first_ref, low_ref, keep_ref, send_ref, sums_ref
):
    grad = second_ref[...] + mm(dq_ref[...], q_mat[...], NT)
    normed, rstd = norm_parts(resid_ref[...])
    sums_ref[0:1, :] = jnp.sum(grad, 0, keepdims=True)
    sums_ref[1:2, :] = jnp.sum(grad * normed, 0, keepdims=True)
    first_in = norm_back(normed, rstd, grad, vec_ref[0:1, :])
    first_ref[...] = first_in
    low = first_in.astype(BF)
    low_ref[...] = low
    sums_ref[2:3, :] = jnp.sum(low.astype(F32), 0, keepdims=True)
    sums_ref[3:4, :] = jnp.sum(dq_ref[...].astype(F32), 0, keepdims=True)
    sums_ref[4:8, :] = jnp.zeros((4, sums_ref.shape[1]), F32)
    mixed_grad = mm(low, o_mat[...]).astype(BF)
    cols = keep_ref.shape[1]
    keep_ref[...] = mixed_grad[:, :cols]
    send_ref[...] = mixed_grad[:, cols:]


def first_back(dq, q_mat, second_in, resid, vec, o_mat):
    rows, width = dq.shape
    cols = width // 2
    return call(
        first_back_kernel,
        [
            struct((rows, width), F32),
            struct((rows, width), BF),
            struct((rows, cols), BF),
            struct((rows, cols), BF),
            struct((8, width), F32),
        ],
        [dq, q_mat, second_in, resid, vec, o_mat],
        [VM] * 6,
        [VM] * 5,
        flops=2 * rows * width * width * 2 * 2,
        moved=width * width * 4 + rows * width * 18,
        name="first_back",
    )


def put_rows(ref, x, full, at, place):
    outer = ref.shape[2]
    depth = full.shape[0] // outer // 2
    for o in range(outer):
        for y in range(2):
            start = (2 * o + y) * depth
            ref[x, y ^ place, o, :depth, at] = full[start : start + depth]


def put_blocks(keep_ref, send_ref, full, i, place):
    piece = full.shape[1] // 4
    at = slice(i * piece, (i + 1) * piece)
    for j in range(4):
        put_rows((keep_ref, send_ref)[j // 2], j % 2, full[:, j * piece : (j + 1) * piece], at, place)


def attn_grads_kernel(
    info, h1_ref, dq_ref, e1_ref, o1_ref, e2_ref, o2_ref, sums_ref,
    fet_ref, own_ref, got_ref, mat_ref, keep_ref, send_ref, grad_ref,
):
    place = info[0]
    width = dq_ref.shape[1]
    piece = width // 4
    outer, rows = keep_ref.shape[2], keep_ref.shape[3]
    for i, (left, right) in enumerate(((h1_ref, dq_ref), (e1_ref, o1_ref), (e2_ref, o2_ref))):
        full = mm(left[...], right[...], TN).astype(BF)
        put_blocks(keep_ref, send_ref, full, i, place)
    total = None
    for i in range(2):
        low = add_low(own_ref[i], got_ref[i])
        full = mm(fet_ref[...], low, TN).astype(BF)
        put_blocks(keep_ref, send_ref, full, 3 + i, place)
        term = mm(low, mat_ref[:, i * width : (i + 1) * width], NT)
        total = term if total is None else total + term
    grad_ref[...] = total.astype(BF)
    parts = [high_low(sums_ref[i : i + 1, :]) for i in range(4)]
    value_sums = high_low(jnp.sum(low.astype(F32), 0, keepdims=True))
    empty = jnp.zeros((1, piece), F32)
    for j in range(4):
        own = slice(j * piece, (j + 1) * piece)
        ref = (keep_ref, send_ref)[j // 2]
        for i in range(5):
            lines = [empty] * 8
            if i < 3:
                lines = [parts[i][0][:, p * piece : (p + 1) * piece] for p in range(4)]
                lines += [parts[i][1][:, p * piece : (p + 1) * piece] for p in range(4)]
            if i == 0:
                lines += [parts[3][0][:, own], parts[3][1][:, own]]
            if i == 4:
                lines += [value_sums[0][:, own], value_sums[1][:, own]]
            block = stack_rows(lines, 16)
            for o in range(outer):
                for y in range(2):
                    ref[j % 2, y, o, rows - 16 :, i * piece : (i + 1) * piece] = block


def attn_grads(info, args, depth):
    rows, width = args[0].shape
    out = struct((2, 2, width // depth // 2, tail_start(depth) + 16, 5 * width // 4), BF)
    return call(
        attn_grads_kernel,
        [out, out, struct((rows, width), BF)],
        [info] + list(args),
        [SM] + [VM] * 11,
        [VM] * 3,
        name="attn_grads",
    )


def self_grads_kernel(info, own_ref, oth_ref, d_ref, a_ref, x_ref, y_ref, xy_ref):
    place = info[0]
    cols = d_ref.shape[3]
    piece = cols // 2
    outer, base = a_ref.shape[0], a_ref.shape[1] - 8
    depth = own_ref.shape[1] // outer // 2
    for i in range(3):
        full = mm(own_ref[...], d_ref[i, 0], TN) + mm(oth_ref[...], d_ref[i, 1], TN)
        full = full.astype(BF)
        at = slice(i * piece, (i + 1) * piece)
        both = d_ref[i, 0].astype(F32) + d_ref[i, 1].astype(F32)
        sums = jnp.sum(both, 0, keepdims=True)
        high = sums.astype(BF).astype(F32)
        row = lax.broadcasted_iota(jnp.int32, (8, cols), 0)
        tail = jnp.where(row == 0, high, jnp.where(row == 1, sums - high, 0.0)).astype(BF)
        for x, (near, away) in enumerate(((a_ref, y_ref), (x_ref, xy_ref))):
            part = slice(x * piece, (x + 1) * piece)
            for o in range(outer):
                start = 2 * o * depth
                first = full[start : start + depth, part]
                second = full[start + depth : start + 2 * depth, part]
                near[o, :depth, at] = jnp.where(place == 0, first, second)
                away[o, :depth, at] = jnp.where(place == 0, second, first)
                near[o, base:, at] = tail[:, part]
                away[o, base:, at] = tail[:, part]


def self_grads(info, own, oth, grads, depth):
    half, width = own.shape
    cols = grads.shape[3]
    out = struct((width // depth // 2, tail_start(depth) + 8, 3 * cols // 2), BF)
    return call(
        self_grads_kernel,
        [out] * 4,
        [info, own, oth, grads],
        [SM] + [VM] * 3,
        [VM] * 4,
        name="self_grads",
    )


def self_back_kernel(d_ref, mat_ref, first_ref, keep_ref, send_ref):
    cols = d_ref.shape[3]
    for rel in (1, 0):
        total = mm(d_ref[0, rel], mat_ref[:, :cols], NT)
        for i in (1, 2):
            total = total + mm(d_ref[i, rel], mat_ref[:, i * cols : (i + 1) * cols], NT)
        if rel == 1:
            send_ref[...] = total.astype(BF)
        else:
            keep_ref[...] = total + first_ref[...]


def self_back(grads, mat, first_in):
    half, width = first_in.shape
    cols = grads.shape[3]
    return call(
        self_back_kernel,
        [struct((half, width), F32), struct((half, width), BF)],
        [grads, mat, first_in],
        [VM] * 3,
        [VM] * 2,
        flops=2 * 2 * half * width * 3 * cols * 2,
        moved=half * width * 10 + half * cols * 12 + width * cols * 6,
        name="self_back",
    )


def fetch_kernel(table, bank_ref, mine_ref, send_ref, sem):
    count = table.shape[0] // 2

    def each(act):
        for group, out_ref in enumerate((mine_ref, send_ref)):

            def body(i, carry, group=group, out_ref=out_ref):
                at = table[group * count + i]
                copy = pltpu.make_async_copy(
                    bank_ref.at[jnp.maximum(at, 0)], out_ref.at[i], sem.at[group * count + i]
                )
                act(copy, at >= 0, out_ref, i)
                return carry

            lax.fori_loop(0, count, body, 0)

    def start(copy, held, out_ref, i):
        @pl.when(held)
        def _():
            copy.start()

        @pl.when(jnp.logical_not(held))
        def _():
            out_ref[i] = jnp.zeros(out_ref.shape[1:], out_ref.dtype)

    def finish(copy, held, out_ref, i):
        @pl.when(held)
        def _():
            copy.wait()

    each(start)
    each(finish)


def fetch(table, bank_blocks):
    count = table.shape[0]
    blk, width = bank_blocks.shape[1:]
    out = struct((count // 2, blk, width), BF)
    mine, send = call(
        fetch_kernel,
        [out, out],
        [table, bank_blocks],
        [SM, ANY],
        [VM, VM],
        [pltpu.SemaphoreType.DMA((count,))],
        moved=count * blk * width * 4,
        name="fetch",
    )
    return [part.reshape(2, count // 4, blk, width) for part in (mine, send)]


def scatter_kernel(table, a_ref, b_ref, c_ref, d_ref, out_ref, slots, sems):
    step = pl.program_id(0)
    per = out_ref.shape[0]

    @pl.when(step == 0)
    def _():
        copies = [
            pltpu.make_async_copy(ref, slots.at[i], sems.at[i])
            for i, ref in enumerate((a_ref, b_ref, c_ref, d_ref))
        ]
        for copy in copies:
            copy.start()
        for copy in copies:
            copy.wait()

    for i in range(per):
        at = table[step * per + i]
        group = jnp.maximum(at, 0) // slots.shape[1]
        place = jnp.maximum(at, 0) % slots.shape[1]
        value = slots[group, place].astype(F32)
        out_ref[i] = jnp.where(at >= 0, value, 0.0)


def scatter(table, parts):
    count = table.shape[0]
    slots, blk, width = parts[0].shape
    per = 4
    return pl.pallas_call(
        scatter_kernel,
        grid_spec=pltpu.PrefetchScalarGridSpec(
            num_scalar_prefetch=1,
            grid=(count // per,),
            in_specs=[ANY] * 4,
            out_specs=pl.BlockSpec((per, blk, width), lambda i, t: (i, 0, 0)),
            scratch_shapes=[
                pltpu.VMEM((4, slots, blk, width), BF),
                pltpu.SemaphoreType.DMA((4,)),
            ],
        ),
        out_shape=struct((count, blk, width), F32),
        compiler_params=pltpu.CompilerParams(vmem_limit_bytes=VMEM_LIMIT),
        cost_estimate=COST,
        name="scatter",
    )(table, *parts)


def sum_all(ref):
    total = ref[0].astype(F32)
    for i in range(1, ref.shape[0]):
        total = total + ref[i].astype(F32)
    return total


def sum_attn_kernel(
    in_ref, q_ref, so_ref, co_ref, k_ref, v_ref, qb_ref, vb_ref, v0_ref, v1_ref, v2_ref
):
    total = sum_all(in_ref)
    piece = total.shape[1] // 5
    depth = q_ref.shape[0]
    q_ref[...] = total[:depth, :piece]
    so_ref[...] = total[:depth, piece : 2 * piece].T
    co_ref[...] = total[:depth, 2 * piece : 3 * piece].T
    k_ref[...] = total[:depth, 3 * piece : 4 * piece]
    v_ref[...] = total[:depth, 4 * piece :]
    tail = total[total.shape[0] - 16 :]
    qb_ref[...] = (tail[8:9, :piece] + tail[9:10, :piece])[0]
    vb_ref[...] = (tail[8:9, 4 * piece :] + tail[9:10, 4 * piece :])[0]
    for i, ref in enumerate((v0_ref, v1_ref, v2_ref)):
        cols = slice(i * piece, (i + 1) * piece)
        parts = [tail[p : p + 1, cols] + tail[p + 4 : p + 5, cols] for p in range(4)]
        ref[...] = jnp.concatenate(parts, axis=1)[0]


def sum_attn(value, depth):
    count, rows, cols = value.shape
    piece = cols // 5
    wide, tall = struct((depth, piece), F32), struct((piece, depth), F32)
    row, vec = struct((piece,), F32), struct((4 * piece,), F32)
    return call(
        sum_attn_kernel,
        [wide, tall, tall, wide, wide, row, row, vec, vec, vec],
        [value],
        [VM],
        [VM] * 10,
        name="sum_attn",
    )


def sum_cols_kernel(in_ref, *refs):
    count = len(refs) // 2
    total = sum_all(in_ref)
    depth, piece = refs[0].shape
    tail = total[total.shape[0] - 8 :]
    for i in range(count):
        cols = slice(i * piece, (i + 1) * piece)
        refs[i][...] = total[:depth, cols]
        refs[count + i][...] = (tail[0:1, cols] + tail[1:2, cols])[0]


def sum_cols(value, depth, count):
    piece = value.shape[2] // count
    return call(
        sum_cols_kernel,
        [struct((depth, piece), F32)] * count + [struct((piece,), F32)] * count,
        [value],
        [VM],
        [VM] * (2 * count),
        name="sum_cols",
    )


def sum_feed_kernel(in_ref, e_ref, s_ref, eb_ref, *vecs):
    total = sum_all(in_ref)
    depth, cols = e_ref.shape
    e_ref[...] = total[:depth, :cols]
    s_ref[...] = total[:depth, cols:]
    tail = total[total.shape[0] - 8 :]
    eb_ref[...] = (tail[0:1, :cols] + tail[1:2, :cols])[0]
    for i in range(3):
        at = 2 + 2 * i
        vecs[i][...] = (tail[at : at + 1, :cols] + tail[at + 1 : at + 2, :cols])[0]
        at = 2 * i
        vecs[3 + i][...] = (tail[at : at + 1, cols:] + tail[at + 1 : at + 2, cols:])[0]


def sum_feed(value, depth):
    cols = value.shape[2] // 2
    return call(
        sum_feed_kernel,
        [struct((depth, cols), F32)] * 2 + [struct((cols,), F32)] * 7,
        [value],
        [VM],
        [VM] * 9,
        name="sum_feed",
    )


def local(
    tokens,
    bank,
    prefix,
    blocks,
    out_grad,
    selfq_weight,
    selfq_bias,
    selfk_weight,
    selfv_weight,
    selfv_bias,
    selfo_weight,
    selfo_bias,
    first_gain,
    first_shift,
    crossq_weight,
    crossq_bias,
    crossk_weight,
    crossv_weight,
    crossv_bias,
    crosso_weight,
    crosso_bias,
    second_gain,
    second_shift,
    expand_weight,
    expand_bias,
    shrink_weight,
    shrink_bias,
    third_gain,
    third_shift,
):
    rank = lax.axis_index("tensor")
    core = rank % 2
    chip = rank // 2
    inner = lax.axis_index("dp") % 2
    outer = outer_count()
    half, width = tokens.shape
    seq_count = prefix.shape[0]
    local_blocks = bank.shape[1] // BLK
    head_cols = selfq_bias.shape[0]
    hidden_cols = expand_bias.shape[0]
    depth = selfq_weight.shape[0]
    slots = NBLK // 2
    two = 2 * head_cols
    attn_cols = 5 * head_cols
    info = jnp.stack([inner, rank, chip]).astype(jnp.int32)

    seq_order = jnp.stack([chip, 1 - chip])
    near = blocks[seq_order].reshape(2, 2, slots)
    near = jnp.stack([near[:, core], near[:, 1 - core]])
    near = near - rank * local_blocks
    held = (near >= 0) & (near < local_blocks)
    fetch_table = jnp.where(held, near + seq_order[None, :, None] * local_blocks, -1)
    fetch_table = fetch_table.reshape(-1).astype(jnp.int32)
    part_mine, part_send = fetch(fetch_table, bank.reshape(seq_count * local_blocks, BLK, width))

    part_got = swap_core(part_send)
    part_away = part_mine[1] + part_got[1]
    part_back = swap_x(part_away)

    self_leaf = call(
        pack_self_kernel,
        struct((outer, depth, 3 * head_cols), BF),
        [gate(selfq_weight, part_away), selfk_weight, selfv_weight],
        [VM] * 3,
        VM,
        name="pack_self",
    )
    bias_own = jnp.concatenate(
        [selfq_bias, selfv_bias, crossq_bias, crossv_bias, expand_bias]
    ).reshape(1, -1)
    bias_two = jnp.concatenate([bias_own, swap_x(bias_own)], axis=0)
    bias_four = jnp.concatenate([bias_two, swap_core(bias_two)], axis=0)
    cq_bias = bias_four[:, two : 3 * head_cols].reshape(-1)
    cv_bias = bias_four[:, 3 * head_cols : 4 * head_cols].reshape(-1)
    ex_bias = bias_four[:, 4 * head_cols :]
    self_bias = jnp.stack(
        [
            bias_two[:, :head_cols].reshape(-1),
            jnp.zeros((two,), F32),
            bias_two[:, head_cols:two].reshape(-1),
        ]
    )
    next_leaf, shrink_leaf = call(
        pack_rest_kernel,
        [
            struct((outer, depth, hidden_cols + attn_cols), BF),
            struct((depth, hidden_cols), BF),
        ],
        [
            gate(crossk_weight, self_leaf, part_away), crossv_weight, crossq_weight, selfo_weight,
            crosso_weight, expand_weight, shrink_weight.T,
        ],
        [VM] * 7,
        [VM] * 2,
        name="pack_rest",
    )
    tokens_oth = swap_core(tokens)
    vecs = jnp.concatenate(
        [
            jnp.stack([crosso_bias, second_gain, second_shift]),
            ex_bias,
            jnp.stack([shrink_bias, third_gain, third_shift]),
        ]
    )
    first_vecs = jnp.stack([selfo_bias, first_gain, first_shift])
    cq_bias, cv_bias = cq_bias.reshape(1, -1), cv_bias.reshape(1, -1)
    my_prefix = lax.dynamic_index_in_dim(prefix, chip, 0, keepdims=False)
    attn_info = jnp.stack([core, my_prefix]).astype(jnp.int32)

    self_z = outer_exchange(self_leaf)

    self_z, self_bias, vecs, first_vecs, cq_bias, cv_bias, next_leaf, attn_info, tokens_oth, part_back = (
        lax.optimization_barrier(
            (self_z, self_bias, vecs, first_vecs, cq_bias, cv_bias, next_leaf, attn_info, tokens_oth, part_back)
        )
    )
    self_near, self_away, self_both = swap_x(self_z), swap_dp(self_z, 1), swap_both(self_z)
    next_z = outer_exchange(next_leaf)

    shrink_leaf = gate(shrink_leaf, self_near)
    shrink_x, shrink_y = swap_x(shrink_leaf), swap_dp(shrink_leaf, 1)
    shrink_xy = swap_both(shrink_leaf)
    shrink_pack = plane_copies(info, shrink_leaf, shrink_x, shrink_y, shrink_xy)
    (
        next_z, tokens_in, self_near, self_away, self_both, shrink_pack, part_got,
    ) = lax.optimization_barrier(
        (next_z, tokens, self_near, self_away, self_both, shrink_pack, part_got)
    )
    expand_z, attn_z = next_z[..., :hidden_cols], next_z[..., hidden_cols:]
    shrink_z = outer_exchange(gate(shrink_pack, next_z))
    attn_x, attn_y, attn_xy = swap_x(attn_z), swap_dp(attn_z, 1), swap_both(attn_z)

    qkv, self_mat, self_own, self_send, self_lse = self_forward(
        jnp.concatenate([info, attn_info]),
        tokens_in,
        tokens_oth,
        self_bias,
        (self_z, self_near, self_away, self_both),
    )
    self_got = swap_core(self_send)
    attn_x, attn_y, attn_xy, self_got = lax.optimization_barrier(
        (attn_x, attn_y, attn_xy, self_got, self_own)
    )[:4]
    attn_own = (attn_z, attn_y, attn_x, attn_xy)
    attn_oth = tuple(swap_core(piece) for piece in attn_own)
    attn_oth, expand_z = lax.optimization_barrier((attn_oth, expand_z))
    expand_x, expand_y = swap_x(expand_z), swap_dp(expand_z, 1)
    cross_kv, cross_q, self_o, cross_o = assemble(info, attn_own + attn_oth)
    cross_kv, expand_x, expand_y = lax.optimization_barrier((cross_kv, expand_x, expand_y))
    expand_xy = swap_both(expand_z)
    fetched, kv_own = project_kv(
        (part_mine[0] + part_got[0]).reshape(slots * BLK, width),
        part_back.reshape(slots * BLK, width),
        cross_kv,
        cv_bias,
    )
    self_got, kv_own = lax.optimization_barrier((self_got, kv_own))
    kv_oth = swap_core(kv_own)
    first_sum, first_out, first_low, queries, mixed_one = first_forward(
        tokens,
        self_own,
        self_got,
        self_o,
        first_vecs,
        cross_q,
        cq_bias,
    )

    queries, kv_oth = lax.optimization_barrier((queries, kv_oth))
    queries, shrink_z = lax.optimization_barrier((queries, shrink_z))
    mixed_two, cross_lse = cross_forward(queries, kv_own, kv_oth)

    expand_oth = tuple(swap_core(piece) for piece in (expand_z, expand_y, expand_x))
    expand_xy, expand_oth, mixed_two = lax.optimization_barrier((expand_xy, expand_oth, mixed_two))
    expand_own = (expand_z, expand_y, expand_x, expand_xy)
    expand_oth = expand_oth + (swap_core(expand_xy),)
    (
        out_act, second_in, cross_low, cross_grad,
        feed_keep, feed_send,
    ) = feed(
        info, mixed_two, first_out, out_grad, vecs, cross_o,
        expand_own + expand_oth, (shrink_z, swap_core(shrink_z)),
    )

    def plane_send(keep, got):
        return tuple(add_low(keep[x, y], got[x, y]) for x, y in ((1, 0), (0, 1), (1, 1)))

    def plane_swap(parts):
        return swap_x(parts[0]), swap_dp(parts[1], 1), swap_both(parts[2])

    def plane_sum(own, got):
        total = sum(part.astype(F32) for part in own)
        return total + sum(part.astype(F32) for part in got)

    def fold(value, dtype):
        return jnp.sum(value.astype(F32), axis=0).astype(dtype)

    feed_got = swap_core(feed_send)
    part_one = cross_backward(queries, kv_own, kv_oth, mixed_two, cross_lse, cross_grad, 0, 2)
    feed_keep = gate(feed_keep, part_one[0])

    def feed_sum(x, y, which, *others):
        at = (x, y, Ellipsis, slice(which * hidden_cols, (which + 1) * hidden_cols))
        total = feed_keep[at].astype(F32) + feed_got[at].astype(F32)
        for other in others:
            total = total + other.astype(F32)
        return total.astype(BF)

    expand_send = feed_sum(1, slice(None), 0)
    shrink_send = feed_sum(slice(None), 1, 1)
    expand_send, shrink_send, part_one = lax.optimization_barrier(
        (expand_send, shrink_send, tuple(part_one))
    )
    expand_got = swap_x(expand_send)
    shrink_got = swap_dp(shrink_send, 1)

    dq, dkv_own, dkv_send, first_in, self_low, grad_own, grad_send, early_vec = cross_first_backward(
        queries, kv_own, kv_oth, mixed_two, cross_lse, cross_grad, 2, part_one,
        cross_q, second_in, first_sum, first_gain.reshape(1, -1), self_o,
    )
    expand_got, shrink_got, dkv_send, grad_send = lax.optimization_barrier(
        (expand_got, shrink_got, dkv_send, grad_send)
    )
    dkv_got = swap_core(dkv_send)
    grad_got = swap_core(grad_send)
    expand_send = feed_sum(0, 1, 0, expand_got[1])
    shrink_send = feed_sum(1, 0, 1, shrink_got[1])
    self_low, dkv_got, grad_got, expand_send, shrink_send = lax.optimization_barrier(
        (self_low, dkv_got, grad_got, expand_send, shrink_send)
    )
    expand_last = swap_dp(expand_send, 1)
    shrink_last = swap_x(shrink_send)
    attn_keep, attn_send, fetched_grad = attn_grads(
        info,
        (
            first_low, dq, self_low, mixed_one, cross_low, mixed_two, early_vec,
            fetched, dkv_own, dkv_got, cross_kv,
        ),
        depth,
    )
    attn_send, grad_got, expand_last, shrink_last = lax.optimization_barrier(
        (attn_send, grad_got, expand_last, shrink_last)
    )
    attn_got = swap_core(attn_send)
    feed_three = jnp.concatenate(
        [
            feed_sum(0, 0, 0, expand_got[0], expand_last),
            feed_sum(0, 0, 1, shrink_got[0], shrink_last),
        ],
        axis=-1,
    )
    feed_three, grad_got = lax.optimization_barrier((feed_three, grad_got))
    feed_last = outer_exchange(feed_three)

    self_args = (attn_info, qkv, self_own, self_send, self_lse, grad_own, grad_got)
    pairs = two // 128
    half_grads = self_backward(*self_args, 0, pairs - 1)
    attn_plane, half_grads, fetched_away = lax.optimization_barrier(
        (plane_send(gate(attn_keep, half_grads), attn_got), half_grads, swap_x(fetched_grad))
    )
    fetched_away = fetched_away.reshape(slots, BLK, width)
    fetched_near = fetched_grad.reshape(slots, BLK, width)
    attn_parts = plane_swap(attn_plane)
    grads = self_backward(*self_args, pairs - 1, 1, (half_grads,))
    self_places = self_grads(info, tokens, tokens_oth, grads, depth)
    self_places, grads = lax.optimization_barrier((tuple(self_places), grads))
    self_parts = (swap_x(self_places[1]), swap_dp(self_places[2], 1), swap_both(self_places[3]))
    back_keep, back_send = self_back(grads, self_mat, first_in)
    back_send, feed_last, attn_parts = lax.optimization_barrier((back_send, feed_last, attn_parts))
    attn_three = plane_sum((attn_keep[0, 0], attn_got[0, 0]), attn_parts).astype(BF)
    attn_last = outer_exchange(attn_three)
    self_three = plane_sum((self_places[0],), self_parts).astype(BF)
    self_last = outer_exchange(
        gate(self_three, attn_last)
    )
    back_got = swap_core(gate(back_send, self_three))
    in_grad = (back_keep + back_got.astype(F32)).astype(BF)

    (
        cq_grad, so_grad, co_grad, ck_grad, cv_grad, cq_rows, cv_rows,
        first_shift_rows, first_gain_rows, so_rows,
    ) = sum_attn(attn_last, depth)
    sq_grad, sk_grad, sv_grad, sq_rows, sk_rows, sv_rows = sum_cols(self_last, depth, 3)
    (
        expand_grad, shrink_grad, expand_rows, third_shift_rows, third_gain_rows, shrink_rows,
        second_shift_rows, second_gain_rows, co_rows,
    ) = sum_feed(feed_last, depth)
    shrink_grad = shrink_grad.T

    near_core = swap_core(gate(fetched_near, self_three))
    away_core = swap_core(gate(fetched_away, near_core))
    slot_ids = jnp.arange(NBLK)
    places = (
        (((slot_ids[None, :] // slots) != core) * 2 + (jnp.arange(seq_count)[:, None] != chip))
        * slots
        + slot_ids[None, :] % slots
    )
    hits = blocks[:, None, :] == (rank * local_blocks + jnp.arange(local_blocks))[None, :, None]
    scatter_table = jnp.max(jnp.where(hits, places[:, None, :], -1), axis=-1)
    bank_grad = scatter(
        scatter_table.reshape(-1).astype(jnp.int32),
        (fetched_near, fetched_away, near_core, away_core),
    ).reshape(bank.shape)

    def line(row):
        return row.reshape(-1)

    return (
        out_act,
        in_grad,
        bank_grad,
        sq_grad,
        line(sq_rows),
        sk_grad,
        sv_grad,
        line(sv_rows),
        so_grad,
        line(so_rows),
        line(first_gain_rows),
        line(first_shift_rows),
        cq_grad,
        line(cq_rows),
        ck_grad,
        cv_grad,
        line(cv_rows),
        co_grad,
        line(co_rows),
        line(second_gain_rows),
        line(second_shift_rows),
        expand_grad,
        line(expand_rows),
        shrink_grad,
        line(shrink_rows),
        line(third_gain_rows),
        line(third_shift_rows),
    )


def solution(mesh):
    rows = P(("dp", "tensor"), None)
    wide = P("dp", "tensor")
    tall = P("tensor", "dp")
    part = P("tensor")
    full = P()
    return jax.shard_map(
        local,
        mesh=mesh,
        in_specs=(
            rows, P("dp", "tensor", None), P("dp"), P("dp", None), rows,
            wide, part, wide, wide, part, tall, full, full, full,
            wide, part, wide, wide, part, tall, full, full, full,
            wide, part, tall, full, full, full,
        ),
        out_specs=(
            rows, rows, P("dp", "tensor", None),
            wide, part, wide, wide, part, tall, full, full, full,
            wide, part, wide, wide, part, tall, full, full, full,
            wide, part, tall, full, full, full,
        ),
        check_vma=False,
    )
```

```python
import functools
import math

import jax
import jax.numpy as jnp
from jax import lax
from jax.experimental import pallas as pl
from jax.experimental.pallas import tpu as pltpu
from jax.sharding import PartitionSpec as P

HD = 64
BLK = 64
NBLK = 16
EPS = 1e-05
NEGATIVE = -1e30
BF = jnp.bfloat16
F32 = jnp.float32

NT = (((1,), (1,)), ((), ()))
NN = (((1,), (0,)), ((), ()))
TN = (((0,), (0,)), ((), ()))

CORE_SWAP = ((0, 1), (1, 0), (2, 3), (3, 2))
X_SWAP = ((0, 2), (2, 0), (1, 3), (3, 1))
VMEM_LIMIT = 48 << 20
COST = pl.CostEstimate(flops=1000, bytes_accessed=1000, transcendentals=0)


def mm(left, right, dims=NN):
    return lax.dot_general(left, right, dims, preferred_element_type=F32)


def swap_core(value):
    return lax.ppermute(value, "tensor", CORE_SWAP)


def swap_x(value):
    return lax.ppermute(value, "tensor", X_SWAP)


def swap_dp(value, bit):
    count = lax.axis_size("dp")
    return lax.ppermute(value, "dp", tuple((i, i ^ bit) for i in range(count)))


def dp_bits():
    count = lax.axis_size("dp")
    bits = []
    bit = count // 2
    while bit >= 1:
        bits.append(bit)
        bit //= 2
    return bits


def pair_backward(q, k, v, grad, lse, delta, mask):
    score = mm(k, q, NT)
    prob = jnp.exp(score - lse)
    if mask is not None:
        prob = jnp.where(mask, prob, 0.0)
    slope = prob * (mm(v, grad, NT) - delta)
    prob = prob.astype(BF)
    slope = slope.astype(BF)
    return mm(k, slope, TN), mm(slope, q, NN), mm(prob, grad, NN)


def delta_row(grad, mixed):
    return jnp.sum((grad.astype(F32) * mixed.astype(F32)).T, 0, keepdims=True)


def self_bwd_kernel(info, q_ref, k_ref, v_ref, oa_ref, ob_ref, lse_ref, ga_ref, gb_ref, *rest):
    out_ref, o_ref, g_ref = rest[-3:]
    dq_ref, dk_ref, dv_ref = out_ref.at[0], out_ref.at[1], out_ref.at[2]
    o_ref[0], o_ref[1] = oa_ref[...], ob_ref[...]
    g_ref[0], g_ref[1] = ga_ref[...], gb_ref[...]
    half = q_ref.shape[1]
    first = info[0]
    second = 1 - first
    prefix = info[1]
    def positions(rows):
        shape = (rows, half)
        return lax.broadcasted_iota(jnp.int32, shape, 0), lax.broadcasted_iota(jnp.int32, shape, 1)

    key_pos, query_pos = positions(half)
    seen = (key_pos <= query_pos) | (key_pos < prefix)
    key_pos, query_pos = positions(2 * half)
    seen_late = key_pos <= query_pos + half
    scale = 1.0 / math.sqrt(HD)
    for h in range(2):
        cols = slice(HD * h, HD * h + HD)

        def rows(ref, at):
            return ref[at, :, cols]

        def both(ref):
            return jnp.concatenate([rows(ref, first), rows(ref, second)], axis=0)

        def one(at, key, value, mask):
            grad = rows(g_ref, at)
            delta = delta_row(grad, rows(o_ref, at))
            lse = lse_ref[0, h, pl.ds(at, 1), :]
            dq, dk, dv = pair_backward(rows(q_ref, at), key, value, grad, lse, delta, mask)
            dq_ref[at, :, cols] = (dq.T.astype(BF) * scale).astype(BF)
            return dk, dv

        dk_a, dv_a = one(first, rows(k_ref, first), rows(v_ref, first), seen)
        dk_b, dv_b = one(second, both(k_ref), both(v_ref), seen_late)
        dk_ref[first, :, cols] = (dk_a + dk_b[:half]).astype(BF)
        dv_ref[first, :, cols] = (dv_a + dv_b[:half]).astype(BF)
        dk_ref[second, :, cols] = dk_b[half:].astype(BF)
        dv_ref[second, :, cols] = dv_b[half:].astype(BF)


def self_backward(info, qkv, mixed_own, mixed_oth, lse, grad_own, grad_oth, start, count, former=()):
    half, width = qkv.shape[1], qkv.shape[2] // 3
    pairs = width // 128

    def spec(which):
        return pl.BlockSpec((2, half, 128), lambda i, info: (0, 0, which * pairs + start + i))

    flat = pl.BlockSpec((half, 128), lambda i, info: (0, start + i))
    cells = 3 * half * half * count * 2
    return pl.pallas_call(
        self_bwd_kernel,
        grid_spec=pltpu.PrefetchScalarGridSpec(
            num_scalar_prefetch=1,
            grid=(count,),
            in_specs=[
                spec(0),
                spec(1),
                spec(2),
                flat,
                flat,
                pl.BlockSpec((1, 2, 2, half), lambda i, info: (start + i, 0, 0, 0)),
                flat,
                flat,
            ]
            + [pl.BlockSpec(memory_space=pl.ANY)] * len(former),
            out_specs=pl.BlockSpec((3, 2, half, 128), lambda i, info: (0, 0, 0, start + i)),
            scratch_shapes=[pltpu.VMEM((2, half, 128), BF)] * 2,
        ),
        out_shape=jax.ShapeDtypeStruct((3, 2, half, width), BF),
        input_output_aliases={9 + i: i for i in range(len(former))},
        compiler_params=pltpu.CompilerParams(vmem_limit_bytes=VMEM_LIMIT),
        cost_estimate=COST,
        name="self_bwd",
    )(info, qkv, qkv, qkv, mixed_own, mixed_oth, lse, grad_own, grad_oth, *former)


def cross_fwd_kernel(q_ref, ka_ref, kb_ref, va_ref, vb_ref, o_ref, lse_ref):
    for h in range(2):
        cols = slice(HD * h, HD * h + HD)
        q = q_ref[:, cols]
        score_a = mm(ka_ref[:, cols], q, NT)
        score_b = mm(kb_ref[:, cols], q, NT)
        top = jnp.maximum(
            jnp.max(score_a, 0, keepdims=True), jnp.max(score_b, 0, keepdims=True)
        )
        expo_a = jnp.exp(score_a - top)
        expo_b = jnp.exp(score_b - top)
        total = jnp.sum(expo_a, 0, keepdims=True) + jnp.sum(expo_b, 0, keepdims=True)
        mixed = (
            mm(va_ref[:, cols], expo_a.astype(BF), TN) + mm(vb_ref[:, cols], expo_b.astype(BF), TN)
        ) / total
        o_ref[:, cols] = mixed.T.astype(BF)
        lse_ref[0, h : h + 1, :] = top + jnp.log(total)


def cross_specs(rows, pairs):
    whole = pl.BlockSpec((rows, 128), lambda i: (0, i))
    turned = pl.BlockSpec((rows, 128), lambda i: (0, (i + pairs // 2) % pairs))
    value = pl.BlockSpec((rows, 128), lambda i: (0, pairs + i))
    value_turned = pl.BlockSpec((rows, 128), lambda i: (0, pairs + (i + pairs // 2) % pairs))
    return whole, turned, value, value_turned


def cross_forward(queries, kv_own, kv_oth):
    rows, width = queries.shape
    pairs = width // 128
    whole, turned, value, value_turned = cross_specs(rows, pairs)
    cells = 2 * rows * rows * pairs * 2
    return pl.pallas_call(
        cross_fwd_kernel,
        grid=(pairs,),
        in_specs=[whole, whole, turned, value, value_turned],
        out_specs=[whole, pl.BlockSpec((1, 2, rows), lambda i: (i, 0, 0))],
        out_shape=[
            jax.ShapeDtypeStruct((rows, width), BF),
            jax.ShapeDtypeStruct((pairs, 2, rows), F32),
        ],
        compiler_params=pltpu.CompilerParams(vmem_limit_bytes=VMEM_LIMIT),
        cost_estimate=COST,
        name="cross_fwd",
    )(queries, kv_own, kv_oth, kv_own, kv_oth)


def cross_bwd_kernel(
    q_ref, ka_ref, kb_ref, va_ref, vb_ref, o_ref, lse_ref, g_ref,
    *rest,
):
    dq_ref, da_ref, db_ref = rest[-3:]
    scale = 1.0 / math.sqrt(HD)
    for h in range(2):
        cols = slice(HD * h, HD * h + HD)
        grad = g_ref[:, cols]
        delta = delta_row(grad, o_ref[:, cols])
        lse = lse_ref[0, h : h + 1, :]
        q = q_ref[:, cols]
        rows = q.shape[0]
        key = jnp.concatenate([ka_ref[:, cols], kb_ref[:, cols]], axis=0)
        value = jnp.concatenate([va_ref[:, cols], vb_ref[:, cols]], axis=0)
        dq, dk, dv = pair_backward(q, key, value, grad, lse, delta, None)
        da_ref[0, :, cols] = dk[:rows].astype(BF)
        da_ref[1, :, cols] = dv[:rows].astype(BF)
        db_ref[0, :, cols] = dk[rows:].astype(BF)
        db_ref[1, :, cols] = dv[rows:].astype(BF)
        dq_ref[:, cols] = (dq.T.astype(BF) * scale).astype(BF)


def cross_backward(queries, kv_own, kv_oth, mixed, lse, grad, start, count, former=()):
    rows, width = queries.shape
    pairs = width // 128

    def turn(i):
        return (start + i + pairs // 2) % pairs

    whole = pl.BlockSpec((rows, 128), lambda i: (0, start + i))
    turned = pl.BlockSpec((rows, 128), lambda i: (0, turn(i)))
    value = pl.BlockSpec((rows, 128), lambda i: (0, pairs + start + i))
    value_turned = pl.BlockSpec((rows, 128), lambda i: (0, pairs + turn(i)))
    cells = 2 * rows * rows * count * 2
    both = jax.ShapeDtypeStruct((2, rows, width), BF)
    return pl.pallas_call(
        cross_bwd_kernel,
        grid=(count,),
        in_specs=[
            whole, whole, turned, value, value_turned, whole,
            pl.BlockSpec((1, 2, rows), lambda i: (start + i, 0, 0)), whole,
        ]
        + [pl.BlockSpec(memory_space=pl.ANY)] * len(former),
        out_specs=[
            whole,
            pl.BlockSpec((2, rows, 128), lambda i: (0, 0, start + i)),
            pl.BlockSpec((2, rows, 128), lambda i: (0, 0, turn(i))),
        ],
        out_shape=[jax.ShapeDtypeStruct((rows, width), BF), both, both],
        input_output_aliases={8 + i: i for i in range(len(former))},
        compiler_params=pltpu.CompilerParams(vmem_limit_bytes=VMEM_LIMIT),
        cost_estimate=COST,
        name="cross_bwd",
    )(queries, kv_own, kv_oth, kv_own, kv_oth, mixed, lse, grad, *former)


def norm_parts(resid):
    center = resid - jnp.mean(resid, axis=-1, keepdims=True)
    rstd = lax.rsqrt(jnp.mean(center * center, axis=-1, keepdims=True) + EPS)
    return center * rstd, rstd


def norm_back(normed, rstd, grad, gain):
    scaled = grad * gain
    return rstd * (
        scaled
        - jnp.mean(scaled, axis=-1, keepdims=True)
        - normed * jnp.mean(scaled * normed, axis=-1, keepdims=True)
    )


def cross_first_kernel(
    q_ref, ka_ref, kb_ref, va_ref, vb_ref, o_ref, lse_ref, g_ref,
    q_mat, second_ref, resid_ref, vec_ref, o_mat, dq_in, former_a, former_b,
    dq_ref, da_ref, db_ref, first_ref, low_ref, keep_ref, send_ref, sums_ref, dq_part,
    *, start, count,
):
    step = pl.program_id(0)

    @pl.when(step == 0)
    def _():
        dq_ref[...] = dq_in[...]

    cross_bwd_kernel(
        q_ref, ka_ref, kb_ref, va_ref, vb_ref, o_ref, lse_ref, g_ref, dq_part, da_ref, db_ref
    )
    at = pl.multiple_of((start + step) * 128, 128)
    dq_ref[:, pl.ds(at, 128)] = dq_part[...]

    @pl.when(step == count - 1)
    def _():
        grad = second_ref[...] + mm(dq_ref[...], q_mat[...], NT)
        normed, rstd = norm_parts(resid_ref[...])
        sums_ref[0:1, :] = jnp.sum(grad, 0, keepdims=True)
        sums_ref[1:2, :] = jnp.sum(grad * normed, 0, keepdims=True)
        first_in = norm_back(normed, rstd, grad, vec_ref[0:1, :])
        first_ref[...] = first_in
        low = first_in.astype(BF)
        low_ref[...] = low
        sums_ref[2:3, :] = jnp.sum(low.astype(F32), 0, keepdims=True)
        sums_ref[3:4, :] = jnp.sum(dq_ref[...].astype(F32), 0, keepdims=True)
        sums_ref[4:8, :] = jnp.zeros((4, sums_ref.shape[1]), F32)
        mixed_grad = mm(low, o_mat[...]).astype(BF)
        cols = keep_ref.shape[1]
        keep_ref[...] = mixed_grad[:, :cols]
        send_ref[...] = mixed_grad[:, cols:]


def cross_first_backward(
    queries, kv_own, kv_oth, mixed, lse, grad, start, former, q_mat, second_in, resid, vec, o_mat
):
    rows, width = queries.shape
    pairs = width // 128
    count = pairs - start

    def turn(i):
        return (start + i + pairs // 2) % pairs

    whole = pl.BlockSpec((rows, 128), lambda i: (0, start + i))
    turned = pl.BlockSpec((rows, 128), lambda i: (0, turn(i)))
    value = pl.BlockSpec((rows, 128), lambda i: (0, pairs + start + i))
    value_turned = pl.BlockSpec((rows, 128), lambda i: (0, pairs + turn(i)))

    def fixed(shape):
        return pl.BlockSpec(shape, lambda i: (0, 0))

    both = jax.ShapeDtypeStruct((2, rows, width), BF)
    return pl.pallas_call(
        functools.partial(cross_first_kernel, start=start, count=count),
        grid=(count,),
        in_specs=[
            whole, whole, turned, value, value_turned, whole,
            pl.BlockSpec((1, 2, rows), lambda i: (start + i, 0, 0)), whole,
            fixed((width, width)), fixed((rows, width)), fixed((rows, width)),
            fixed((1, width)), fixed((width, width)), fixed((rows, width)),
            pl.BlockSpec(memory_space=pl.ANY), pl.BlockSpec(memory_space=pl.ANY),
        ],
        out_specs=[
            fixed((rows, width)),
            pl.BlockSpec((2, rows, 128), lambda i: (0, 0, start + i)),
            pl.BlockSpec((2, rows, 128), lambda i: (0, 0, turn(i))),
            fixed((rows, width)),
            fixed((rows, width)),
            fixed((rows, width // 2)),
            fixed((rows, width // 2)),
            fixed((8, width)),
        ],
        out_shape=[
            jax.ShapeDtypeStruct((rows, width), BF),
            both,
            both,
            jax.ShapeDtypeStruct((rows, width), F32),
            jax.ShapeDtypeStruct((rows, width), BF),
            jax.ShapeDtypeStruct((rows, width // 2), BF),
            jax.ShapeDtypeStruct((rows, width // 2), BF),
            jax.ShapeDtypeStruct((8, width), F32),
        ],
        scratch_shapes=[pltpu.VMEM((rows, 128), BF)],
        input_output_aliases={14: 1, 15: 2},
        compiler_params=pltpu.CompilerParams(vmem_limit_bytes=VMEM_LIMIT),
        cost_estimate=COST,
        name="cross_first",
    )(
        queries, kv_own, kv_oth, kv_own, kv_oth, mixed, lse, grad,
        q_mat, second_in, resid, vec, o_mat, *former,
    )


def gate(value, *others):
    return lax.optimization_barrier((value,) + others)[0]


def outer_count():
    return lax.axis_size("dp") // 2


def swap_both(value):
    count = lax.axis_size("dp")
    pairs = tuple(
        (d * 4 + t, (d ^ 1) * 4 + (t ^ 2)) for d in range(count) for t in range(4)
    )
    return lax.ppermute(value, ("dp", "tensor"), pairs)


def outer_exchange(value):
    groups = [[inner + 2 * o for o in range(outer_count())] for inner in range(2)]
    return lax.all_to_all(value, "dp", 0, 0, axis_index_groups=groups, tiled=True)


def plane_exchange(value):
    groups = [
        [(o * 2 + inner) * 4 + chip * 2 + core for chip in range(2) for inner in range(2)]
        for o in range(outer_count())
        for core in range(2)
    ]
    return lax.all_to_all(value, ("dp", "tensor"), 0, 0, axis_index_groups=groups, tiled=True)


def add_low(left, right):
    return (left.astype(F32) + right.astype(F32)).astype(BF)


def total_dp(value):
    for bit in dp_bits():
        value = value + swap_dp(value, bit)
    return value


ANY = pl.BlockSpec(memory_space=pl.ANY)
VM = pl.BlockSpec(memory_space=pltpu.VMEM)
SM = pl.BlockSpec(memory_space=pltpu.SMEM)


def call(kernel, out_shape, args, in_specs, out_specs, scratch=(), flops=0, moved=0, name=None):
    return pl.pallas_call(
        kernel,
        out_shape=out_shape,
        in_specs=in_specs,
        out_specs=out_specs,
        scratch_shapes=list(scratch),
        compiler_params=pltpu.CompilerParams(vmem_limit_bytes=58 << 20),
        cost_estimate=COST,
        name=name,
    )(*args)


def struct(shape, dtype):
    return jax.ShapeDtypeStruct(shape, dtype)


def tail_start(depth):
    return (depth + 15) // 16 * 16


def high_low(row):
    high = row.astype(BF).astype(F32)
    return high, row - high


def stack_rows(rows, count):
    cols = rows[0].shape[1]
    at = lax.broadcasted_iota(jnp.int32, (count, cols), 0)
    total = jnp.zeros((count, cols), F32)
    for i, row in enumerate(rows):
        total = jnp.where(at == i, row, total)
    return total.astype(BF)


def pack_self_kernel(q_ref, k_ref, v_ref, out_ref):
    cols = q_ref.shape[1]
    for i, ref in enumerate((q_ref, k_ref, v_ref)):
        low = ref[...].astype(BF)
        for copy in range(out_ref.shape[0]):
            out_ref[copy, :, i * cols : (i + 1) * cols] = low


def turned(ref):
    depth = ref.shape[1]
    eye = (
        lax.broadcasted_iota(jnp.int32, (depth, depth), 0)
        == lax.broadcasted_iota(jnp.int32, (depth, depth), 1)
    )
    eye = jnp.where(eye, 1.0, 0.0).astype(BF)
    return mm(eye, ref[...].astype(BF), NT).astype(BF)


def pack_rest_kernel(ck_ref, cv_ref, cq_ref, so_ref, co_ref, ex_ref, sh_ref, next_ref, sh_out):
    cols = ck_ref.shape[1]
    wide = ex_ref.shape[1]
    parts = [ref[...].astype(BF) for ref in (ck_ref, cv_ref, cq_ref)]
    parts += [turned(so_ref), turned(co_ref)]
    expand = ex_ref[...].astype(BF)
    for copy in range(next_ref.shape[0]):
        next_ref[copy, :, :wide] = expand
        for i, low in enumerate(parts):
            next_ref[copy, :, wide + i * cols : wide + (i + 1) * cols] = low
    sh_out[...] = sh_ref[...].astype(BF)


def self_forward_kernel(
    info, own_ref, oth_ref, bias_ref, w_ref, wx_ref, wy_ref, wxy_ref,
    qkv_ref, mat_ref, oa_ref, ob_ref, lse_ref, w_own, w_x, o_ref, sems,
):
    pair = pl.program_id(0)
    width = own_ref.shape[1]
    half = own_ref.shape[0]
    wide = qkv_ref.shape[2] // 3

    @pl.when(pair == 0)
    def _():
        place = info[0]
        cols = w_own.shape[3]
        copies = [
            pltpu.make_async_copy(w_ref, w_own.at[:, place], sems.at[0]),
            pltpu.make_async_copy(wy_ref, w_own.at[:, 1 - place], sems.at[1]),
            pltpu.make_async_copy(wx_ref, w_x.at[:, place], sems.at[2]),
            pltpu.make_async_copy(wxy_ref, w_x.at[:, 1 - place], sems.at[3]),
        ]
        for copy in copies:
            copy.start()
        for copy in copies:
            copy.wait()
        piece = cols // 3
        scale = 1.0 / math.sqrt(HD)
        for x, ref in enumerate((w_own, w_x)):
            mat = ref[...].reshape(width, cols)
            for i in range(3):
                at = (2 * i + x) * piece
                mat_ref[:, at : at + piece] = mat[:, i * piece : (i + 1) * piece]
        for rel, src in enumerate((own_ref, oth_ref)):
            for i in range(3):
                at = slice(wide * i, wide * (i + 1))
                part = mm(src[...], mat_ref[:, at]) + bias_ref[i : i + 1, :]
                if i == 0:
                    part = part * scale
                qkv_ref[rel, :, at] = part.astype(BF)

    first = info[3]
    second = 1 - first
    prefix = info[4]
    key_pos = lax.broadcasted_iota(jnp.int32, (half, half), 0)
    query_pos = lax.broadcasted_iota(jnp.int32, (half, half), 1)
    causal = key_pos <= query_pos
    seen = causal | (key_pos < prefix)

    def load(which, at):
        start = pl.multiple_of(which * wide + pair * 128, 128)
        return qkv_ref[at, :, pl.ds(start, 128)]

    q_both = (load(0, first), load(0, second))
    k_both = (load(1, first), load(1, second))
    v_both = (load(2, first), load(2, second))
    for h in range(2):
        cols = slice(HD * h, HD * h + HD)
        k0, k1 = (k[:, cols] for k in k_both)
        v0, v1 = (v[:, cols] for v in v_both)
        q0, q1 = (q[:, cols] for q in q_both)
        score = jnp.where(seen, mm(k0, q0, NT), NEGATIVE)
        top = jnp.max(score, 0, keepdims=True)
        expo = jnp.exp(score - top)
        total = jnp.sum(expo, 0, keepdims=True)
        mixed = mm(v0, expo.astype(BF), TN) / total
        o_ref[first, :, cols] = mixed.T.astype(BF)
        lse_ref[0, h, pl.ds(first, 1), :] = top + jnp.log(total)

        score_a = mm(k0, q1, NT)
        score_b = jnp.where(causal, mm(k1, q1, NT), NEGATIVE)
        top = jnp.maximum(
            jnp.max(score_a, 0, keepdims=True), jnp.max(score_b, 0, keepdims=True)
        )
        expo_a = jnp.exp(score_a - top)
        expo_b = jnp.exp(score_b - top)
        total = jnp.sum(expo_a, 0, keepdims=True) + jnp.sum(expo_b, 0, keepdims=True)
        mixed = (mm(v0, expo_a.astype(BF), TN) + mm(v1, expo_b.astype(BF), TN)) / total
        o_ref[second, :, cols] = mixed.T.astype(BF)
        lse_ref[0, h, pl.ds(second, 1), :] = top + jnp.log(total)
    oa_ref[...] = o_ref[0]
    ob_ref[...] = o_ref[1]


def self_forward(info, own, oth, bias, pieces):
    half, width = own.shape
    outer, depth, cols = pieces[0].shape
    wide = 2 * cols // 3
    pairs = wide // 128
    fixed2 = pl.BlockSpec((half, width), lambda i, info: (0, 0))
    pair_cols = pl.BlockSpec((half, 128), lambda i, info: (0, i))
    return pl.pallas_call(
        self_forward_kernel,
        grid_spec=pltpu.PrefetchScalarGridSpec(
            num_scalar_prefetch=1,
            grid=(pairs,),
            in_specs=[
                fixed2,
                fixed2,
                pl.BlockSpec(bias.shape, lambda i, info: (0, 0)),
                ANY,
                ANY,
                ANY,
                ANY,
            ],
            out_specs=[
                pl.BlockSpec((2, half, 3 * wide), lambda i, info: (0, 0, 0)),
                pl.BlockSpec((width, 3 * wide), lambda i, info: (0, 0)),
                pair_cols,
                pair_cols,
                pl.BlockSpec((1, 2, 2, half), lambda i, info: (i, 0, 0, 0)),
            ],
            scratch_shapes=[
                pltpu.VMEM((outer, 2, depth, cols), BF),
                pltpu.VMEM((outer, 2, depth, cols), BF),
                pltpu.VMEM((2, half, 128), BF),
                pltpu.SemaphoreType.DMA((4,)),
            ],
        ),
        out_shape=[
            struct((2, half, 3 * wide), BF),
            struct((width, 3 * wide), BF),
            struct((half, wide), BF),
            struct((half, wide), BF),
            struct((pairs, 2, 2, half), F32),
        ],
        compiler_params=pltpu.CompilerParams(vmem_limit_bytes=VMEM_LIMIT),
        cost_estimate=COST,
        name="self_fwd",
    )(info, own, oth, bias, *pieces)


def assemble_kernel(info, *refs):
    pieces, (kv_ref, q_ref, so_ref, co_ref) = refs[:8], refs[8:]
    place = info[0]
    outer, depth, cols = pieces[0].shape
    piece = cols // 5
    for j in range(4):
        for y in range(2):
            at = place if y == 0 else 1 - place
            for o in range(outer):
                value = pieces[2 * j + y][o]
                own = slice(piece * j, piece * (j + 1))
                low = slice(4 * piece + piece * j, 4 * piece + piece * (j + 1))
                kv_ref[o, at, :, own] = value[:, :piece]
                kv_ref[o, at, :, low] = value[:, piece : 2 * piece]
                q_ref[o, at, :, own] = value[:, 2 * piece : 3 * piece]
                so_ref[o, at, :, own] = value[:, 3 * piece : 4 * piece]
                co_ref[o, at, :, own] = value[:, 4 * piece :]


def assemble(info, pieces):
    outer, depth, cols = pieces[0].shape
    wide = cols // 5 * 4
    outs = call(
        assemble_kernel,
        [struct((outer, 2, depth, 2 * wide), BF)] + [struct((outer, 2, depth, wide), BF)] * 3,
        [info] + list(pieces),
        [SM] + [VM] * 8,
        [VM] * 4,
        moved=pieces[0].size * 32,
        name="assemble",
    )
    return [out.reshape(-1, out.shape[-1]) for out in outs]


def copies_kernel(info, own_ref, x_ref, y_ref, xy_ref, out_ref):
    place = info[0]
    for copy in range(out_ref.shape[0]):
        out_ref[copy, 0, place] = own_ref[...]
        out_ref[copy, 0, 1 - place] = y_ref[...]
        out_ref[copy, 1, place] = x_ref[...]
        out_ref[copy, 1, 1 - place] = xy_ref[...]


def plane_copies(info, own, x, y, xy):
    depth, cols = own.shape
    outer = outer_count()
    return call(
        copies_kernel,
        struct((outer, 2, 2, depth, cols), BF),
        [info, own, x, y, xy],
        [SM] + [VM] * 4,
        VM,
        moved=own.size * 2 * 4 * (outer + 1),
        name="plane_copies",
    )


def first_forward_kernel(
    tok_ref, own_ref, oth_ref, o_mat, vec_ref, q_mat, qb_ref,
    resid_ref, first_ref, low_ref, q_ref, mixed_ref,
):
    cols = own_ref.shape[1]
    mixed_ref[:, :cols] = own_ref[...]
    mixed_ref[:, cols:] = oth_ref[...]
    resid = tok_ref[...].astype(F32) + mm(mixed_ref[...], o_mat[...], NT) + vec_ref[0:1, :]
    resid_ref[...] = resid
    normed, rstd = norm_parts(resid)
    first = normed * vec_ref[1:2, :] + vec_ref[2:3, :]
    first_ref[...] = first
    low_ref[...] = first.astype(BF)
    scale = 1.0 / math.sqrt(HD)
    q_ref[...] = ((mm(low_ref[...], q_mat[...]) + qb_ref[...]) * scale).astype(BF)


def first_forward(tokens, own, oth, o_mat, vecs, q_mat, q_bias):
    rows, width = tokens.shape
    return call(
        first_forward_kernel,
        [struct((rows, width), F32)] * 2 + [struct((rows, width), BF)] * 3,
        [tokens, own, oth, o_mat, vecs, q_mat, q_bias],
        [VM] * 7,
        [VM] * 5,
        flops=2 * rows * width * width * 2 * 2,
        moved=width * width * 4 + rows * width * 18,
        name="first_forward",
    )


def project_kv_kernel(keep_ref, got_ref, mat_ref, bias_ref, fet_ref, out_ref):
    fet_ref[...] = keep_ref[...] + got_ref[...]
    width = fet_ref.shape[1]
    out_ref[:, :width] = mm(fet_ref[...], mat_ref[:, :width]).astype(BF)
    out_ref[:, width:] = (mm(fet_ref[...], mat_ref[:, width:]) + bias_ref[...]).astype(BF)


def project_kv(keep, got, mat, bias):
    rows, width = keep.shape
    return call(
        project_kv_kernel,
        [struct((rows, width), BF), struct((rows, 2 * width), BF)],
        [keep, got, mat, bias],
        [VM] * 4,
        [VM] * 2,
        name="project_kv",
    )


def feed_kernel(
    info, mixed_ref, first_ref, cot_ref, vec_ref, wo_hbm,
    e0, e1, e2, e3, e4, e5, e6, e7, s0, s1,
    out_ref, second_ref, low_ref, grad_ref,
    keep_ref, send_ref, sums_ref, tail,
    wo, we, ws, hid, slo, out_a, out_b, norm2, h2low, e3low, acc, wsem, osem, tsem,
):
    first_copy = pltpu.make_async_copy(wo_hbm, wo, wsem.at[0])
    first_copy.start()
    place = info[0]
    copies = []
    for j, pair in enumerate(((e0, e1), (e2, e3), (e4, e5), (e6, e7))):
        for y, ref in enumerate(pair):
            at = place if y == 0 else 1 - place
            copies.append(pltpu.make_async_copy(ref, we.at[j, :, at], wsem.at[1 + 2 * j + y]))
    for j in range(4):
        ref = (s0, s1)[j // 2]
        copies.append(pltpu.make_async_copy(ref.at[:, j % 2], ws.at[j], wsem.at[9 + j]))
    for copy in copies:
        copy.start()

    width = first_ref.shape[1]
    hidden_cols = we.shape[-1]
    outer, depth = we.shape[1], we.shape[3]
    base = out_a.shape[3]

    def expand_mat(j):
        return we[j].reshape(width, hidden_cols)

    def shrink_mat(j):
        return ws[j].reshape(width, hidden_cols)

    def row(i):
        return vec_ref[i : i + 1, :]

    first_copy.wait()
    resid = first_ref[...] + mm(mixed_ref[...], wo[...], NT) + row(0)
    normed, rstd2 = norm_parts(resid)
    norm2[...] = normed
    second = normed * row(1) + row(2)
    h2low[...] = second.astype(BF)
    acc[...] = second + row(7)
    for copy in copies:
        copy.wait()

    def forward(j, carry):
        inner = mm(h2low[...], expand_mat(j)) + vec_ref[pl.ds(3 + j, 1), :]
        phi = 0.5 + 0.5 * lax.erf(inner * (1.0 / math.sqrt(2.0)))
        hidden = (inner * phi).astype(BF)
        hid[j] = hidden
        bell = jnp.exp(-0.5 * inner * inner) * (1.0 / math.sqrt(2.0 * math.pi))
        slo[j] = (phi + inner * bell).astype(BF)
        acc[...] += mm(hidden, shrink_mat(j), NT)
        return carry

    lax.fori_loop(0, 4, forward, 0)
    norm3, rstd3 = norm_parts(acc[...])
    out_ref[...] = (norm3 * row(8) + row(9)).astype(BF)
    cot = cot_ref[...].astype(F32)
    sums_ref[0:1, :] = jnp.sum(cot, 0, keepdims=True)
    sums_ref[1:2, :] = jnp.sum(cot * norm3, 0, keepdims=True)
    third = norm_back(norm3, rstd3, cot, row(8))
    low = third.astype(BF)
    e3low[...] = low
    sums_ref[2:3, :] = jnp.sum(low.astype(F32), 0, keepdims=True)
    acc[...] = third

    def out_copies(to, at, slot):
        copies = []
        for y in range(2):
            for i, part in enumerate((out_a, out_b)):
                copies.append(
                    pltpu.make_async_copy(
                        part.at[slot, :, y],
                        to.at[
                            at, y ^ place, :, :base, i * hidden_cols : (i + 1) * hidden_cols
                        ],
                        osem.at[i, slot, y],
                    )
                )
        return copies

    def backward(step, carry):
        j = (step + 2) % 4
        slot = step % 2
        slope = slo[j].astype(F32)
        inner_grad = (mm(e3low[...], shrink_mat(j)) * slope).astype(BF)
        sums_ref[pl.ds(8 + j, 1), :] = jnp.sum(
            inner_grad.astype(F32), 0, keepdims=True
        )

        @pl.when(step >= 2)
        def _():
            for copy in out_copies(send_ref, slot, slot):
                copy.wait()

        shape = (outer, 2, depth, hidden_cols)
        out_a[slot, :, :, :depth] = mm(h2low[...], inner_grad, TN).astype(BF).reshape(shape)
        out_b[slot, :, :, :depth] = mm(e3low[...], hid[j], TN).astype(BF).reshape(shape)

        @pl.when(step < 2)
        def _():
            for copy in out_copies(send_ref, slot, slot):
                copy.start()

        @pl.when(step >= 2)
        def _():
            for copy in out_copies(keep_ref, slot, slot):
                copy.start()

        acc[...] += mm(inner_grad, expand_mat(j), NT)
        return carry

    lax.fori_loop(0, 4, backward, 0)
    grad = acc[...]
    normed = norm2[...]
    sums_ref[3:4, :] = jnp.sum(grad, 0, keepdims=True)
    sums_ref[4:5, :] = jnp.sum(grad * normed, 0, keepdims=True)
    second_in = norm_back(normed, rstd2, grad, row(1))
    second_ref[...] = second_in
    low = second_in.astype(BF)
    low_ref[...] = low
    sums_ref[5:6, :] = jnp.sum(low.astype(F32), 0, keepdims=True)
    tails = []
    pairs = [high_low(sums_ref[i : i + 1, :]) for i in range(6)]
    for j in range(4):
        rows_e = list(high_low(sums_ref[8 + j : 9 + j, :])) + [r for p in pairs[:3] for r in p]
        rows_s = [r for p in pairs[3:] for r in p]
        for o in range(outer):
            tail[j, o, :, :hidden_cols] = stack_rows(rows_e, 8)
            tail[j, o, :, hidden_cols:] = stack_rows(rows_s, 8)
        for y in range(2):
            to = (keep_ref, send_ref)[j // 2]
            tails.append(
                pltpu.make_async_copy(tail.at[j], to.at[j % 2, y, :, base:, :], tsem.at[2 * j + y])
            )
    for copy in tails:
        copy.start()
    grad_ref[...] = mm(low, wo[...]).astype(BF)
    for slot in range(2):
        for copy in out_copies(keep_ref, slot, slot):
            copy.wait()
    for copy in tails:
        copy.wait()


def feed(info, mixed, first, cot, vecs, wo, expand, shrink):
    rows, width = mixed.shape
    outer, depth, hidden = expand[0].shape
    base = tail_start(depth)
    grads = struct((2, 2, outer, base + 8, 2 * hidden), BF)
    return call(
        feed_kernel,
        [
            struct((rows, width), BF),
            struct((rows, width), F32),
            struct((rows, width), BF),
            struct((rows, width), BF),
            grads,
            grads,
        ],
        [info, mixed, first, cot, vecs, wo] + list(expand) + list(shrink),
        [SM, VM, VM, VM, VM] + [ANY] * 11,
        [VM] * 4 + [ANY] * 2,
        [
            pltpu.VMEM((16, width), F32),
            pltpu.VMEM((4, outer, 8, 2 * hidden), BF),
            pltpu.VMEM((width, width), BF),
            pltpu.VMEM((4, outer, 2, depth, hidden), BF),
            pltpu.VMEM((4, outer, 2, depth, hidden), BF),
            pltpu.VMEM((4, rows, hidden), BF),
            pltpu.VMEM((4, rows, hidden), BF),
            pltpu.VMEM((2, outer, 2, base, hidden), BF),
            pltpu.VMEM((2, outer, 2, base, hidden), BF),
            pltpu.VMEM((rows, width), F32),
            pltpu.VMEM((rows, width), BF),
            pltpu.VMEM((rows, width), BF),
            pltpu.VMEM((rows, width), F32),
            pltpu.SemaphoreType.DMA((13,)),
            pltpu.SemaphoreType.DMA((2, 2, 2)),
            pltpu.SemaphoreType.DMA((8,)),
        ],
        flops=2 * rows * width * (6 * 4 * hidden + 2 * width) * 2,
        moved=width * hidden * 4 * 4 * 2,
        name="feed",
    )


def first_back_kernel(
    dq_ref, q_mat, second_ref, resid_ref, vec_ref, o_mat, first_ref, low_ref, keep_ref, send_ref, sums_ref
):
    grad = second_ref[...] + mm(dq_ref[...], q_mat[...], NT)
    normed, rstd = norm_parts(resid_ref[...])
    sums_ref[0:1, :] = jnp.sum(grad, 0, keepdims=True)
    sums_ref[1:2, :] = jnp.sum(grad * normed, 0, keepdims=True)
    first_in = norm_back(normed, rstd, grad, vec_ref[0:1, :])
    first_ref[...] = first_in
    low = first_in.astype(BF)
    low_ref[...] = low
    sums_ref[2:3, :] = jnp.sum(low.astype(F32), 0, keepdims=True)
    sums_ref[3:4, :] = jnp.sum(dq_ref[...].astype(F32), 0, keepdims=True)
    sums_ref[4:8, :] = jnp.zeros((4, sums_ref.shape[1]), F32)
    mixed_grad = mm(low, o_mat[...]).astype(BF)
    cols = keep_ref.shape[1]
    keep_ref[...] = mixed_grad[:, :cols]
    send_ref[...] = mixed_grad[:, cols:]


def first_back(dq, q_mat, second_in, resid, vec, o_mat):
    rows, width = dq.shape
    cols = width // 2
    return call(
        first_back_kernel,
        [
            struct((rows, width), F32),
            struct((rows, width), BF),
            struct((rows, cols), BF),
            struct((rows, cols), BF),
            struct((8, width), F32),
        ],
        [dq, q_mat, second_in, resid, vec, o_mat],
        [VM] * 6,
        [VM] * 5,
        flops=2 * rows * width * width * 2 * 2,
        moved=width * width * 4 + rows * width * 18,
        name="first_back",
    )


def put_rows(ref, x, full, at, place):
    outer = ref.shape[2]
    depth = full.shape[0] // outer // 2
    for o in range(outer):
        for y in range(2):
            start = (2 * o + y) * depth
            ref[x, y ^ place, o, :depth, at] = full[start : start + depth]


def put_blocks(keep_ref, send_ref, full, i, place):
    piece = full.shape[1] // 4
    at = slice(i * piece, (i + 1) * piece)
    for j in range(4):
        put_rows((keep_ref, send_ref)[j // 2], j % 2, full[:, j * piece : (j + 1) * piece], at, place)


def attn_grads_kernel(
    info, h1_ref, dq_ref, e1_ref, o1_ref, e2_ref, o2_ref, sums_ref,
    fet_ref, own_ref, got_ref, mat_ref, keep_ref, send_ref, grad_ref,
):
    place = info[0]
    width = dq_ref.shape[1]
    piece = width // 4
    outer, rows = keep_ref.shape[2], keep_ref.shape[3]
    for i, (left, right) in enumerate(((h1_ref, dq_ref), (e1_ref, o1_ref), (e2_ref, o2_ref))):
        full = mm(left[...], right[...], TN).astype(BF)
        put_blocks(keep_ref, send_ref, full, i, place)
    total = None
    for i in range(2):
        low = add_low(own_ref[i], got_ref[i])
        full = mm(fet_ref[...], low, TN).astype(BF)
        put_blocks(keep_ref, send_ref, full, 3 + i, place)
        term = mm(low, mat_ref[:, i * width : (i + 1) * width], NT)
        total = term if total is None else total + term
    grad_ref[...] = total.astype(BF)
    parts = [high_low(sums_ref[i : i + 1, :]) for i in range(4)]
    value_sums = high_low(jnp.sum(low.astype(F32), 0, keepdims=True))
    empty = jnp.zeros((1, piece), F32)
    for j in range(4):
        own = slice(j * piece, (j + 1) * piece)
        ref = (keep_ref, send_ref)[j // 2]
        for i in range(5):
            lines = [empty] * 8
            if i < 3:
                lines = [parts[i][0][:, p * piece : (p + 1) * piece] for p in range(4)]
                lines += [parts[i][1][:, p * piece : (p + 1) * piece] for p in range(4)]
            if i == 0:
                lines += [parts[3][0][:, own], parts[3][1][:, own]]
            if i == 4:
                lines += [value_sums[0][:, own], value_sums[1][:, own]]
            block = stack_rows(lines, 16)
            for o in range(outer):
                for y in range(2):
                    ref[j % 2, y, o, rows - 16 :, i * piece : (i + 1) * piece] = block


def attn_grads(info, args, depth):
    rows, width = args[0].shape
    out = struct((2, 2, width // depth // 2, tail_start(depth) + 16, 5 * width // 4), BF)
    return call(
        attn_grads_kernel,
        [out, out, struct((rows, width), BF)],
        [info] + list(args),
        [SM] + [VM] * 11,
        [VM] * 3,
        name="attn_grads",
    )


def self_grads_kernel(info, own_ref, oth_ref, d_ref, a_ref, x_ref, y_ref, xy_ref):
    place = info[0]
    cols = d_ref.shape[3]
    piece = cols // 2
    outer, base = a_ref.shape[0], a_ref.shape[1] - 8
    depth = own_ref.shape[1] // outer // 2
    for i in range(3):
        full = mm(own_ref[...], d_ref[i, 0], TN) + mm(oth_ref[...], d_ref[i, 1], TN)
        full = full.astype(BF)
        at = slice(i * piece, (i + 1) * piece)
        both = d_ref[i, 0].astype(F32) + d_ref[i, 1].astype(F32)
        sums = jnp.sum(both, 0, keepdims=True)
        high = sums.astype(BF).astype(F32)
        row = lax.broadcasted_iota(jnp.int32, (8, cols), 0)
        tail = jnp.where(row == 0, high, jnp.where(row == 1, sums - high, 0.0)).astype(BF)
        for x, (near, away) in enumerate(((a_ref, y_ref), (x_ref, xy_ref))):
            part = slice(x * piece, (x + 1) * piece)
            for o in range(outer):
                start = 2 * o * depth
                first = full[start : start + depth, part]
                second = full[start + depth : start + 2 * depth, part]
                near[o, :depth, at] = jnp.where(place == 0, first, second)
                away[o, :depth, at] = jnp.where(place == 0, second, first)
                near[o, base:, at] = tail[:, part]
                away[o, base:, at] = tail[:, part]


def self_grads(info, own, oth, grads, depth):
    half, width = own.shape
    cols = grads.shape[3]
    out = struct((width // depth // 2, tail_start(depth) + 8, 3 * cols // 2), BF)
    return call(
        self_grads_kernel,
        [out] * 4,
        [info, own, oth, grads],
        [SM] + [VM] * 3,
        [VM] * 4,
        name="self_grads",
    )


def self_back_kernel(d_ref, mat_ref, first_ref, keep_ref, send_ref):
    cols = d_ref.shape[3]
    for rel in (1, 0):
        total = mm(d_ref[0, rel], mat_ref[:, :cols], NT)
        for i in (1, 2):
            total = total + mm(d_ref[i, rel], mat_ref[:, i * cols : (i + 1) * cols], NT)
        if rel == 1:
            send_ref[...] = total.astype(BF)
        else:
            keep_ref[...] = total + first_ref[...]


def self_back(grads, mat, first_in):
    half, width = first_in.shape
    cols = grads.shape[3]
    return call(
        self_back_kernel,
        [struct((half, width), F32), struct((half, width), BF)],
        [grads, mat, first_in],
        [VM] * 3,
        [VM] * 2,
        flops=2 * 2 * half * width * 3 * cols * 2,
        moved=half * width * 10 + half * cols * 12 + width * cols * 6,
        name="self_back",
    )


def fetch_kernel(blocks_ref, bank_ref, mine_ref, send_ref, sem):
    rank = lax.axis_index("tensor")
    core, chip = rank % 2, rank // 2
    count = mine_ref.shape[0]
    slots = count // 2
    here = bank_ref.shape[0] // blocks_ref.shape[0]

    def each(act):
        for group, out_ref in enumerate((mine_ref, send_ref)):

            def body(i, carry, group=group, out_ref=out_ref):
                seq = (i // slots + chip) % 2
                half = (group + core) % 2
                at = blocks_ref[seq, half * slots + i % slots] - rank * here
                held = (at >= 0) & (at < here)
                copy = pltpu.make_async_copy(
                    bank_ref.at[jnp.where(held, at + seq * here, 0)],
                    out_ref.at[i],
                    sem.at[group * count + i],
                )
                act(copy, held, out_ref, i)
                return carry

            lax.fori_loop(0, count, body, 0)

    def start(copy, held, out_ref, i):
        @pl.when(held)
        def _():
            copy.start()

        @pl.when(jnp.logical_not(held))
        def _():
            out_ref[i] = jnp.zeros(out_ref.shape[1:], out_ref.dtype)

    def finish(copy, held, out_ref, i):
        @pl.when(held)
        def _():
            copy.wait()

    each(start)
    each(finish)


def fetch(blocks, bank_blocks):
    count = 2 * blocks.shape[1]
    blk, width = bank_blocks.shape[1:]
    out = struct((count // 2, blk, width), BF)
    mine, send = call(
        fetch_kernel,
        [out, out],
        [blocks, bank_blocks],
        [SM, ANY],
        [VM, VM],
        [pltpu.SemaphoreType.DMA((count,))],
        name="fetch",
    )
    return [part.reshape(2, count // 4, blk, width) for part in (mine, send)]


def scatter_kernel(table, a_ref, b_ref, c_ref, d_ref, out_ref, slots, sems):
    step = pl.program_id(0)
    per = out_ref.shape[0]

    @pl.when(step == 0)
    def _():
        copies = [
            pltpu.make_async_copy(ref, slots.at[i], sems.at[i])
            for i, ref in enumerate((a_ref, b_ref, c_ref, d_ref))
        ]
        for copy in copies:
            copy.start()
        for copy in copies:
            copy.wait()

    for i in range(per):
        at = table[step * per + i]
        group = jnp.maximum(at, 0) // slots.shape[1]
        place = jnp.maximum(at, 0) % slots.shape[1]
        value = slots[group, place].astype(F32)
        out_ref[i] = jnp.where(at >= 0, value, 0.0)


def scatter(table, parts):
    count = table.shape[0]
    slots, blk, width = parts[0].shape
    per = 4
    return pl.pallas_call(
        scatter_kernel,
        grid_spec=pltpu.PrefetchScalarGridSpec(
            num_scalar_prefetch=1,
            grid=(count // per,),
            in_specs=[ANY] * 4,
            out_specs=pl.BlockSpec((per, blk, width), lambda i, t: (i, 0, 0)),
            scratch_shapes=[
                pltpu.VMEM((4, slots, blk, width), BF),
                pltpu.SemaphoreType.DMA((4,)),
            ],
        ),
        out_shape=struct((count, blk, width), F32),
        compiler_params=pltpu.CompilerParams(vmem_limit_bytes=VMEM_LIMIT),
        cost_estimate=COST,
        name="scatter",
    )(table, *parts)


def sum_all(ref):
    total = ref[0].astype(F32)
    for i in range(1, ref.shape[0]):
        total = total + ref[i].astype(F32)
    return total


def sum_attn_kernel(
    in_ref, q_ref, so_ref, co_ref, k_ref, v_ref, qb_ref, vb_ref, v0_ref, v1_ref, v2_ref
):
    total = sum_all(in_ref)
    piece = total.shape[1] // 5
    depth = q_ref.shape[0]
    q_ref[...] = total[:depth, :piece]
    so_ref[...] = total[:depth, piece : 2 * piece].T
    co_ref[...] = total[:depth, 2 * piece : 3 * piece].T
    k_ref[...] = total[:depth, 3 * piece : 4 * piece]
    v_ref[...] = total[:depth, 4 * piece :]
    tail = total[total.shape[0] - 16 :]
    qb_ref[...] = (tail[8:9, :piece] + tail[9:10, :piece])[0]
    vb_ref[...] = (tail[8:9, 4 * piece :] + tail[9:10, 4 * piece :])[0]
    for i, ref in enumerate((v0_ref, v1_ref, v2_ref)):
        cols = slice(i * piece, (i + 1) * piece)
        parts = [tail[p : p + 1, cols] + tail[p + 4 : p + 5, cols] for p in range(4)]
        ref[...] = jnp.concatenate(parts, axis=1)[0]


def sum_attn(value, depth):
    count, rows, cols = value.shape
    piece = cols // 5
    wide, tall = struct((depth, piece), F32), struct((piece, depth), F32)
    row, vec = struct((piece,), F32), struct((4 * piece,), F32)
    return call(
        sum_attn_kernel,
        [wide, tall, tall, wide, wide, row, row, vec, vec, vec],
        [value],
        [VM],
        [VM] * 10,
        name="sum_attn",
    )


def sum_cols_kernel(in_ref, *refs):
    count = len(refs) // 2
    total = sum_all(in_ref)
    depth, piece = refs[0].shape
    tail = total[total.shape[0] - 8 :]
    for i in range(count):
        cols = slice(i * piece, (i + 1) * piece)
        refs[i][...] = total[:depth, cols]
        refs[count + i][...] = (tail[0:1, cols] + tail[1:2, cols])[0]


def sum_cols(value, depth, count):
    piece = value.shape[2] // count
    return call(
        sum_cols_kernel,
        [struct((depth, piece), F32)] * count + [struct((piece,), F32)] * count,
        [value],
        [VM],
        [VM] * (2 * count),
        name="sum_cols",
    )


def sum_feed_kernel(in_ref, e_ref, s_ref, eb_ref, *vecs):
    total = sum_all(in_ref)
    depth, cols = e_ref.shape
    e_ref[...] = total[:depth, :cols]
    s_ref[...] = total[:depth, cols:]
    tail = total[total.shape[0] - 8 :]
    eb_ref[...] = (tail[0:1, :cols] + tail[1:2, :cols])[0]
    for i in range(3):
        at = 2 + 2 * i
        vecs[i][...] = (tail[at : at + 1, :cols] + tail[at + 1 : at + 2, :cols])[0]
        at = 2 * i
        vecs[3 + i][...] = (tail[at : at + 1, cols:] + tail[at + 1 : at + 2, cols:])[0]


def sum_feed(value, depth):
    cols = value.shape[2] // 2
    return call(
        sum_feed_kernel,
        [struct((depth, cols), F32)] * 2 + [struct((cols,), F32)] * 7,
        [value],
        [VM],
        [VM] * 9,
        name="sum_feed",
    )


def local(
    tokens,
    bank,
    prefix,
    blocks,
    out_grad,
    selfq_weight,
    selfq_bias,
    selfk_weight,
    selfv_weight,
    selfv_bias,
    selfo_weight,
    selfo_bias,
    first_gain,
    first_shift,
    crossq_weight,
    crossq_bias,
    crossk_weight,
    crossv_weight,
    crossv_bias,
    crosso_weight,
    crosso_bias,
    second_gain,
    second_shift,
    expand_weight,
    expand_bias,
    shrink_weight,
    shrink_bias,
    third_gain,
    third_shift,
):
    rank = lax.axis_index("tensor")
    core = rank % 2
    chip = rank // 2
    inner = lax.axis_index("dp") % 2
    outer = outer_count()
    half, width = tokens.shape
    seq_count = prefix.shape[0]
    local_blocks = bank.shape[1] // BLK
    head_cols = selfq_bias.shape[0]
    hidden_cols = expand_bias.shape[0]
    depth = selfq_weight.shape[0]
    slots = NBLK // 2
    two = 2 * head_cols
    attn_cols = 5 * head_cols
    info = jnp.stack([inner, rank, chip]).astype(jnp.int32)

    part_mine, part_send = fetch(blocks, bank.reshape(seq_count * local_blocks, BLK, width))

    part_got = swap_core(part_send)
    part_away = part_mine[1] + part_got[1]
    part_back = swap_x(part_away)

    self_leaf = call(
        pack_self_kernel,
        struct((outer, depth, 3 * head_cols), BF),
        [gate(selfq_weight, part_away), selfk_weight, selfv_weight],
        [VM] * 3,
        VM,
        name="pack_self",
    )
    bias_own = jnp.concatenate(
        [selfq_bias, selfv_bias, crossq_bias, crossv_bias, expand_bias]
    ).reshape(1, -1)
    bias_two = jnp.concatenate([bias_own, swap_x(bias_own)], axis=0)
    bias_four = jnp.concatenate([bias_two, swap_core(bias_two)], axis=0)
    cq_bias = bias_four[:, two : 3 * head_cols].reshape(-1)
    cv_bias = bias_four[:, 3 * head_cols : 4 * head_cols].reshape(-1)
    ex_bias = bias_four[:, 4 * head_cols :]
    self_bias = jnp.stack(
        [
            bias_two[:, :head_cols].reshape(-1),
            jnp.zeros((two,), F32),
            bias_two[:, head_cols:two].reshape(-1),
        ]
    )
    next_leaf, shrink_leaf = call(
        pack_rest_kernel,
        [
            struct((outer, depth, hidden_cols + attn_cols), BF),
            struct((depth, hidden_cols), BF),
        ],
        [
            gate(crossk_weight, self_leaf, part_away), crossv_weight, crossq_weight, selfo_weight,
            crosso_weight, expand_weight, shrink_weight.T,
        ],
        [VM] * 7,
        [VM] * 2,
        name="pack_rest",
    )
    tokens_oth = swap_core(tokens)
    vecs = jnp.concatenate(
        [
            jnp.stack([crosso_bias, second_gain, second_shift]),
            ex_bias,
            jnp.stack([shrink_bias, third_gain, third_shift]),
        ]
    )
    first_vecs = jnp.stack([selfo_bias, first_gain, first_shift])
    cq_bias, cv_bias = cq_bias.reshape(1, -1), cv_bias.reshape(1, -1)
    my_prefix = lax.dynamic_index_in_dim(prefix, chip, 0, keepdims=False)
    attn_info = jnp.stack([core, my_prefix]).astype(jnp.int32)

    self_z = outer_exchange(self_leaf)

    self_z, self_bias, vecs, first_vecs, cq_bias, cv_bias, next_leaf, attn_info, tokens_oth, part_back = (
        lax.optimization_barrier(
            (self_z, self_bias, vecs, first_vecs, cq_bias, cv_bias, next_leaf, attn_info, tokens_oth, part_back)
        )
    )
    self_near, self_away, self_both = swap_x(self_z), swap_dp(self_z, 1), swap_both(self_z)
    next_z = outer_exchange(next_leaf)

    shrink_leaf = gate(shrink_leaf, self_near)
    shrink_x, shrink_y = swap_x(shrink_leaf), swap_dp(shrink_leaf, 1)
    shrink_xy = swap_both(shrink_leaf)
    shrink_pack = plane_copies(info, shrink_leaf, shrink_x, shrink_y, shrink_xy)
    (
        next_z, tokens_in, self_near, self_away, self_both, shrink_pack, part_got,
    ) = lax.optimization_barrier(
        (next_z, tokens, self_near, self_away, self_both, shrink_pack, part_got)
    )
    expand_z, attn_z = next_z[..., :hidden_cols], next_z[..., hidden_cols:]
    shrink_z = outer_exchange(gate(shrink_pack, next_z))
    attn_x, attn_y, attn_xy = swap_x(attn_z), swap_dp(attn_z, 1), swap_both(attn_z)

    qkv, self_mat, self_own, self_send, self_lse = self_forward(
        jnp.concatenate([info, attn_info]),
        tokens_in,
        tokens_oth,
        self_bias,
        (self_z, self_near, self_away, self_both),
    )
    self_got = swap_core(self_send)
    attn_x, attn_y, attn_xy, self_got = lax.optimization_barrier(
        (attn_x, attn_y, attn_xy, self_got, self_own)
    )[:4]
    attn_own = (attn_z, attn_y, attn_x, attn_xy)
    attn_oth = tuple(swap_core(piece) for piece in attn_own)
    attn_oth, expand_z = lax.optimization_barrier((attn_oth, expand_z))
    expand_x, expand_y = swap_x(expand_z), swap_dp(expand_z, 1)
    cross_kv, cross_q, self_o, cross_o = assemble(info, attn_own + attn_oth)
    cross_kv, expand_x, expand_y = lax.optimization_barrier((cross_kv, expand_x, expand_y))
    expand_xy = swap_both(expand_z)
    fetched, kv_own = project_kv(
        (part_mine[0] + part_got[0]).reshape(slots * BLK, width),
        part_back.reshape(slots * BLK, width),
        cross_kv,
        cv_bias,
    )
    self_got, kv_own = lax.optimization_barrier((self_got, kv_own))
    kv_oth = swap_core(kv_own)
    first_sum, first_out, first_low, queries, mixed_one = first_forward(
        tokens,
        self_own,
        self_got,
        self_o,
        first_vecs,
        cross_q,
        cq_bias,
    )

    queries, kv_oth = lax.optimization_barrier((queries, kv_oth))
    queries, shrink_z = lax.optimization_barrier((queries, shrink_z))
    mixed_two, cross_lse = cross_forward(queries, kv_own, kv_oth)

    expand_oth = tuple(swap_core(piece) for piece in (expand_z, expand_y, expand_x))
    expand_xy, expand_oth, mixed_two = lax.optimization_barrier((expand_xy, expand_oth, mixed_two))
    expand_own = (expand_z, expand_y, expand_x, expand_xy)
    expand_oth = expand_oth + (swap_core(expand_xy),)
    (
        out_act, second_in, cross_low, cross_grad,
        feed_keep, feed_send,
    ) = feed(
        info, mixed_two, first_out, out_grad, vecs, cross_o,
        expand_own + expand_oth, (shrink_z, swap_core(shrink_z)),
    )

    def plane_send(keep, got):
        return tuple(add_low(keep[x, y], got[x, y]) for x, y in ((1, 0), (0, 1), (1, 1)))

    def plane_swap(parts):
        return swap_x(parts[0]), swap_dp(parts[1], 1), swap_both(parts[2])

    def plane_sum(own, got):
        total = sum(part.astype(F32) for part in own)
        return total + sum(part.astype(F32) for part in got)

    def fold(value, dtype):
        return jnp.sum(value.astype(F32), axis=0).astype(dtype)

    feed_got = swap_core(feed_send)
    part_one = cross_backward(queries, kv_own, kv_oth, mixed_two, cross_lse, cross_grad, 0, 2)
    feed_keep = gate(feed_keep, part_one[0])

    def feed_sum(x, y, which, *others):
        at = (x, y, Ellipsis, slice(which * hidden_cols, (which + 1) * hidden_cols))
        total = feed_keep[at].astype(F32) + feed_got[at].astype(F32)
        for other in others:
            total = total + other.astype(F32)
        return total.astype(BF)

    expand_send = feed_sum(1, slice(None), 0)
    shrink_send = feed_sum(slice(None), 1, 1)
    expand_send, shrink_send, part_one = lax.optimization_barrier(
        (expand_send, shrink_send, tuple(part_one))
    )
    expand_got = swap_x(expand_send)
    shrink_got = swap_dp(shrink_send, 1)

    dq, dkv_own, dkv_send, first_in, self_low, grad_own, grad_send, early_vec = cross_first_backward(
        queries, kv_own, kv_oth, mixed_two, cross_lse, cross_grad, 2, part_one,
        cross_q, second_in, first_sum, first_gain.reshape(1, -1), self_o,
    )
    expand_got, shrink_got, dkv_send, grad_send = lax.optimization_barrier(
        (expand_got, shrink_got, dkv_send, grad_send)
    )
    dkv_got = swap_core(dkv_send)
    grad_got = swap_core(grad_send)
    expand_send = feed_sum(0, 1, 0, expand_got[1])
    shrink_send = feed_sum(1, 0, 1, shrink_got[1])
    self_low, dkv_got, grad_got, expand_send, shrink_send = lax.optimization_barrier(
        (self_low, dkv_got, grad_got, expand_send, shrink_send)
    )
    expand_last = swap_dp(expand_send, 1)
    shrink_last = swap_x(shrink_send)
    attn_keep, attn_send, fetched_grad = attn_grads(
        info,
        (
            first_low, dq, self_low, mixed_one, cross_low, mixed_two, early_vec,
            fetched, dkv_own, dkv_got, cross_kv,
        ),
        depth,
    )
    attn_send, grad_got, expand_last, shrink_last = lax.optimization_barrier(
        (attn_send, grad_got, expand_last, shrink_last)
    )
    attn_got = swap_core(attn_send)
    feed_three = jnp.concatenate(
        [
            feed_sum(0, 0, 0, expand_got[0], expand_last),
            feed_sum(0, 0, 1, shrink_got[0], shrink_last),
        ],
        axis=-1,
    )
    feed_three, grad_got = lax.optimization_barrier((feed_three, grad_got))
    feed_last = outer_exchange(feed_three)

    self_args = (attn_info, qkv, self_own, self_send, self_lse, grad_own, grad_got)
    pairs = two // 128
    half_grads = self_backward(*self_args, 0, pairs - 1)
    attn_plane, half_grads, fetched_away = lax.optimization_barrier(
        (plane_send(gate(attn_keep, half_grads), attn_got), half_grads, swap_x(fetched_grad))
    )
    fetched_away = fetched_away.reshape(slots, BLK, width)
    fetched_near = fetched_grad.reshape(slots, BLK, width)
    attn_parts = plane_swap(attn_plane)
    grads = self_backward(*self_args, pairs - 1, 1, (half_grads,))
    self_places = self_grads(info, tokens, tokens_oth, grads, depth)
    self_places, grads = lax.optimization_barrier((tuple(self_places), grads))
    self_parts = (swap_x(self_places[1]), swap_dp(self_places[2], 1), swap_both(self_places[3]))
    back_keep, back_send = self_back(grads, self_mat, first_in)
    back_send, feed_last, attn_parts = lax.optimization_barrier((back_send, feed_last, attn_parts))
    attn_three = plane_sum((attn_keep[0, 0], attn_got[0, 0]), attn_parts).astype(BF)
    attn_last = outer_exchange(attn_three)
    self_three = plane_sum((self_places[0],), self_parts).astype(BF)
    self_last = outer_exchange(
        gate(self_three, attn_last)
    )
    back_got = swap_core(gate(back_send, self_three))
    in_grad = (back_keep + back_got.astype(F32)).astype(BF)

    (
        cq_grad, so_grad, co_grad, ck_grad, cv_grad, cq_rows, cv_rows,
        first_shift_rows, first_gain_rows, so_rows,
    ) = sum_attn(attn_last, depth)
    sq_grad, sk_grad, sv_grad, sq_rows, sk_rows, sv_rows = sum_cols(self_last, depth, 3)
    (
        expand_grad, shrink_grad, expand_rows, third_shift_rows, third_gain_rows, shrink_rows,
        second_shift_rows, second_gain_rows, co_rows,
    ) = sum_feed(feed_last, depth)
    shrink_grad = shrink_grad.T

    near_core = swap_core(gate(fetched_near, self_three))
    away_core = swap_core(gate(fetched_away, near_core))
    slot_ids = jnp.arange(NBLK)
    places = (
        (((slot_ids[None, :] // slots) != core) * 2 + (jnp.arange(seq_count)[:, None] != chip))
        * slots
        + slot_ids[None, :] % slots
    )
    hits = blocks[:, None, :] == (rank * local_blocks + jnp.arange(local_blocks))[None, :, None]
    scatter_table = jnp.max(jnp.where(hits, places[:, None, :], -1), axis=-1)
    bank_grad = scatter(
        scatter_table.reshape(-1).astype(jnp.int32),
        (fetched_near, fetched_away, near_core, away_core),
    ).reshape(bank.shape)

    def line(row):
        return row.reshape(-1)

    return (
        out_act,
        in_grad,
        bank_grad,
        sq_grad,
        line(sq_rows),
        sk_grad,
        sv_grad,
        line(sv_rows),
        so_grad,
        line(so_rows),
        line(first_gain_rows),
        line(first_shift_rows),
        cq_grad,
        line(cq_rows),
        ck_grad,
        cv_grad,
        line(cv_rows),
        co_grad,
        line(co_rows),
        line(second_gain_rows),
        line(second_shift_rows),
        expand_grad,
        line(expand_rows),
        shrink_grad,
        line(shrink_rows),
        line(third_gain_rows),
        line(third_shift_rows),
    )


def solution(mesh):
    rows = P(("dp", "tensor"), None)
    wide = P("dp", "tensor")
    tall = P("tensor", "dp")
    part = P("tensor")
    full = P()
    return jax.shard_map(
        local,
        mesh=mesh,
        in_specs=(
            rows, P("dp", "tensor", None), P("dp"), P("dp", None), rows,
            wide, part, wide, wide, part, tall, full, full, full,
            wide, part, wide, wide, part, tall, full, full, full,
            wide, part, tall, full, full, full,
        ),
        out_specs=(
            rows, rows, P("dp", "tensor", None),
            wide, part, wide, wide, part, tall, full, full, full,
            wide, part, wide, wide, part, tall, full, full, full,
            wide, part, tall, full, full, full,
        ),
        check_vma=False,
    )
```
